32 devices in a mesh: wide: 4 (over y, x), narrow: 8 (over z, core).
Axes of the slice: x: 2, y: 2, z: 4, core: 2. Of those that a mesh axis runs over, the one named last changes fastest.
Arguments:
- tokens: bfloat16 [16384, 1024], P(('wide', 'narrow')), may hold values from -6 to 6
- cotangent: bfloat16 [16384, 1024], P(('wide', 'narrow')), may hold values from -6 to 6
- item_lengths: int32 [4, 4], P('wide'), may hold values from 0 to 4096, as said below
- attn_gain: bfloat16 [1024], replicated, may hold values from 0.099609375 to 1.8984375
- attn_bias: bfloat16 [1024], replicated, may hold values from -0.099609375 to 0.099609375
- qkv_weight: bfloat16 [1024, 3072], P(None, 'narrow'), may hold values from -0.1875 to 0.1875
- proj_weight: bfloat16 [1024, 1024], P('narrow'), may hold values from -3 to 3
- mlp_gain: bfloat16 [1024], replicated, may hold values from 0.099609375 to 1.8984375
- mlp_bias: bfloat16 [1024], replicated, may hold values from -0.19921875 to 0.19921875
- up_weight: bfloat16 [1024, 4096], P(None, 'narrow'), may hold values from -0.1875 to 0.1875
- down_weight: bfloat16 [4096, 1024], P('narrow'), may hold values from -0.09375 to 0.09375
Outputs:
- output: bfloat16 [16384, 1024], P(('wide', 'narrow'))
- grad_tokens: bfloat16 [16384, 1024], P(('wide', 'narrow'))
- grad_attn_gain: float32 [1024], P('narrow')
- grad_attn_bias: float32 [1024], P('narrow')
- grad_qkv: float32 [1024, 3072], P(None, 'narrow')
- grad_proj: float32 [1024, 1024], P('narrow')
- grad_mlp_gain: float32 [1024], P('narrow')
- grad_mlp_bias: float32 [1024], P('narrow')
- grad_up: float32 [1024, 4096], P(None, 'narrow')
- grad_down: float32 [4096, 1024], P('narrow')
The draws below stay inside these ranges and needn't reach their ends.
Inputs may be any that keep to these rules, and one draw needn't show every extreme that they name: `item_lengths`: each row sums to 4096. In every draw one wide position holds a single item of 4096 patches followed by zeros; every other position holds 4 items of 1024 plus or minus up to 3 * (128) patches.
All inputs are finite; a program needn't handle non-finite values.
Results may differ from the reference program's by a relative error of at most 0.015.
Values may be sent and summed in bfloat16 or wider, within the bound.
A program may use at most 192 MiB of HBM per device.

```python
import jax
import jax.numpy as jnp
from jax import lax

D = 1024
HEADS = 16
HEAD_DIM = 64
FF = 4096
CAP = 4096
ITEMS_DEV = 4
QBLOCK = 512
ROWS = 16384
N_WIDE = 4


def draw_item_lengths(key, part):
    long_key = jax.random.fold_in(key, 11)
    jitter_key = jax.random.fold_in(key, 12)
    long_position = jax.random.randint(long_key, (), 0, N_WIDE)
    jitter_step = CAP // (8 * ITEMS_DEV)
    base_length = CAP // ITEMS_DEV
    shifts = jax.random.randint(jitter_key, (N_WIDE, ITEMS_DEV // 2), -3, 4)
    paired = jnp.stack([shifts, -shifts], axis=-1).reshape(N_WIDE, ITEMS_DEV)
    short_rows = base_length + jitter_step * paired
    long_row = jnp.zeros((ITEMS_DEV,), jnp.int32).at[0].set(CAP)
    position = jnp.arange(N_WIDE, dtype=jnp.int32)
    return jnp.where((position == long_position)[:, None], long_row[None, :], short_rows).astype(jnp.int32)


def block_scale(key, extent, split, low, top_value):
    def one(dim, parts):
        heights = jax.random.uniform(jax.random.fold_in(jax.random.fold_in(key, 6), dim), (parts,), jnp.float32, low / len(split), top_value / len(split))
        return jnp.repeat(jnp.exp(heights), extent[dim] // parts).reshape((-1,) + (1,) * (len(extent) - dim - 1))

    gain = one(*split[0])
    for cut in split[1:]:
        gain = gain * one(*cut)
    return gain


def normal_values(key, shape, spread, reach, shards=(), kind=jnp.bfloat16):
    values = jax.random.normal(key, shape, jnp.float32) * spread
    if len(shards) > 0:
        values = block_scale(key, shape, shards, -0.22, 0.18) * values
    return jnp.clip(values, min=-reach, max=reach).astype(kind)


def setup_inputs(seed: int = 0) -> dict:
    splits = jax.random.split(jax.random.key(seed), 12)
    tokens = normal_values(splits[0], (ROWS, D), 1.0, 6.0, ((0, 32),))
    cotangent = normal_values(splits[1], (ROWS, D), 1.0, 6.0, ((0, 32),))
    item_lengths = draw_item_lengths(jax.random.fold_in(splits[11], 71), 0)
    attn_gain = jnp.clip(1.0 + 0.18 * jax.random.normal(splits[3], (D,), jnp.float32), 0.099609375, 1.8984375).astype(jnp.bfloat16)
    attn_bias = jnp.clip(jax.random.uniform(splits[4], (D,), jnp.float32, -0.099609375, 0.099609375), -0.099609375, 0.099609375).astype(jnp.bfloat16)
    qkv_weight = normal_values(splits[5], (D, 3 * HEADS * HEAD_DIM), D ** -0.5, 0.1875, ((1, 8),))
    proj_weight = normal_values(splits[6], (HEADS * HEAD_DIM, D), (max(1, 16 * D // CAP)) ** -0.5, 3.0, ((0, 8),))
    mlp_gain = jnp.clip(1.0 + 0.18 * jax.random.normal(splits[7], (D,), jnp.float32), 0.099609375, 1.8984375).astype(jnp.bfloat16)
    mlp_bias = jnp.clip(jax.random.uniform(splits[8], (D,), jnp.float32, -0.19921875, 0.19921875), -0.19921875, 0.19921875).astype(jnp.bfloat16)
    up_weight = normal_values(splits[9], (D, FF), D ** -0.5, 0.1875, ((1, 8),))
    down_weight = normal_values(splits[10], (FF, D), FF ** -0.5, 0.09375, ((0, 8),))
    return {"tokens": tokens, "cotangent": cotangent, "item_lengths": item_lengths, "attn_gain": attn_gain, "attn_bias": attn_bias, "qkv_weight": qkv_weight, "proj_weight": proj_weight, "mlp_gain": mlp_gain, "mlp_bias": mlp_bias, "up_weight": up_weight, "down_weight": down_weight}


epsilon = 1e-05

@jax.custom_vjp
def low(v):
    return lax.optimization_barrier(v.astype(jnp.bfloat16)).astype(jnp.float32)

@jax.custom_vjp
def low_back(v):
    return v

def low_keep(v):
    return (low(v), None)

def low_pass(kept, grad):
    return (grad,)

def back_keep(v):
    return (v, None)

def back_low(kept, grad):
    return (low(grad),)
low.defvjp(low_keep, low_pass)
low_back.defvjp(back_keep, back_low)

def matmul(left_side, right_side):
    return jnp.dot(left_side, right_side, precision=lax.Precision.HIGHEST, preferred_element_type=jnp.float32)

def layer_norm(values, norm_gain, norm_bias):
    average = lax.optimization_barrier(jnp.mean(values, axis=-1, keepdims=True))
    centred = values - average
    variance = lax.optimization_barrier(jnp.mean(centred * centred, axis=-1, keepdims=True))
    return centred * lax.rsqrt(variance + epsilon) * norm_gain + norm_bias

def attention(packed, segment):
    queries = packed[:, :, 0]
    keys_all = packed[:, :, 1]
    values_all = packed[:, :, 2]
    score_scale = HEAD_DIM ** (-0.5)
    blocks = CAP // QBLOCK

    def one_block(block_in):
        query_block, segment_block = block_in
        scores = jnp.einsum('qhd,khd->hqk', query_block, keys_all, precision=lax.Precision.HIGHEST) * score_scale
        scores = low_back(scores)
        same_item = segment_block[:, None] == segment[None, :]
        scores = jnp.where(same_item[None], scores, -1e+30)
        maximum = lax.optimization_barrier(jnp.max(scores, axis=-1, keepdims=True))
        raised = jnp.exp(scores - maximum)
        probability = raised / lax.optimization_barrier(jnp.sum(raised, axis=-1, keepdims=True))
        return jnp.einsum('hqk,khd->qhd', low(probability), values_all, precision=lax.Precision.HIGHEST)
    attended = lax.map(jax.checkpoint(one_block), (queries.reshape(blocks, QBLOCK, HEADS, HEAD_DIM), segment.reshape(blocks, QBLOCK)))
    return attended.reshape(CAP, HEADS * HEAD_DIM)

def block_forward(tokens, segment, params):
    qkv_weight, proj_weight, up_weight, down_weight, attn_gain, attn_bias, mlp_gain, mlp_bias = params
    normed = low(layer_norm(tokens, attn_gain, attn_bias))
    packed = low(low_back(matmul(normed, qkv_weight)))
    attended = low(low_back(attention(packed.reshape(CAP, HEADS, 3, HEAD_DIM), segment)))
    middle = tokens + low_back(matmul(attended, proj_weight))
    expand_in = low(layer_norm(middle, mlp_gain, mlp_bias))
    hidden = low(jax.nn.gelu(low_back(matmul(expand_in, up_weight)), approximate=False))
    return middle + matmul(hidden, down_weight)

def reference(tokens, cotangent, item_lengths, attn_gain, attn_bias, qkv_weight, proj_weight, mlp_gain, mlp_bias, up_weight, down_weight):
    weights = tuple((matrix.astype(jnp.float32) for matrix in (qkv_weight, proj_weight, up_weight, down_weight, attn_gain, attn_bias, mlp_gain, mlp_bias)))
    token_blocks = tokens.astype(jnp.float32).reshape(N_WIDE, CAP, D)
    grad_blocks = cotangent.astype(jnp.float32).reshape(N_WIDE, CAP, D)
    row_index = jnp.arange(CAP, dtype=jnp.int32)

    def per_position(totals, position_in):
        token_rows, grad_rows, lengths = position_in
        item_ends = jnp.cumsum(lengths).astype(jnp.int32)
        segment = lax.optimization_barrier(jnp.sum((row_index[:, None] >= item_ends[None, :]).astype(jnp.int32), axis=1))

        def forward(token_in, *params):
            return block_forward(token_in, segment, params)
        output, pullback = jax.vjp(forward, token_rows, *weights)
        gradients = pullback(grad_rows)
        totals = tuple((running + gradient for running, gradient in zip(totals, gradients[1:])))
        return (totals, (output.astype(jnp.bfloat16), gradients[0].astype(jnp.bfloat16)))
    initial = tuple((jnp.zeros(matrix.shape, jnp.float32) for matrix in weights))
    totals, (outputs, input_grads) = lax.scan(per_position, initial, (token_blocks, grad_blocks, item_lengths))
    return (outputs.reshape(N_WIDE * CAP, D), input_grads.reshape(N_WIDE * CAP, D), totals[4], totals[5], totals[0], totals[1], totals[6], totals[7], totals[2], totals[3])
```

```python
import functools

import jax
import jax.numpy as jnp
from jax import lax
from jax.experimental import pallas as pl
from jax.experimental.pallas import tpu as pltpu
from jax.sharding import PartitionSpec as P

HEAD_DIM = 64
EXTRA = 16
EXCLUDED = -1e30
bf16 = jnp.bfloat16
f32 = jnp.float32
epsilon = 1e-05


def norm_forward(values, norm_gain, norm_bias):
    average = jnp.mean(values, axis=-1, keepdims=True)
    centred = values - average
    variance = jnp.mean(centred * centred, axis=-1, keepdims=True)
    return centred * lax.rsqrt(variance + epsilon) * norm_gain + norm_bias


def gelu_exact(values):
    return jax.nn.gelu(values, approximate=False)


def mask_rows(item_lengths, rows):
    lengths = item_lengths[0]
    items = lengths.shape[0]
    index = jnp.arange(items)
    ends = jnp.sum(jnp.where(index[:, None] >= index[None, :], lengths[None, :], 0), axis=1)
    segment = jnp.sum((jnp.arange(rows)[None, :] >= ends[:, None]).astype(jnp.int32), axis=0)
    extra = jnp.arange(EXTRA)[:, None]
    own = segment[None, :] == extra
    query_extra = jnp.where(own & (extra <= items), 1.0, 0.0).astype(bf16)
    key_extra = jnp.where(
        extra <= items,
        jnp.where(own, 0.0, EXCLUDED),
        jnp.where(extra <= items + 3, 1.0, 0.0),
    ).astype(bf16)
    return query_extra, key_extra


def forward_kernel(block, rows, qx_ref, kx_ref, q_ref, k_ref, v_ref, o_ref, log_ref, keys):
    width = q_ref.shape[-1]

    @pl.when(pl.program_id(1) == 0)
    def _():
        keys[...] = jnp.concatenate([k_ref[0], kx_ref[...]], axis=0).T

    query = jnp.concatenate([q_ref[0] * jnp.asarray(0.125, bf16), qx_ref[...]], axis=0)
    maximum = jnp.full((1, width), -3e38, f32)
    total = jnp.zeros((1, width), f32)
    gathered = jnp.zeros((HEAD_DIM, width), f32)
    for i in range(rows // block):
        part = pl.ds(i * block, block)
        scores = jnp.dot(keys[part, :], query, preferred_element_type=f32)
        larger = jnp.maximum(maximum, jnp.max(scores, axis=0, keepdims=True))
        raised = jnp.exp(scores - larger)
        shrink = jnp.exp(maximum - larger)
        total = shrink * total + jnp.sum(raised, axis=0, keepdims=True)
        gathered = shrink * gathered + jnp.dot(
            v_ref[0, :, part], raised.astype(bf16), preferred_element_type=f32
        )
        maximum = larger
    o_ref[0] = (gathered / total).astype(bf16)
    log_ref[0] = maximum + jnp.log(total)


def attend_forward(packed, query_extra, key_extra, width=1024, block=1024):
    heads, _, _, rows = packed.shape

    def whole(j):
        return pl.BlockSpec((1, None, HEAD_DIM, rows), lambda h, i: (h, j, 0, 0))

    return pl.pallas_call(
        functools.partial(forward_kernel, block, rows),
        grid=(heads, rows // width),
        in_specs=[
            pl.BlockSpec((EXTRA, width), lambda h, i: (0, i)),
            pl.BlockSpec((EXTRA, rows), lambda h, i: (0, 0)),
            pl.BlockSpec((1, None, HEAD_DIM, width), lambda h, i: (h, 0, 0, i)),
            whole(1),
            whole(2),
        ],
        out_specs=(
            pl.BlockSpec((1, HEAD_DIM, width), lambda h, i: (h, 0, i)),
            pl.BlockSpec((1, 1, width), lambda h, i: (h, 0, i)),
        ),
        out_shape=(
            jax.ShapeDtypeStruct((heads, HEAD_DIM, rows), bf16),
            jax.ShapeDtypeStruct((heads, 1, rows), f32),
        ),
        scratch_shapes=[pltpu.VMEM((rows, HEAD_DIM + EXTRA), bf16)],
        compiler_params=pltpu.CompilerParams(vmem_limit_bytes=48 << 20),
        cost_estimate=pl.CostEstimate(
            flops=4 * heads * rows * rows * 256,
            bytes_accessed=heads * rows * HEAD_DIM * 8,
            transcendentals=heads * rows * rows,
        ),
        name="attend_forward",
    )(query_extra, key_extra, packed, packed, packed)


def backward_kernel(
    block, rows, items, qx_ref, kx_ref, q_ref, k_ref, v_ref, o_ref, do_ref, log_ref,
    grad_ref, keys, values, grad_k, grad_v,
):
    width = q_ref.shape[-1]
    step = pl.program_id(1)

    @pl.when(step == 0)
    def _():
        keys[...] = jnp.concatenate([k_ref[0], kx_ref[...]], axis=0)
        values[...] = jnp.concatenate([v_ref[0], kx_ref[...]], axis=0)
        grad_k[...] = jnp.zeros_like(grad_k)
        grad_v[...] = jnp.zeros_like(grad_v)

    row = lax.broadcasted_iota(jnp.int32, (EXTRA, width), 0) - items

    def pieces(term, base):
        high = term.astype(bf16).astype(f32)
        middle = (term - high).astype(bf16).astype(f32)
        small = term - high - middle
        return jnp.where(
            row == 1, high, jnp.where(row == 2, middle, jnp.where(row == 3, small, base))
        ).astype(bf16)

    query = q_ref[0] * jnp.asarray(0.125, bf16)
    grad = do_ref[0]
    inner = jnp.sum(grad.astype(f32) * o_ref[0].astype(f32), axis=0, keepdims=True)
    query_wide = jnp.concatenate(
        [query, pieces(-log_ref[0], qx_ref[...].astype(f32))], axis=0
    ).T
    grad_wide = jnp.concatenate(
        [grad, pieces(-inner, jnp.zeros((EXTRA, width), f32))], axis=0
    ).T
    grad_q = jnp.zeros((HEAD_DIM, width), f32)
    for i in range(rows // block):
        part = pl.ds(i * block, block)
        probs = jnp.exp(jnp.dot(query_wide, keys[:, part], preferred_element_type=f32))
        grad_scores = (
            probs * jnp.dot(grad_wide, values[:, part], preferred_element_type=f32)
        ).astype(bf16)
        grad_v[:, part] += jnp.dot(grad, probs.astype(bf16), preferred_element_type=f32)
        grad_k[:, part] += jnp.dot(query, grad_scores, preferred_element_type=f32)
        grad_q += lax.dot_general(
            k_ref[0, :, part], grad_scores, (((1,), (1,)), ((), ())), preferred_element_type=f32
        )
    grad_ref[0, 0, :, pl.ds(pl.multiple_of(step * width, width), width)] = (
        grad_q * 0.125
    ).astype(bf16)

    @pl.when(step == pl.num_programs(1) - 1)
    def _():
        grad_ref[0, 1] = grad_k[...].astype(bf16)
        grad_ref[0, 2] = grad_v[...].astype(bf16)


def attend_backward(packed, query_extra, key_extra, attended, grad, log_total, items, width=1024, block=512):
    heads, _, _, rows = packed.shape

    def whole(j):
        return pl.BlockSpec((1, None, HEAD_DIM, rows), lambda h, i: (h, j, 0, 0))

    part = pl.BlockSpec((1, HEAD_DIM, width), lambda h, i: (h, 0, i))
    return pl.pallas_call(
        functools.partial(backward_kernel, block, rows, items),
        grid=(heads, rows // width),
        in_specs=[
            pl.BlockSpec((EXTRA, width), lambda h, i: (0, i)),
            pl.BlockSpec((EXTRA, rows), lambda h, i: (0, 0)),
            pl.BlockSpec((1, None, HEAD_DIM, width), lambda h, i: (h, 0, 0, i)),
            whole(1),
            whole(2),
            part,
            part,
            pl.BlockSpec((1, 1, width), lambda h, i: (h, 0, i)),
        ],
        out_specs=pl.BlockSpec((1, 3, HEAD_DIM, rows), lambda h, i: (h, 0, 0, 0)),
        out_shape=jax.ShapeDtypeStruct((heads, 3, HEAD_DIM, rows), bf16),
        scratch_shapes=[
            pltpu.VMEM((HEAD_DIM + EXTRA, rows), bf16),
            pltpu.VMEM((HEAD_DIM + EXTRA, rows), bf16),
            pltpu.VMEM((HEAD_DIM, rows), f32),
            pltpu.VMEM((HEAD_DIM, rows), f32),
        ],
        compiler_params=pltpu.CompilerParams(vmem_limit_bytes=48 << 20),
        cost_estimate=pl.CostEstimate(
            flops=10 * heads * rows * rows * 256,
            bytes_accessed=heads * rows * HEAD_DIM * 16,
            transcendentals=heads * rows * rows,
        ),
        name="attend_backward",
    )(query_extra, key_extra, packed, packed, packed, attended, grad, log_total)


def product(spec, left, right):
    return jnp.einsum(spec, left, right, preferred_element_type=f32)


def scatter_rows(partial_sum):
    return lax.psum_scatter(
        partial_sum.astype(bf16), "narrow", scatter_dimension=0, tiled=True
    ).astype(f32)


def body(
    tokens, cotangent, item_lengths, attn_gain, attn_bias, qkv_weight, proj_weight,
    mlp_gain, mlp_bias, up_weight, down_weight,
):
    items = item_lengths.shape[1]
    token_rows = tokens.astype(f32)
    heads = qkv_weight.shape[1] // (3 * HEAD_DIM)
    gain_one, bias_one = attn_gain.astype(f32), attn_bias.astype(f32)
    gain_two, bias_two = mlp_gain.astype(f32), mlp_bias.astype(f32)
    normed = norm_forward(token_rows, gain_one, bias_one).astype(bf16)
    normed_all = lax.all_gather(normed, "narrow", axis=0, tiled=True)
    rows = normed_all.shape[0]
    query_extra, key_extra = mask_rows(item_lengths, rows)
    packed = (
        product("rd,dc->cr", normed_all, qkv_weight).astype(bf16).reshape(heads, 3, HEAD_DIM, rows)
    )
    attended, log_total = attend_forward(packed, query_extra, key_extra)
    attended_flat = attended.reshape(heads * HEAD_DIM, rows)
    branch = scatter_rows(product("ar,ad->rd", attended_flat, proj_weight))
    middle = token_rows + branch
    expand_in = norm_forward(middle, gain_two, bias_two).astype(bf16)
    expand_all = lax.all_gather(expand_in, "narrow", axis=0, tiled=True)
    hidden_pre = product("rd,df->rf", expand_all, up_weight)
    hidden = gelu_exact(hidden_pre).astype(bf16)
    output = (middle + scatter_rows(product("rf,fd->rd", hidden, down_weight))).astype(bf16)

    grad_rows = lax.all_gather(cotangent, "narrow", axis=0, tiled=True)
    grad_down = product("rf,rd->fd", hidden, grad_rows)
    grad_hidden = product("rd,fd->rf", grad_rows, down_weight)
    grad_pre = jax.vjp(gelu_exact, hidden_pre)[1](grad_hidden)[0].astype(bf16)
    grad_up = product("rd,rf->df", expand_all, grad_pre)
    grad_expand = scatter_rows(product("rf,df->rd", grad_pre, up_weight))
    grad_middle_norm, grad_gain_two, grad_bias_two = jax.vjp(
        norm_forward, middle, gain_two, bias_two
    )[1](grad_expand)
    grad_middle = cotangent.astype(f32) + grad_middle_norm
    grad_branch_all = lax.all_gather(grad_middle.astype(bf16), "narrow", axis=0, tiled=True)
    grad_proj = product("ar,rd->ad", attended_flat, grad_branch_all)
    grad_attended = (
        product("rd,ad->ar", grad_branch_all, proj_weight)
        .astype(bf16)
        .reshape(heads, HEAD_DIM, rows)
    )
    grad_packed = attend_backward(
        packed, query_extra, key_extra, attended, grad_attended, log_total, items
    ).reshape(heads * 3 * HEAD_DIM, rows)
    grad_qkv = product("rd,cr->dc", normed_all, grad_packed)
    grad_normed = scatter_rows(product("cr,dc->rd", grad_packed, qkv_weight))
    grad_token_norm, grad_gain_one, grad_bias_one = jax.vjp(
        norm_forward, token_rows, gain_one, bias_one
    )[1](grad_normed)
    grad_tokens = (grad_middle + grad_token_norm).astype(bf16)
    norm_parts = jnp.stack([grad_gain_one, grad_bias_one, grad_gain_two, grad_bias_two])
    norm_shares = lax.psum_scatter(norm_parts, "narrow", scatter_dimension=1, tiled=True)

    def over_items(share):
        return lax.psum(share.astype(bf16), "wide").astype(f32)

    shares = over_items(norm_shares)
    return (
        output, grad_tokens, shares[0], shares[1], over_items(grad_qkv), over_items(grad_proj),
        shares[2], shares[3], over_items(grad_up), over_items(grad_down),
    )


def solution(mesh):
    by_rows = P(("wide", "narrow"), None)
    return jax.shard_map(
        body,
        mesh=mesh,
        in_specs=(
            by_rows, by_rows, P("wide", None), P(), P(), P(None, "narrow"), P("narrow", None),
            P(), P(), P(None, "narrow"), P("narrow", None),
        ),
        out_specs=(
            by_rows, by_rows, P("narrow"), P("narrow"), P(None, "narrow"), P("narrow", None),
            P("narrow"), P("narrow"), P(None, "narrow"), P("narrow", None),
        ),
        check_vma=False,
    )
```

```python
import functools
import math

import jax
import jax.numpy as jnp
from jax import lax
from jax.experimental import pallas as pl
from jax.experimental.pallas import tpu as pltpu
from jax.sharding import PartitionSpec as P

HEAD_DIM = 64
EXTRA = 16
EXCLUDED = -1e30
bf16 = jnp.bfloat16
f32 = jnp.float32
MESH = pl.DeviceIdType.MESH
epsilon = 1e-05


def norm_forward(values, norm_gain, norm_bias):
    average = jnp.mean(values, axis=-1, keepdims=True)
    centred = values - average
    variance = jnp.mean(centred * centred, axis=-1, keepdims=True)
    return centred * lax.rsqrt(variance + epsilon) * norm_gain + norm_bias


def gelu_exact(values):
    return jax.nn.gelu(values, approximate=False)


def mask_rows(item_lengths, rows):
    lengths = item_lengths[0]
    items = lengths.shape[0]
    index = jnp.arange(items)
    ends = jnp.sum(jnp.where(index[:, None] >= index[None, :], lengths[None, :], 0), axis=1)
    segment = jnp.sum((jnp.arange(rows)[None, :] >= ends[:, None]).astype(jnp.int32), axis=0)
    extra = jnp.arange(EXTRA)[:, None]
    own = segment[None, :] == extra
    query_extra = jnp.where(own & (extra <= items), 1.0, 0.0).astype(bf16)
    key_extra = jnp.where(
        extra <= items,
        jnp.where(own, 0.0, EXCLUDED),
        jnp.where(extra <= items + 3, 1.0, 0.0),
    ).astype(bf16)
    return query_extra, key_extra


def forward_kernel(block, rows, qx_ref, kx_ref, q_ref, k_ref, v_ref, o_ref, log_ref, keys):
    width = q_ref.shape[-1]

    @pl.when(pl.program_id(1) == 0)
    def _():
        keys[...] = jnp.concatenate([k_ref[0], kx_ref[...]], axis=0).T

    query = jnp.concatenate([q_ref[0] * jnp.asarray(0.125, bf16), qx_ref[...]], axis=0)
    maximum = jnp.full((1, width), -3e38, f32)
    total = jnp.zeros((1, width), f32)
    gathered = jnp.zeros((HEAD_DIM, width), f32)
    for i in range(rows // block):
        part = pl.ds(i * block, block)
        scores = jnp.dot(keys[part, :], query, preferred_element_type=f32)
        larger = jnp.maximum(maximum, jnp.max(scores, axis=0, keepdims=True))
        raised = jnp.exp(scores - larger)
        shrink = jnp.exp(maximum - larger)
        total = shrink * total + jnp.sum(raised, axis=0, keepdims=True)
        gathered = shrink * gathered + jnp.dot(
            v_ref[0, :, part], raised.astype(bf16), preferred_element_type=f32
        )
        maximum = larger
    o_ref[0] = (gathered / total).astype(bf16)
    log_ref[0] = maximum + jnp.log(total)


def attend_forward(packed, query_extra, key_extra, width=1024, block=1024):
    heads, _, _, rows = packed.shape

    def whole(j):
        return pl.BlockSpec((1, None, HEAD_DIM, rows), lambda h, i: (h, j, 0, 0))

    return pl.pallas_call(
        functools.partial(forward_kernel, block, rows),
        grid=(heads, rows // width),
        in_specs=[
            pl.BlockSpec((EXTRA, width), lambda h, i: (0, i)),
            pl.BlockSpec((EXTRA, rows), lambda h, i: (0, 0)),
            pl.BlockSpec((1, None, HEAD_DIM, width), lambda h, i: (h, 0, 0, i)),
            whole(1),
            whole(2),
        ],
        out_specs=(
            pl.BlockSpec((1, HEAD_DIM, width), lambda h, i: (h, 0, i)),
            pl.BlockSpec((1, 1, width), lambda h, i: (h, 0, i)),
        ),
        out_shape=(
            jax.ShapeDtypeStruct((heads, HEAD_DIM, rows), bf16),
            jax.ShapeDtypeStruct((heads, 1, rows), f32),
        ),
        scratch_shapes=[pltpu.VMEM((rows, HEAD_DIM + EXTRA), bf16)],
        compiler_params=pltpu.CompilerParams(vmem_limit_bytes=48 << 20),
        cost_estimate=pl.CostEstimate(
            flops=4 * heads * rows * rows * 256,
            bytes_accessed=heads * rows * HEAD_DIM * 8,
            transcendentals=heads * rows * rows,
        ),
        name="attend_forward",
    )(query_extra, key_extra, packed, packed, packed)


def backward_kernel(
    block, rows, items, qx_ref, kx_ref, q_ref, k_ref, v_ref, o_ref, do_ref, log_ref,
    grad_ref, keys, values, grad_k, grad_v,
):
    width = q_ref.shape[-1]
    step = pl.program_id(1)

    @pl.when(step == 0)
    def _():
        keys[...] = jnp.concatenate([k_ref[0], kx_ref[...]], axis=0)
        values[...] = jnp.concatenate([v_ref[0], kx_ref[...]], axis=0)
        grad_k[...] = jnp.zeros_like(grad_k)
        grad_v[...] = jnp.zeros_like(grad_v)

    row = lax.broadcasted_iota(jnp.int32, (EXTRA, width), 0) - items

    def pieces(term, base):
        high = term.astype(bf16).astype(f32)
        middle = (term - high).astype(bf16).astype(f32)
        small = term - high - middle
        return jnp.where(
            row == 1, high, jnp.where(row == 2, middle, jnp.where(row == 3, small, base))
        ).astype(bf16)

    query = q_ref[0] * jnp.asarray(0.125, bf16)
    grad = do_ref[0]
    inner = jnp.sum(grad.astype(f32) * o_ref[0].astype(f32), axis=0, keepdims=True)
    query_wide = jnp.concatenate(
        [query, pieces(-log_ref[0], qx_ref[...].astype(f32))], axis=0
    ).T
    grad_wide = jnp.concatenate(
        [grad, pieces(-inner, jnp.zeros((EXTRA, width), f32))], axis=0
    ).T
    grad_q = jnp.zeros((HEAD_DIM, width), f32)
    for i in range(rows // block):
        part = pl.ds(i * block, block)
        probs = jnp.exp(jnp.dot(query_wide, keys[:, part], preferred_element_type=f32))
        grad_scores = (
            probs * jnp.dot(grad_wide, values[:, part], preferred_element_type=f32)
        ).astype(bf16)
        grad_v[:, part] += jnp.dot(grad, probs.astype(bf16), preferred_element_type=f32)
        grad_k[:, part] += jnp.dot(query, grad_scores, preferred_element_type=f32)
        grad_q += lax.dot_general(
            k_ref[0, :, part], grad_scores, (((1,), (1,)), ((), ())), preferred_element_type=f32
        )
    grad_ref[0, 0, :, pl.ds(pl.multiple_of(step * width, width), width)] = (
        grad_q * 0.125
    ).astype(bf16)

    @pl.when(step == pl.num_programs(1) - 1)
    def _():
        grad_ref[0, 1] = grad_k[...].astype(bf16)
        grad_ref[0, 2] = grad_v[...].astype(bf16)


def attend_backward(packed, query_extra, key_extra, attended, grad, log_total, items, width=1024, block=512):
    heads, _, _, rows = packed.shape

    def whole(j):
        return pl.BlockSpec((1, None, HEAD_DIM, rows), lambda h, i: (h, j, 0, 0))

    part = pl.BlockSpec((1, HEAD_DIM, width), lambda h, i: (h, 0, i))
    return pl.pallas_call(
        functools.partial(backward_kernel, block, rows, items),
        grid=(heads, rows // width),
        in_specs=[
            pl.BlockSpec((EXTRA, width), lambda h, i: (0, i)),
            pl.BlockSpec((EXTRA, rows), lambda h, i: (0, 0)),
            pl.BlockSpec((1, None, HEAD_DIM, width), lambda h, i: (h, 0, 0, i)),
            whole(1),
            whole(2),
            part,
            part,
            pl.BlockSpec((1, 1, width), lambda h, i: (h, 0, i)),
        ],
        out_specs=pl.BlockSpec((1, 3, HEAD_DIM, rows), lambda h, i: (h, 0, 0, 0)),
        out_shape=jax.ShapeDtypeStruct((heads, 3, HEAD_DIM, rows), bf16),
        scratch_shapes=[
            pltpu.VMEM((HEAD_DIM + EXTRA, rows), bf16),
            pltpu.VMEM((HEAD_DIM + EXTRA, rows), bf16),
            pltpu.VMEM((HEAD_DIM, rows), f32),
            pltpu.VMEM((HEAD_DIM, rows), f32),
        ],
        compiler_params=pltpu.CompilerParams(vmem_limit_bytes=48 << 20),
        cost_estimate=pl.CostEstimate(
            flops=10 * heads * rows * rows * 256,
            bytes_accessed=heads * rows * HEAD_DIM * 16,
            transcendentals=heads * rows * rows,
        ),
        name="attend_backward",
    )(query_extra, key_extra, packed, packed, packed, attended, grad, log_total)


def product(spec, left, right):
    return jnp.einsum(spec, left, right, preferred_element_type=f32)


def scatter_rows(partial_sum):
    return lax.psum_scatter(
        partial_sum.astype(bf16), "narrow", scatter_dimension=0, tiled=True
    ).astype(f32)


def greet(W,N,w,n):
    bar=pltpu.get_barrier_semaphore()
    z=n//2; core=lax.rem(n,2)
    def col(t,_):
        nn=lax.rem(n+t,N)
        pl.semaphore_signal(bar,inc=1,device_id=(w,nn),device_id_type=MESH); return 0
    lax.fori_loop(1,N,col,0)
    def plane(t,_):
        ww=lax.rem(w+t,W)
        pl.semaphore_signal(bar,inc=1,device_id=(ww,n),device_id_type=MESH); return 0
    lax.fori_loop(1,W,plane,0)
    pl.semaphore_wait(bar,N-1+W-1)

def gather_kernel(W,N,own,out,lsem,s1,s1b,r1,s2,r2,s3,r3,fs0,fr0,fs1,fr1,fs2,fr2,fs3,fr3):
    w=lax.axis_index("wide"); n=lax.axis_index("narrow")
    W1=math.isqrt(W); H=N//2
    a=w//W1; b=lax.rem(w,W1); z=n//2; core=lax.rem(n,2); sib=n+1-2*core
    greet(W,N,w,n)
    def rc(src,dst,ss,rs,dw,dn):
        return pltpu.make_async_remote_copy(src_ref=src,dst_ref=dst,send_sem=ss,recv_sem=rs,device_id=(dw,dn),device_id_type=MESH)
    def arrived(ref,sem):
        pltpu.make_async_copy(ref,ref,sem).wait()
    oa=lambda i: lax.rem(a+i,W1)
    ob=lambda i: lax.rem(b+i,W1)
    def d1(zs,step):
        return rc(out.at[2*zs+core,a,b],out.at[2*zs+core,a,b],s1b.at[zs],r1.at[zs],w,n+2*step)
    def own1(step):
        return rc(own.at[a,b],out.at[n,a,b],s1.at[z+step],r1.at[z],w,n+2*step)
    def d2(ns,zs,h,i):
        if h==0: return rc(out.at[ns,a,b,0],out.at[ns,a,b,0],s2.at[zs,0,i],r2.at[zs,0,b],a*W1+ob(i),n)
        return rc(out.at[ns,a,b,1],out.at[ns,a,b,1],s2.at[zs,1,i],r2.at[zs,1,a],oa(i)*W1+b,n)
    def d3(ns,zs,h,i):
        if h==0: return rc(out.at[ns,a,:,0],out.at[ns,a,:,0],s3.at[zs,0,i],r3.at[zs,0,a],oa(i)*W1+b,n)
        return rc(out.at[ns,:,b,1],out.at[ns,:,b,1],s3.at[zs,1,i],r3.at[zs,1,b],a*W1+ob(i),n)
    f0=rc(own,out.at[n],fs0,fr0,w,sib)
    def f1(ns,zs): return rc(out.at[ns,a,b],out.at[ns,a,b],fs1.at[zs],fr1.at[zs],w,sib)
    def f2(ns,zs,h,i):
        v=out.at[ns,a,ob(i),0] if h==0 else out.at[ns,oa(i),b,1]
        k=ob(i) if h==0 else oa(i)
        return rc(v,v,fs2.at[zs,h,k],fr2.at[zs,h,k],w,sib)
    def f3(ns,zs,h,i):
        v=out.at[ns,oa(i),:,0] if h==0 else out.at[ns,:,ob(i),1]
        k=oa(i) if h==0 else ob(i)
        return rc(v,v,fs3.at[zs,h,k],fr3.at[zs,h,k],w,sib)
    local=pltpu.make_async_copy(own,out.at[n],lsem)
    up=z<H-1; down=z>0
    @pl.when(up)
    def _(): own1(1).start()
    @pl.when(down)
    def _(): own1(-1).start()
    local.start(); f0.start()
    def sides(d,f):
        @pl.when(jnp.logical_and(d<=H-1,z-d>=0))
        def _(): f(z-d,1,up)
        @pl.when(jnp.logical_and(d<=H-1,z+d<=H-1))
        def _(): f(z+d,-1,down)
    def step1(zs,step,more):
        ns=2*zs+core
        arrived(out.at[ns,a,b],r1.at[zs])
        @pl.when(more)
        def _(): d1(zs,step).start()
        for i in range(1,W1):
            d2(ns,zs,0,i).start(); d2(ns,zs,1,i).start()
        f1(ns,zs).start()
    def step2(zs,step,more):
        ns=2*zs+core
        for i in range(1,W1):
            arrived(out.at[ns,a,ob(i),0],r2.at[zs,0,ob(i)])
        for i in range(1,W1): d3(ns,zs,0,i).start()
        for i in range(1,W1):
            arrived(out.at[ns,oa(i),b,1],r2.at[zs,1,oa(i)])
        for i in range(1,W1): d3(ns,zs,1,i).start()
        for i in range(1,W1):
            f2(ns,zs,0,i).start(); f2(ns,zs,1,i).start()
    def step3(zs,step,more):
        ns=2*zs+core
        for i in range(1,W1):
            arrived(out.at[ns,oa(i),:,0],r3.at[zs,0,oa(i)])
            f3(ns,zs,0,i).start()
            arrived(out.at[ns,:,ob(i),1],r3.at[zs,1,ob(i)])
            f3(ns,zs,1,i).start()
    def run(d,_):
        sides(d,step1)
        @pl.when(d>1)
        def _(): sides(d-1,step2)
        @pl.when(d>2)
        def _(): sides(d-2,step3)
        return 0
    lax.fori_loop(1,H+2,run,0)
    local.wait()
    f0.wait_send(); arrived(out.at[sib],fr0)
    @pl.when(up)
    def _(): own1(1).wait_send()
    @pl.when(down)
    def _(): own1(-1).wait_send()
    def finish(zs,step,more):
        ns=2*zs+core; nb=ns+1-2*core
        @pl.when(more)
        def _(): d1(zs,step).wait_send()
        f1(ns,zs).wait_send(); arrived(out.at[nb,a,b],fr1.at[zs])
        for h in (0,1):
            for i in range(1,W1):
                d2(ns,zs,h,i).wait_send(); d3(ns,zs,h,i).wait_send()
                f2(ns,zs,h,i).wait_send(); f3(ns,zs,h,i).wait_send()
                v2=out.at[nb,a,ob(i),0] if h==0 else out.at[nb,oa(i),b,1]
                arrived(v2,fr2.at[zs,h,ob(i) if h==0 else oa(i)])
                v3=out.at[nb,oa(i),:,0] if h==0 else out.at[nb,:,ob(i),1]
                arrived(v3,fr3.at[zs,h,oa(i) if h==0 else ob(i)])
    def fin(d,_):
        sides(d,finish); return 0
    lax.fori_loop(1,H,fin,0)

def gather_weights(W,N,own):
    W1=math.isqrt(W); H=N//2
    D=pltpu.SemaphoreType.DMA
    return pl.pallas_call(functools.partial(gather_kernel,W,N),out_shape=jax.ShapeDtypeStruct((N,)+own.shape,bf16),
      in_specs=[pl.BlockSpec(memory_space=pl.ANY)],out_specs=pl.BlockSpec(memory_space=pl.ANY),
      scratch_shapes=[D(()),D((H,)),D((H,)),D((H,)),D((H,2,W1)),D((H,2,W1)),D((H,2,W1)),D((H,2,W1)),D(()),D(()),D((H,)),D((H,)),D((H,2,W1)),D((H,2,W1)),D((H,2,W1)),D((H,2,W1))],
      compiler_params=pltpu.CompilerParams(collective_id=1,has_side_effects=True,vmem_limit_bytes=1<<20),name="gather_weights")(own)

def scatter_share(partial_sum):
    part = lax.psum_scatter(
        partial_sum.astype(bf16), "narrow", scatter_dimension=0, tiled=True
    )
    return lax.psum(part, "wide").astype(f32)


def body(
    tokens, cotangent, item_lengths, attn_gain, attn_bias, qkv_weight, proj_weight,
    mlp_gain, mlp_bias, up_weight, down_weight,
):
    items = item_lengths.shape[1]
    token_rows = tokens.astype(f32)
    heads = qkv_weight.shape[1] // (3 * HEAD_DIM)
    gain_one, bias_one = attn_gain.astype(f32), attn_bias.astype(f32)
    gain_two, bias_two = mlp_gain.astype(f32), mlp_bias.astype(f32)
    wide, narrow = lax.axis_size("wide"), lax.axis_size("narrow")
    side = math.isqrt(wide)

    def cut(shard):
        return shard.reshape(side, side, 2, shard.shape[0] // (2 * wide), shard.shape[1])

    shards = [cut(up_weight.T), cut(down_weight), cut(proj_weight)]
    everything = gather_weights(wide, narrow, jnp.concatenate(shards, axis=3))
    first = shards[0].shape[3]
    features = tokens.shape[1]
    normed = norm_forward(token_rows, gain_one, bias_one).astype(bf16)
    normed_all = lax.all_gather(normed, "narrow", axis=0, tiled=True)
    normed_all, everything = lax.optimization_barrier((normed_all, everything))
    rows = normed_all.shape[0]
    query_extra, key_extra = mask_rows(item_lengths, rows)
    packed = (
        product("rd,dc->cr", normed_all, qkv_weight).astype(bf16).reshape(heads, 3, HEAD_DIM, rows)
    )
    attended, log_total = attend_forward(packed, query_extra, key_extra)
    up_all = everything[:, :, :, :, :first].reshape(-1, tokens.shape[1])
    down_all = everything[:, :, :, :, first : 2 * first].reshape(-1, tokens.shape[1])
    proj_all = everything[:, :, :, :, 2 * first :].reshape(-1, tokens.shape[1])
    attended_rows = lax.all_to_all(
        attended.reshape(heads * HEAD_DIM, rows), "narrow", split_axis=1, concat_axis=0, tiled=True
    )
    branch = product("ar,ad->rd", attended_rows, proj_all)
    middle = token_rows + branch
    expand_in = norm_forward(middle, gain_two, bias_two).astype(bf16)
    hidden_pre = product("rd,fd->rf", expand_in, up_all)
    hidden = gelu_exact(hidden_pre).astype(bf16)
    output = (middle + product("rf,fd->rd", hidden, down_all)).astype(bf16)

    grad_hidden = product("rd,fd->rf", cotangent, down_all)
    grad_pre = jax.vjp(gelu_exact, hidden_pre)[1](grad_hidden)[0].astype(bf16)
    grad_expand = product("rf,fd->rd", grad_pre, up_all)
    grad_middle_norm, grad_gain_two, grad_bias_two = jax.vjp(
        norm_forward, middle, gain_two, bias_two
    )[1](grad_expand)
    grad_middle = cotangent.astype(f32) + grad_middle_norm
    grad_branch = grad_middle.astype(bf16)
    grad_attended = lax.all_to_all(
        product("rd,ad->ar", grad_branch, proj_all).astype(bf16),
        "narrow", split_axis=0, concat_axis=1, tiled=True,
    ).reshape(heads, HEAD_DIM, rows)
    grad_down = scatter_share(product("rf,rd->fd", hidden, cotangent))
    grad_up = scatter_share(product("rf,rd->fd", grad_pre, expand_in)).T
    grad_proj = scatter_share(product("ar,rd->ad", attended_rows, grad_branch))
    grad_packed = attend_backward(
        packed, query_extra, key_extra, attended, grad_attended, log_total, items
    ).reshape(heads * 3 * HEAD_DIM, rows)
    grad_normed = scatter_rows(product("cr,dc->rd", grad_packed, qkv_weight))
    grad_qkv = product("rd,cr->dc", normed_all, grad_packed)
    grad_token_norm, grad_gain_one, grad_bias_one = jax.vjp(
        norm_forward, token_rows, gain_one, bias_one
    )[1](grad_normed)
    grad_tokens = (grad_middle + grad_token_norm).astype(bf16)
    norm_parts = jnp.stack([grad_gain_one, grad_bias_one, grad_gain_two, grad_bias_two])
    norm_sums = lax.psum(norm_parts, ("wide", "narrow"))
    share = norm_sums.shape[1] // lax.axis_size("narrow")
    shares = lax.dynamic_slice_in_dim(norm_sums, lax.axis_index("narrow") * share, share, 1)
    grad_qkv = lax.psum(grad_qkv.astype(bf16), "wide").astype(f32)
    return (
        output, grad_tokens, shares[0], shares[1], grad_qkv, grad_proj,
        shares[2], shares[3], grad_up, grad_down,
    )


def solution(mesh):
    by_rows = P(("wide", "narrow"), None)
    return jax.shard_map(
        body,
        mesh=mesh,
        in_specs=(
            by_rows, by_rows, P("wide", None), P(), P(), P(None, "narrow"), P("narrow", None),
            P(), P(), P(None, "narrow"), P("narrow", None),
        ),
        out_specs=(
            by_rows, by_rows, P("narrow"), P("narrow"), P(None, "narrow"), P("narrow", None),
            P("narrow"), P("narrow"), P(None, "narrow"), P("narrow", None),
        ),
        check_vma=False,
    )
```

```python
import functools
import math

import jax
import jax.numpy as jnp
from jax import lax
from jax.experimental import pallas as pl
from jax.experimental.pallas import tpu as pltpu
from jax.sharding import PartitionSpec as P

HEAD_DIM = 64
EXTRA = 16
ATTENTION_STEPS = 16
EXCLUDED = -1e30
bf16 = jnp.bfloat16
f32 = jnp.float32
MESH = pl.DeviceIdType.MESH
epsilon = 1e-05


def norm_forward(values, norm_gain, norm_bias):
    average = jnp.mean(values, axis=-1, keepdims=True)
    centred = values - average
    variance = jnp.mean(centred * centred, axis=-1, keepdims=True)
    return centred * lax.rsqrt(variance + epsilon) * norm_gain + norm_bias


def gelu_exact(values):
    return jax.nn.gelu(values, approximate=False)


def mask_rows(item_lengths, rows):
    lengths = item_lengths[0]
    items = lengths.shape[0]
    index = jnp.arange(items)
    ends = jnp.sum(jnp.where(index[:, None] >= index[None, :], lengths[None, :], 0), axis=1)
    segment = jnp.sum((jnp.arange(rows)[None, :] >= ends[:, None]).astype(jnp.int32), axis=0)
    extra = jnp.arange(EXTRA)[:, None]
    own = segment[None, :] == extra
    query_extra = jnp.where(own & (extra <= items), 1.0, 0.0).astype(bf16)
    key_extra = jnp.where(
        extra <= items,
        jnp.where(own, 0.0, EXCLUDED),
        jnp.where(extra <= items + 3, 1.0, 0.0),
    ).astype(bf16)
    return query_extra, key_extra


def forward_kernel(block, rows, qx_ref, kx_ref, q_ref, k_ref, v_ref, o_ref, log_ref, keys):
    width = q_ref.shape[-1]

    @pl.when(pl.program_id(1) == 0)
    def _():
        keys[...] = jnp.concatenate([k_ref[0], kx_ref[...]], axis=0).T

    query = jnp.concatenate([q_ref[0] * jnp.asarray(0.125, bf16), qx_ref[...]], axis=0)
    maximum = jnp.full((1, width), -3e38, f32)
    total = jnp.zeros((1, width), f32)
    gathered = jnp.zeros((HEAD_DIM, width), f32)
    for i in range(rows // block):
        part = pl.ds(i * block, block)
        scores = jnp.dot(keys[part, :], query, preferred_element_type=f32)
        larger = jnp.maximum(maximum, jnp.max(scores, axis=0, keepdims=True))
        raised = jnp.exp(scores - larger)
        shrink = jnp.exp(maximum - larger)
        total = shrink * total + jnp.sum(raised, axis=0, keepdims=True)
        gathered = shrink * gathered + jnp.dot(
            v_ref[0, :, part], raised.astype(bf16), preferred_element_type=f32
        )
        maximum = larger
    o_ref[0] = (gathered / total).astype(bf16)
    log_ref[0] = maximum + jnp.log(total)


def attend_forward(packed, query_extra, key_extra, width=1024, block=1024):
    heads, _, _, rows = packed.shape

    def whole(j):
        return pl.BlockSpec((1, None, HEAD_DIM, rows), lambda h, i: (h, j, 0, 0))

    return pl.pallas_call(
        functools.partial(forward_kernel, block, rows),
        grid=(heads, rows // width),
        in_specs=[
            pl.BlockSpec((EXTRA, width), lambda h, i: (0, i)),
            pl.BlockSpec((EXTRA, rows), lambda h, i: (0, 0)),
            pl.BlockSpec((1, None, HEAD_DIM, width), lambda h, i: (h, 0, 0, i)),
            whole(1),
            whole(2),
        ],
        out_specs=(
            pl.BlockSpec((1, HEAD_DIM, width), lambda h, i: (h, 0, i)),
            pl.BlockSpec((1, 1, width), lambda h, i: (h, 0, i)),
        ),
        out_shape=(
            jax.ShapeDtypeStruct((heads, HEAD_DIM, rows), bf16),
            jax.ShapeDtypeStruct((heads, 1, rows), f32),
        ),
        scratch_shapes=[pltpu.VMEM((rows, HEAD_DIM + EXTRA), bf16)],
        compiler_params=pltpu.CompilerParams(vmem_limit_bytes=48 << 20),
        cost_estimate=pl.CostEstimate(
            flops=4 * heads * rows * rows * 256,
            bytes_accessed=heads * rows * HEAD_DIM * 8,
            transcendentals=heads * rows * rows,
        ),
        name="attend_forward",
    )(query_extra, key_extra, packed, packed, packed)


def remote(src, dst, sent, received, wide_to, narrow_to):
    return pltpu.make_async_remote_copy(
        src_ref=src,
        dst_ref=dst,
        send_sem=sent,
        recv_sem=received,
        device_id=(wide_to, narrow_to),
        device_id_type=MESH,
    )


def arrived(ref, semaphore):
    pltpu.make_async_copy(ref, ref, semaphore).wait()


def greet(wide, narrow, w, n):
    barrier = pltpu.get_barrier_semaphore()

    def column(t, carry):
        pl.semaphore_signal(
            barrier, inc=1, device_id=(w, lax.rem(n + t, narrow)), device_id_type=MESH
        )
        return carry

    def plane(t, carry):
        pl.semaphore_signal(
            barrier, inc=1, device_id=(lax.rem(w + t, wide), n), device_id_type=MESH
        )
        return carry

    lax.fori_loop(1, narrow, column, 0)
    lax.fori_loop(1, wide, plane, 0)
    pl.semaphore_wait(barrier, narrow + wide - 2)


def accumulate(into, *others):
    rows = into.shape[0]
    few = max([d for d in (16, 32, 48, 64) if rows % d == 0], default=rows)

    def piece(j, carry):
        part = pl.ds(j * few if rows == few else pl.multiple_of(j * few, few), few)
        total = into[part, :].astype(f32)
        for other in others:
            total = total + other[part, :].astype(f32)
        into[part, :] = total.astype(bf16)
        return carry

    if rows == few:
        piece(0, 0)
    else:
        lax.fori_loop(0, rows // few, piece, 0)


def reduce_steps(
    wide, narrow, parts, final, held, from_sibling, from_first, from_second, from_line,
    loaded, sib_sent, sib_got, first_sent, first_got, second_sent, second_got, line_sent, line_got,
):
    w, n = lax.axis_index("wide"), lax.axis_index("narrow")
    side, lines = math.isqrt(wide), narrow // 2
    a, b, z, core = w // side, lax.rem(w, side), n // 2, lax.rem(n, 2)
    sibling = n + 1 - 2 * core

    def other_a(i):
        return lax.rem(a + i, side)

    def other_b(i):
        return lax.rem(b + i, side)

    def to_sibling(zs):
        return remote(
            parts.at[2 * zs + 1 - core], from_sibling.at[zs], sib_sent.at[zs], sib_got.at[zs], w, sibling
        )

    def load(zs):
        return pltpu.make_async_copy(parts.at[2 * zs + core], held.at[zs], loaded.at[zs])

    def first(zs, h, i):
        if h == 0:
            src, to = held.at[zs, other_a(i), :, 0], other_a(i) * side + b
        else:
            src, to = held.at[zs, :, other_b(i), 1], a * side + other_b(i)
        k = i - 1
        return remote(
            src, from_first.at[zs, h, k], first_sent.at[zs, h, k], first_got.at[zs, h, k], to, n
        )

    def second(zs, h, i):
        if h == 0:
            src, to = held.at[zs, a, other_b(i), 0], a * side + other_b(i)
        else:
            src, to = held.at[zs, other_a(i), b, 1], other_a(i) * side + b
        k = i - 1
        return remote(
            src, from_second.at[zs, h, k], second_sent.at[zs, h, k], second_got.at[zs, h, k], to, n
        )

    def along(zs):
        slot = jnp.where(z < zs, z, z - 1)
        return remote(
            held.at[zs, a, b], from_line.at[slot], line_sent.at[zs], line_got.at[slot], w, 2 * zs + core
        )

    order = []
    for i in range((lines + 1) // 2):
        order += [lines - 1 - i] if lines - 1 - i == i else [lines - 1 - i, i]
    halves = [(h, i) for i in range(1, side) for h in (0, 1)]

    def begin():
        greet(wide, narrow, w, n)
        for zs in order:
            to_sibling(zs).start()
            load(zs).start()

    def combine(zs):
        load(zs).wait()
        arrived(from_sibling.at[zs], sib_got.at[zs])

        def piece(j, carry):
            p, q = j // side, lax.rem(j, side)
            for h in (0, 1):
                accumulate(held.at[zs, p, q, h], from_sibling.at[zs, p, q, h])
            return carry

        lax.fori_loop(0, wide, piece, 0)
        for h, i in halves:
            first(zs, h, i).start()

    def narrow_down(zs):
        for h in (0, 1):
            for i in range(1, side):
                arrived(from_first.at[zs, h, i - 1], first_got.at[zs, h, i - 1])

            def piece(j, carry, h=h):
                into = held.at[zs, a, j, 0] if h == 0 else held.at[zs, j, b, 1]
                accumulate(into, *[from_first.at[zs, h, i, j] for i in range(side - 1)])
                return carry

            lax.fori_loop(0, side, piece, 0)
        for h, i in halves:
            second(zs, h, i).start()

    def send_home(zs):
        for h, i in halves:
            arrived(from_second.at[zs, h, i - 1], second_got.at[zs, h, i - 1])
        for h in (0, 1):
            accumulate(
                held.at[zs, a, b, h], *[from_second.at[zs, h, i] for i in range(side - 1)]
            )

        @pl.when(z != zs)
        def _():
            along(zs).start()

    def finish():
        for slot in range(lines - 1):
            arrived(from_line.at[slot], line_got.at[slot])
        for h in (0, 1):
            total = held[z, a, b, h].astype(f32)
            for slot in range(lines - 1):
                total = total + from_line[slot, h].astype(f32)
            final[h] = total.astype(bf16)
        for zs in order:
            to_sibling(zs).wait_send()
            for h, i in halves:
                first(zs, h, i).wait_send()
                second(zs, h, i).wait_send()

            @pl.when(z != zs)
            def _():
                along(zs).wait_send()

    steps = [(0.0, begin)]
    for i, zs in enumerate(order):
        at = 1 + 4 * i
        steps += [
            (at, functools.partial(combine, zs)),
            (at + 3.2, functools.partial(narrow_down, zs)),
            (at + 5.4, functools.partial(send_home, zs)),
        ]
    steps.append((99, finish))
    return [step for _, step in sorted(steps, key=lambda s: s[0])], sorted(at for at, _ in steps)


def reduce_scratch(wide, narrow, rows, features):
    side, lines = math.isqrt(wide), narrow // 2
    dma = pltpu.SemaphoreType.DMA
    return [
        pltpu.VMEM((lines, side, side, 2, rows, features), bf16),
        pltpu.VMEM((lines, side, side, 2, rows, features), bf16),
        pltpu.VMEM((lines, 2, side - 1, side, rows, features), bf16),
        pltpu.VMEM((lines, 2, side - 1, rows, features), bf16),
        pltpu.VMEM((lines - 1, 2, rows, features), bf16),
        dma((lines,)),
        dma((lines,)),
        dma((lines,)),
        dma((lines, 2, side - 1)),
        dma((lines, 2, side - 1)),
        dma((lines, 2, side - 1)),
        dma((lines, 2, side - 1)),
        dma((lines,)),
        dma((lines - 1,)),
    ]


def backward_kernel(
    block, rows, items, wide, narrow, qx_ref, kx_ref, q_ref, k_ref, v_ref, o_ref, do_ref, log_ref,
    parts_ref, grad_ref, final_ref, keys, values, grad_k, grad_v, *reduce_refs,
):
    width = q_ref.shape[-1]
    step = pl.program_id(1)
    steps_per_head = pl.num_programs(1)
    moment = pl.program_id(0) * steps_per_head + step
    ticks = ATTENTION_STEPS
    moves, times = reduce_steps(wide, narrow, parts_ref, final_ref, *reduce_refs)

    def perform(lower, upper):
        for move, time in zip(moves, times):
            if lower <= time < upper:
                move()

    for tick in range(ticks):

        @pl.when(moment == tick)
        def _():
            perform(tick, tick + 1)

    @pl.when(step == 0)
    def _():
        keys[...] = jnp.concatenate([k_ref[0], kx_ref[...]], axis=0)
        values[...] = jnp.concatenate([v_ref[0], kx_ref[...]], axis=0)
        grad_k[...] = jnp.zeros_like(grad_k)
        grad_v[...] = jnp.zeros_like(grad_v)

    row = lax.broadcasted_iota(jnp.int32, (EXTRA, width), 0) - items

    def pieces(term, base):
        high = term.astype(bf16).astype(f32)
        middle = (term - high).astype(bf16).astype(f32)
        small = term - high - middle
        return jnp.where(
            row == 1, high, jnp.where(row == 2, middle, jnp.where(row == 3, small, base))
        ).astype(bf16)

    query = q_ref[0] * jnp.asarray(0.125, bf16)
    grad = do_ref[0]
    inner = jnp.sum(grad.astype(f32) * o_ref[0].astype(f32), axis=0, keepdims=True)
    query_wide = jnp.concatenate(
        [query, pieces(-log_ref[0], qx_ref[...].astype(f32))], axis=0
    ).T
    grad_wide = jnp.concatenate(
        [grad, pieces(-inner, jnp.zeros((EXTRA, width), f32))], axis=0
    ).T
    grad_q = jnp.zeros((HEAD_DIM, width), f32)
    for i in range(rows // block):
        part = pl.ds(i * block, block)
        probs = jnp.exp(jnp.dot(query_wide, keys[:, part], preferred_element_type=f32))
        grad_scores = (
            probs * jnp.dot(grad_wide, values[:, part], preferred_element_type=f32)
        ).astype(bf16)
        grad_v[:, part] += jnp.dot(grad, probs.astype(bf16), preferred_element_type=f32)
        grad_k[:, part] += jnp.dot(query, grad_scores, preferred_element_type=f32)
        grad_q += lax.dot_general(
            k_ref[0, :, part], grad_scores, (((1,), (1,)), ((), ())), preferred_element_type=f32
        )
    grad_ref[0, 0, :, pl.ds(pl.multiple_of(step * width, width), width)] = (
        grad_q * 0.125
    ).astype(bf16)

    @pl.when(step == steps_per_head - 1)
    def _():
        grad_ref[0, 1] = grad_k[...].astype(bf16)
        grad_ref[0, 2] = grad_v[...].astype(bf16)

    @pl.when(moment == ticks - 1)
    def _():
        perform(ticks, 1000)


def attend_backward(
    wide, narrow, packed, query_extra, key_extra, attended, grad, log_total, parts, items, block=512
):
    heads, _, _, rows = packed.shape
    width = heads * rows // ATTENTION_STEPS
    piece = parts.shape[4:]

    def whole(j):
        return pl.BlockSpec((1, None, HEAD_DIM, rows), lambda h, i: (h, j, 0, 0))

    part = pl.BlockSpec((1, HEAD_DIM, width), lambda h, i: (h, 0, i))
    return pl.pallas_call(
        functools.partial(backward_kernel, block, rows, items, wide, narrow),
        grid=(heads, rows // width),
        in_specs=[
            pl.BlockSpec((EXTRA, width), lambda h, i: (0, i)),
            pl.BlockSpec((EXTRA, rows), lambda h, i: (0, 0)),
            pl.BlockSpec((1, None, HEAD_DIM, width), lambda h, i: (h, 0, 0, i)),
            whole(1),
            whole(2),
            part,
            part,
            pl.BlockSpec((1, 1, width), lambda h, i: (h, 0, i)),
            pl.BlockSpec(memory_space=pl.ANY),
        ],
        out_specs=(
            pl.BlockSpec((1, 3, HEAD_DIM, rows), lambda h, i: (h, 0, 0, 0)),
            pl.BlockSpec((2, *piece), lambda h, i: (0, 0, 0)),
        ),
        out_shape=(
            jax.ShapeDtypeStruct((heads, 3, HEAD_DIM, rows), bf16),
            jax.ShapeDtypeStruct((2, *piece), bf16),
        ),
        scratch_shapes=[
            pltpu.VMEM((HEAD_DIM + EXTRA, rows), bf16),
            pltpu.VMEM((HEAD_DIM + EXTRA, rows), bf16),
            pltpu.VMEM((HEAD_DIM, rows), f32),
            pltpu.VMEM((HEAD_DIM, rows), f32),
            *reduce_scratch(wide, narrow, *piece),
        ],
        compiler_params=pltpu.CompilerParams(
            vmem_limit_bytes=58 << 20, collective_id=2, has_side_effects=True
        ),
        cost_estimate=pl.CostEstimate(
            flops=10 * heads * rows * rows * 256,
            bytes_accessed=heads * rows * HEAD_DIM * 16,
            transcendentals=heads * rows * rows,
        ),
        name="attend_backward",
    )(query_extra, key_extra, packed, packed, packed, attended, grad, log_total, parts)


def finish_kernel(
    wide, narrow, chunks,
    packed_ref, weight_ref, normed_ref, token_ref, middle_ref, gain_ref, norm_ref, piece_ref,
    tokens_out, qkv_out, shard_out, norms_out,
    normed, held, for_sibling, from_sibling, from_line, total_qkv, own_qkv, first_qkv, second_qkv,
    half_qkv, norms, norm_column, norm_half, norm_plane,
    loaded, copied, sib_sent, sib_got, line_sent, line_got, piece_sent, piece_got,
    first_sent, first_got, second_sent, second_got, column_sent, column_got, plane_sent, plane_got,
):
    w, n = lax.axis_index("wide"), lax.axis_index("narrow")
    side, lines = math.isqrt(wide), narrow // 2
    a, b, z, core = w // side, lax.rem(w, side), n // 2, lax.rem(n, 2)
    sibling = n + 1 - 2 * core
    rows, features = held.shape[1:]
    step = rows // chunks
    load = pltpu.make_async_copy(normed_ref, normed, loaded)
    load.start()
    greet(wide, narrow, w, n)

    keep = pltpu.make_async_copy(piece_ref, shard_out.at[w], copied)
    keep.start()

    def spread(t):
        return remote(
            piece_ref, shard_out.at[w], piece_sent.at[t], piece_got.at[t], lax.rem(w + t, wide), n
        )

    for t in range(1, wide):
        spread(t).start()

    order = []
    for i in range((lines + 1) // 2):
        order += [lines - 1 - i] if lines - 1 - i == i else [lines - 1 - i, i]

    def block(owner):
        columns = pl.ds(pl.multiple_of(owner * rows, rows), rows)
        return lax.dot_general(
            packed_ref[:, columns], weight_ref[...], (((0,), (0,)), ((), ())),
            preferred_element_type=f32,
        ).astype(bf16)

    def to_sibling(zs):
        return remote(
            for_sibling.at[zs], from_sibling.at[zs], sib_sent.at[zs], sib_got.at[zs], w, sibling
        )

    def pass_on(zs, c, up):
        part = pl.ds(c * step, step)
        slot = zs if up else jnp.where(z - 1 == zs, lines, zs)
        to = n + 2 if up else n - 2
        return remote(
            held.at[zs, part], from_line.at[slot, part], line_sent.at[zs, c], line_got.at[slot, c], w, to
        )

    def merge(zs):
        arrived(from_sibling.at[zs], sib_got.at[zs])
        accumulate(held.at[zs], from_sibling.at[zs])

    def feed(t):
        @pl.when(z == 0)
        def _():
            for c in range(chunks):
                pass_on(lines - 1 - t, c, True).start()

        @pl.when(z == lines - 1)
        def _():
            for c in range(chunks):
                pass_on(t, c, False).start()

    def fed(t):
        @pl.when(z == 0)
        def _():
            for c in range(chunks):
                pass_on(lines - 1 - t, c, True).wait_send()

        @pl.when(z == lines - 1)
        def _():
            for c in range(chunks):
                pass_on(t, c, False).wait_send()

    for i, zs in enumerate(order):
        for_sibling[zs] = block(2 * zs + 1 - core)
        to_sibling(zs).start()
        held[zs] = block(2 * zs + core)
        if i >= 1:
            merge(order[i - 1])
        if i == 2:
            feed(0)
    merge(order[-1])
    if lines <= 2:
        feed(0)

    load.wait()
    total_qkv[...] = jnp.dot(packed_ref[...], normed[...], preferred_element_type=f32)
    half = total_qkv.shape[0] // 2
    for h in (0, 1):
        own_qkv[h] = total_qkv[h * half : (h + 1) * half].astype(bf16)

    def along(h, i):
        if h == 0:
            return lax.rem(a + i, side) * side + b
        return a * side + lax.rem(b + i, side)

    halves = [(h, i) for i in range(1, side) for h in (0, 1)]

    def first(h, i):
        return remote(
            own_qkv.at[h], first_qkv.at[h, i - 1], first_sent.at[h, i - 1], first_got.at[h, i - 1],
            along(h, i), n,
        )

    def second(h, i):
        return remote(
            half_qkv.at[h], second_qkv.at[h, i - 1], second_sent.at[h, i - 1], second_got.at[h, i - 1],
            along(1 - h, i), n,
        )

    def qkv_first():
        for h, i in halves:
            first(h, i).start()

    def qkv_second():
        for h, i in halves:
            arrived(first_qkv.at[h, i - 1], first_got.at[h, i - 1])
        for h in (0, 1):
            total = own_qkv[h].astype(f32)
            for i in range(1, side):
                total = total + first_qkv[h, i - 1].astype(f32)
            half_qkv[h] = total.astype(bf16)
        for h, i in halves:
            second(h, i).start()

    def qkv_last():
        for h, i in halves:
            arrived(second_qkv.at[h, i - 1], second_got.at[h, i - 1])
        for h in (0, 1):
            total = half_qkv[h].astype(f32)
            for i in range(1, side):
                total = total + second_qkv[h, i - 1].astype(f32)
            qkv_out[h * half : (h + 1) * half] = total.astype(bf16)

    qkv_first()
    for t in range(1, lines):
        if t <= lines - 2:
            fed(t - 1)
            feed(t)
        below, above = lines - 1 - (t - z), t - (lines - 1 - z)
        for c in range(chunks):
            part = pl.ds(c * step, step)
            if t < lines - 1:

                @pl.when(jnp.logical_and(z >= 1, t >= z))
                def _():
                    arrived(from_line.at[below, part], line_got.at[below, c])
                    accumulate(held.at[below, part], from_line.at[below, part])
                    pass_on(below, c, True).start()

                @pl.when(jnp.logical_and(z <= lines - 2, above >= 0))
                def _():
                    arrived(from_line.at[above, part], line_got.at[above, c])
                    accumulate(held.at[above, part], from_line.at[above, part])
                    pass_on(above, c, False).start()
        if t == 1:
            qkv_second()
        if t == min(2, lines - 1):
            qkv_last()

    def zero_edges(at_edge, slot):
        @pl.when(at_edge)
        def _():
            from_line[slot] = jnp.zeros((rows, features), bf16)

    zero_edges(z == 0, z)
    zero_edges(z == lines - 1, lines)
    for c in range(chunks):
        part = pl.ds(c * step, step)

        @pl.when(z >= 1)
        def _():
            arrived(from_line.at[z, part], line_got.at[z, c])

        @pl.when(z <= lines - 2)
        def _():
            arrived(from_line.at[lines, part], line_got.at[lines, c])

        def norm_rows(j, carry):
            gain_sum, bias_sum = carry
            few = pl.ds(pl.multiple_of(c * step + j * 32, 32), 32)
            grad = (
                held[z, few].astype(f32)
                + from_line[z, few].astype(f32)
                + from_line[lines, few].astype(f32)
            )
            values = token_ref[few, :].astype(f32)
            centred = values - jnp.mean(values, axis=-1, keepdims=True)
            inverse = lax.rsqrt(jnp.mean(centred * centred, axis=-1, keepdims=True) + epsilon)
            scaled = centred * inverse
            term = grad * gain_ref[...]
            back = inverse * (
                term
                - jnp.mean(term, axis=-1, keepdims=True)
                - scaled * jnp.mean(term * scaled, axis=-1, keepdims=True)
            )
            tokens_out[few, :] = (middle_ref[few, :] + back).astype(bf16)
            gain_sum = gain_sum + jnp.sum(grad * scaled, axis=0, keepdims=True)
            bias_sum = bias_sum + jnp.sum(grad, axis=0, keepdims=True)
            return gain_sum, bias_sum

        start = (jnp.zeros((1, features), f32), jnp.zeros((1, features), f32))
        sums = lax.fori_loop(0, step // 32, norm_rows, start)
        if c == 0:
            gain_sum, bias_sum = sums
        else:
            gain_sum, bias_sum = gain_sum + sums[0], bias_sum + sums[1]

    row = lax.broadcasted_iota(jnp.int32, (8, features), 0)
    norms[...] = jnp.where(row == 0, gain_sum, jnp.where(row == 1, bias_sum, norm_ref[...]))

    def down_column(t):
        return remote(
            norms, norm_column.at[t - 1], column_sent.at[t - 1], column_got.at[t - 1],
            w, lax.rem(n + t, narrow),
        )

    def over_plane(t):
        return remote(
            norm_half, norm_plane.at[t - 1], plane_sent.at[t - 1], plane_got.at[t - 1],
            lax.rem(w + t, wide), n,
        )

    for t in range(1, narrow):
        down_column(t).start()
    total = norms[...]
    for t in range(1, narrow):
        arrived(norm_column.at[t - 1], column_got.at[t - 1])
        total = total + norm_column[t - 1]
    norm_half[...] = total
    for t in range(1, wide):
        over_plane(t).start()
    for t in range(1, wide):
        arrived(norm_plane.at[t - 1], plane_got.at[t - 1])
        total = total + norm_plane[t - 1]
    norms_out[...] = total

    keep.wait()
    for t in range(1, wide):
        spread(t).wait_send()
        arrived(shard_out.at[lax.rem(w + wide - t, wide)], piece_got.at[t])
        over_plane(t).wait_send()
    for t in range(1, narrow):
        down_column(t).wait_send()
    for h, i in halves:
        first(h, i).wait_send()
        second(h, i).wait_send()
    for zs in order:
        to_sibling(zs).wait_send()
    fed(lines - 2)
    for zs in range(lines):
        for c in range(chunks):

            @pl.when(jnp.logical_and(z >= 1, zs > z))
            def _():
                pass_on(zs, c, True).wait_send()

            @pl.when(jnp.logical_and(z <= lines - 2, zs < z))
            def _():
                pass_on(zs, c, False).wait_send()


def finish(wide, narrow, packed, weight, normed, tokens, middle, gain, norm_parts, piece, chunks=2):
    side, lines = math.isqrt(wide), narrow // 2
    rows, features = tokens.shape
    columns = packed.shape[0]
    dma = pltpu.SemaphoreType.DMA
    vmem = pl.BlockSpec(memory_space=pltpu.VMEM)
    anywhere = pl.BlockSpec(memory_space=pl.ANY)
    return pl.pallas_call(
        functools.partial(finish_kernel, wide, narrow, chunks),
        in_specs=[vmem, vmem, anywhere, vmem, vmem, vmem, vmem, anywhere],
        out_specs=(vmem, vmem, anywhere, vmem),
        out_shape=(
            jax.ShapeDtypeStruct((rows, features), bf16),
            jax.ShapeDtypeStruct((columns, features), bf16),
            jax.ShapeDtypeStruct((wide, *piece.shape), bf16),
            jax.ShapeDtypeStruct((8, features), f32),
        ),
        scratch_shapes=[
            pltpu.VMEM(normed.shape, bf16),
            pltpu.VMEM((lines, rows, features), bf16),
            pltpu.VMEM((lines, rows, features), bf16),
            pltpu.VMEM((lines, rows, features), bf16),
            pltpu.VMEM((lines + 1, rows, features), bf16),
            pltpu.VMEM((columns, features), f32),
            pltpu.VMEM((2, columns // 2, features), bf16),
            pltpu.VMEM((2, side - 1, columns // 2, features), bf16),
            pltpu.VMEM((2, side - 1, columns // 2, features), bf16),
            pltpu.VMEM((2, columns // 2, features), bf16),
            pltpu.VMEM((8, features), f32),
            pltpu.VMEM((narrow - 1, 8, features), f32),
            pltpu.VMEM((8, features), f32),
            pltpu.VMEM((wide - 1, 8, features), f32),
            dma(()),
            dma(()),
            dma((lines,)),
            dma((lines,)),
            dma((lines, chunks)),
            dma((lines + 1, chunks)),
            dma((wide,)),
            dma((wide,)),
            dma((2, side - 1)),
            dma((2, side - 1)),
            dma((2, side - 1)),
            dma((2, side - 1)),
            dma((narrow - 1,)),
            dma((narrow - 1,)),
            dma((wide - 1,)),
            dma((wide - 1,)),
        ],
        compiler_params=pltpu.CompilerParams(
            vmem_limit_bytes=58 << 20, collective_id=3, has_side_effects=True
        ),
        name="finish",
    )(packed, weight, normed, tokens, middle, gain, norm_parts, piece)


def product(spec, left, right):
    return jnp.einsum(spec, left, right, preferred_element_type=f32)


def gather_kernel(W,N,own,out,lsem,s1,s1b,r1,s2,r2,s3,r3,fs0,fr0,fs1,fr1,fs2,fr2,fs3,fr3):
    w=lax.axis_index("wide"); n=lax.axis_index("narrow")
    W1=math.isqrt(W); H=N//2
    a=w//W1; b=lax.rem(w,W1); z=n//2; core=lax.rem(n,2); sib=n+1-2*core
    greet(W,N,w,n)
    def rc(src,dst,ss,rs,dw,dn):
        return pltpu.make_async_remote_copy(src_ref=src,dst_ref=dst,send_sem=ss,recv_sem=rs,device_id=(dw,dn),device_id_type=MESH)
    def arrived(ref,sem):
        pltpu.make_async_copy(ref,ref,sem).wait()
    oa=lambda i: lax.rem(a+i,W1)
    ob=lambda i: lax.rem(b+i,W1)
    def d1(zs,step):
        return rc(out.at[2*zs+core,a,b],out.at[2*zs+core,a,b],s1b.at[zs],r1.at[zs],w,n+2*step)
    def own1(step):
        return rc(own.at[a,b],out.at[n,a,b],s1.at[z+step],r1.at[z],w,n+2*step)
    def d2(ns,zs,h,i):
        if h==0: return rc(out.at[ns,a,b,0],out.at[ns,a,b,0],s2.at[zs,0,i],r2.at[zs,0,b],a*W1+ob(i),n)
        return rc(out.at[ns,a,b,1],out.at[ns,a,b,1],s2.at[zs,1,i],r2.at[zs,1,a],oa(i)*W1+b,n)
    def d3(ns,zs,h,i):
        if h==0: return rc(out.at[ns,a,:,0],out.at[ns,a,:,0],s3.at[zs,0,i],r3.at[zs,0,a],oa(i)*W1+b,n)
        return rc(out.at[ns,:,b,1],out.at[ns,:,b,1],s3.at[zs,1,i],r3.at[zs,1,b],a*W1+ob(i),n)
    f0=rc(own,out.at[n],fs0,fr0,w,sib)
    def f1(ns,zs): return rc(out.at[ns,a,b],out.at[ns,a,b],fs1.at[zs],fr1.at[zs],w,sib)
    def f2(ns,zs,h,i):
        v=out.at[ns,a,ob(i),0] if h==0 else out.at[ns,oa(i),b,1]
        k=ob(i) if h==0 else oa(i)
        return rc(v,v,fs2.at[zs,h,k],fr2.at[zs,h,k],w,sib)
    def f3(ns,zs,h,i):
        v=out.at[ns,oa(i),:,0] if h==0 else out.at[ns,:,ob(i),1]
        k=oa(i) if h==0 else ob(i)
        return rc(v,v,fs3.at[zs,h,k],fr3.at[zs,h,k],w,sib)
    local=pltpu.make_async_copy(own,out.at[n],lsem)
    up=z<H-1; down=z>0
    @pl.when(up)
    def _(): own1(1).start()
    @pl.when(down)
    def _(): own1(-1).start()
    local.start(); f0.start()
    def sides(d,f):
        @pl.when(jnp.logical_and(d<=H-1,z-d>=0))
        def _(): f(z-d,1,up)
        @pl.when(jnp.logical_and(d<=H-1,z+d<=H-1))
        def _(): f(z+d,-1,down)
    def step1(zs,step,more):
        ns=2*zs+core
        arrived(out.at[ns,a,b],r1.at[zs])
        @pl.when(more)
        def _(): d1(zs,step).start()
        for i in range(1,W1):
            d2(ns,zs,0,i).start(); d2(ns,zs,1,i).start()
        f1(ns,zs).start()
    def step2(zs,step,more):
        ns=2*zs+core
        for i in range(1,W1):
            arrived(out.at[ns,a,ob(i),0],r2.at[zs,0,ob(i)])
        for i in range(1,W1): d3(ns,zs,0,i).start()
        for i in range(1,W1):
            arrived(out.at[ns,oa(i),b,1],r2.at[zs,1,oa(i)])
        for i in range(1,W1): d3(ns,zs,1,i).start()
        for i in range(1,W1):
            f2(ns,zs,0,i).start(); f2(ns,zs,1,i).start()
    def step3(zs,step,more):
        ns=2*zs+core
        for i in range(1,W1):
            arrived(out.at[ns,oa(i),:,0],r3.at[zs,0,oa(i)])
            f3(ns,zs,0,i).start()
            arrived(out.at[ns,:,ob(i),1],r3.at[zs,1,ob(i)])
            f3(ns,zs,1,i).start()
    def run(d,_):
        sides(d,step1)
        @pl.when(d>1)
        def _(): sides(d-1,step2)
        @pl.when(d>2)
        def _(): sides(d-2,step3)
        return 0
    lax.fori_loop(1,H+2,run,0)
    local.wait()
    f0.wait_send(); arrived(out.at[sib],fr0)
    @pl.when(up)
    def _(): own1(1).wait_send()
    @pl.when(down)
    def _(): own1(-1).wait_send()
    def finish(zs,step,more):
        ns=2*zs+core; nb=ns+1-2*core
        @pl.when(more)
        def _(): d1(zs,step).wait_send()
        f1(ns,zs).wait_send(); arrived(out.at[nb,a,b],fr1.at[zs])
        for h in (0,1):
            for i in range(1,W1):
                d2(ns,zs,h,i).wait_send(); d3(ns,zs,h,i).wait_send()
                f2(ns,zs,h,i).wait_send(); f3(ns,zs,h,i).wait_send()
                v2=out.at[nb,a,ob(i),0] if h==0 else out.at[nb,oa(i),b,1]
                arrived(v2,fr2.at[zs,h,ob(i) if h==0 else oa(i)])
                v3=out.at[nb,oa(i),:,0] if h==0 else out.at[nb,:,ob(i),1]
                arrived(v3,fr3.at[zs,h,oa(i) if h==0 else ob(i)])
    def fin(d,_):
        sides(d,finish); return 0
    lax.fori_loop(1,H,fin,0)

def gather_weights(W,N,own):
    W1=math.isqrt(W); H=N//2
    D=pltpu.SemaphoreType.DMA
    return pl.pallas_call(functools.partial(gather_kernel,W,N),out_shape=jax.ShapeDtypeStruct((N,)+own.shape,bf16),
      in_specs=[pl.BlockSpec(memory_space=pl.ANY)],out_specs=pl.BlockSpec(memory_space=pl.ANY),
      scratch_shapes=[D(()),D((H,)),D((H,)),D((H,)),D((H,2,W1)),D((H,2,W1)),D((H,2,W1)),D((H,2,W1)),D(()),D(()),D((H,)),D((H,)),D((H,2,W1)),D((H,2,W1)),D((H,2,W1)),D((H,2,W1))],
      compiler_params=pltpu.CompilerParams(collective_id=1,has_side_effects=True,vmem_limit_bytes=1<<20),name="gather_weights")(own)

def body(
    tokens, cotangent, item_lengths, attn_gain, attn_bias, qkv_weight, proj_weight,
    mlp_gain, mlp_bias, up_weight, down_weight,
):
    items = item_lengths.shape[1]
    token_rows = tokens.astype(f32)
    heads = qkv_weight.shape[1] // (3 * HEAD_DIM)
    gain_one, bias_one = attn_gain.astype(f32), attn_bias.astype(f32)
    gain_two, bias_two = mlp_gain.astype(f32), mlp_bias.astype(f32)
    wide, narrow = lax.axis_size("wide"), lax.axis_size("narrow")
    qkv_turned = qkv_weight.T
    side = math.isqrt(wide)

    def cut(shard):
        return shard.reshape(side, side, 2, shard.shape[0] // (2 * wide), shard.shape[1])

    def split_parts(total):
        return total.reshape(narrow, side, side, 2, -1, total.shape[1])

    shards = [cut(up_weight.T), cut(down_weight), cut(proj_weight)]
    everything = gather_weights(wide, narrow, jnp.concatenate(shards, axis=3))
    first = shards[0].shape[3]
    features = tokens.shape[1]
    normed = norm_forward(token_rows, gain_one, bias_one).astype(bf16)
    normed_all = lax.all_gather(normed, "narrow", axis=0, tiled=True)
    normed_all, everything = lax.optimization_barrier((normed_all, everything))
    rows = normed_all.shape[0]
    query_extra, key_extra = mask_rows(item_lengths, rows)
    packed = (
        product("rd,cd->cr", normed_all, qkv_turned).astype(bf16).reshape(heads, 3, HEAD_DIM, rows)
    )
    attended, log_total = attend_forward(packed, query_extra, key_extra)
    up_all = everything[:, :, :, :, :first].reshape(-1, tokens.shape[1])
    down_all = everything[:, :, :, :, first : 2 * first].reshape(-1, tokens.shape[1])
    proj_all = everything[:, :, :, :, 2 * first :].reshape(-1, tokens.shape[1])
    attended_rows = lax.all_to_all(
        attended.reshape(heads * HEAD_DIM, rows), "narrow", split_axis=1, concat_axis=0, tiled=True
    )
    branch = product("ar,ad->rd", attended_rows, proj_all)
    middle = token_rows + branch
    expand_in = norm_forward(middle, gain_two, bias_two).astype(bf16)
    hidden_pre = product("rd,fd->rf", expand_in, up_all)
    hidden = gelu_exact(hidden_pre).astype(bf16)
    output = (middle + product("rf,fd->rd", hidden, down_all)).astype(bf16)

    grad_hidden = product("rd,fd->rf", cotangent, down_all)
    grad_pre = jax.vjp(gelu_exact, hidden_pre)[1](grad_hidden)[0].astype(bf16)
    grad_expand = product("rf,fd->rd", grad_pre, up_all)
    grad_middle_norm, grad_gain_two, grad_bias_two = jax.vjp(
        norm_forward, middle, gain_two, bias_two
    )[1](grad_expand)
    grad_middle = cotangent.astype(f32) + grad_middle_norm
    grad_branch = grad_middle.astype(bf16)
    grad_attended = lax.all_to_all(
        product("rd,ad->ar", grad_branch, proj_all).astype(bf16),
        "narrow", split_axis=0, concat_axis=1, tiled=True,
    ).reshape(heads, HEAD_DIM, rows)
    grad_parts = jnp.concatenate(
        [
            split_parts(product("rf,rd->fd", grad_pre, expand_in).astype(bf16)),
            split_parts(product("rf,rd->fd", hidden, cotangent).astype(bf16)),
            split_parts(product("ar,rd->ad", attended_rows, grad_branch).astype(bf16)),
        ],
        axis=4,
    )
    grad_packed, grad_piece = attend_backward(
        wide, narrow, packed, query_extra, key_extra, attended, grad_attended, log_total,
        grad_parts, items,
    )
    grad_packed = grad_packed.reshape(heads * 3 * HEAD_DIM, rows)
    norm_parts = jnp.zeros((8, tokens.shape[1]), f32)
    norm_parts = norm_parts.at[2].set(grad_gain_two).at[3].set(grad_bias_two)
    grad_tokens, grad_qkv, grad_shard, norm_sums = finish(
        wide, narrow, grad_packed, qkv_turned, normed_all, tokens, grad_middle,
        gain_one.reshape(1, -1), norm_parts, grad_piece,
    )
    grad_shard = grad_shard.astype(f32)
    grad_up = grad_shard[:, :, :first].reshape(-1, tokens.shape[1]).T
    grad_down = grad_shard[:, :, first : 2 * first].reshape(-1, tokens.shape[1])
    grad_proj = grad_shard[:, :, 2 * first :].reshape(-1, tokens.shape[1])
    share = norm_sums.shape[1] // narrow
    shares = lax.dynamic_slice_in_dim(norm_sums, lax.axis_index("narrow") * share, share, 1)
    return (
        output, grad_tokens, shares[0], shares[1], grad_qkv.T.astype(f32), grad_proj,
        shares[2], shares[3], grad_up, grad_down,
    )


def solution(mesh):
    by_rows = P(("wide", "narrow"), None)
    return jax.shard_map(
        body,
        mesh=mesh,
        in_specs=(
            by_rows, by_rows, P("wide", None), P(), P(), P(None, "narrow"), P("narrow", None),
            P(), P(), P(None, "narrow"), P("narrow", None),
        ),
        out_specs=(
            by_rows, by_rows, P("narrow"), P("narrow"), P(None, "narrow"), P("narrow", None),
            P("narrow"), P("narrow"), P(None, "narrow"), P("narrow", None),
        ),
        check_vma=False,
    )
```

```python
import functools
import math

import jax
import jax.numpy as jnp
from jax import lax
from jax.experimental import pallas as pl
from jax.experimental.pallas import tpu as pltpu
from jax.sharding import PartitionSpec as P

HEAD_DIM = 64
EXTRA = 16
ATTENTION_STEPS = 16
EXCLUDED = -1e30
bf16 = jnp.bfloat16
f32 = jnp.float32
MESH = pl.DeviceIdType.MESH
epsilon = 1e-05


def mask_rows(item_lengths, rows):
    lengths = item_lengths[0]
    items = lengths.shape[0]
    index = jnp.arange(items)
    ends = jnp.sum(jnp.where(index[:, None] >= index[None, :], lengths[None, :], 0), axis=1)
    segment = jnp.sum((jnp.arange(rows)[None, :] >= ends[:, None]).astype(jnp.int32), axis=0)
    extra = jnp.arange(EXTRA)[:, None]
    own = segment[None, :] == extra
    query_extra = jnp.where(own & (extra <= items), 1.0, 0.0).astype(bf16)
    key_extra = jnp.where(
        extra <= items,
        jnp.where(own, 0.0, EXCLUDED),
        jnp.where(extra <= items + 3, 1.0, 0.0),
    ).astype(bf16)
    return query_extra, key_extra


def forward_kernel(
    wide, narrow, qx_ref, kx_ref, q_ref, k_ref, v_ref, own_ref, o_ref, log_ref, rows_ref, gathered,
    keys, ready, copied, sent, got, *gather_refs,
):
    gather = Gather(wide, narrow, own_ref, gathered, *gather_refs)
    w, n, lines = gather.w, gather.n, gather.lines
    head, step = pl.program_id(0), pl.program_id(1)
    moment = head * narrow + step
    width = q_ref.shape[-1] // narrow
    last = heads_of(ready, narrow) * narrow - 1

    moves = [(0.0, lambda: greet(wide, narrow, w, n)), (0.1, gather.begin)]
    for d in range(1, lines):
        moves += [
            (3.0 * d, functools.partial(gather.sides, d, gather.one)),
            (3.0 * d + 2.1, functools.partial(gather.sides, d, gather.two)),
            (3.0 * d + 5.2, functools.partial(gather.sides, d, gather.three)),
        ]
    moves.append((900.0, gather.finish))
    moves.sort(key=lambda move: move[0])

    def perform(lower, upper):
        for time, move in moves:
            if lower <= time < upper:
                move()

    for tick in range(last + 1):

        @pl.when(moment == tick)
        def _():
            perform(tick, tick + 1)

    @pl.when(step == 0)
    def _():
        keys[...] = jnp.concatenate([k_ref[0], kx_ref[...]], axis=0).T

    owner = lax.rem(n + 1 + step, narrow)
    columns = pl.ds(pl.multiple_of(owner * width, width), width)
    query = jnp.concatenate(
        [q_ref[0, :, columns] * jnp.asarray(0.125, bf16), qx_ref[:, columns]], axis=0
    )
    scores = jnp.dot(keys[...], query, preferred_element_type=f32)
    maximum = jnp.max(scores, axis=0, keepdims=True)
    raised = jnp.exp(scores - maximum)
    total = jnp.sum(raised, axis=0, keepdims=True)
    gathered_values = jnp.dot(v_ref[0], raised.astype(bf16), preferred_element_type=f32)
    result = (gathered_values / total).astype(bf16)
    o_ref[0, :, columns] = result
    log_ref[0, :, columns] = maximum + jnp.log(total)
    ready[moment] = result

    def deliver(k, owner, h):
        return remote(ready.at[k], rows_ref.at[n, h], sent.at[k], got.at[n, h], w, owner)

    def deliver_here(k, h):
        return pltpu.make_async_copy(ready.at[k], rows_ref.at[n, h], copied.at[h])

    @pl.when(step < narrow - 1)
    def _():
        deliver(moment, owner, head).start()

    @pl.when(step == narrow - 1)
    def _():
        deliver_here(moment, head).start()

    @pl.when(moment == last)
    def _():
        perform(last + 1, 1000)
        for h in range((last + 1) // narrow):
            deliver_here(h * narrow + narrow - 1, h).wait()
            for t in range(narrow - 1):
                deliver(h * narrow + t, lax.rem(n + 1 + t, narrow), h).wait_send()
                source = lax.rem(n + narrow - 1 - t, narrow)
                arrived(rows_ref.at[source, h], got.at[source, h])


def heads_of(ready, narrow):
    return ready.shape[0] // narrow


def attend_forward(wide, narrow, packed, query_extra, key_extra, own):
    heads, _, _, rows = packed.shape
    width = rows // narrow
    dma = pltpu.SemaphoreType.DMA

    def whole(j):
        return pl.BlockSpec((1, None, HEAD_DIM, rows), lambda h, i: (h, j, 0, 0))

    extra = pl.BlockSpec((EXTRA, rows), lambda h, i: (0, 0))
    anywhere = pl.BlockSpec(memory_space=pl.ANY)
    return pl.pallas_call(
        functools.partial(forward_kernel, wide, narrow),
        grid=(heads, narrow),
        in_specs=[extra, extra, whole(0), whole(1), whole(2), anywhere],
        out_specs=(
            pl.BlockSpec((1, HEAD_DIM, rows), lambda h, i: (h, 0, 0)),
            pl.BlockSpec((1, 1, rows), lambda h, i: (h, 0, 0)),
            anywhere,
            anywhere,
        ),
        out_shape=(
            jax.ShapeDtypeStruct((heads, HEAD_DIM, rows), bf16),
            jax.ShapeDtypeStruct((heads, 1, rows), f32),
            jax.ShapeDtypeStruct((narrow, heads, HEAD_DIM, width), bf16),
            jax.ShapeDtypeStruct((narrow, *own.shape), bf16),
        ),
        scratch_shapes=[
            pltpu.VMEM((rows, HEAD_DIM + EXTRA), bf16),
            pltpu.VMEM((heads * narrow, HEAD_DIM, width), bf16),
            dma((heads,)),
            dma((heads * narrow,)),
            dma((narrow, heads)),
            *Gather.scratch(wide, narrow),
        ],
        compiler_params=pltpu.CompilerParams(
            vmem_limit_bytes=58 << 20, collective_id=4, has_side_effects=True
        ),
        name="attend_forward",
    )(query_extra, key_extra, packed, packed, packed, own)


def remote(src, dst, sent, received, wide_to, narrow_to):
    return pltpu.make_async_remote_copy(
        src_ref=src,
        dst_ref=dst,
        send_sem=sent,
        recv_sem=received,
        device_id=(wide_to, narrow_to),
        device_id_type=MESH,
    )


def arrived(ref, semaphore):
    pltpu.make_async_copy(ref, ref, semaphore).wait()


def greet(wide, narrow, w, n):
    barrier = pltpu.get_barrier_semaphore()

    def column(t, carry):
        pl.semaphore_signal(
            barrier, inc=1, device_id=(w, lax.rem(n + t, narrow)), device_id_type=MESH
        )
        return carry

    def plane(t, carry):
        pl.semaphore_signal(
            barrier, inc=1, device_id=(lax.rem(w + t, wide), n), device_id_type=MESH
        )
        return carry

    lax.fori_loop(1, narrow, column, 0)
    lax.fori_loop(1, wide, plane, 0)
    pl.semaphore_wait(barrier, narrow + wide - 2)


def accumulate(into, *others):
    rows = into.shape[0]
    few = max([d for d in (16, 32, 48, 64) if rows % d == 0], default=rows)

    def piece(j, carry):
        part = pl.ds(j * few if rows == few else pl.multiple_of(j * few, few), few)
        total = into[part, :].astype(f32)
        for other in others:
            total = total + other[part, :].astype(f32)
        into[part, :] = total.astype(bf16)
        return carry

    if rows == few:
        piece(0, 0)
    else:
        lax.fori_loop(0, rows // few, piece, 0)


def reduce_steps(
    wide, narrow, parts, proj_parts, final, held, from_sibling, from_first, from_second, from_line,
    loaded, sib_sent, sib_got, first_sent, first_got, second_sent, second_got, line_sent, line_got,
):
    w, n = lax.axis_index("wide"), lax.axis_index("narrow")
    side, lines = math.isqrt(wide), narrow // 2
    a, b, z, core = w // side, lax.rem(w, side), n // 2, lax.rem(n, 2)
    sibling = n + 1 - 2 * core

    def other_a(i):
        return lax.rem(a + i, side)

    def other_b(i):
        return lax.rem(b + i, side)

    most, least = parts.shape[4], proj_parts.shape[4]
    sources = [(parts, pl.ds(0, most)), (proj_parts, pl.ds(most, least))]

    def to_sibling(zs):
        shard = 2 * zs + 1 - core
        return [
            remote(
                src.at[shard], from_sibling.at[zs, :, :, :, rows],
                sib_sent.at[k, zs], sib_got.at[k, zs], w, sibling,
            )
            for k, (src, rows) in enumerate(sources)
        ]

    def load(zs):
        shard = 2 * zs + core
        return [
            pltpu.make_async_copy(src.at[shard], held.at[zs, :, :, :, rows], loaded.at[k, zs])
            for k, (src, rows) in enumerate(sources)
        ]

    def first(zs, h, i):
        if h == 0:
            src, to = held.at[zs, other_a(i), :, 0], other_a(i) * side + b
        else:
            src, to = held.at[zs, :, other_b(i), 1], a * side + other_b(i)
        k = i - 1
        return remote(
            src, from_first.at[zs, h, k], first_sent.at[zs, h, k], first_got.at[zs, h, k], to, n
        )

    def second(zs, h, i):
        if h == 0:
            src, to = held.at[zs, a, other_b(i), 0], a * side + other_b(i)
        else:
            src, to = held.at[zs, other_a(i), b, 1], other_a(i) * side + b
        k = i - 1
        return remote(
            src, from_second.at[zs, h, k], second_sent.at[zs, h, k], second_got.at[zs, h, k], to, n
        )

    def along(zs):
        slot = jnp.where(z < zs, z, z - 1)
        return remote(
            held.at[zs, a, b], from_line.at[slot], line_sent.at[zs], line_got.at[slot], w, 2 * zs + core
        )

    order = []
    for i in range((lines + 1) // 2):
        order += [lines - 1 - i] if lines - 1 - i == i else [lines - 1 - i, i]
    halves = [(h, i) for i in range(1, side) for h in (0, 1)]

    def begin():
        greet(wide, narrow, w, n)
        for zs in order:
            for copy in to_sibling(zs) + load(zs):
                copy.start()

    def combine(zs):
        for copy in load(zs):
            copy.wait()
        for k, (_, rows) in enumerate(sources):
            arrived(from_sibling.at[zs, :, :, :, rows], sib_got.at[k, zs])

        def piece(j, carry):
            p, q = j // side, lax.rem(j, side)
            for h in (0, 1):
                accumulate(held.at[zs, p, q, h], from_sibling.at[zs, p, q, h])
            return carry

        lax.fori_loop(0, wide, piece, 0)
        for h, i in halves:
            first(zs, h, i).start()

    def narrow_down(zs):
        for h in (0, 1):
            for i in range(1, side):
                arrived(from_first.at[zs, h, i - 1], first_got.at[zs, h, i - 1])

            def piece(j, carry, h=h):
                into = held.at[zs, a, j, 0] if h == 0 else held.at[zs, j, b, 1]
                accumulate(into, *[from_first.at[zs, h, i, j] for i in range(side - 1)])
                return carry

            lax.fori_loop(0, side, piece, 0)
        for h, i in halves:
            second(zs, h, i).start()

    def send_home(zs):
        for h, i in halves:
            arrived(from_second.at[zs, h, i - 1], second_got.at[zs, h, i - 1])
        for h in (0, 1):
            accumulate(
                held.at[zs, a, b, h], *[from_second.at[zs, h, i] for i in range(side - 1)]
            )

        @pl.when(z != zs)
        def _():
            along(zs).start()

    def finish():
        for slot in range(lines - 1):
            arrived(from_line.at[slot], line_got.at[slot])
        for h in (0, 1):
            total = held[z, a, b, h].astype(f32)
            for slot in range(lines - 1):
                total = total + from_line[slot, h].astype(f32)
            final[h] = total.astype(bf16)
        for zs in order:
            for copy in to_sibling(zs):
                copy.wait_send()
            for h, i in halves:
                first(zs, h, i).wait_send()
                second(zs, h, i).wait_send()

            @pl.when(z != zs)
            def _():
                along(zs).wait_send()

    steps = [(0.0, begin)]
    for i, zs in enumerate(order):
        at = 1 + 4 * i
        steps += [
            (at, functools.partial(combine, zs)),
            (at + 3.2, functools.partial(narrow_down, zs)),
            (at + 5.4, functools.partial(send_home, zs)),
        ]
    steps.append((99, finish))
    return [step for _, step in sorted(steps, key=lambda s: s[0])], sorted(at for at, _ in steps)


def reduce_scratch(wide, narrow, rows, features):
    side, lines = math.isqrt(wide), narrow // 2
    dma = pltpu.SemaphoreType.DMA
    return [
        pltpu.VMEM((lines, side, side, 2, rows, features), bf16),
        pltpu.VMEM((lines, side, side, 2, rows, features), bf16),
        pltpu.VMEM((lines, 2, side - 1, side, rows, features), bf16),
        pltpu.VMEM((lines, 2, side - 1, rows, features), bf16),
        pltpu.VMEM((lines - 1, 2, rows, features), bf16),
        dma((2, lines)),
        dma((2, lines)),
        dma((2, lines)),
        dma((lines, 2, side - 1)),
        dma((lines, 2, side - 1)),
        dma((lines, 2, side - 1)),
        dma((lines, 2, side - 1)),
        dma((lines,)),
        dma((lines - 1,)),
    ]


def backward_kernel(
    block, rows, items, wide, narrow, qx_ref, kx_ref, q_ref, k_ref, v_ref, o_ref, do_ref, log_ref,
    parts_ref, proj_parts_ref, grad_ref, final_ref, keys, values, grad_k, grad_v, *reduce_refs,
):
    width = q_ref.shape[-1]
    step = pl.program_id(1)
    steps_per_head = pl.num_programs(1)
    moment = pl.program_id(0) * steps_per_head + step
    ticks = ATTENTION_STEPS
    moves, times = reduce_steps(wide, narrow, parts_ref, proj_parts_ref, final_ref, *reduce_refs)

    def perform(lower, upper):
        for move, time in zip(moves, times):
            if lower <= time < upper:
                move()

    for tick in range(ticks):

        @pl.when(moment == tick)
        def _():
            perform(tick, tick + 1)

    @pl.when(step == 0)
    def _():
        keys[...] = jnp.concatenate([k_ref[0], kx_ref[...]], axis=0)
        values[...] = jnp.concatenate([v_ref[0], kx_ref[...]], axis=0)
        grad_k[...] = jnp.zeros_like(grad_k)
        grad_v[...] = jnp.zeros_like(grad_v)

    row = lax.broadcasted_iota(jnp.int32, (EXTRA, width), 0) - items

    def pieces(term, base):
        high = term.astype(bf16).astype(f32)
        middle = (term - high).astype(bf16).astype(f32)
        small = term - high - middle
        return jnp.where(
            row == 1, high, jnp.where(row == 2, middle, jnp.where(row == 3, small, base))
        ).astype(bf16)

    query = q_ref[0] * jnp.asarray(0.125, bf16)
    grad = do_ref[0]
    inner = jnp.sum(grad.astype(f32) * o_ref[0].astype(f32), axis=0, keepdims=True)
    query_wide = jnp.concatenate(
        [query, pieces(-log_ref[0], qx_ref[...].astype(f32))], axis=0
    ).T
    grad_wide = jnp.concatenate(
        [grad, pieces(-inner, jnp.zeros((EXTRA, width), f32))], axis=0
    ).T
    grad_q = jnp.zeros((HEAD_DIM, width), f32)
    for i in range(rows // block):
        part = pl.ds(i * block, block)
        probs = jnp.exp(jnp.dot(query_wide, keys[:, part], preferred_element_type=f32))
        grad_scores = (
            probs * jnp.dot(grad_wide, values[:, part], preferred_element_type=f32)
        ).astype(bf16)
        grad_v[:, part] += jnp.dot(grad, probs.astype(bf16), preferred_element_type=f32)
        grad_k[:, part] += jnp.dot(query, grad_scores, preferred_element_type=f32)
        grad_q += lax.dot_general(
            k_ref[0, :, part], grad_scores, (((1,), (1,)), ((), ())), preferred_element_type=f32
        )
    grad_ref[0, 0, :, pl.ds(pl.multiple_of(step * width, width), width)] = (
        grad_q * 0.125
    ).astype(bf16)

    @pl.when(step == steps_per_head - 1)
    def _():
        grad_ref[0, 1] = grad_k[...].astype(bf16)
        grad_ref[0, 2] = grad_v[...].astype(bf16)

    @pl.when(moment == ticks - 1)
    def _():
        perform(ticks, 1000)


def attend_backward(
    wide, narrow, packed, query_extra, key_extra, attended, grad, log_total, parts,
    proj_parts, items, block=512,
):
    heads, _, _, rows = packed.shape
    width = heads * rows // ATTENTION_STEPS
    piece = (parts.shape[4] + proj_parts.shape[4], parts.shape[5])

    def whole(j):
        return pl.BlockSpec((1, None, HEAD_DIM, rows), lambda h, i: (h, j, 0, 0))

    part = pl.BlockSpec((1, HEAD_DIM, width), lambda h, i: (h, 0, i))
    return pl.pallas_call(
        functools.partial(backward_kernel, block, rows, items, wide, narrow),
        grid=(heads, rows // width),
        in_specs=[
            pl.BlockSpec((EXTRA, width), lambda h, i: (0, i)),
            pl.BlockSpec((EXTRA, rows), lambda h, i: (0, 0)),
            pl.BlockSpec((1, None, HEAD_DIM, width), lambda h, i: (h, 0, 0, i)),
            whole(1),
            whole(2),
            part,
            part,
            pl.BlockSpec((1, 1, width), lambda h, i: (h, 0, i)),
            pl.BlockSpec(memory_space=pl.ANY),
            pl.BlockSpec(memory_space=pl.ANY),
        ],
        out_specs=(
            pl.BlockSpec((1, 3, HEAD_DIM, rows), lambda h, i: (h, 0, 0, 0)),
            pl.BlockSpec((2, *piece), lambda h, i: (0, 0, 0)),
        ),
        out_shape=(
            jax.ShapeDtypeStruct((heads, 3, HEAD_DIM, rows), bf16),
            jax.ShapeDtypeStruct((2, *piece), bf16),
        ),
        scratch_shapes=[
            pltpu.VMEM((HEAD_DIM + EXTRA, rows), bf16),
            pltpu.VMEM((HEAD_DIM + EXTRA, rows), bf16),
            pltpu.VMEM((HEAD_DIM, rows), f32),
            pltpu.VMEM((HEAD_DIM, rows), f32),
            *reduce_scratch(wide, narrow, *piece),
        ],
        compiler_params=pltpu.CompilerParams(
            vmem_limit_bytes=58 << 20, collective_id=2, has_side_effects=True
        ),
        cost_estimate=pl.CostEstimate(
            flops=10 * heads * rows * rows * 256,
            bytes_accessed=heads * rows * HEAD_DIM * 16,
            transcendentals=heads * rows * rows,
        ),
        name="attend_backward",
    )(query_extra, key_extra, packed, packed, packed, attended, grad, log_total, parts, proj_parts)


def contract(left, right, left_axis, right_axis):
    return lax.dot_general(
        left, right, (((left_axis,), (right_axis,)), ((), ())), preferred_element_type=f32
    )


def gelu_pair(values):
    half = 0.5 + 0.5 * lax.erf(values * 0.7071067811865476)
    slope = half + values * (jnp.exp(values * values * -0.5) * 0.3989422804014327)
    return values * half, slope


def mlp_kernel(
    att_ref, proj_ref, token_ref, cot_ref, gain_ref, bias_ref, up_ref, down_ref,
    out_ref, middle_out, att_out, proj_out, parts_ref, norm_ref,
    middle, expand, out_total, expand_total,
):
    step = pl.program_id(0)
    rows, features = token_ref.shape
    few = 64

    def by_rows(change):
        def body(j, carry):
            return change(pl.ds(pl.multiple_of(j * few, few), few), carry)

        return body

    @pl.when(step == 0)
    def _():
        middle[...] = token_ref[...].astype(f32) + contract(att_ref[...], proj_ref[...], 0, 0)
        out_total[...] = jnp.zeros_like(out_total)
        expand_total[...] = jnp.zeros_like(expand_total)

        def norm(part, carry):
            values = middle[part, :]
            centred = values - jnp.mean(values, axis=-1, keepdims=True)
            variance = jnp.mean(centred * centred, axis=-1, keepdims=True)
            expand[part, :] = (
                centred * lax.rsqrt(variance + epsilon) * gain_ref[...] + bias_ref[...]
            ).astype(bf16)
            return carry

        lax.fori_loop(0, rows // few, by_rows(norm), 0)

    def flat(ref):
        if ref.shape[4] % 16:
            return ref[0].astype(f32).reshape(-1, features).astype(bf16)
        return ref[0].reshape(-1, features)

    up, down = flat(up_ref), flat(down_ref)
    units = up_ref.shape[4]
    pieces = up_ref.shape[1:4]
    hidden_parts, grad_parts = [], []
    for part in (pl.ds(0, rows // 2), pl.ds(rows // 2, rows // 2)):
        hidden, slope = gelu_pair(contract(expand[part, :], up, 1, 1))
        grad_pre = (contract(cot_ref[part, :], down, 1, 1) * slope).astype(bf16)
        hidden = hidden.astype(bf16)
        out_total[part, :] += jnp.dot(hidden, down, preferred_element_type=f32)
        expand_total[part, :] += jnp.dot(grad_pre, up, preferred_element_type=f32)
        hidden_parts.append(hidden)
        grad_parts.append(grad_pre)
    grad_up = contract(jnp.concatenate(grad_parts, axis=0), expand[...], 0, 0)
    grad_down = contract(jnp.concatenate(hidden_parts, axis=0), cot_ref[...], 0, 0)
    parts_ref[0, :, :, :, 0:units, :] = grad_up.reshape(*pieces, units, features).astype(bf16)
    parts_ref[0, :, :, :, units : 2 * units, :] = grad_down.reshape(
        *pieces, units, features
    ).astype(bf16)

    @pl.when(step == pl.num_programs(0) - 1)
    def _():
        def finish_rows(part, carry):
            gain_sum, bias_sum = carry
            values = middle[part, :]
            out_ref[part, :] = (values + out_total[part, :]).astype(bf16)
            centred = values - jnp.mean(values, axis=-1, keepdims=True)
            inverse = lax.rsqrt(jnp.mean(centred * centred, axis=-1, keepdims=True) + epsilon)
            scaled = centred * inverse
            grad = expand_total[part, :]
            term = grad * gain_ref[...]
            back = inverse * (
                term
                - jnp.mean(term, axis=-1, keepdims=True)
                - scaled * jnp.mean(term * scaled, axis=-1, keepdims=True)
            )
            total = cot_ref[part, :].astype(f32) + back
            middle_out[part, :] = total
            expand[part, :] = total.astype(bf16)
            gain_sum = gain_sum + jnp.sum(grad * scaled, axis=0, keepdims=True)
            bias_sum = bias_sum + jnp.sum(grad, axis=0, keepdims=True)
            return gain_sum, bias_sum

        start = (jnp.zeros((1, features), f32), jnp.zeros((1, features), f32))
        gain_sum, bias_sum = lax.fori_loop(0, rows // few, by_rows(finish_rows), start)
        row = lax.broadcasted_iota(jnp.int32, (8, features), 0)
        norm_ref[...] = jnp.where(row == 2, gain_sum, jnp.where(row == 3, bias_sum, 0.0))
        branch = expand[...]
        att_out[...] = contract(proj_ref[...], branch, 1, 1).astype(bf16)
        proj_out[...] = jnp.dot(att_ref[...], branch, preferred_element_type=f32).astype(bf16)


def mlp(attended, proj, tokens, cotangent, gain, bias, up_all, down_all, units):
    rows, features = tokens.shape
    narrow, side = up_all.shape[:2]

    def whole(*shape):
        return pl.BlockSpec(shape, lambda i: (0,) * len(shape))

    weights = pl.BlockSpec((1, side, side, 2, units, features), lambda i: (i, 0, 0, 0, 0, 0))
    return pl.pallas_call(
        mlp_kernel,
        grid=(narrow,),
        in_specs=[
            whole(*attended.shape),
            whole(*proj.shape),
            whole(rows, features),
            whole(rows, features),
            whole(1, features),
            whole(1, features),
            weights,
            weights,
        ],
        out_specs=(
            whole(rows, features),
            whole(rows, features),
            whole(*attended.shape),
            whole(*proj.shape),
            pl.BlockSpec(
                (1, side, side, 2, 2 * units, features), lambda i: (i, 0, 0, 0, 0, 0)
            ),
            whole(8, features),
        ),
        out_shape=(
            jax.ShapeDtypeStruct((rows, features), bf16),
            jax.ShapeDtypeStruct((rows, features), f32),
            jax.ShapeDtypeStruct(attended.shape, bf16),
            jax.ShapeDtypeStruct(proj.shape, bf16),
            jax.ShapeDtypeStruct((narrow, side, side, 2, 2 * units, features), bf16),
            jax.ShapeDtypeStruct((8, features), f32),
        ),
        scratch_shapes=[
            pltpu.VMEM((rows, features), f32),
            pltpu.VMEM((rows, features), bf16),
            pltpu.VMEM((rows, features), f32),
            pltpu.VMEM((rows, features), f32),
        ],
        compiler_params=pltpu.CompilerParams(vmem_limit_bytes=58 << 20),
        name="mlp",
    )(attended, proj, tokens, cotangent, gain, bias, up_all, down_all)


def finish_kernel(
    wide, narrow, chunks,
    packed_ref, weight_ref, normed_ref, token_ref, middle_ref, gain_ref, norm_ref, piece_ref,
    tokens_out, qkv_out, shard_out, norms_out,
    normed, held, for_sibling, from_sibling, from_line, total_qkv, own_qkv, first_qkv, second_qkv,
    half_qkv, norms, norm_column, norm_half, norm_plane,
    loaded, copied, sib_sent, sib_got, line_sent, line_got, piece_sent, piece_got,
    first_sent, first_got, second_sent, second_got, column_sent, column_got, plane_sent, plane_got,
):
    w, n = lax.axis_index("wide"), lax.axis_index("narrow")
    side, lines = math.isqrt(wide), narrow // 2
    a, b, z, core = w // side, lax.rem(w, side), n // 2, lax.rem(n, 2)
    sibling = n + 1 - 2 * core
    rows, features = held.shape[1:]
    step = rows // chunks
    load = pltpu.make_async_copy(normed_ref, normed, loaded)
    load.start()
    greet(wide, narrow, w, n)

    keep = pltpu.make_async_copy(piece_ref, shard_out.at[w], copied)
    keep.start()

    def spread(t):
        return remote(
            piece_ref, shard_out.at[w], piece_sent.at[t], piece_got.at[t], lax.rem(w + t, wide), n
        )

    for t in range(1, wide):
        spread(t).start()

    order = []
    for i in range((lines + 1) // 2):
        order += [lines - 1 - i] if lines - 1 - i == i else [lines - 1 - i, i]

    def block(owner):
        columns = pl.ds(pl.multiple_of(owner * rows, rows), rows)
        return lax.dot_general(
            packed_ref[:, columns], weight_ref[...], (((0,), (0,)), ((), ())),
            preferred_element_type=f32,
        ).astype(bf16)

    def to_sibling(zs):
        return remote(
            for_sibling.at[zs], from_sibling.at[zs], sib_sent.at[zs], sib_got.at[zs], w, sibling
        )

    def pass_on(zs, c, up):
        part = pl.ds(c * step, step)
        slot = zs if up else jnp.where(z - 1 == zs, lines, zs)
        to = n + 2 if up else n - 2
        return remote(
            held.at[zs, part], from_line.at[slot, part], line_sent.at[zs, c], line_got.at[slot, c], w, to
        )

    def merge(zs):
        arrived(from_sibling.at[zs], sib_got.at[zs])
        accumulate(held.at[zs], from_sibling.at[zs])

    def feed(t):
        @pl.when(z == 0)
        def _():
            for c in range(chunks):
                pass_on(lines - 1 - t, c, True).start()

        @pl.when(z == lines - 1)
        def _():
            for c in range(chunks):
                pass_on(t, c, False).start()

    def fed(t):
        @pl.when(z == 0)
        def _():
            for c in range(chunks):
                pass_on(lines - 1 - t, c, True).wait_send()

        @pl.when(z == lines - 1)
        def _():
            for c in range(chunks):
                pass_on(t, c, False).wait_send()

    for i, zs in enumerate(order):
        for_sibling[zs] = block(2 * zs + 1 - core)
        to_sibling(zs).start()
        held[zs] = block(2 * zs + core)
        if i >= 1:
            merge(order[i - 1])
        if i == 2:
            feed(0)
    merge(order[-1])
    if lines <= 2:
        feed(0)

    load.wait()
    total_qkv[...] = jnp.dot(packed_ref[...], normed[...], preferred_element_type=f32)
    half = total_qkv.shape[0] // 2
    for h in (0, 1):
        own_qkv[h] = total_qkv[h * half : (h + 1) * half].astype(bf16)

    def along(h, i):
        if h == 0:
            return lax.rem(a + i, side) * side + b
        return a * side + lax.rem(b + i, side)

    halves = [(h, i) for i in range(1, side) for h in (0, 1)]

    def first(h, i):
        return remote(
            own_qkv.at[h], first_qkv.at[h, i - 1], first_sent.at[h, i - 1], first_got.at[h, i - 1],
            along(h, i), n,
        )

    def second(h, i):
        return remote(
            half_qkv.at[h], second_qkv.at[h, i - 1], second_sent.at[h, i - 1], second_got.at[h, i - 1],
            along(1 - h, i), n,
        )

    def qkv_first():
        for h, i in halves:
            first(h, i).start()

    def qkv_second():
        for h, i in halves:
            arrived(first_qkv.at[h, i - 1], first_got.at[h, i - 1])
        for h in (0, 1):
            total = own_qkv[h].astype(f32)
            for i in range(1, side):
                total = total + first_qkv[h, i - 1].astype(f32)
            half_qkv[h] = total.astype(bf16)
        for h, i in halves:
            second(h, i).start()

    def qkv_last():
        for h, i in halves:
            arrived(second_qkv.at[h, i - 1], second_got.at[h, i - 1])
        for h in (0, 1):
            total = half_qkv[h].astype(f32)
            for i in range(1, side):
                total = total + second_qkv[h, i - 1].astype(f32)
            qkv_out[h * half : (h + 1) * half] = total.astype(bf16)

    qkv_first()
    for t in range(1, lines):
        if t <= lines - 2:
            fed(t - 1)
            feed(t)
        below, above = lines - 1 - (t - z), t - (lines - 1 - z)
        for c in range(chunks):
            part = pl.ds(c * step, step)
            if t < lines - 1:

                @pl.when(jnp.logical_and(z >= 1, t >= z))
                def _():
                    arrived(from_line.at[below, part], line_got.at[below, c])
                    accumulate(held.at[below, part], from_line.at[below, part])
                    pass_on(below, c, True).start()

                @pl.when(jnp.logical_and(z <= lines - 2, above >= 0))
                def _():
                    arrived(from_line.at[above, part], line_got.at[above, c])
                    accumulate(held.at[above, part], from_line.at[above, part])
                    pass_on(above, c, False).start()
        if t == 1:
            qkv_second()
        if t == min(2, lines - 1):
            qkv_last()

    def zero_edges(at_edge, slot):
        @pl.when(at_edge)
        def _():
            from_line[slot] = jnp.zeros((rows, features), bf16)

    zero_edges(z == 0, z)
    zero_edges(z == lines - 1, lines)
    for c in range(chunks):
        part = pl.ds(c * step, step)

        @pl.when(z >= 1)
        def _():
            arrived(from_line.at[z, part], line_got.at[z, c])

        @pl.when(z <= lines - 2)
        def _():
            arrived(from_line.at[lines, part], line_got.at[lines, c])

        def norm_rows(j, carry):
            gain_sum, bias_sum = carry
            few = pl.ds(pl.multiple_of(c * step + j * 32, 32), 32)
            grad = (
                held[z, few].astype(f32)
                + from_line[z, few].astype(f32)
                + from_line[lines, few].astype(f32)
            )
            values = token_ref[few, :].astype(f32)
            centred = values - jnp.mean(values, axis=-1, keepdims=True)
            inverse = lax.rsqrt(jnp.mean(centred * centred, axis=-1, keepdims=True) + epsilon)
            scaled = centred * inverse
            term = grad * gain_ref[...]
            back = inverse * (
                term
                - jnp.mean(term, axis=-1, keepdims=True)
                - scaled * jnp.mean(term * scaled, axis=-1, keepdims=True)
            )
            tokens_out[few, :] = (middle_ref[few, :] + back).astype(bf16)
            gain_sum = gain_sum + jnp.sum(grad * scaled, axis=0, keepdims=True)
            bias_sum = bias_sum + jnp.sum(grad, axis=0, keepdims=True)
            return gain_sum, bias_sum

        start = (jnp.zeros((1, features), f32), jnp.zeros((1, features), f32))
        sums = lax.fori_loop(0, step // 32, norm_rows, start)
        if c == 0:
            gain_sum, bias_sum = sums
        else:
            gain_sum, bias_sum = gain_sum + sums[0], bias_sum + sums[1]

    row = lax.broadcasted_iota(jnp.int32, (8, features), 0)
    norms[...] = jnp.where(row == 0, gain_sum, jnp.where(row == 1, bias_sum, norm_ref[...]))

    def down_column(t):
        return remote(
            norms, norm_column.at[t - 1], column_sent.at[t - 1], column_got.at[t - 1],
            w, lax.rem(n + t, narrow),
        )

    def over_plane(t):
        return remote(
            norm_half, norm_plane.at[t - 1], plane_sent.at[t - 1], plane_got.at[t - 1],
            lax.rem(w + t, wide), n,
        )

    for t in range(1, narrow):
        down_column(t).start()
    total = norms[...]
    for t in range(1, narrow):
        arrived(norm_column.at[t - 1], column_got.at[t - 1])
        total = total + norm_column[t - 1]
    norm_half[...] = total
    for t in range(1, wide):
        over_plane(t).start()
    for t in range(1, wide):
        arrived(norm_plane.at[t - 1], plane_got.at[t - 1])
        total = total + norm_plane[t - 1]
    norms_out[...] = total

    keep.wait()
    for t in range(1, wide):
        spread(t).wait_send()
        arrived(shard_out.at[lax.rem(w + wide - t, wide)], piece_got.at[t])
        over_plane(t).wait_send()
    for t in range(1, narrow):
        down_column(t).wait_send()
    for h, i in halves:
        first(h, i).wait_send()
        second(h, i).wait_send()
    for zs in order:
        to_sibling(zs).wait_send()
    fed(lines - 2)
    for zs in range(lines):
        for c in range(chunks):

            @pl.when(jnp.logical_and(z >= 1, zs > z))
            def _():
                pass_on(zs, c, True).wait_send()

            @pl.when(jnp.logical_and(z <= lines - 2, zs < z))
            def _():
                pass_on(zs, c, False).wait_send()


def finish(wide, narrow, packed, weight, normed, tokens, middle, gain, norm_parts, piece, chunks=2):
    side, lines = math.isqrt(wide), narrow // 2
    rows, features = tokens.shape
    columns = packed.shape[0]
    dma = pltpu.SemaphoreType.DMA
    vmem = pl.BlockSpec(memory_space=pltpu.VMEM)
    anywhere = pl.BlockSpec(memory_space=pl.ANY)
    return pl.pallas_call(
        functools.partial(finish_kernel, wide, narrow, chunks),
        in_specs=[vmem, vmem, anywhere, vmem, vmem, vmem, vmem, anywhere],
        out_specs=(vmem, vmem, anywhere, vmem),
        out_shape=(
            jax.ShapeDtypeStruct((rows, features), bf16),
            jax.ShapeDtypeStruct((columns, features), bf16),
            jax.ShapeDtypeStruct((wide, *piece.shape), bf16),
            jax.ShapeDtypeStruct((8, features), f32),
        ),
        scratch_shapes=[
            pltpu.VMEM(normed.shape, bf16),
            pltpu.VMEM((lines, rows, features), bf16),
            pltpu.VMEM((lines, rows, features), bf16),
            pltpu.VMEM((lines, rows, features), bf16),
            pltpu.VMEM((lines + 1, rows, features), bf16),
            pltpu.VMEM((columns, features), f32),
            pltpu.VMEM((2, columns // 2, features), bf16),
            pltpu.VMEM((2, side - 1, columns // 2, features), bf16),
            pltpu.VMEM((2, side - 1, columns // 2, features), bf16),
            pltpu.VMEM((2, columns // 2, features), bf16),
            pltpu.VMEM((8, features), f32),
            pltpu.VMEM((narrow - 1, 8, features), f32),
            pltpu.VMEM((8, features), f32),
            pltpu.VMEM((wide - 1, 8, features), f32),
            dma(()),
            dma(()),
            dma((lines,)),
            dma((lines,)),
            dma((lines, chunks)),
            dma((lines + 1, chunks)),
            dma((wide,)),
            dma((wide,)),
            dma((2, side - 1)),
            dma((2, side - 1)),
            dma((2, side - 1)),
            dma((2, side - 1)),
            dma((narrow - 1,)),
            dma((narrow - 1,)),
            dma((wide - 1,)),
            dma((wide - 1,)),
        ],
        compiler_params=pltpu.CompilerParams(
            vmem_limit_bytes=58 << 20, collective_id=3, has_side_effects=True
        ),
        name="finish",
    )(packed, weight, normed, tokens, middle, gain, norm_parts, piece)


class Gather:
    def __init__(self, wide, narrow, own, out, *semaphores):
        self.own, self.out = own, out
        self.w, self.n = lax.axis_index("wide"), lax.axis_index("narrow")
        self.side, self.lines = math.isqrt(wide), narrow // 2
        self.a, self.b = self.w // self.side, lax.rem(self.w, self.side)
        self.z, self.core = self.n // 2, lax.rem(self.n, 2)
        self.sibling = self.n + 1 - 2 * self.core
        (
            self.copied, self.own_sent, self.passed, self.line_got, self.first_sent, self.first_got,
            self.second_sent, self.second_got, self.f0_sent, self.f0_got, self.f1_sent, self.f1_got,
            self.f2_sent, self.f2_got, self.f3_sent, self.f3_got,
        ) = semaphores
        self.pairs = [(h, i) for i in range(1, self.side) for h in (0, 1)]

    @staticmethod
    def scratch(wide, narrow):
        side, lines = math.isqrt(wide), narrow // 2
        dma = pltpu.SemaphoreType.DMA
        line, plane = (lines,), (lines, 2, side)
        shapes = [(), line, line, line, plane, plane, plane, plane, (), (), line, line]
        return [dma(shape) for shape in shapes + [plane] * 4]

    def other_a(self, i):
        return lax.rem(self.a + i, self.side)

    def other_b(self, i):
        return lax.rem(self.b + i, self.side)

    def own_on(self, way):
        return remote(
            self.own.at[self.a, self.b], self.out.at[self.n, self.a, self.b],
            self.own_sent.at[self.z + way], self.line_got.at[self.z], self.w, self.n + 2 * way,
        )

    def pass_on(self, zs, way):
        piece = self.out.at[2 * zs + self.core, self.a, self.b]
        return remote(
            piece, piece, self.passed.at[zs], self.line_got.at[zs], self.w, self.n + 2 * way
        )

    def first(self, zs, h, i):
        shard = 2 * zs + self.core
        piece = self.out.at[shard, self.a, self.b, h]
        if h == 0:
            to, mine = self.a * self.side + self.other_b(i), self.b
        else:
            to, mine = self.other_a(i) * self.side + self.b, self.a
        return remote(
            piece, piece, self.first_sent.at[zs, h, i], self.first_got.at[zs, h, mine], to, self.n
        )

    def second(self, zs, h, i):
        shard = 2 * zs + self.core
        if h == 0:
            piece = self.out.at[shard, self.a, :, 0]
            to, mine = self.other_a(i) * self.side + self.b, self.a
        else:
            piece = self.out.at[shard, :, self.b, 1]
            to, mine = self.a * self.side + self.other_b(i), self.b
        return remote(
            piece, piece, self.second_sent.at[zs, h, i], self.second_got.at[zs, h, mine], to, self.n
        )

    def first_from(self, shard, h, i):
        if h == 0:
            return self.out.at[shard, self.a, self.other_b(i), 0], self.other_b(i)
        return self.out.at[shard, self.other_a(i), self.b, 1], self.other_a(i)

    def second_from(self, shard, h, i):
        if h == 0:
            return self.out.at[shard, self.other_a(i), :, 0], self.other_a(i)
        return self.out.at[shard, :, self.other_b(i), 1], self.other_b(i)

    def hand0(self):
        return remote(
            self.own, self.out.at[self.n], self.f0_sent, self.f0_got, self.w, self.sibling
        )

    def hand1(self, zs):
        piece = self.out.at[2 * zs + self.core, self.a, self.b]
        return remote(piece, piece, self.f1_sent.at[zs], self.f1_got.at[zs], self.w, self.sibling)

    def hand2(self, zs, h, i):
        piece, k = self.first_from(2 * zs + self.core, h, i)
        return remote(
            piece, piece, self.f2_sent.at[zs, h, k], self.f2_got.at[zs, h, k], self.w, self.sibling
        )

    def hand3(self, zs, h, i):
        piece, k = self.second_from(2 * zs + self.core, h, i)
        return remote(
            piece, piece, self.f3_sent.at[zs, h, k], self.f3_got.at[zs, h, k], self.w, self.sibling
        )

    def keep(self):
        return pltpu.make_async_copy(self.own, self.out.at[self.n], self.copied)

    def sides(self, d, act):
        if not 1 <= d <= self.lines - 1:
            return
        z, last = self.z, self.lines - 1

        @pl.when(z >= d)
        def _():
            act(z - d, 1, z < last)

        @pl.when(z + d <= last)
        def _():
            act(z + d, -1, z > 0)

    def begin(self):
        @pl.when(self.z < self.lines - 1)
        def _():
            self.own_on(1).start()

        @pl.when(self.z > 0)
        def _():
            self.own_on(-1).start()

        self.keep().start()
        self.hand0().start()

    def one(self, zs, way, more):
        arrived(self.out.at[2 * zs + self.core, self.a, self.b], self.line_got.at[zs])

        @pl.when(more)
        def _():
            self.pass_on(zs, way).start()

        for h, i in self.pairs:
            self.first(zs, h, i).start()
        self.hand1(zs).start()

    def two(self, zs, way, more):
        for h in (0, 1):
            for i in range(1, self.side):
                piece, k = self.first_from(2 * zs + self.core, h, i)
                arrived(piece, self.first_got.at[zs, h, k])
            for i in range(1, self.side):
                self.second(zs, h, i).start()
        for h, i in self.pairs:
            self.hand2(zs, h, i).start()

    def three(self, zs, way, more):
        for h, i in self.pairs:
            piece, k = self.second_from(2 * zs + self.core, h, i)
            arrived(piece, self.second_got.at[zs, h, k])
            self.hand3(zs, h, i).start()

    def round(self, d):
        self.sides(d, self.one)
        self.sides(d - 1, self.two)
        self.sides(d - 2, self.three)

    def finish_side(self, zs, way, more):
        theirs = 2 * zs + 1 - self.core

        @pl.when(more)
        def _():
            self.pass_on(zs, way).wait_send()

        self.hand1(zs).wait_send()
        arrived(self.out.at[theirs, self.a, self.b], self.f1_got.at[zs])
        for h, i in self.pairs:
            self.first(zs, h, i).wait_send()
            self.second(zs, h, i).wait_send()
            self.hand2(zs, h, i).wait_send()
            self.hand3(zs, h, i).wait_send()
            piece, k = self.first_from(theirs, h, i)
            arrived(piece, self.f2_got.at[zs, h, k])
            piece, k = self.second_from(theirs, h, i)
            arrived(piece, self.f3_got.at[zs, h, k])

    def finish(self):
        @pl.when(self.z < self.lines - 1)
        def _():
            self.own_on(1).wait_send()

        @pl.when(self.z > 0)
        def _():
            self.own_on(-1).wait_send()

        self.keep().wait()
        self.hand0().wait_send()
        arrived(self.out.at[self.sibling], self.f0_got)
        for d in range(1, self.lines):
            self.sides(d, self.finish_side)


def start_kernel(
    wide, narrow, token_ref, gain_ref, bias_ref, weight_ref, own_ref,
    normed, packed, gathered, line_sent, line_got, sib_sent, sib_got, *gather_refs,
):
    gather = Gather(wide, narrow, own_ref, gathered, *gather_refs)
    w, n, z, core = gather.w, gather.n, gather.z, gather.core
    lines, sibling = gather.lines, gather.sibling
    rows = token_ref.shape[0]

    def norm_rows(j, carry):
        part = pl.ds(pl.multiple_of(j * 64, 64), 64)
        values = token_ref[part, :].astype(f32)
        centred = values - jnp.mean(values, axis=-1, keepdims=True)
        variance = jnp.mean(centred * centred, axis=-1, keepdims=True)
        normed[n, part, :] = (
            centred * lax.rsqrt(variance + epsilon) * gain_ref[...] + bias_ref[...]
        ).astype(bf16)
        return carry

    lax.fori_loop(0, rows // 64, norm_rows, 0)
    greet(wide, narrow, w, n)

    def pass_on(zs, way):
        block = normed.at[2 * zs + core]
        k = (1 - way) // 2
        return remote(block, block, line_sent.at[zs, k], line_got.at[zs], w, n + 2 * way)

    def hand(zs):
        block = normed.at[2 * zs + core]
        return remote(block, block, sib_sent.at[zs], sib_got.at[zs], w, sibling)

    def project(owner):
        columns = pl.ds(pl.multiple_of(owner * rows, rows), rows)
        packed[:, columns] = contract(weight_ref[...], normed[owner], 1, 1).astype(bf16)

    @pl.when(z < lines - 1)
    def _():
        pass_on(z, 1).start()

    @pl.when(z > 0)
    def _():
        pass_on(z, -1).start()

    hand(z).start()
    project(n)

    def receive(zs, way, more):
        arrived(normed.at[2 * zs + core], line_got.at[zs])

        @pl.when(more)
        def _():
            pass_on(zs, way).start()

        hand(zs).start()

    def project_side(zs, way, more):
        project(2 * zs + core)

    def project_sibling(zs, way, more):
        arrived(normed.at[2 * zs + 1 - core], sib_got.at[zs])
        project(2 * zs + 1 - core)

    for d in range(1, lines):
        gather.sides(d, receive)
        if d == 1:
            gather.begin()
            project_sibling(z, 0, None)
        else:
            gather.round(d - 1)
            gather.sides(d - 1, project_sibling)
        gather.sides(d, project_side)
    gather.round(lines - 1)
    gather.sides(lines - 1, project_sibling)
    gather.round(lines)
    gather.round(lines + 1)
    gather.finish()

    def sent_side(zs, way, more):
        hand(zs).wait_send()

        @pl.when(more)
        def _():
            pass_on(zs, way).wait_send()

    @pl.when(z < lines - 1)
    def _():
        pass_on(z, 1).wait_send()

    @pl.when(z > 0)
    def _():
        pass_on(z, -1).wait_send()

    hand(z).wait_send()
    for d in range(1, lines):
        gather.sides(d, sent_side)


def start(wide, narrow, tokens, gain, bias, weight, own):
    rows, features = tokens.shape
    lines = narrow // 2
    dma = pltpu.SemaphoreType.DMA
    vmem = pl.BlockSpec(memory_space=pltpu.VMEM)
    anywhere = pl.BlockSpec(memory_space=pl.ANY)
    return pl.pallas_call(
        functools.partial(start_kernel, wide, narrow),
        in_specs=[vmem, vmem, vmem, vmem, anywhere],
        out_specs=(vmem, vmem, anywhere),
        out_shape=(
            jax.ShapeDtypeStruct((narrow, rows, features), bf16),
            jax.ShapeDtypeStruct((weight.shape[0], narrow * rows), bf16),
            jax.ShapeDtypeStruct((narrow, *own.shape), bf16),
        ),
        scratch_shapes=[
            dma((lines, 2)), dma((lines,)), dma((lines,)), dma((lines,)),
            *Gather.scratch(wide, narrow),
        ],
        compiler_params=pltpu.CompilerParams(
            vmem_limit_bytes=58 << 20, collective_id=1, has_side_effects=True
        ),
        name="start",
    )(tokens, gain, bias, weight, own)


def body(
    tokens, cotangent, item_lengths, attn_gain, attn_bias, qkv_weight, proj_weight,
    mlp_gain, mlp_bias, up_weight, down_weight,
):
    items = item_lengths.shape[1]
    heads = qkv_weight.shape[1] // (3 * HEAD_DIM)
    gain_one, bias_one = attn_gain.astype(f32), attn_bias.astype(f32)
    gain_two, bias_two = mlp_gain.astype(f32), mlp_bias.astype(f32)
    wide, narrow = lax.axis_size("wide"), lax.axis_size("narrow")
    side = math.isqrt(wide)
    rows = narrow * tokens.shape[0]
    qkv_turned = qkv_weight.T

    def cut(shard):
        return shard.reshape(side, side, 2, shard.shape[0] // (2 * wide), shard.shape[1])

    def split_parts(total):
        return total.reshape(narrow, side, side, 2, -1, total.shape[1])

    own_up, own_rest = cut(up_weight.T), jnp.concatenate([cut(down_weight), cut(proj_weight)], axis=3)
    first = own_up.shape[3]
    query_extra, key_extra = mask_rows(item_lengths, rows)
    normed_all, packed, up_all = start(
        wide, narrow, tokens, gain_one.reshape(1, -1), bias_one.reshape(1, -1), qkv_turned, own_up
    )
    normed_all = normed_all.reshape(rows, -1)
    packed = packed.reshape(heads, 3, HEAD_DIM, rows)
    attended, log_total, attended_rows, rest_all = attend_forward(
        wide, narrow, packed, query_extra, key_extra, own_rest
    )
    attended_rows = attended_rows.reshape(-1, tokens.shape[0])
    proj_all = rest_all[:, :, :, :, first:].reshape(-1, tokens.shape[1])
    output, grad_middle, grad_attended, grad_proj, grad_parts, norm_parts = mlp(
        attended_rows, proj_all, tokens, cotangent, gain_two.reshape(1, -1),
        bias_two.reshape(1, -1), up_all, rest_all, first,
    )
    grad_attended = lax.all_to_all(
        grad_attended, "narrow", split_axis=0, concat_axis=1, tiled=True
    ).reshape(heads, HEAD_DIM, rows)
    grad_proj_parts = split_parts(grad_proj)
    grad_packed, grad_piece = attend_backward(
        wide, narrow, packed, query_extra, key_extra, attended, grad_attended, log_total,
        grad_parts, grad_proj_parts, items,
    )
    grad_packed = grad_packed.reshape(heads * 3 * HEAD_DIM, rows)
    grad_tokens, grad_qkv, grad_shard, norm_sums = finish(
        wide, narrow, grad_packed, qkv_turned, normed_all, tokens, grad_middle,
        gain_one.reshape(1, -1), norm_parts, grad_piece,
    )
    grad_shard = grad_shard.astype(f32)
    grad_up = grad_shard[:, :, :first].reshape(-1, tokens.shape[1]).T
    grad_down = grad_shard[:, :, first : 2 * first].reshape(-1, tokens.shape[1])
    grad_proj = grad_shard[:, :, 2 * first :].reshape(-1, tokens.shape[1])
    share = norm_sums.shape[1] // narrow
    shares = lax.dynamic_slice_in_dim(norm_sums, lax.axis_index("narrow") * share, share, 1)
    return (
        output, grad_tokens, shares[0], shares[1], grad_qkv.T.astype(f32), grad_proj,
        shares[2], shares[3], grad_up, grad_down,
    )


def solution(mesh):
    by_rows = P(("wide", "narrow"), None)
    return jax.shard_map(
        body,
        mesh=mesh,
        in_specs=(
            by_rows, by_rows, P("wide", None), P(), P(), P(None, "narrow"), P("narrow", None),
            P(), P(), P(None, "narrow"), P("narrow", None),
        ),
        out_specs=(
            by_rows, by_rows, P("narrow"), P("narrow"), P(None, "narrow"), P("narrow", None),
            P("narrow"), P("narrow"), P(None, "narrow"), P("narrow", None),
        ),
        check_vma=False,
    )
```

```python
import functools
import math

import jax
import jax.numpy as jnp
from jax import lax
from jax.experimental import pallas as pl
from jax.experimental.pallas import tpu as pltpu
from jax.sharding import PartitionSpec as P

HEAD_DIM = 64
EXTRA = 16
CHUNKS = 2
EXCLUDED = -1e30
bf16 = jnp.bfloat16
f32 = jnp.float32
MESH = pl.DeviceIdType.MESH
epsilon = 1e-05


def mask_rows(item_lengths, rows):
    lengths = item_lengths[0]
    items = lengths.shape[0]
    ends = [sum(lengths[j] for j in range(i + 1)) for i in range(items)]
    position = jnp.arange(rows)
    segment = sum((position >= ends[i]).astype(jnp.int32) for i in range(items))
    extra = jnp.arange(EXTRA)[:, None]
    own = segment[None, :] == extra
    mask = extra <= items
    query_extra = jnp.where(own & mask, 1.0, 0.0)
    key_extra = jnp.where(
        mask, jnp.where(own, 0.0, EXCLUDED), jnp.where(extra <= items + 3, 1.0, 0.0)
    )
    return jnp.where(jnp.arange(2)[:, None, None] == 0, query_extra, key_extra).astype(bf16)


def forward_kernel(
    wide, narrow, qx_ref, kx_ref, q_ref, k_ref, v_ref, own_ref, more_ref, o_ref, log_ref, rows_ref, gathered,
    keys, ready, copied, sent, got, *gather_refs,
):
    gather = Gather(wide, narrow, [own_ref, more_ref], gathered, *gather_refs)
    w, n, lines = gather.w, gather.n, gather.lines
    head, step = pl.program_id(0), pl.program_id(1)
    moment = head * narrow + step
    width = q_ref.shape[-1] // narrow
    last = heads_of(ready, narrow) * narrow - 1

    moves = [(0.0, lambda: greet(wide, narrow, w, n)), (0.1, gather.begin)]
    for d in range(1, lines):
        moves += [
            (3.0 * d, functools.partial(gather.sides, d, gather.one)),
            (3.0 * d + 2.1, functools.partial(gather.sides, d, gather.two)),
            (3.0 * d + 5.2, functools.partial(gather.sides, d, gather.three)),
        ]
    moves.append((900.0, gather.finish))
    moves.sort(key=lambda move: move[0])

    def perform(lower, upper):
        for time, move in moves:
            if lower <= time < upper:
                move()

    for tick in range(last + 1):

        @pl.when(moment == tick)
        def _():
            perform(tick, tick + 1)

    @pl.when(step == 0)
    def _():
        keys[...] = jnp.concatenate([k_ref[0], kx_ref[...]], axis=0).T

    owner = lax.rem(n + 1 + step, narrow)
    columns = pl.ds(pl.multiple_of(owner * width, width), width)
    query = jnp.concatenate(
        [q_ref[0, :, columns] * jnp.asarray(0.125, bf16), qx_ref[:, columns]], axis=0
    )
    scores = jnp.dot(keys[...], query, preferred_element_type=f32)
    maximum = jnp.max(scores, axis=0, keepdims=True)
    raised = jnp.exp(scores - maximum)
    total = jnp.sum(raised, axis=0, keepdims=True)
    gathered_values = jnp.dot(v_ref[0], raised.astype(bf16), preferred_element_type=f32)
    result = (gathered_values / total).astype(bf16)
    o_ref[0, :, columns] = result
    log_ref[0, :, columns] = maximum + jnp.log(total)
    ready[moment] = result

    def deliver(k, owner, h):
        return remote(ready.at[k], rows_ref.at[n, h], sent.at[k], got.at[n, h], w, owner)

    def deliver_here(k, h):
        return pltpu.make_async_copy(ready.at[k], rows_ref.at[n, h], copied.at[h])

    @pl.when(step < narrow - 1)
    def _():
        deliver(moment, owner, head).start()

    @pl.when(step == narrow - 1)
    def _():
        deliver_here(moment, head).start()

    @pl.when(moment == last)
    def _():
        perform(last + 1, 1000)
        for h in range((last + 1) // narrow):
            deliver_here(h * narrow + narrow - 1, h).wait()
            for t in range(narrow - 1):
                deliver(h * narrow + t, lax.rem(n + 1 + t, narrow), h).wait_send()
                source = lax.rem(n + narrow - 1 - t, narrow)
                arrived(rows_ref.at[source, h], got.at[source, h])


def heads_of(ready, narrow):
    return ready.shape[0] // narrow


def attend_forward(wide, narrow, packed, extras, own, more):
    heads, _, _, rows = packed.shape
    width = rows // narrow
    gathered = (narrow, *own.shape[:3], own.shape[3] + more.shape[3], own.shape[4])
    dma = pltpu.SemaphoreType.DMA

    def whole(j):
        return pl.BlockSpec((1, None, HEAD_DIM, rows), lambda h, i: (h, j, 0, 0))

    def extra(j):
        return pl.BlockSpec((None, EXTRA, rows), lambda h, i: (j, 0, 0))

    anywhere = pl.BlockSpec(memory_space=pl.ANY)
    return pl.pallas_call(
        functools.partial(forward_kernel, wide, narrow),
        grid=(heads, narrow),
        in_specs=[extra(0), extra(1), whole(0), whole(1), whole(2), anywhere, anywhere],
        out_specs=(
            pl.BlockSpec((1, HEAD_DIM, rows), lambda h, i: (h, 0, 0)),
            pl.BlockSpec((1, 1, rows), lambda h, i: (h, 0, 0)),
            anywhere,
            anywhere,
        ),
        out_shape=(
            jax.ShapeDtypeStruct((heads, HEAD_DIM, rows), bf16),
            jax.ShapeDtypeStruct((heads, 1, rows), f32),
            jax.ShapeDtypeStruct((narrow, heads, HEAD_DIM, width), bf16),
            jax.ShapeDtypeStruct(gathered, bf16),
        ),
        scratch_shapes=[
            pltpu.VMEM((rows, HEAD_DIM + EXTRA), bf16),
            pltpu.VMEM((heads * narrow, HEAD_DIM, width), bf16),
            dma((heads,)),
            dma((heads * narrow,)),
            dma((narrow, heads)),
            *Gather.scratch(wide, narrow, gathered[4:]),
        ],
        compiler_params=pltpu.CompilerParams(
            vmem_limit_bytes=58 << 20, collective_id=4, has_side_effects=True
        ),
        name="attend_forward",
    )(extras, extras, packed, packed, packed, own, more)


def remote(src, dst, sent, received, wide_to, narrow_to):
    return pltpu.make_async_remote_copy(
        src_ref=src,
        dst_ref=dst,
        send_sem=sent,
        recv_sem=received,
        device_id=(wide_to, narrow_to),
        device_id_type=MESH,
    )


def arrived(ref, semaphore):
    pltpu.make_async_copy(ref, ref, semaphore).wait()


def greet(wide, narrow, w, n):
    barrier = pltpu.get_barrier_semaphore()

    def column(t, carry):
        pl.semaphore_signal(
            barrier, inc=1, device_id=(w, lax.rem(n + t, narrow)), device_id_type=MESH
        )
        return carry

    def plane(t, carry):
        pl.semaphore_signal(
            barrier, inc=1, device_id=(lax.rem(w + t, wide), n), device_id_type=MESH
        )
        return carry

    lax.fori_loop(1, narrow, column, 0)
    lax.fori_loop(1, wide, plane, 0)
    pl.semaphore_wait(barrier, narrow + wide - 2)


def accumulate(into, *others):
    rows = into.shape[0]
    few = max([d for d in (16, 32, 48, 64) if rows % d == 0], default=rows)

    def piece(j, carry):
        part = pl.ds(j * few if rows == few else pl.multiple_of(j * few, few), few)
        total = into[part, :].astype(f32)
        for other in others:
            total = total + other[part, :].astype(f32)
        into[part, :] = total.astype(bf16)
        return carry

    if rows == few:
        piece(0, 0)
    else:
        lax.fori_loop(0, rows // few, piece, 0)


def reduce_steps(
    wide, narrow, parts, proj_parts, final, held, from_sibling, from_first, from_second, from_line,
    loaded, sib_sent, sib_got, first_sent, first_got, second_sent, second_got, line_sent, line_got,
):
    w, n = lax.axis_index("wide"), lax.axis_index("narrow")
    side, lines = math.isqrt(wide), narrow // 2
    a, b, z, core = w // side, lax.rem(w, side), n // 2, lax.rem(n, 2)
    sibling = n + 1 - 2 * core

    def other_a(i):
        return lax.rem(a + i, side)

    def other_b(i):
        return lax.rem(b + i, side)

    most, least = parts.shape[4], proj_parts.shape[4]
    sources = [(parts, pl.ds(0, most)), (proj_parts, pl.ds(most, least))]

    def to_sibling(zs):
        shard = 2 * zs + 1 - core
        return [
            remote(
                src.at[shard], from_sibling.at[zs, :, :, :, rows],
                sib_sent.at[k, zs], sib_got.at[k, zs], w, sibling,
            )
            for k, (src, rows) in enumerate(sources)
        ]

    def load(zs):
        shard = 2 * zs + core
        return [
            pltpu.make_async_copy(src.at[shard], held.at[zs, :, :, :, rows], loaded.at[k, zs])
            for k, (src, rows) in enumerate(sources)
        ]

    def first(zs, h, i):
        if h == 0:
            src, to = held.at[zs, other_a(i), :, 0], other_a(i) * side + b
        else:
            src, to = held.at[zs, :, other_b(i), 1], a * side + other_b(i)
        k = i - 1
        return remote(
            src, from_first.at[zs, h, k], first_sent.at[zs, h, k], first_got.at[zs, h, k], to, n
        )

    def second(zs, h, i):
        if h == 0:
            src, to = held.at[zs, a, other_b(i), 0], a * side + other_b(i)
        else:
            src, to = held.at[zs, other_a(i), b, 1], other_a(i) * side + b
        k = i - 1
        return remote(
            src, from_second.at[zs, h, k], second_sent.at[zs, h, k], second_got.at[zs, h, k], to, n
        )

    def along(zs):
        slot = jnp.where(z < zs, z, z - 1)
        return remote(
            held.at[zs, a, b], from_line.at[slot], line_sent.at[zs], line_got.at[slot], w, 2 * zs + core
        )

    order = []
    for i in range((lines + 1) // 2):
        order += [lines - 1 - i] if lines - 1 - i == i else [lines - 1 - i, i]
    halves = [(h, i) for i in range(1, side) for h in (0, 1)]

    def begin():
        for zs in order:
            for copy in to_sibling(zs) + load(zs):
                copy.start()

    def combine(zs):
        for copy in load(zs):
            copy.wait()
        for k, (_, rows) in enumerate(sources):
            arrived(from_sibling.at[zs, :, :, :, rows], sib_got.at[k, zs])

        def piece(j, carry):
            p, q = j // side, lax.rem(j, side)
            for h in (0, 1):
                accumulate(held.at[zs, p, q, h], from_sibling.at[zs, p, q, h])
            return carry

        lax.fori_loop(0, wide, piece, 0)
        for h, i in halves:
            first(zs, h, i).start()

    def narrow_down(zs):
        for h in (0, 1):
            for i in range(1, side):
                arrived(from_first.at[zs, h, i - 1], first_got.at[zs, h, i - 1])

            def piece(j, carry, h=h):
                into = held.at[zs, a, j, 0] if h == 0 else held.at[zs, j, b, 1]
                accumulate(into, *[from_first.at[zs, h, i, j] for i in range(side - 1)])
                return carry

            lax.fori_loop(0, side, piece, 0)
        for h, i in halves:
            second(zs, h, i).start()

    def send_home(zs):
        for h, i in halves:
            arrived(from_second.at[zs, h, i - 1], second_got.at[zs, h, i - 1])
        for h in (0, 1):
            accumulate(
                held.at[zs, a, b, h], *[from_second.at[zs, h, i] for i in range(side - 1)]
            )

        @pl.when(z != zs)
        def _():
            along(zs).start()

    def finish():
        for slot in range(lines - 1):
            arrived(from_line.at[slot], line_got.at[slot])
        for h in (0, 1):
            total = held[z, a, b, h].astype(f32)
            for slot in range(lines - 1):
                total = total + from_line[slot, h].astype(f32)
            final[h] = total.astype(bf16)
        for zs in order:
            for copy in to_sibling(zs):
                copy.wait_send()
            for h, i in halves:
                first(zs, h, i).wait_send()
                second(zs, h, i).wait_send()

            @pl.when(z != zs)
            def _():
                along(zs).wait_send()

    steps = [(0.0, begin)]
    for i, zs in enumerate(order):
        at = 1 + 4 * i
        steps += [
            (at, functools.partial(combine, zs)),
            (at + 3.2, functools.partial(narrow_down, zs)),
            (at + 5.4, functools.partial(send_home, zs)),
        ]
    steps.append((99, finish))
    return [step for _, step in sorted(steps, key=lambda s: s[0])], sorted(at for at, _ in steps)


def reduce_scratch(wide, narrow, rows, features):
    side, lines = math.isqrt(wide), narrow // 2
    dma = pltpu.SemaphoreType.DMA
    return [
        pltpu.VMEM((lines, side, side, 2, rows, features), bf16),
        pltpu.VMEM((lines, side, side, 2, rows, features), bf16),
        pltpu.VMEM((lines, 2, side - 1, side, rows, features), bf16),
        pltpu.VMEM((lines, 2, side - 1, rows, features), bf16),
        pltpu.VMEM((lines - 1, 2, rows, features), bf16),
        dma((2, lines)),
        dma((2, lines)),
        dma((2, lines)),
        dma((lines, 2, side - 1)),
        dma((lines, 2, side - 1)),
        dma((lines, 2, side - 1)),
        dma((lines, 2, side - 1)),
        dma((lines,)),
        dma((lines - 1,)),
    ]


def backward_kernel(
    block, rows, items, wide, narrow, qx_ref, kx_ref, q_ref, k_ref, v_ref, o_ref, log_ref, own_ref,
    parts_ref, proj_parts_ref, grad_ref, final_ref, keys, values, grad_k, grad_v,
    theirs, own_copied, sent, got, *reduce_refs,
):
    width = rows // narrow
    head, step = pl.program_id(0), pl.program_id(1)
    moment = head * narrow + step
    ticks = own_ref.shape[1] * narrow
    moves, times = reduce_steps(wide, narrow, parts_ref, proj_parts_ref, final_ref, *reduce_refs)
    w, n = lax.axis_index("wide"), lax.axis_index("narrow")

    def keep():
        return pltpu.make_async_copy(own_ref.at[n], theirs.at[n], own_copied)

    def deliver(t):
        to = lax.rem(n + t, narrow)
        return remote(own_ref.at[to], theirs.at[n], sent.at[t], got.at[n], w, to)

    @pl.when(moment == 0)
    def _():
        greet(wide, narrow, w, n)
        keep().start()
        for t in range(1, narrow):
            deliver(t).start()

    def perform(lower, upper):
        for move, time in zip(moves, times):
            if lower <= time < upper:
                move()

    for tick in range(ticks):

        @pl.when(moment == tick)
        def _():
            perform(tick, tick + 1)

    @pl.when(step == 0)
    def _():
        keys[...] = jnp.concatenate([k_ref[0], kx_ref[...]], axis=0)
        values[...] = jnp.concatenate([v_ref[0], kx_ref[...]], axis=0)
        grad_k[...] = jnp.zeros_like(grad_k)
        grad_v[...] = jnp.zeros_like(grad_v)

    row = lax.broadcasted_iota(jnp.int32, (EXTRA, width), 0) - items

    def pieces(term, base):
        high = term.astype(bf16).astype(f32)
        middle = (term - high).astype(bf16).astype(f32)
        small = term - high - middle
        return jnp.where(
            row == 1, high, jnp.where(row == 2, middle, jnp.where(row == 3, small, base))
        ).astype(bf16)

    owner = lax.rem(n + narrow - step, narrow)
    columns = pl.ds(pl.multiple_of(owner * width, width), width)

    @pl.when(moment == 0)
    def _():
        keep().wait()

    @pl.when(jnp.logical_and(moment > 0, head == 0))
    def _():
        arrived(theirs.at[owner], got.at[owner])

    query = q_ref[0, :, columns] * jnp.asarray(0.125, bf16)
    grad = theirs[owner, head]
    attended = o_ref[0, :, columns].astype(f32)
    inner = jnp.sum(grad.astype(f32) * attended, axis=0, keepdims=True)
    query_wide = jnp.concatenate(
        [query, pieces(-log_ref[0, :, columns], qx_ref[:, columns].astype(f32))], axis=0
    ).T
    grad_wide = jnp.concatenate(
        [grad, pieces(-inner, jnp.zeros((EXTRA, width), f32))], axis=0
    ).T
    grad_q = jnp.zeros((HEAD_DIM, width), f32)
    for i in range(rows // block):
        part = pl.ds(i * block, block)
        probs = jnp.exp(jnp.dot(query_wide, keys[:, part], preferred_element_type=f32))
        grad_scores = (
            probs * jnp.dot(grad_wide, values[:, part], preferred_element_type=f32)
        ).astype(bf16)
        grad_v[:, part] += jnp.dot(grad, probs.astype(bf16), preferred_element_type=f32)
        grad_k[:, part] += jnp.dot(query, grad_scores, preferred_element_type=f32)
        grad_q += lax.dot_general(
            k_ref[0, :, part], grad_scores, (((1,), (1,)), ((), ())), preferred_element_type=f32
        )
    grad_ref[0, 0, :, columns] = (grad_q * 0.125).astype(bf16)

    @pl.when(step == narrow - 1)
    def _():
        grad_ref[0, 1] = grad_k[...].astype(bf16)
        grad_ref[0, 2] = grad_v[...].astype(bf16)

    @pl.when(moment == ticks - 1)
    def _():
        perform(ticks, 1000)
        for t in range(1, narrow):
            deliver(t).wait_send()


def attend_backward(
    wide, narrow, packed, extras, attended, grad, log_total, parts,
    proj_parts, items, block=512,
):
    heads, _, _, rows = packed.shape
    piece = (parts.shape[4] + proj_parts.shape[4], parts.shape[5])
    dma = pltpu.SemaphoreType.DMA

    def whole(j):
        return pl.BlockSpec((1, None, HEAD_DIM, rows), lambda h, i: (h, j, 0, 0))

    def extra(j):
        return pl.BlockSpec((None, EXTRA, rows), lambda h, i: (j, 0, 0))

    anywhere = pl.BlockSpec(memory_space=pl.ANY)
    return pl.pallas_call(
        functools.partial(backward_kernel, block, rows, items, wide, narrow),
        grid=(heads, narrow),
        in_specs=[
            extra(0),
            extra(1),
            whole(0),
            whole(1),
            whole(2),
            pl.BlockSpec((1, HEAD_DIM, rows), lambda h, i: (h, 0, 0)),
            pl.BlockSpec((1, 1, rows), lambda h, i: (h, 0, 0)),
            anywhere,
            anywhere,
            anywhere,
        ],
        out_specs=(
            pl.BlockSpec((1, 3, HEAD_DIM, rows), lambda h, i: (h, 0, 0, 0)),
            pl.BlockSpec((2, *piece), lambda h, i: (0, 0, 0)),
        ),
        out_shape=(
            jax.ShapeDtypeStruct((heads, 3, HEAD_DIM, rows), bf16),
            jax.ShapeDtypeStruct((2, *piece), bf16),
        ),
        scratch_shapes=[
            pltpu.VMEM((HEAD_DIM + EXTRA, rows), bf16),
            pltpu.VMEM((HEAD_DIM + EXTRA, rows), bf16),
            pltpu.VMEM((HEAD_DIM, rows), f32),
            pltpu.VMEM((HEAD_DIM, rows), f32),
            pltpu.VMEM(grad.shape, bf16),
            dma(()),
            dma((narrow,)),
            dma((narrow,)),
            *reduce_scratch(wide, narrow, *piece),
        ],
        compiler_params=pltpu.CompilerParams(
            vmem_limit_bytes=58 << 20, collective_id=2, has_side_effects=True
        ),
        cost_estimate=pl.CostEstimate(
            flops=10 * heads * rows * rows * 256,
            bytes_accessed=heads * rows * HEAD_DIM * 16,
            transcendentals=heads * rows * rows,
        ),
        name="attend_backward",
    )(extras, extras, packed, packed, packed, attended, log_total, grad, parts, proj_parts)


def as_row(ref):
    return ref[...].astype(f32).reshape(1, -1)


def contract(left, right, left_axis, right_axis):
    return lax.dot_general(
        left, right, (((left_axis,), (right_axis,)), ((), ())), preferred_element_type=f32
    )


def gelu_pair(values):
    half = 0.5 + 0.5 * lax.erf(values * 0.7071067811865476)
    slope = half + values * (jnp.exp(values * values * -0.5) * 0.3989422804014327)
    return values * half, slope


def mlp_kernel(
    att_ref, proj_ref, token_ref, cot_ref, gain_ref, bias_ref, up_ref, down_ref,
    out_ref, middle_out, att_out, proj_out, parts_ref, norm_ref,
    middle, expand, out_total, expand_total,
):
    step = pl.program_id(0)
    rows, features = token_ref.shape
    few = 64

    def by_rows(change):
        def body(j, carry):
            return change(pl.ds(pl.multiple_of(j * few, few), few), carry)

        return body

    @pl.when(step == 0)
    def _():
        middle[...] = token_ref[...].astype(f32) + contract(att_ref[...], proj_ref[...], 0, 0)
        out_total[...] = jnp.zeros_like(out_total)
        expand_total[...] = jnp.zeros_like(expand_total)

        def norm(part, carry):
            values = middle[part, :]
            centred = values - jnp.mean(values, axis=-1, keepdims=True)
            variance = jnp.mean(centred * centred, axis=-1, keepdims=True)
            expand[part, :] = (
                centred * lax.rsqrt(variance + epsilon) * as_row(gain_ref) + as_row(bias_ref)
            ).astype(bf16)
            return carry

        lax.fori_loop(0, rows // few, by_rows(norm), 0)

    def flat(ref):
        if ref.shape[4] % 16:
            return ref[0].astype(f32).reshape(-1, ref.shape[5]).astype(bf16)
        return ref[0].reshape(-1, ref.shape[5])

    up, down = flat(up_ref), flat(down_ref)
    units = down_ref.shape[4]
    pieces = up_ref.shape[1:4]
    columns = up_ref.shape[5]
    hidden_parts, grad_parts = [], []
    for part in (pl.ds(0, rows // 2), pl.ds(rows // 2, rows // 2)):
        hidden, slope = gelu_pair(
            jnp.dot(expand[part, :], up, preferred_element_type=f32)
        )
        grad_pre = (contract(cot_ref[part, :], down, 1, 1) * slope).astype(bf16)
        hidden = hidden.astype(bf16)
        out_total[part, :] += jnp.dot(hidden, down, preferred_element_type=f32)
        expand_total[part, :] += contract(grad_pre, up, 1, 1)
        hidden_parts.append(hidden)
        grad_parts.append(grad_pre)
    grad_up = contract(expand[...], jnp.concatenate(grad_parts, axis=0), 0, 0)
    grad_down = contract(jnp.concatenate(hidden_parts, axis=0), cot_ref[...], 0, 0)
    groups = features // columns
    grad_up = grad_up.reshape(*pieces, groups, units, columns)
    for g in range(groups):
        parts_ref[0, :, :, :, 0:units, g * columns : (g + 1) * columns] = grad_up[
            :, :, :, g
        ].astype(bf16)
    parts_ref[0, :, :, :, units : 2 * units, :] = grad_down.reshape(
        *pieces, units, features
    ).astype(bf16)

    @pl.when(step == pl.num_programs(0) - 1)
    def _():
        def finish_rows(part, carry):
            gain_sum, bias_sum = carry
            values = middle[part, :]
            out_ref[part, :] = (values + out_total[part, :]).astype(bf16)
            centred = values - jnp.mean(values, axis=-1, keepdims=True)
            inverse = lax.rsqrt(jnp.mean(centred * centred, axis=-1, keepdims=True) + epsilon)
            scaled = centred * inverse
            grad = expand_total[part, :]
            term = grad * as_row(gain_ref)
            back = inverse * (
                term
                - jnp.mean(term, axis=-1, keepdims=True)
                - scaled * jnp.mean(term * scaled, axis=-1, keepdims=True)
            )
            total = cot_ref[part, :].astype(f32) + back
            middle_out[part, :] = total
            expand[part, :] = total.astype(bf16)
            gain_sum = gain_sum + jnp.sum(grad * scaled, axis=0, keepdims=True)
            bias_sum = bias_sum + jnp.sum(grad, axis=0, keepdims=True)
            return gain_sum, bias_sum

        start = (jnp.zeros((1, features), f32), jnp.zeros((1, features), f32))
        gain_sum, bias_sum = lax.fori_loop(0, rows // few, by_rows(finish_rows), start)
        row = lax.broadcasted_iota(jnp.int32, (8, features), 0)
        norm_ref[...] = jnp.where(row == 2, gain_sum, jnp.where(row == 3, bias_sum, 0.0))
        branch = expand[...]
        att_out[...] = contract(proj_ref[...], branch, 1, 1).astype(bf16)
        proj_out[...] = jnp.dot(att_ref[...], branch, preferred_element_type=f32).astype(bf16)


def mlp(attended, proj, tokens, cotangent, gain, bias, up_all, down_all, units):
    rows, features = tokens.shape
    narrow, side = up_all.shape[:2]

    def whole(*shape):
        return pl.BlockSpec(shape, lambda i: (0,) * len(shape))

    def weights(*piece):
        return pl.BlockSpec((1, side, side, 2, *piece), lambda i: (i, 0, 0, 0, 0, 0))

    return pl.pallas_call(
        mlp_kernel,
        grid=(narrow,),
        in_specs=[
            whole(*attended.shape),
            whole(*proj.shape),
            whole(rows, features),
            whole(rows, features),
            whole(*gain.shape),
            whole(*bias.shape),
            weights(*up_all.shape[4:]),
            weights(units, features),
        ],
        out_specs=(
            whole(rows, features),
            whole(rows, features),
            whole(*attended.shape),
            whole(*proj.shape),
            pl.BlockSpec(
                (1, side, side, 2, 2 * units, features), lambda i: (i, 0, 0, 0, 0, 0)
            ),
            whole(8, features),
        ),
        out_shape=(
            jax.ShapeDtypeStruct((rows, features), bf16),
            jax.ShapeDtypeStruct((rows, features), f32),
            jax.ShapeDtypeStruct(attended.shape, bf16),
            jax.ShapeDtypeStruct(proj.shape, bf16),
            jax.ShapeDtypeStruct((narrow, side, side, 2, 2 * units, features), bf16),
            jax.ShapeDtypeStruct((8, features), f32),
        ),
        scratch_shapes=[
            pltpu.VMEM((rows, features), f32),
            pltpu.VMEM((rows, features), bf16),
            pltpu.VMEM((rows, features), f32),
            pltpu.VMEM((rows, features), f32),
        ],
        compiler_params=pltpu.CompilerParams(vmem_limit_bytes=58 << 20),
        name="mlp",
    )(attended, proj, tokens, cotangent, gain, bias, up_all, down_all)


def finish_kernel(
    wide, narrow, chunks,
    packed_ref, weight_ref, normed_ref, token_ref, middle_ref, gain_ref, norm_ref, piece_ref,
    tokens_out, qkv_out, shard_out, norms_out,
    normed, held, for_sibling, from_sibling, from_line, total_qkv, own_qkv, first_qkv, second_qkv,
    half_qkv, norms, norm_column, norm_half, norm_plane,
    loaded, copied, sib_sent, sib_got, line_sent, line_got, piece_sent, piece_got,
    first_sent, first_got, second_sent, second_got, column_sent, column_got, plane_sent, plane_got,
):
    w, n = lax.axis_index("wide"), lax.axis_index("narrow")
    side, lines = math.isqrt(wide), narrow // 2
    a, b, z, core = w // side, lax.rem(w, side), n // 2, lax.rem(n, 2)
    sibling = n + 1 - 2 * core
    rows, features = held.shape[1:]
    step = rows // chunks
    load = pltpu.make_async_copy(normed_ref, normed, loaded)
    load.start()
    greet(wide, narrow, w, n)

    keep = pltpu.make_async_copy(piece_ref, shard_out.at[w], copied)
    keep.start()

    def spread(t):
        return remote(
            piece_ref, shard_out.at[w], piece_sent.at[t], piece_got.at[t], lax.rem(w + t, wide), n
        )

    for t in range(1, wide):
        spread(t).start()

    lower = z < lines // 2
    order = [jnp.where(lower, lines - 1 - k, k) for k in range(lines)]

    def block(owner):
        columns = pl.ds(pl.multiple_of(owner * rows, rows), rows)
        return lax.dot_general(
            packed_ref[:, columns], weight_ref[...], (((0,), (0,)), ((), ())),
            preferred_element_type=f32,
        ).astype(bf16)

    def to_sibling(zs):
        return remote(
            for_sibling.at[zs], from_sibling.at[zs], sib_sent.at[zs], sib_got.at[zs], w, sibling
        )

    def pass_on(zs, c, up):
        part = pl.ds(c * step, step)
        slot = zs if up else jnp.where(z - 1 == zs, lines, zs)
        to = n + 2 if up else n - 2
        return remote(
            held.at[zs, part], from_line.at[slot, part], line_sent.at[zs, c], line_got.at[slot, c], w, to
        )

    def merge(zs):
        arrived(from_sibling.at[zs], sib_got.at[zs])
        accumulate(held.at[zs], from_sibling.at[zs])

    flight = 2

    def fed(k):
        t, c = divmod(k, chunks)

        @pl.when(z == 0)
        def _():
            pass_on(lines - 1 - t, c, True).wait_send()

        @pl.when(z == lines - 1)
        def _():
            pass_on(t, c, False).wait_send()

    def feed(k):
        t, c = divmod(k, chunks)
        if k >= flight:
            fed(k - flight)

        @pl.when(z == 0)
        def _():
            pass_on(lines - 1 - t, c, True).start()

        @pl.when(z == lines - 1)
        def _():
            pass_on(t, c, False).start()

    for i, zs in enumerate(order):
        for_sibling[zs] = block(2 * zs + 1 - core)
        to_sibling(zs).start()
        held[zs] = block(2 * zs + core)
        if i >= 1:
            merge(order[i - 1])
        if i == 1:
            for k in range(flight):
                feed(k)
    merge(order[-1])

    load.wait()
    total_qkv[...] = jnp.dot(packed_ref[...], normed[...], preferred_element_type=f32)
    half = total_qkv.shape[0] // 2
    for h in (0, 1):
        own_qkv[h] = total_qkv[h * half : (h + 1) * half].astype(bf16)

    def along(h, i):
        if h == 0:
            return lax.rem(a + i, side) * side + b
        return a * side + lax.rem(b + i, side)

    halves = [(h, i) for i in range(1, side) for h in (0, 1)]

    def first(h, i):
        return remote(
            own_qkv.at[h], first_qkv.at[h, i - 1], first_sent.at[h, i - 1], first_got.at[h, i - 1],
            along(h, i), n,
        )

    def second(h, i):
        return remote(
            half_qkv.at[h], second_qkv.at[h, i - 1], second_sent.at[h, i - 1], second_got.at[h, i - 1],
            along(1 - h, i), n,
        )

    def qkv_first():
        for h, i in halves:
            first(h, i).start()

    def qkv_second():
        for h, i in halves:
            arrived(first_qkv.at[h, i - 1], first_got.at[h, i - 1])
        for h in (0, 1):
            total = own_qkv[h].astype(f32)
            for i in range(1, side):
                total = total + first_qkv[h, i - 1].astype(f32)
            half_qkv[h] = total.astype(bf16)
        for h, i in halves:
            second(h, i).start()

    def qkv_last():
        for h, i in halves:
            arrived(second_qkv.at[h, i - 1], second_got.at[h, i - 1])
        for h in (0, 1):
            total = half_qkv[h].astype(f32)
            for i in range(1, side):
                total = total + second_qkv[h, i - 1].astype(f32)
            qkv_out[h * half : (h + 1) * half] = total.astype(bf16)

    qkv_first()
    for t in range(1, lines):
        below, above = lines - 1 - (t - z), t - (lines - 1 - z)
        for c in range(chunks):
            part = pl.ds(c * step, step)
            k = (t - 1) * chunks + c + flight
            if k < (lines - 1) * chunks:
                feed(k)
            if t < lines - 1:

                @pl.when(jnp.logical_and(z >= 1, t >= z))
                def _():
                    arrived(from_line.at[below, part], line_got.at[below, c])
                    accumulate(held.at[below, part], from_line.at[below, part])
                    pass_on(below, c, True).start()

                @pl.when(jnp.logical_and(z <= lines - 2, above >= 0))
                def _():
                    arrived(from_line.at[above, part], line_got.at[above, c])
                    accumulate(held.at[above, part], from_line.at[above, part])
                    pass_on(above, c, False).start()
        if t == 1:
            qkv_second()
        if t == min(2, lines - 1):
            qkv_last()

    def zero_edges(at_edge, slot):
        @pl.when(at_edge)
        def _():
            from_line[slot] = jnp.zeros((rows, features), bf16)

    zero_edges(z == 0, z)
    zero_edges(z == lines - 1, lines)
    for c in range(chunks):
        part = pl.ds(c * step, step)

        @pl.when(z >= 1)
        def _():
            arrived(from_line.at[z, part], line_got.at[z, c])

        @pl.when(z <= lines - 2)
        def _():
            arrived(from_line.at[lines, part], line_got.at[lines, c])

        def norm_rows(j, carry):
            gain_sum, bias_sum = carry
            few = pl.ds(pl.multiple_of(c * step + j * 32, 32), 32)
            grad = (
                held[z, few].astype(f32)
                + from_line[z, few].astype(f32)
                + from_line[lines, few].astype(f32)
            )
            values = token_ref[few, :].astype(f32)
            centred = values - jnp.mean(values, axis=-1, keepdims=True)
            inverse = lax.rsqrt(jnp.mean(centred * centred, axis=-1, keepdims=True) + epsilon)
            scaled = centred * inverse
            term = grad * as_row(gain_ref)
            back = inverse * (
                term
                - jnp.mean(term, axis=-1, keepdims=True)
                - scaled * jnp.mean(term * scaled, axis=-1, keepdims=True)
            )
            tokens_out[few, :] = (middle_ref[few, :] + back).astype(bf16)
            gain_sum = gain_sum + jnp.sum(grad * scaled, axis=0, keepdims=True)
            bias_sum = bias_sum + jnp.sum(grad, axis=0, keepdims=True)
            return gain_sum, bias_sum

        start = (jnp.zeros((1, features), f32), jnp.zeros((1, features), f32))
        sums = lax.fori_loop(0, step // 32, norm_rows, start)
        if c == 0:
            gain_sum, bias_sum = sums
        else:
            gain_sum, bias_sum = gain_sum + sums[0], bias_sum + sums[1]

    row = lax.broadcasted_iota(jnp.int32, (8, features), 0)
    parts = jnp.where(row == 0, gain_sum, jnp.where(row == 1, bias_sum, norm_ref[...]))
    share = features // narrow
    for owner in range(narrow):
        norms[owner] = parts[:, owner * share : (owner + 1) * share]

    def down_column(t):
        to = lax.rem(n + t, narrow)
        return remote(
            norms.at[to], norm_column.at[t - 1], column_sent.at[t - 1], column_got.at[t - 1], w, to
        )

    def over_plane(t):
        return remote(
            norm_half, norm_plane.at[t - 1], plane_sent.at[t - 1], plane_got.at[t - 1],
            lax.rem(w + t, wide), n,
        )

    for t in range(1, narrow):
        down_column(t).start()
    total = norms[n]
    for t in range(1, narrow):
        arrived(norm_column.at[t - 1], column_got.at[t - 1])
        total = total + norm_column[t - 1]
    norm_half[...] = total
    for t in range(1, wide):
        over_plane(t).start()
    for t in range(1, wide):
        arrived(norm_plane.at[t - 1], plane_got.at[t - 1])
        total = total + norm_plane[t - 1]
    norms_out[...] = total

    keep.wait()
    for t in range(1, wide):
        spread(t).wait_send()
        arrived(shard_out.at[lax.rem(w + wide - t, wide)], piece_got.at[t])
        over_plane(t).wait_send()
    for t in range(1, narrow):
        down_column(t).wait_send()
    for h, i in halves:
        first(h, i).wait_send()
        second(h, i).wait_send()
    for zs in order:
        to_sibling(zs).wait_send()
    for k in range(flight):
        fed((lines - 1) * chunks - 1 - k)
    for zs in range(lines):
        for c in range(chunks):

            @pl.when(jnp.logical_and(z >= 1, zs > z))
            def _():
                pass_on(zs, c, True).wait_send()

            @pl.when(jnp.logical_and(z <= lines - 2, zs < z))
            def _():
                pass_on(zs, c, False).wait_send()


def finish(wide, narrow, packed, weight, normed, tokens, middle, gain, norm_parts, piece, chunks=4):
    side, lines = math.isqrt(wide), narrow // 2
    rows, features = tokens.shape
    columns = packed.shape[0]
    dma = pltpu.SemaphoreType.DMA
    vmem = pl.BlockSpec(memory_space=pltpu.VMEM)
    anywhere = pl.BlockSpec(memory_space=pl.ANY)
    return pl.pallas_call(
        functools.partial(finish_kernel, wide, narrow, chunks),
        in_specs=[vmem, vmem, anywhere, vmem, vmem, vmem, vmem, anywhere],
        out_specs=(vmem, vmem, anywhere, vmem),
        out_shape=(
            jax.ShapeDtypeStruct((rows, features), bf16),
            jax.ShapeDtypeStruct((columns, features), bf16),
            jax.ShapeDtypeStruct((wide, *piece.shape), bf16),
            jax.ShapeDtypeStruct((8, features // narrow), f32),
        ),
        scratch_shapes=[
            pltpu.VMEM(normed.shape, bf16),
            pltpu.VMEM((lines, rows, features), bf16),
            pltpu.VMEM((lines, rows, features), bf16),
            pltpu.VMEM((lines, rows, features), bf16),
            pltpu.VMEM((lines + 1, rows, features), bf16),
            pltpu.VMEM((columns, features), f32),
            pltpu.VMEM((2, columns // 2, features), bf16),
            pltpu.VMEM((2, side - 1, columns // 2, features), bf16),
            pltpu.VMEM((2, side - 1, columns // 2, features), bf16),
            pltpu.VMEM((2, columns // 2, features), bf16),
            pltpu.VMEM((narrow, 8, features // narrow), f32),
            pltpu.VMEM((narrow - 1, 8, features // narrow), f32),
            pltpu.VMEM((8, features // narrow), f32),
            pltpu.VMEM((wide - 1, 8, features // narrow), f32),
            dma(()),
            dma(()),
            dma((lines,)),
            dma((lines,)),
            dma((lines, chunks)),
            dma((lines + 1, chunks)),
            dma((wide,)),
            dma((wide,)),
            dma((2, side - 1)),
            dma((2, side - 1)),
            dma((2, side - 1)),
            dma((2, side - 1)),
            dma((narrow - 1,)),
            dma((narrow - 1,)),
            dma((wide - 1,)),
            dma((wide - 1,)),
        ],
        compiler_params=pltpu.CompilerParams(
            vmem_limit_bytes=58 << 20, collective_id=3, has_side_effects=True
        ),
        name="finish",
    )(packed, weight, normed, tokens, middle, gain, norm_parts, piece)


def unpack_kernel(shard_ref, qkv_ref, qkv_out, proj_out, up_out, down_out):
    wide = shard_ref.shape[0]
    features = shard_ref.shape[3]
    columns = up_out.shape[1]
    groups = features // columns
    units, few = down_out.shape[0] // (2 * wide), proj_out.shape[0] // (2 * wide)
    for j in range(2 * wide):
        w, h = divmod(j, 2)
        for g in range(groups):
            up_out[(j * groups + g) * units : (j * groups + g + 1) * units, :] = shard_ref[
                w, h, 0:units, g * columns : (g + 1) * columns
            ].astype(f32)
        down_out[j * units : (j + 1) * units, :] = shard_ref[w, h, units : 2 * units, :].astype(f32)
        proj_out[j * few : (j + 1) * few, :] = shard_ref[w, h, 2 * units :, :].astype(f32)
    qkv_out[...] = qkv_ref[...].astype(f32).T


def unpack(shard, qkv, proj_shape, up_shape, down_shape):
    return pl.pallas_call(
        unpack_kernel,
        out_shape=tuple(
            jax.ShapeDtypeStruct(shape, f32)
            for shape in (qkv.shape[::-1], proj_shape, up_shape, down_shape)
        ),
        compiler_params=pltpu.CompilerParams(vmem_limit_bytes=48 << 20),
        name="unpack",
    )(shard, qkv)


class Gather:
    def __init__(self, wide, narrow, owns, out, mine, *semaphores):
        self.owns, self.out, self.mine = owns, out, mine
        self.w, self.n = lax.axis_index("wide"), lax.axis_index("narrow")
        self.side, self.lines = math.isqrt(wide), narrow // 2
        self.a, self.b = self.w // self.side, lax.rem(self.w, self.side)
        self.z, self.core = self.n // 2, lax.rem(self.n, 2)
        self.sibling = self.n + 1 - 2 * self.core
        (
            self.loaded, self.copied, self.own_sent, self.passed, self.line_got, self.first_sent, self.first_got,
            self.second_sent, self.second_got, self.f0_sent, self.f0_got, self.f1_sent, self.f1_got,
            self.f2_sent, self.f2_got, self.f3_sent, self.f3_got,
        ) = semaphores
        self.pairs = [(h, i) for i in range(1, self.side) for h in (0, 1)]

    @staticmethod
    def scratch(wide, narrow, piece):
        side, lines = math.isqrt(wide), narrow // 2
        dma = pltpu.SemaphoreType.DMA
        line, plane = (lines,), (lines, 2, side)
        shapes = [(2,), (), line, line, line, plane, plane, plane, plane, (), (), line, line]
        mine = pltpu.VMEM((side, side, 2, *piece), bf16)
        return [mine, *[dma(shape) for shape in shapes + [plane] * 4]]

    def other_a(self, i):
        return lax.rem(self.a + i, self.side)

    def other_b(self, i):
        return lax.rem(self.b + i, self.side)

    def own_on(self, way):
        return remote(
            self.mine.at[self.a, self.b], self.out.at[self.n, self.a, self.b],
            self.own_sent.at[self.z + way], self.line_got.at[self.z], self.w, self.n + 2 * way,
        )

    def pass_on(self, zs, way):
        piece = self.out.at[2 * zs + self.core, self.a, self.b]
        return remote(
            piece, piece, self.passed.at[zs], self.line_got.at[zs], self.w, self.n + 2 * way
        )

    def first(self, zs, h, i):
        shard = 2 * zs + self.core
        piece = self.out.at[shard, self.a, self.b, h]
        if h == 0:
            to, mine = self.a * self.side + self.other_b(i), self.b
        else:
            to, mine = self.other_a(i) * self.side + self.b, self.a
        return remote(
            piece, piece, self.first_sent.at[zs, h, i], self.first_got.at[zs, h, mine], to, self.n
        )

    def second(self, zs, h, i):
        shard = 2 * zs + self.core
        if h == 0:
            piece = self.out.at[shard, self.a, :, 0]
            to, mine = self.other_a(i) * self.side + self.b, self.a
        else:
            piece = self.out.at[shard, :, self.b, 1]
            to, mine = self.a * self.side + self.other_b(i), self.b
        return remote(
            piece, piece, self.second_sent.at[zs, h, i], self.second_got.at[zs, h, mine], to, self.n
        )

    def first_from(self, shard, h, i):
        if h == 0:
            return self.out.at[shard, self.a, self.other_b(i), 0], self.other_b(i)
        return self.out.at[shard, self.other_a(i), self.b, 1], self.other_a(i)

    def second_from(self, shard, h, i):
        if h == 0:
            return self.out.at[shard, self.other_a(i), :, 0], self.other_a(i)
        return self.out.at[shard, :, self.other_b(i), 1], self.other_b(i)

    def hand0(self):
        return remote(
            self.mine, self.out.at[self.n], self.f0_sent, self.f0_got, self.w, self.sibling
        )

    def hand1(self, zs):
        piece = self.out.at[2 * zs + self.core, self.a, self.b]
        return remote(piece, piece, self.f1_sent.at[zs], self.f1_got.at[zs], self.w, self.sibling)

    def hand2(self, zs, h, i):
        piece, k = self.first_from(2 * zs + self.core, h, i)
        return remote(
            piece, piece, self.f2_sent.at[zs, h, k], self.f2_got.at[zs, h, k], self.w, self.sibling
        )

    def hand3(self, zs, h, i):
        piece, k = self.second_from(2 * zs + self.core, h, i)
        return remote(
            piece, piece, self.f3_sent.at[zs, h, k], self.f3_got.at[zs, h, k], self.w, self.sibling
        )

    def load(self):
        copies, row = [], 0
        for k, own in enumerate(self.owns):
            part = self.mine.at[:, :, :, pl.ds(row, own.shape[3])]
            copies.append(pltpu.make_async_copy(own, part, self.loaded.at[k]))
            row += own.shape[3]
        return copies

    def keep(self):
        return pltpu.make_async_copy(self.mine, self.out.at[self.n], self.copied)

    def sides(self, d, act):
        if not 1 <= d <= self.lines - 1:
            return
        z, last = self.z, self.lines - 1

        @pl.when(z >= d)
        def _():
            act(z - d, 1, z < last)

        @pl.when(z + d <= last)
        def _():
            act(z + d, -1, z > 0)

    def begin(self):
        for copy in self.load():
            copy.start()
        for copy in self.load():
            copy.wait()

        @pl.when(self.z < self.lines - 1)
        def _():
            self.own_on(1).start()

        @pl.when(self.z > 0)
        def _():
            self.own_on(-1).start()

        self.keep().start()
        self.hand0().start()

    def one(self, zs, way, more):
        arrived(self.out.at[2 * zs + self.core, self.a, self.b], self.line_got.at[zs])

        @pl.when(more)
        def _():
            self.pass_on(zs, way).start()

        for h, i in self.pairs:
            self.first(zs, h, i).start()
        self.hand1(zs).start()

    def two(self, zs, way, more):
        for h in (0, 1):
            for i in range(1, self.side):
                piece, k = self.first_from(2 * zs + self.core, h, i)
                arrived(piece, self.first_got.at[zs, h, k])
            for i in range(1, self.side):
                self.second(zs, h, i).start()
        for h, i in self.pairs:
            self.hand2(zs, h, i).start()

    def three(self, zs, way, more):
        for h, i in self.pairs:
            piece, k = self.second_from(2 * zs + self.core, h, i)
            arrived(piece, self.second_got.at[zs, h, k])
            self.hand3(zs, h, i).start()

    def round(self, d):
        self.sides(d, self.one)
        self.sides(d - 1, self.two)
        self.sides(d - 2, self.three)

    def finish_side(self, zs, way, more):
        theirs = 2 * zs + 1 - self.core

        @pl.when(more)
        def _():
            self.pass_on(zs, way).wait_send()

        self.hand1(zs).wait_send()
        arrived(self.out.at[theirs, self.a, self.b], self.f1_got.at[zs])
        for h, i in self.pairs:
            self.first(zs, h, i).wait_send()
            self.second(zs, h, i).wait_send()
            self.hand2(zs, h, i).wait_send()
            self.hand3(zs, h, i).wait_send()
            piece, k = self.first_from(theirs, h, i)
            arrived(piece, self.f2_got.at[zs, h, k])
            piece, k = self.second_from(theirs, h, i)
            arrived(piece, self.f3_got.at[zs, h, k])

    def finish(self):
        @pl.when(self.z < self.lines - 1)
        def _():
            self.own_on(1).wait_send()

        @pl.when(self.z > 0)
        def _():
            self.own_on(-1).wait_send()

        self.keep().wait()
        self.hand0().wait_send()
        arrived(self.out.at[self.sibling], self.f0_got)
        for d in range(1, self.lines):
            self.sides(d, self.finish_side)


def start_kernel(
    wide, narrow, token_ref, gain_ref, bias_ref, weight_ref, own_ref,
    normed, packed, turned, gathered, line_sent, line_got, sib_sent, sib_got, *gather_refs,
):
    gather = Gather(wide, narrow, [own_ref], gathered, *gather_refs)
    w, n, z, core = gather.w, gather.n, gather.z, gather.core
    lines, sibling = gather.lines, gather.sibling
    rows = token_ref.shape[0]

    def norm_rows(j, carry):
        part = pl.ds(pl.multiple_of(j * 64, 64), 64)
        values = token_ref[part, :].astype(f32)
        centred = values - jnp.mean(values, axis=-1, keepdims=True)
        variance = jnp.mean(centred * centred, axis=-1, keepdims=True)
        normed[n, part, :] = (
            centred * lax.rsqrt(variance + epsilon) * as_row(gain_ref) + as_row(bias_ref)
        ).astype(bf16)
        return carry

    lax.fori_loop(0, rows // 64, norm_rows, 0)
    greet(wide, narrow, w, n)

    step = rows // CHUNKS

    def part_of(shard, c):
        return normed.at[shard, pl.ds(c * step, step)]

    def pass_on(zs, c, way):
        block = part_of(2 * zs + core, c)
        k = (1 - way) // 2
        return remote(block, block, line_sent.at[zs, c, k], line_got.at[zs, c], w, n + 2 * way)

    def hand(zs, c):
        block = part_of(2 * zs + core, c)
        return remote(block, block, sib_sent.at[zs, c], sib_got.at[zs, c], w, sibling)

    def project(owner, c):
        columns = pl.ds(pl.multiple_of(owner * rows + c * step, step), step)
        packed[:, columns] = contract(
            turned[...], normed[owner, pl.ds(c * step, step)], 1, 1
        ).astype(bf16)

    gather.begin()
    for c in range(CHUNKS):

        @pl.when(z < lines - 1)
        def _():
            pass_on(z, c, 1).start()

        @pl.when(z > 0)
        def _():
            pass_on(z, c, -1).start()

        hand(z, c).start()
    turned[...] = weight_ref[...].T
    for c in range(CHUNKS):
        project(n, c)

    def receive(c, zs, way, more):
        arrived(part_of(2 * zs + core, c), line_got.at[zs, c])

        @pl.when(more)
        def _():
            pass_on(zs, c, way).start()

        hand(zs, c).start()

    def project_side(zs, way, more):
        for c in range(CHUNKS):
            project(2 * zs + core, c)

    def project_sibling(zs, way, more):
        for c in range(CHUNKS):
            arrived(part_of(2 * zs + 1 - core, c), sib_got.at[zs, c])
            project(2 * zs + 1 - core, c)

    project_sibling(z, 0, None)
    for d in range(1, lines):
        gather.round(d)
        if d == lines - 1:
            gather.round(lines)
            gather.round(lines + 1)
        for c in range(CHUNKS):
            gather.sides(d, functools.partial(receive, c))
        if d > 1:
            gather.sides(d - 1, project_sibling)
        gather.sides(d, project_side)
    gather.sides(lines - 1, project_sibling)
    gather.finish()

    def sent_side(zs, way, more):
        for c in range(CHUNKS):
            hand(zs, c).wait_send()

            @pl.when(more)
            def _():
                pass_on(zs, c, way).wait_send()

    for c in range(CHUNKS):

        @pl.when(z < lines - 1)
        def _():
            pass_on(z, c, 1).wait_send()

        @pl.when(z > 0)
        def _():
            pass_on(z, c, -1).wait_send()

        hand(z, c).wait_send()
    for d in range(1, lines):
        gather.sides(d, sent_side)


def start(wide, narrow, tokens, gain, bias, weight, own):
    rows, features = tokens.shape
    lines = narrow // 2
    dma = pltpu.SemaphoreType.DMA
    vmem = pl.BlockSpec(memory_space=pltpu.VMEM)
    anywhere = pl.BlockSpec(memory_space=pl.ANY)
    return pl.pallas_call(
        functools.partial(start_kernel, wide, narrow),
        in_specs=[vmem, vmem, vmem, vmem, anywhere],
        out_specs=(vmem, vmem, vmem, anywhere),
        out_shape=(
            jax.ShapeDtypeStruct((narrow, rows, features), bf16),
            jax.ShapeDtypeStruct((weight.shape[1], narrow * rows), bf16),
            jax.ShapeDtypeStruct((weight.shape[1], features), bf16),
            jax.ShapeDtypeStruct((narrow, *own.shape), bf16),
        ),
        scratch_shapes=[
            dma((lines, CHUNKS, 2)), dma((lines, CHUNKS)), dma((lines, CHUNKS)), dma((lines, CHUNKS)),
            *Gather.scratch(wide, narrow, own.shape[3:]),
        ],
        compiler_params=pltpu.CompilerParams(
            vmem_limit_bytes=58 << 20, collective_id=1, has_side_effects=True
        ),
        name="start",
    )(tokens, gain, bias, weight, own)


def body(
    tokens, cotangent, item_lengths, attn_gain, attn_bias, qkv_weight, proj_weight,
    mlp_gain, mlp_bias, up_weight, down_weight,
):
    items = item_lengths.shape[1]
    heads = qkv_weight.shape[1] // (3 * HEAD_DIM)
    wide, narrow = lax.axis_size("wide"), lax.axis_size("narrow")
    side = math.isqrt(wide)
    rows = narrow * tokens.shape[0]

    def cut(shard):
        return shard.reshape(side, side, 2, shard.shape[0] // (2 * wide), shard.shape[1])

    def split_parts(total):
        return total.reshape(narrow, side, side, 2, -1, total.shape[1])

    first = down_weight.shape[0] // (2 * wide)
    extras = mask_rows(item_lengths, rows)
    normed_all, packed, qkv_turned, up_all = start(
        wide, narrow, tokens, attn_gain, attn_bias, qkv_weight, cut(up_weight)
    )
    normed_all = normed_all.reshape(rows, -1)
    packed = packed.reshape(heads, 3, HEAD_DIM, rows)
    attended, log_total, attended_rows, rest_all = attend_forward(
        wide, narrow, packed, extras, cut(down_weight), cut(proj_weight)
    )
    attended_rows = attended_rows.reshape(-1, tokens.shape[0])
    proj_all = rest_all[:, :, :, :, first:].reshape(-1, tokens.shape[1])
    output, grad_middle, grad_attended, grad_proj, grad_parts, norm_parts = mlp(
        attended_rows, proj_all, tokens, cotangent, mlp_gain, mlp_bias, up_all, rest_all, first
    )
    grad_attended = grad_attended.reshape(narrow, heads, HEAD_DIM, -1)
    grad_proj_parts = split_parts(grad_proj)
    grad_packed, grad_piece = attend_backward(
        wide, narrow, packed, extras, attended, grad_attended, log_total,
        grad_parts, grad_proj_parts, items,
    )
    grad_packed = grad_packed.reshape(heads * 3 * HEAD_DIM, rows)
    grad_tokens, grad_qkv, grad_shard, shares = finish(
        wide, narrow, grad_packed, qkv_turned, normed_all, tokens, grad_middle,
        attn_gain, norm_parts, grad_piece,
    )
    grad_qkv, grad_proj, grad_up, grad_down = unpack(
        grad_shard, grad_qkv, proj_weight.shape, up_weight.shape, down_weight.shape
    )
    return (
        output, grad_tokens, shares[0], shares[1], grad_qkv, grad_proj,
        shares[2], shares[3], grad_up, grad_down,
    )


def solution(mesh):
    by_rows = P(("wide", "narrow"), None)
    return jax.shard_map(
        body,
        mesh=mesh,
        in_specs=(
            by_rows, by_rows, P("wide", None), P(), P(), P(None, "narrow"), P("narrow", None),
            P(), P(), P(None, "narrow"), P("narrow", None),
        ),
        out_specs=(
            by_rows, by_rows, P("narrow"), P("narrow"), P(None, "narrow"), P("narrow", None),
            P("narrow"), P("narrow"), P(None, "narrow"), P("narrow", None),
        ),
        check_vma=False,
    )
```

```python
import functools
import math

import jax
import jax.numpy as jnp
from jax import lax
from jax.experimental import pallas as pl
from jax.experimental.pallas import tpu as pltpu
from jax.sharding import PartitionSpec as P

HEAD_DIM = 64
EXTRA = 16
CHUNKS = 2
REDUCE_START, REDUCE_STEP, REDUCE_FIRST, REDUCE_SECOND, SPREAD_AT = 2, 11, 8, 12, 8
EARLY_RELAY = 17
EXCLUDED = -1e30
bf16 = jnp.bfloat16
f32 = jnp.float32
MESH = pl.DeviceIdType.MESH
epsilon = 1e-05


def mask_rows(item_lengths, rows):
    lengths = item_lengths[0]
    items = lengths.shape[0]
    ends = [sum(lengths[j] for j in range(i + 1)) for i in range(items)]
    position = jnp.arange(rows)
    segment = sum((position >= ends[i]).astype(jnp.int32) for i in range(items))
    extra = jnp.arange(EXTRA)[:, None]
    own = segment[None, :] == extra
    mask = extra <= items
    query_extra = jnp.where(own & mask, 1.0, 0.0)
    key_extra = jnp.where(
        mask, jnp.where(own, 0.0, EXCLUDED), jnp.where(extra <= items + 3, 1.0, 0.0)
    )
    return jnp.where(jnp.arange(2)[:, None, None] == 0, query_extra, key_extra).astype(bf16)


def forward_kernel(
    wide, narrow, qx_ref, kx_ref, q_ref, k_ref, v_ref, own_ref, more_ref, o_ref, log_ref, rows_ref, gathered,
    keys, ready, copied, sent, got, *gather_refs,
):
    gather = Gather(wide, narrow, [own_ref, more_ref], gathered, *gather_refs)
    w, n, lines = gather.w, gather.n, gather.lines
    head, step = pl.program_id(0), pl.program_id(1)
    moment = head * narrow + step
    width = q_ref.shape[-1] // narrow
    last = heads_of(ready, narrow) * narrow - 1

    moves = [(0.0, lambda: greet(wide, narrow, w, n)), (0.1, gather.begin)]
    for d in range(1, lines):
        moves += [
            (3.0 * d, functools.partial(gather.sides, d, gather.one)),
            (3.0 * d + 2.1, functools.partial(gather.sides, d, gather.two)),
            (3.0 * d + 5.2, functools.partial(gather.sides, d, gather.three)),
        ]
    moves.append((900.0, gather.finish))
    moves.sort(key=lambda move: move[0])

    def perform(lower, upper):
        for time, move in moves:
            if lower <= time < upper:
                move()

    for tick in range(last + 1):

        @pl.when(moment == tick)
        def _():
            perform(tick, tick + 1)

    @pl.when(step == 0)
    def _():
        keys[...] = jnp.concatenate([k_ref[0], kx_ref[...]], axis=0).T

    owner = lax.rem(n + 1 + step, narrow)
    columns = pl.ds(pl.multiple_of(owner * width, width), width)
    query = jnp.concatenate(
        [q_ref[0, :, columns], qx_ref[:, columns]], axis=0
    )
    scores = jnp.dot(keys[...], query, preferred_element_type=f32)
    maximum = jnp.max(scores, axis=0, keepdims=True)
    raised = jnp.exp(scores - maximum)
    total = jnp.sum(raised, axis=0, keepdims=True)
    gathered_values = jnp.dot(v_ref[0], raised.astype(bf16), preferred_element_type=f32)
    result = (gathered_values / total).astype(bf16)
    o_ref[0, :, columns] = result
    log_ref[0, :, columns] = maximum + jnp.log(total)
    ready[moment] = result

    def deliver(k, owner, h):
        return remote(ready.at[k], rows_ref.at[n, h], sent.at[k], got.at[n, h], w, owner)

    def deliver_here(k, h):
        return pltpu.make_async_copy(ready.at[k], rows_ref.at[n, h], copied.at[h])

    @pl.when(step < narrow - 1)
    def _():
        deliver(moment, owner, head).start()

    @pl.when(step == narrow - 1)
    def _():
        deliver_here(moment, head).start()

    @pl.when(moment == last)
    def _():
        perform(last + 1, 1000)
        for h in range((last + 1) // narrow):
            deliver_here(h * narrow + narrow - 1, h).wait()
            for t in range(narrow - 1):
                deliver(h * narrow + t, lax.rem(n + 1 + t, narrow), h).wait_send()
                source = lax.rem(n + narrow - 1 - t, narrow)
                arrived(rows_ref.at[source, h], got.at[source, h])


def heads_of(ready, narrow):
    return ready.shape[0] // narrow


def attend_forward(wide, narrow, packed, extras, own, more):
    heads, _, _, rows = packed.shape
    width = rows // narrow
    gathered = (narrow, *own.shape[:3], own.shape[3] + more.shape[3], own.shape[4])
    dma = pltpu.SemaphoreType.DMA

    def whole(j):
        return pl.BlockSpec((1, None, HEAD_DIM, rows), lambda h, i: (h, j, 0, 0))

    def extra(j):
        return pl.BlockSpec((None, EXTRA, rows), lambda h, i: (j, 0, 0))

    anywhere = pl.BlockSpec(memory_space=pl.ANY)
    return pl.pallas_call(
        functools.partial(forward_kernel, wide, narrow),
        grid=(heads, narrow),
        in_specs=[extra(0), extra(1), whole(0), whole(1), whole(2), anywhere, anywhere],
        out_specs=(
            pl.BlockSpec((1, HEAD_DIM, rows), lambda h, i: (h, 0, 0)),
            pl.BlockSpec((1, 1, rows), lambda h, i: (h, 0, 0)),
            anywhere,
            anywhere,
        ),
        out_shape=(
            jax.ShapeDtypeStruct((heads, HEAD_DIM, rows), bf16),
            jax.ShapeDtypeStruct((heads, 1, rows), f32),
            jax.ShapeDtypeStruct((narrow, heads, HEAD_DIM, width), bf16),
            jax.ShapeDtypeStruct(gathered, bf16),
        ),
        scratch_shapes=[
            pltpu.VMEM((rows, HEAD_DIM + EXTRA), bf16),
            pltpu.VMEM((heads * narrow, HEAD_DIM, width), bf16),
            dma((heads,)),
            dma((heads * narrow,)),
            dma((narrow, heads)),
            *Gather.scratch(wide, narrow, gathered[4:]),
        ],
        compiler_params=pltpu.CompilerParams(
            vmem_limit_bytes=58 << 20, collective_id=4, has_side_effects=True
        ),
        name="attend_forward",
    )(extras, extras, packed, packed, packed, own, more)


def remote(src, dst, sent, received, wide_to, narrow_to):
    return pltpu.make_async_remote_copy(
        src_ref=src,
        dst_ref=dst,
        send_sem=sent,
        recv_sem=received,
        device_id=(wide_to, narrow_to),
        device_id_type=MESH,
    )


def arrived(ref, semaphore):
    pltpu.make_async_copy(ref, ref, semaphore).wait()


def greet(wide, narrow, w, n):
    barrier = pltpu.get_barrier_semaphore()

    def column(t, carry):
        pl.semaphore_signal(
            barrier, inc=1, device_id=(w, lax.rem(n + t, narrow)), device_id_type=MESH
        )
        return carry

    def plane(t, carry):
        pl.semaphore_signal(
            barrier, inc=1, device_id=(lax.rem(w + t, wide), n), device_id_type=MESH
        )
        return carry

    lax.fori_loop(1, narrow, column, 0)
    lax.fori_loop(1, wide, plane, 0)
    pl.semaphore_wait(barrier, narrow + wide - 2)


def accumulate(into, *others):
    rows = into.shape[0]
    few = max([d for d in (16, 32, 48, 64) if rows % d == 0], default=rows)

    def piece(j, carry):
        part = pl.ds(j * few if rows == few else pl.multiple_of(j * few, few), few)
        total = into[part, :].astype(f32)
        for other in others:
            total = total + other[part, :].astype(f32)
        into[part, :] = total.astype(bf16)
        return carry

    if rows == few:
        piece(0, 0)
    else:
        lax.fori_loop(0, rows // few, piece, 0)


def reduce_steps(
    wide, narrow, parts, proj_parts, landed, final, held, staged, from_first, from_second, from_line,
    mine, loaded, sib_sent, sib_got, first_sent, first_got, second_sent, second_got, line_sent, line_got,
):
    w, n = lax.axis_index("wide"), lax.axis_index("narrow")
    side, lines = math.isqrt(wide), narrow // 2
    a, b, z, core = w // side, lax.rem(w, side), n // 2, lax.rem(n, 2)
    sibling = n + 1 - 2 * core
    slots = held.shape[0]
    most, least = parts.shape[4], proj_parts.shape[4]
    sources = [(parts, pl.ds(0, most)), (proj_parts, pl.ds(most, least))]
    order = [lax.rem(z + 1 + j, lines) for j in range(lines)]
    halves = [(h, i) for i in range(1, side) for h in (0, 1)]

    def other_a(i):
        return lax.rem(a + i, side)

    def other_b(i):
        return lax.rem(b + i, side)

    def to_sibling(j):
        shard = 2 * order[j] + 1 - core
        return [
            remote(
                src.at[shard], landed.at[j, :, :, :, rows],
                sib_sent.at[k, j], sib_got.at[k, j], w, sibling,
            )
            for k, (src, rows) in enumerate(sources)
        ]

    def load(j):
        shard, slot = 2 * order[j] + core, j % slots
        return [
            pltpu.make_async_copy(src.at[shard], held.at[slot, :, :, :, rows], loaded.at[k])
            for k, (src, rows) in enumerate(sources)
        ]

    def stage(j):
        return pltpu.make_async_copy(landed.at[j], staged, loaded.at[2])

    def first(j, h, i):
        slot, k = j % slots, i - 1
        if h == 0:
            src, to = held.at[slot, other_a(i), :, 0], other_a(i) * side + b
        else:
            src, to = held.at[slot, :, other_b(i), 1], a * side + other_b(i)
        return remote(
            src, from_first.at[j, h, k], first_sent.at[j, h, k], first_got.at[j, h, k], to, n
        )

    def second(j, h, i):
        slot, k = j % slots, i - 1
        if h == 0:
            src, to = held.at[slot, a, other_b(i), 0], a * side + other_b(i)
        else:
            src, to = held.at[slot, other_a(i), b, 1], other_a(i) * side + b
        return remote(
            src, from_second.at[j, h, k], second_sent.at[j, h, k], second_got.at[j, h, k], to, n
        )

    def along(j):
        zs = order[j]
        place = jnp.where(z < zs, z, z - 1)
        return remote(
            held.at[j % slots, a, b], from_line.at[place], line_sent.at[j], line_got.at[place],
            w, 2 * zs + core,
        )

    def begin():
        for j in range(lines):
            for copy in to_sibling(j):
                copy.start()

    def sent(j):
        for h, i in halves:
            first(j, h, i).wait_send()
            second(j, h, i).wait_send()

        if j < lines - 1:
            along(j).wait_send()

    def combine(j):
        slot = j % slots
        if j >= slots:
            sent(j - slots)
        for copy in load(j):
            copy.start()
        for k, (_, rows) in enumerate(sources):
            arrived(landed.at[j, :, :, :, rows], sib_got.at[k, j])
        stage(j).start()
        for copy in load(j):
            copy.wait()
        stage(j).wait()

        def piece(t, carry):
            p, q = t // side, lax.rem(t, side)
            for h in (0, 1):
                accumulate(held.at[slot, p, q, h], staged.at[p, q, h])
            return carry

        lax.fori_loop(0, wide, piece, 0)
        for h, i in halves:
            first(j, h, i).start()

    def narrow_down(j):
        slot = j % slots
        for h in (0, 1):
            for i in range(1, side):
                arrived(from_first.at[j, h, i - 1], first_got.at[j, h, i - 1])

            def piece(t, carry, h=h):
                into = held.at[slot, a, t, 0] if h == 0 else held.at[slot, t, b, 1]
                accumulate(into, *[from_first.at[j, h, i, t] for i in range(side - 1)])
                return carry

            lax.fori_loop(0, side, piece, 0)
        for h, i in halves:
            second(j, h, i).start()

    def send_home(j):
        slot = j % slots
        for h, i in halves:
            arrived(from_second.at[j, h, i - 1], second_got.at[j, h, i - 1])
        for h in (0, 1):
            accumulate(
                held.at[slot, a, b, h], *[from_second.at[j, h, i] for i in range(side - 1)]
            )

        if j < lines - 1:
            along(j).start()
        else:
            mine[...] = held[slot, a, b]

    def finish():
        for place in range(lines - 1):
            arrived(from_line.at[place], line_got.at[place])
        for h in (0, 1):
            total = mine[h].astype(f32)
            for place in range(lines - 1):
                total = total + from_line[place, h].astype(f32)
            final[h] = total.astype(bf16)

    def close():
        for j in range(lines):
            for copy in to_sibling(j):
                copy.wait_send()
        for j in range(max(0, lines - slots), lines):
            sent(j)

    steps = [(0.0, begin)]
    for j in range(lines):
        at = REDUCE_START + REDUCE_STEP * j
        steps += [
            (at, functools.partial(combine, j)),
            (at + REDUCE_FIRST, functools.partial(narrow_down, j)),
            (at + REDUCE_SECOND, functools.partial(send_home, j)),
        ]
    return sorted(steps, key=lambda step: step[0]), finish, close


def reduce_scratch(wide, narrow, rows, features, slots=3):
    side, lines = math.isqrt(wide), narrow // 2
    dma = pltpu.SemaphoreType.DMA
    plane = (lines, 2, side - 1)
    return [
        pltpu.VMEM((slots, side, side, 2, rows, features), bf16),
        pltpu.VMEM((side, side, 2, rows, features), bf16),
        pltpu.VMEM((lines, 2, side - 1, side, rows, features), bf16),
        pltpu.VMEM((lines, 2, side - 1, rows, features), bf16),
        pltpu.VMEM((lines - 1, 2, rows, features), bf16),
        pltpu.VMEM((2, rows, features), bf16),
        *[dma(shape) for shape in [(3,), (2, lines), (2, lines), plane, plane, plane, plane]],
        dma((lines,)),
        dma((lines - 1,)),
    ]


def as_row(ref):
    return ref[...].astype(f32).reshape(1, -1)


def contract(left, right, left_axis, right_axis):
    return lax.dot_general(
        left, right, (((left_axis,), (right_axis,)), ((), ())), preferred_element_type=f32
    )


def gelu_pair(values):
    half = 0.5 + 0.5 * lax.erf(values * 0.7071067811865476)
    slope = half + values * (jnp.exp(values * values * -0.5) * 0.3989422804014327)
    return values * half, slope


def mlp_kernel(
    att_ref, proj_ref, token_ref, cot_ref, gain_ref, bias_ref, up_ref, down_ref,
    out_ref, middle_out, att_out, proj_out, parts_ref, norm_ref,
    middle, expand, out_total, expand_total,
):
    step = pl.program_id(0)
    rows, features = token_ref.shape
    few = 64

    def by_rows(change):
        def body(j, carry):
            return change(pl.ds(pl.multiple_of(j * few, few), few), carry)

        return body

    @pl.when(step == 0)
    def _():
        middle[...] = token_ref[...].astype(f32) + contract(att_ref[...], proj_ref[...], 0, 0)
        out_total[...] = jnp.zeros_like(out_total)
        expand_total[...] = jnp.zeros_like(expand_total)

        def norm(part, carry):
            values = middle[part, :]
            centred = values - jnp.mean(values, axis=-1, keepdims=True)
            variance = jnp.mean(centred * centred, axis=-1, keepdims=True)
            expand[part, :] = (
                centred * lax.rsqrt(variance + epsilon) * as_row(gain_ref) + as_row(bias_ref)
            ).astype(bf16)
            return carry

        lax.fori_loop(0, rows // few, by_rows(norm), 0)

    def flat(ref):
        if ref.shape[4] % 16:
            return ref[0].astype(f32).reshape(-1, ref.shape[5]).astype(bf16)
        return ref[0].reshape(-1, ref.shape[5])

    up, down = flat(up_ref), flat(down_ref)
    units = down_ref.shape[4]
    pieces = up_ref.shape[1:4]
    columns = up_ref.shape[5]
    hidden_parts, grad_parts = [], []
    for part in (pl.ds(0, rows // 2), pl.ds(rows // 2, rows // 2)):
        hidden, slope = gelu_pair(
            jnp.dot(expand[part, :], up, preferred_element_type=f32)
        )
        grad_pre = (contract(cot_ref[part, :], down, 1, 1) * slope).astype(bf16)
        hidden = hidden.astype(bf16)
        out_total[part, :] += jnp.dot(hidden, down, preferred_element_type=f32)
        expand_total[part, :] += contract(grad_pre, up, 1, 1)
        hidden_parts.append(hidden)
        grad_parts.append(grad_pre)
    grad_up = contract(expand[...], jnp.concatenate(grad_parts, axis=0), 0, 0)
    grad_down = contract(jnp.concatenate(hidden_parts, axis=0), cot_ref[...], 0, 0)
    groups = features // columns
    grad_up = grad_up.reshape(*pieces, groups, units, columns)
    for g in range(groups):
        parts_ref[0, :, :, :, 0:units, g * columns : (g + 1) * columns] = grad_up[
            :, :, :, g
        ].astype(bf16)
    parts_ref[0, :, :, :, units : 2 * units, :] = grad_down.reshape(
        *pieces, units, features
    ).astype(bf16)

    @pl.when(step == pl.num_programs(0) - 1)
    def _():
        def finish_rows(part, carry):
            gain_sum, bias_sum = carry
            values = middle[part, :]
            out_ref[part, :] = (values + out_total[part, :]).astype(bf16)
            centred = values - jnp.mean(values, axis=-1, keepdims=True)
            inverse = lax.rsqrt(jnp.mean(centred * centred, axis=-1, keepdims=True) + epsilon)
            scaled = centred * inverse
            grad = expand_total[part, :]
            term = grad * as_row(gain_ref)
            back = inverse * (
                term
                - jnp.mean(term, axis=-1, keepdims=True)
                - scaled * jnp.mean(term * scaled, axis=-1, keepdims=True)
            )
            total = cot_ref[part, :].astype(f32) + back
            middle_out[part, :] = total
            expand[part, :] = total.astype(bf16)
            gain_sum = gain_sum + jnp.sum(grad * scaled, axis=0, keepdims=True)
            bias_sum = bias_sum + jnp.sum(grad, axis=0, keepdims=True)
            return gain_sum, bias_sum

        start = (jnp.zeros((1, features), f32), jnp.zeros((1, features), f32))
        gain_sum, bias_sum = lax.fori_loop(0, rows // few, by_rows(finish_rows), start)
        row = lax.broadcasted_iota(jnp.int32, (8, features), 0)
        norm_ref[...] = jnp.where(row == 2, gain_sum, jnp.where(row == 3, bias_sum, 0.0))
        branch = expand[...]
        att_out[...] = contract(proj_ref[...], branch, 1, 1).astype(bf16)
        proj_out[...] = jnp.dot(att_ref[...], branch, preferred_element_type=f32).astype(bf16)


def mlp(attended, proj, tokens, cotangent, gain, bias, up_all, down_all, units):
    rows, features = tokens.shape
    narrow, side = up_all.shape[:2]

    def whole(*shape):
        return pl.BlockSpec(shape, lambda i: (0,) * len(shape))

    def weights(*piece):
        return pl.BlockSpec((1, side, side, 2, *piece), lambda i: (i, 0, 0, 0, 0, 0))

    return pl.pallas_call(
        mlp_kernel,
        grid=(narrow,),
        in_specs=[
            whole(*attended.shape),
            whole(*proj.shape),
            whole(rows, features),
            whole(rows, features),
            whole(*gain.shape),
            whole(*bias.shape),
            weights(*up_all.shape[4:]),
            weights(units, features),
        ],
        out_specs=(
            whole(rows, features),
            whole(rows, features),
            whole(*attended.shape),
            whole(*proj.shape),
            pl.BlockSpec(
                (1, side, side, 2, 2 * units, features), lambda i: (i, 0, 0, 0, 0, 0)
            ),
            whole(8, features),
        ),
        out_shape=(
            jax.ShapeDtypeStruct((rows, features), bf16),
            jax.ShapeDtypeStruct((rows, features), f32),
            jax.ShapeDtypeStruct(attended.shape, bf16),
            jax.ShapeDtypeStruct(proj.shape, bf16),
            jax.ShapeDtypeStruct((narrow, side, side, 2, 2 * units, features), bf16),
            jax.ShapeDtypeStruct((8, features), f32),
        ),
        scratch_shapes=[
            pltpu.VMEM((rows, features), f32),
            pltpu.VMEM((rows, features), bf16),
            pltpu.VMEM((rows, features), f32),
            pltpu.VMEM((rows, features), f32),
        ],
        compiler_params=pltpu.CompilerParams(vmem_limit_bytes=58 << 20),
        name="mlp",
    )(attended, proj, tokens, cotangent, gain, bias, up_all, down_all)


def backward_kernel(
    wide, narrow, items, chunks,
    extra_ref, packed_ref, att_ref, log_ref, own_ref, parts_ref, proj_parts_ref, weight_ref,
    normed_ref, token_ref, middle_ref, gain_ref, norm_ref,
    tokens_out, qkv_out, shard_out, norms_out, landed,
    keys, values, queries, grads, grad_q, grad_k, grad_v, block_grad,
    normed, total_qkv, for_sibling, from_sibling, held, from_line,
    first_qkv, second_qkv, norms, norm_column, norm_half, norm_plane, piece,
    middle,
    packed_got, own_got, do_sent, do_got, normed_got, middle_got, copied, sib_sent, sib_got,
    line_sent, line_got, piece_sent, piece_got, first_sent, first_got, second_sent, second_got,
    column_sent, column_got, plane_sent, plane_got, *reduce_refs,
):
    w, n = lax.axis_index("wide"), lax.axis_index("narrow")
    side, lines = math.isqrt(wide), narrow // 2
    a, b, z, core = w // side, lax.rem(w, side), n // 2, lax.rem(n, 2)
    sibling = n + 1 - 2 * core
    heads = keys.shape[0]
    rows, features = token_ref.shape
    step = rows // chunks
    lower = z < lines // 2
    moves, reduce_finish, reduce_close = reduce_steps(
        wide, narrow, parts_ref, proj_parts_ref, landed, piece, *reduce_refs
    )

    def line_at(k):
        climbing = jnp.where(
            k < lines - 1 - z, lines - 1 - k, jnp.where(k < lines - 1, k - (lines - 1 - z), z)
        )
        falling = jnp.where(k < z, k, jnp.where(k < lines - 1, lines - 1 - (k - z), z))
        return jnp.where(lower, climbing, falling)

    def block_at(j):
        odd = lax.rem(j, 2)
        return 2 * line_at(j // 2) + jnp.where(odd == 1, core, 1 - core)

    def columns(owner):
        return pl.ds(pl.multiple_of(owner * rows, rows), rows)

    def packed_copy(h, j):
        into = (queries, keys, values)[j]
        return pltpu.make_async_copy(
            packed_ref.at[h, j], into.at[h, pl.ds(0, HEAD_DIM)], packed_got.at[h, j]
        )

    def keep(h):
        return pltpu.make_async_copy(
            own_ref.at[n, h], grads.at[h, pl.ds(0, HEAD_DIM), columns(n)], own_got.at[h]
        )

    def deliver(t, h):
        to = lax.rem(n + t, narrow)
        return remote(
            own_ref.at[to, h], grads.at[h, pl.ds(0, HEAD_DIM), columns(n)],
            do_sent.at[t, h], do_got.at[n, h], w, to,
        )

    def fetch(j):
        owner = block_at(j)
        return pltpu.make_async_copy(
            normed_ref.at[pl.ds(pl.multiple_of(owner * rows, rows), rows)],
            normed.at[lax.rem(j, 2)], normed_got.at[lax.rem(j, 2)],
        )

    for h in range(heads):
        for j in range(3):
            packed_copy(h, j).start()
        keep(h).start()
    fetch(0).start()
    greet(wide, narrow, w, n)
    for t in range(1, narrow):
        for h in range(heads):
            deliver(t, h).start()
    grad_q[...] = jnp.zeros_like(grad_q)
    grad_k[...] = jnp.zeros_like(grad_k)
    grad_v[...] = jnp.zeros_like(grad_v)
    total_qkv[...] = jnp.zeros_like(total_qkv)
    for h in range(heads):
        keys[h, HEAD_DIM:, :] = extra_ref[1]
        values[h, HEAD_DIM:, :] = extra_ref[1]
    for h in range(heads):
        for j in range(3):
            packed_copy(h, j).wait()
        keep(h).wait()

    row = lax.broadcasted_iota(jnp.int32, (EXTRA, rows), 0) - items

    def pieces(term, base):
        high = term.astype(bf16).astype(f32)
        mid = (term - high).astype(bf16).astype(f32)
        small = term - high - mid
        return jnp.where(
            row == 1, high, jnp.where(row == 2, mid, jnp.where(row == 3, small, base))
        ).astype(bf16)

    def prepare(j):
        owner = block_at(j)
        where = columns(owner)

        @pl.when(owner != n)
        def _():
            for h in range(heads):
                arrived(grads.at[h, pl.ds(0, HEAD_DIM), where], do_got.at[owner, h])

        for h in range(heads):
            grad = grads[h, 0:HEAD_DIM, where].astype(f32)
            inner = jnp.sum(grad * att_ref[h, :, where].astype(f32), axis=0, keepdims=True)
            grads[h, HEAD_DIM:, where] = pieces(-inner, jnp.zeros((EXTRA, rows), f32))
            queries[h, HEAD_DIM:, where] = pieces(
                -log_ref[h, :, where], extra_ref[0, :, where].astype(f32)
            )

    def to_sibling(zs, slot):
        return remote(
            for_sibling.at[slot], from_sibling.at[zs], sib_sent.at[slot], sib_got.at[zs], w, sibling
        )

    def pass_on(zs, c, up):
        part = pl.ds(c * step, step)
        place = zs if up else jnp.where(z - 1 == zs, lines, zs)
        return remote(
            held.at[zs, part], from_line.at[place, part], line_sent.at[zs, c],
            line_got.at[place, c], w, n + 2 if up else n - 2,
        )

    def relay(zs, c, up):
        part = pl.ds(c * step, step)
        arrived(from_line.at[zs, part], line_got.at[zs, c])
        accumulate(held.at[zs, part], from_line.at[zs, part])
        pass_on(zs, c, up).start()

    def early_relay():
        @pl.when(jnp.logical_and(lower, z >= 1))
        def _():
            for c in range(chunks):
                relay(lines - 1, c, True)

        @pl.when(jnp.logical_and(z >= lines // 2, z <= lines - 2))
        def _():
            for c in range(chunks):
                relay(0, c, False)

    def emit(j):
        j = jnp.asarray(j, jnp.int32)
        owner = block_at(j)
        where = columns(owner)
        for h in range(heads):
            for k, total in enumerate((grad_q, grad_k, grad_v)):
                at = (h * 3 + k) * HEAD_DIM
                value = total[h, :, where]
                block_grad[at : at + HEAD_DIM, :] = (
                    value * HEAD_DIM**-0.5 if k == 0 else value
                ).astype(bf16)
        zs, slot = line_at(j // 2), lax.rem(j // 2, 2)
        product = contract(block_grad[...], weight_ref[...], 0, 0).astype(bf16)

        @pl.when(lax.rem(j, 2) == 0)
        def _():
            @pl.when(j >= 4)
            def _():
                to_sibling(zs, slot).wait_send()

            for_sibling[slot] = product
            to_sibling(zs, slot).start()

        @pl.when(lax.rem(j, 2) == 1)
        def _():
            held[zs] = product

        fetch(j).wait()

        @pl.when(j < narrow - 1)
        def _():
            fetch(j + 1).start()

        total_qkv[...] += jnp.dot(
            block_grad[...], normed[lax.rem(j, 2)], preferred_element_type=f32
        )

        @pl.when(lax.rem(j, 2) == 1)
        def _():
            arrived(from_sibling.at[zs], sib_got.at[zs])
            accumulate(held.at[zs], from_sibling.at[zs])

            @pl.when(jnp.logical_and(z == 0, zs != z))
            def _():
                for c in range(chunks):
                    pass_on(zs, c, True).start()

            @pl.when(jnp.logical_and(z == lines - 1, zs != z))
            def _():
                for c in range(chunks):
                    pass_on(zs, c, False).start()

    def spread(t):
        return remote(
            piece, shard_out.at[w], piece_sent.at[t], piece_got.at[t], lax.rem(w + t, wide), n
        )

    stay = pltpu.make_async_copy(piece, shard_out.at[w], copied)

    def spread_all():
        reduce_finish()
        stay.start()
        for t in range(1, wide):
            spread(t).start()

    prepare(narrow - 1)
    pairs = narrow * narrow
    moves = moves + [(6 * narrow - 8 + EARLY_RELAY, early_relay), (pairs - SPREAD_AT, spread_all)]
    moves.sort(key=lambda move: move[0])
    ticks = {}
    for time, move in moves:
        ticks.setdefault(min(int(time), pairs - 1), []).append(move)

    def pair(p, carry):
        for tick, group in ticks.items():

            @pl.when(p == tick)
            def _():
                for move in group:
                    move()

        late = p - 2 * narrow
        stage = sum(
            (late >= j * (2 * narrow - 2 - j)).astype(jnp.int32) for j in range(1, narrow - 2)
        )
        r = late - stage * (2 * narrow - 2 - stage)
        across = r < narrow - stage
        near = late < 0
        qi = jnp.where(
            near,
            jnp.where(p < narrow, narrow - 1, narrow - 2),
            jnp.where(across, stage, 2 * stage + 1 + r - narrow),
        )
        ki = jnp.where(near, lax.rem(p, narrow), jnp.where(across, stage + r, stage))

        @pl.when((p == narrow) | (late == 0) | ((stage == 0) & (r >= narrow)))
        def _():
            prepare(qi)

        at_q, at_k = columns(block_at(qi)), columns(block_at(ki))
        for h in range(heads):
            probs = jnp.exp(contract(queries[h, :, at_q], keys[h, :, at_k], 0, 0))
            scores = (probs * contract(grads[h, :, at_q], values[h, :, at_k], 0, 0)).astype(bf16)
            grad_v[h, :, at_k] += jnp.dot(
                grads[h, 0:HEAD_DIM, at_q], probs.astype(bf16), preferred_element_type=f32
            )
            grad_k[h, :, at_k] += jnp.dot(
                queries[h, 0:HEAD_DIM, at_q], scores, preferred_element_type=f32
            )
            grad_q[h, :, at_q] += contract(keys[h, 0:HEAD_DIM, at_k], scores, 1, 1)

        @pl.when(r == 2 * (narrow - stage) - 4)
        def _():
            emit(stage)

        return carry

    lax.fori_loop(0, pairs, pair, 0)
    emit(narrow - 2)
    emit(narrow - 1)

    half = total_qkv.shape[0] // 2
    own_qkv, half_qkv = for_sibling.at[:, 0:half], normed.at[:, 0:half]
    for slot in range(min(2, lines)):
        to_sibling(0, slot).wait_send()
    for h in (0, 1):
        own_qkv[h] = total_qkv[h * half : (h + 1) * half].astype(bf16)
    halves = [(h, i) for i in range(1, side) for h in (0, 1)]

    def plane_at(h, i):
        if h == 0:
            return lax.rem(a + i, side) * side + b
        return a * side + lax.rem(b + i, side)

    def first(h, i):
        return remote(
            own_qkv.at[h], first_qkv.at[h, i - 1], first_sent.at[h, i - 1], first_got.at[h, i - 1],
            plane_at(h, i), n,
        )

    def second(h, i):
        return remote(
            half_qkv.at[h], second_qkv.at[h, i - 1], second_sent.at[h, i - 1],
            second_got.at[h, i - 1], plane_at(1 - h, i), n,
        )

    def qkv_second():
        for h, i in halves:
            arrived(first_qkv.at[h, i - 1], first_got.at[h, i - 1])
        for h in (0, 1):
            total = own_qkv[h].astype(f32)
            for i in range(1, side):
                total = total + first_qkv[h, i - 1].astype(f32)
            half_qkv[h] = total.astype(bf16)
        for h, i in halves:
            second(h, i).start()

    def qkv_last():
        for h, i in halves:
            arrived(second_qkv.at[h, i - 1], second_got.at[h, i - 1])
        for h in (0, 1):
            total = half_qkv[h].astype(f32)
            for i in range(1, side):
                total = total + second_qkv[h, i - 1].astype(f32)
            qkv_out[h * half : (h + 1) * half] = total.astype(bf16)

    for h, i in halves:
        first(h, i).start()

    def fetch_middle(c):
        return pltpu.make_async_copy(middle_ref.at[pl.ds(c * step, step)], middle, middle_got)

    fetch_middle(0).start()
    for t in range(1, lines):
        below, above = lines - 1 - (t - z), t - (lines - 1 - z)
        for c in range(chunks):
            if t < lines - 1:

                @pl.when((z >= 1) & (t >= z) & ~(lower & (t == z)))
                def _():
                    relay(below, c, True)

                @pl.when((z <= lines - 2) & (above >= 0) & ~((z >= lines // 2) & (above == 0)))
                def _():
                    relay(above, c, False)

    qkv_second()

    def zero_edges(at_edge, place):
        @pl.when(at_edge)
        def _():
            from_line[place] = jnp.zeros((rows, features), bf16)

    zero_edges(z == 0, z)
    zero_edges(z == lines - 1, lines)
    gain_sum = bias_sum = jnp.zeros((1, features), f32)
    for c in range(chunks):
        part = pl.ds(c * step, step)

        @pl.when(z >= 1)
        def _():
            arrived(from_line.at[z, part], line_got.at[z, c])

        @pl.when(z <= lines - 2)
        def _():
            arrived(from_line.at[lines, part], line_got.at[lines, c])

        fetch_middle(c).wait()

        def norm_rows(j, carry):
            gain_sum, bias_sum = carry
            few = pl.ds(pl.multiple_of(c * step + j * 32, 32), 32)
            near = pl.ds(pl.multiple_of(j * 32, 32), 32)
            grad = (
                held[z, few].astype(f32)
                + from_line[z, few].astype(f32)
                + from_line[lines, few].astype(f32)
            )
            values = token_ref[few, :].astype(f32)
            centred = values - jnp.mean(values, axis=-1, keepdims=True)
            inverse = lax.rsqrt(jnp.mean(centred * centred, axis=-1, keepdims=True) + epsilon)
            scaled = centred * inverse
            term = grad * as_row(gain_ref)
            back = inverse * (
                term
                - jnp.mean(term, axis=-1, keepdims=True)
                - scaled * jnp.mean(term * scaled, axis=-1, keepdims=True)
            )
            tokens_out[few, :] = (middle[near, :] + back).astype(bf16)
            gain_sum = gain_sum + jnp.sum(grad * scaled, axis=0, keepdims=True)
            bias_sum = bias_sum + jnp.sum(grad, axis=0, keepdims=True)
            return gain_sum, bias_sum

        gain_sum, bias_sum = lax.fori_loop(0, step // 32, norm_rows, (gain_sum, bias_sum))
        if c + 1 < chunks:
            fetch_middle(c + 1).start()

    row = lax.broadcasted_iota(jnp.int32, (8, features), 0)
    parts = jnp.where(row == 0, gain_sum, jnp.where(row == 1, bias_sum, norm_ref[...]))
    share = features // narrow
    for owner in range(narrow):
        norms[owner] = parts[:, owner * share : (owner + 1) * share]

    def down_column(t):
        to = lax.rem(n + t, narrow)
        return remote(
            norms.at[to], norm_column.at[t - 1], column_sent.at[t - 1], column_got.at[t - 1], w, to
        )

    def over_plane(t):
        return remote(
            norm_half, norm_plane.at[t - 1], plane_sent.at[t - 1], plane_got.at[t - 1],
            lax.rem(w + t, wide), n,
        )

    for t in range(1, narrow):
        down_column(t).start()
    total = norms[n]
    for t in range(1, narrow):
        arrived(norm_column.at[t - 1], column_got.at[t - 1])
        total = total + norm_column[t - 1]
    norm_half[...] = total
    for t in range(1, wide):
        over_plane(t).start()
    for t in range(1, wide):
        arrived(norm_plane.at[t - 1], plane_got.at[t - 1])
        total = total + norm_plane[t - 1]
    norms_out[...] = total

    qkv_last()
    stay.wait()
    reduce_close()
    for t in range(1, wide):
        spread(t).wait_send()
        arrived(shard_out.at[lax.rem(w + wide - t, wide)], piece_got.at[t])
        over_plane(t).wait_send()
    for t in range(1, narrow):
        down_column(t).wait_send()
        for h in range(heads):
            deliver(t, h).wait_send()
    for h, i in halves:
        first(h, i).wait_send()
        second(h, i).wait_send()
    for zs in range(lines):
        for c in range(chunks):

            @pl.when(zs > z)
            def _():
                pass_on(zs, c, True).wait_send()

            @pl.when(zs < z)
            def _():
                pass_on(zs, c, False).wait_send()


def backward(
    wide, narrow, extras, packed, attended, log_total, grad, parts, proj_parts, weight, normed,
    tokens, middle, gain, norm_parts, items, chunks=4,
):
    side, lines = math.isqrt(wide), narrow // 2
    heads, _, _, total_rows = packed.shape
    rows, features = tokens.shape
    held_columns = weight.shape[0]
    piece = (parts.shape[4] + proj_parts.shape[4], features)
    depth = HEAD_DIM + EXTRA
    dma = pltpu.SemaphoreType.DMA
    vmem = pl.BlockSpec(memory_space=pltpu.VMEM)
    anywhere = pl.BlockSpec(memory_space=pl.ANY)
    plane = (2, side - 1)
    return pl.pallas_call(
        functools.partial(backward_kernel, wide, narrow, items, chunks),
        in_specs=[
            vmem, anywhere, vmem, vmem, anywhere, anywhere, anywhere, vmem,
            anywhere, vmem, anywhere, vmem, vmem,
        ],
        out_specs=(vmem, vmem, anywhere, vmem, anywhere),
        out_shape=(
            jax.ShapeDtypeStruct((rows, features), bf16),
            jax.ShapeDtypeStruct((held_columns, features), bf16),
            jax.ShapeDtypeStruct((wide, 2, *piece), bf16),
            jax.ShapeDtypeStruct((8, features // narrow), f32),
            jax.ShapeDtypeStruct((lines, side, side, 2, *piece), bf16),
        ),
        scratch_shapes=[
            *[pltpu.VMEM((heads, depth, total_rows), bf16)] * 4,
            *[pltpu.VMEM((heads, HEAD_DIM, total_rows), f32)] * 3,
            pltpu.VMEM((held_columns, rows), bf16),
            pltpu.VMEM((2, rows, features), bf16),
            pltpu.VMEM((held_columns, features), f32),
            pltpu.VMEM((2, rows, features), bf16),
            pltpu.VMEM((lines, rows, features), bf16),
            pltpu.VMEM((lines, rows, features), bf16),
            pltpu.VMEM((lines + 1, rows, features), bf16),
            pltpu.VMEM((2, side - 1, held_columns // 2, features), bf16),
            pltpu.VMEM((2, side - 1, held_columns // 2, features), bf16),
            pltpu.VMEM((narrow, 8, features // narrow), f32),
            pltpu.VMEM((narrow - 1, 8, features // narrow), f32),
            pltpu.VMEM((8, features // narrow), f32),
            pltpu.VMEM((wide - 1, 8, features // narrow), f32),
            pltpu.VMEM((2, *piece), bf16),
            pltpu.VMEM((rows // chunks, features), f32),
            dma((heads, 3)),
            dma((heads,)),
            dma((narrow, heads)),
            dma((narrow, heads)),
            dma((2,)),
            dma(()),
            dma(()),
            dma((2,)),
            dma((lines,)),
            dma((lines, chunks)),
            dma((lines + 1, chunks)),
            dma((wide,)),
            dma((wide,)),
            dma(plane),
            dma(plane),
            dma(plane),
            dma(plane),
            dma((narrow - 1,)),
            dma((narrow - 1,)),
            dma((wide - 1,)),
            dma((wide - 1,)),
            *reduce_scratch(wide, narrow, *piece),
        ],
        compiler_params=pltpu.CompilerParams(
            vmem_limit_bytes=61 << 20, collective_id=2, has_side_effects=True
        ),
        name="backward",
    )(
        extras, packed, attended, log_total, grad, parts, proj_parts, weight, normed,
        tokens, middle, gain, norm_parts,
    )


def unpack_kernel(shard_ref, qkv_ref, qkv_out, proj_out, up_out, down_out):
    wide = shard_ref.shape[0]
    features = shard_ref.shape[3]
    columns = up_out.shape[1]
    groups = features // columns
    units, few = down_out.shape[0] // (2 * wide), proj_out.shape[0] // (2 * wide)
    for j in range(2 * wide):
        w, h = divmod(j, 2)
        for g in range(groups):
            up_out[(j * groups + g) * units : (j * groups + g + 1) * units, :] = shard_ref[
                w, h, 0:units, g * columns : (g + 1) * columns
            ].astype(f32)
        down_out[j * units : (j + 1) * units, :] = shard_ref[w, h, units : 2 * units, :].astype(f32)
        proj_out[j * few : (j + 1) * few, :] = shard_ref[w, h, 2 * units :, :].astype(f32)
    qkv_out[...] = qkv_ref[...].astype(f32).T


def unpack(shard, qkv, proj_shape, up_shape, down_shape):
    return pl.pallas_call(
        unpack_kernel,
        out_shape=tuple(
            jax.ShapeDtypeStruct(shape, f32)
            for shape in (qkv.shape[::-1], proj_shape, up_shape, down_shape)
        ),
        compiler_params=pltpu.CompilerParams(vmem_limit_bytes=48 << 20),
        name="unpack",
    )(shard, qkv)


class Gather:
    def __init__(self, wide, narrow, owns, out, mine, *semaphores):
        self.owns, self.out, self.mine = owns, out, mine
        self.w, self.n = lax.axis_index("wide"), lax.axis_index("narrow")
        self.side, self.lines = math.isqrt(wide), narrow // 2
        self.a, self.b = self.w // self.side, lax.rem(self.w, self.side)
        self.z, self.core = self.n // 2, lax.rem(self.n, 2)
        self.sibling = self.n + 1 - 2 * self.core
        (
            self.loaded, self.copied, self.own_sent, self.passed, self.line_got, self.first_sent, self.first_got,
            self.second_sent, self.second_got, self.f0_sent, self.f0_got, self.f1_sent, self.f1_got,
            self.f2_sent, self.f2_got, self.f3_sent, self.f3_got,
        ) = semaphores
        self.pairs = [(h, i) for i in range(1, self.side) for h in (0, 1)]

    @staticmethod
    def scratch(wide, narrow, piece):
        side, lines = math.isqrt(wide), narrow // 2
        dma = pltpu.SemaphoreType.DMA
        line, plane = (lines,), (lines, 2, side)
        shapes = [(2,), (), line, line, line, plane, plane, plane, plane, (), (), line, line]
        mine = pltpu.VMEM((side, side, 2, *piece), bf16)
        return [mine, *[dma(shape) for shape in shapes + [plane] * 4]]

    def other_a(self, i):
        return lax.rem(self.a + i, self.side)

    def other_b(self, i):
        return lax.rem(self.b + i, self.side)

    def own_on(self, way):
        return remote(
            self.mine.at[self.a, self.b], self.out.at[self.n, self.a, self.b],
            self.own_sent.at[self.z + way], self.line_got.at[self.z], self.w, self.n + 2 * way,
        )

    def pass_on(self, zs, way):
        piece = self.out.at[2 * zs + self.core, self.a, self.b]
        return remote(
            piece, piece, self.passed.at[zs], self.line_got.at[zs], self.w, self.n + 2 * way
        )

    def first(self, zs, h, i):
        shard = 2 * zs + self.core
        piece = self.out.at[shard, self.a, self.b, h]
        if h == 0:
            to, mine = self.a * self.side + self.other_b(i), self.b
        else:
            to, mine = self.other_a(i) * self.side + self.b, self.a
        return remote(
            piece, piece, self.first_sent.at[zs, h, i], self.first_got.at[zs, h, mine], to, self.n
        )

    def second(self, zs, h, i):
        shard = 2 * zs + self.core
        if h == 0:
            piece = self.out.at[shard, self.a, :, 0]
            to, mine = self.other_a(i) * self.side + self.b, self.a
        else:
            piece = self.out.at[shard, :, self.b, 1]
            to, mine = self.a * self.side + self.other_b(i), self.b
        return remote(
            piece, piece, self.second_sent.at[zs, h, i], self.second_got.at[zs, h, mine], to, self.n
        )

    def first_from(self, shard, h, i):
        if h == 0:
            return self.out.at[shard, self.a, self.other_b(i), 0], self.other_b(i)
        return self.out.at[shard, self.other_a(i), self.b, 1], self.other_a(i)

    def second_from(self, shard, h, i):
        if h == 0:
            return self.out.at[shard, self.other_a(i), :, 0], self.other_a(i)
        return self.out.at[shard, :, self.other_b(i), 1], self.other_b(i)

    def hand0(self):
        return remote(
            self.mine, self.out.at[self.n], self.f0_sent, self.f0_got, self.w, self.sibling
        )

    def hand1(self, zs):
        piece = self.out.at[2 * zs + self.core, self.a, self.b]
        return remote(piece, piece, self.f1_sent.at[zs], self.f1_got.at[zs], self.w, self.sibling)

    def hand2(self, zs, h, i):
        piece, k = self.first_from(2 * zs + self.core, h, i)
        return remote(
            piece, piece, self.f2_sent.at[zs, h, k], self.f2_got.at[zs, h, k], self.w, self.sibling
        )

    def hand3(self, zs, h, i):
        piece, k = self.second_from(2 * zs + self.core, h, i)
        return remote(
            piece, piece, self.f3_sent.at[zs, h, k], self.f3_got.at[zs, h, k], self.w, self.sibling
        )

    def load(self):
        copies, row = [], 0
        for k, own in enumerate(self.owns):
            part = self.mine.at[:, :, :, pl.ds(row, own.shape[3])]
            copies.append(pltpu.make_async_copy(own, part, self.loaded.at[k]))
            row += own.shape[3]
        return copies

    def keep(self):
        return pltpu.make_async_copy(self.mine, self.out.at[self.n], self.copied)

    def sides(self, d, act):
        if not 1 <= d <= self.lines - 1:
            return
        z, last = self.z, self.lines - 1

        @pl.when(z >= d)
        def _():
            act(z - d, 1, z < last)

        @pl.when(z + d <= last)
        def _():
            act(z + d, -1, z > 0)

    def begin(self):
        for copy in self.load():
            copy.start()
        for copy in self.load():
            copy.wait()

        @pl.when(self.z < self.lines - 1)
        def _():
            self.own_on(1).start()

        @pl.when(self.z > 0)
        def _():
            self.own_on(-1).start()

        self.keep().start()
        self.hand0().start()

    def one(self, zs, way, more):
        arrived(self.out.at[2 * zs + self.core, self.a, self.b], self.line_got.at[zs])

        @pl.when(more)
        def _():
            self.pass_on(zs, way).start()

        for h, i in self.pairs:
            self.first(zs, h, i).start()
        self.hand1(zs).start()

    def two(self, zs, way, more):
        for h in (0, 1):
            for i in range(1, self.side):
                piece, k = self.first_from(2 * zs + self.core, h, i)
                arrived(piece, self.first_got.at[zs, h, k])
            for i in range(1, self.side):
                self.second(zs, h, i).start()
        for h, i in self.pairs:
            self.hand2(zs, h, i).start()

    def three(self, zs, way, more):
        for h, i in self.pairs:
            piece, k = self.second_from(2 * zs + self.core, h, i)
            arrived(piece, self.second_got.at[zs, h, k])
            self.hand3(zs, h, i).start()

    def round(self, d):
        self.sides(d, self.one)
        self.sides(d - 1, self.two)
        self.sides(d - 2, self.three)

    def finish_side(self, zs, way, more):
        theirs = 2 * zs + 1 - self.core

        @pl.when(more)
        def _():
            self.pass_on(zs, way).wait_send()

        self.hand1(zs).wait_send()
        arrived(self.out.at[theirs, self.a, self.b], self.f1_got.at[zs])
        for h, i in self.pairs:
            self.first(zs, h, i).wait_send()
            self.second(zs, h, i).wait_send()
            self.hand2(zs, h, i).wait_send()
            self.hand3(zs, h, i).wait_send()
            piece, k = self.first_from(theirs, h, i)
            arrived(piece, self.f2_got.at[zs, h, k])
            piece, k = self.second_from(theirs, h, i)
            arrived(piece, self.f3_got.at[zs, h, k])

    def finish(self):
        @pl.when(self.z < self.lines - 1)
        def _():
            self.own_on(1).wait_send()

        @pl.when(self.z > 0)
        def _():
            self.own_on(-1).wait_send()

        self.keep().wait()
        self.hand0().wait_send()
        arrived(self.out.at[self.sibling], self.f0_got)
        for d in range(1, self.lines):
            self.sides(d, self.finish_side)


def start_kernel(
    wide, narrow, token_ref, gain_ref, bias_ref, weight_ref, own_ref,
    normed, packed, turned, gathered, line_sent, line_got, sib_sent, sib_got, *gather_refs,
):
    gather = Gather(wide, narrow, [own_ref], gathered, *gather_refs)
    w, n, z, core = gather.w, gather.n, gather.z, gather.core
    lines, sibling = gather.lines, gather.sibling
    rows = token_ref.shape[0]

    def norm_rows(j, carry):
        part = pl.ds(pl.multiple_of(j * 64, 64), 64)
        values = token_ref[part, :].astype(f32)
        centred = values - jnp.mean(values, axis=-1, keepdims=True)
        variance = jnp.mean(centred * centred, axis=-1, keepdims=True)
        normed[n, part, :] = (
            centred * lax.rsqrt(variance + epsilon) * as_row(gain_ref) + as_row(bias_ref)
        ).astype(bf16)
        return carry

    lax.fori_loop(0, rows // 64, norm_rows, 0)
    greet(wide, narrow, w, n)

    step = rows // CHUNKS

    def part_of(shard, c):
        return normed.at[shard, pl.ds(c * step, step)]

    def pass_on(zs, c, way):
        block = part_of(2 * zs + core, c)
        k = (1 - way) // 2
        return remote(block, block, line_sent.at[zs, c, k], line_got.at[zs, c], w, n + 2 * way)

    def hand(zs, c):
        block = part_of(2 * zs + core, c)
        return remote(block, block, sib_sent.at[zs, c], sib_got.at[zs, c], w, sibling)

    def project(owner, c):
        columns = pl.ds(pl.multiple_of(owner * rows + c * step, step), step)
        product = contract(turned[...], normed[owner, pl.ds(c * step, step)], 1, 1).astype(bf16)
        for j in range(product.shape[0] // HEAD_DIM):
            part = product[j * HEAD_DIM : (j + 1) * HEAD_DIM]
            if j % 3 == 0:
                part = part * jnp.asarray(HEAD_DIM**-0.5, bf16)
            packed[j * HEAD_DIM : (j + 1) * HEAD_DIM, columns] = part

    gather.begin()
    for c in range(CHUNKS):

        @pl.when(z < lines - 1)
        def _():
            pass_on(z, c, 1).start()

        @pl.when(z > 0)
        def _():
            pass_on(z, c, -1).start()

        hand(z, c).start()
    turned[...] = weight_ref[...].T
    for c in range(CHUNKS):
        project(n, c)

    def receive(c, zs, way, more):
        arrived(part_of(2 * zs + core, c), line_got.at[zs, c])

        @pl.when(more)
        def _():
            pass_on(zs, c, way).start()

        hand(zs, c).start()

    def project_side(zs, way, more):
        for c in range(CHUNKS):
            project(2 * zs + core, c)

    def project_sibling(zs, way, more):
        for c in range(CHUNKS):
            arrived(part_of(2 * zs + 1 - core, c), sib_got.at[zs, c])
            project(2 * zs + 1 - core, c)

    project_sibling(z, 0, None)
    for d in range(1, lines):
        gather.round(d)
        if d == lines - 1:
            gather.round(lines)
            gather.round(lines + 1)
        for c in range(CHUNKS):
            gather.sides(d, functools.partial(receive, c))
        if d > 1:
            gather.sides(d - 1, project_sibling)
        gather.sides(d, project_side)
    gather.sides(lines - 1, project_sibling)
    gather.finish()

    def sent_side(zs, way, more):
        for c in range(CHUNKS):
            hand(zs, c).wait_send()

            @pl.when(more)
            def _():
                pass_on(zs, c, way).wait_send()

    for c in range(CHUNKS):

        @pl.when(z < lines - 1)
        def _():
            pass_on(z, c, 1).wait_send()

        @pl.when(z > 0)
        def _():
            pass_on(z, c, -1).wait_send()

        hand(z, c).wait_send()
    for d in range(1, lines):
        gather.sides(d, sent_side)


def start(wide, narrow, tokens, gain, bias, weight, own):
    rows, features = tokens.shape
    lines = narrow // 2
    dma = pltpu.SemaphoreType.DMA
    vmem = pl.BlockSpec(memory_space=pltpu.VMEM)
    anywhere = pl.BlockSpec(memory_space=pl.ANY)
    return pl.pallas_call(
        functools.partial(start_kernel, wide, narrow),
        in_specs=[vmem, vmem, vmem, vmem, anywhere],
        out_specs=(vmem, vmem, vmem, anywhere),
        out_shape=(
            jax.ShapeDtypeStruct((narrow, rows, features), bf16),
            jax.ShapeDtypeStruct((weight.shape[1], narrow * rows), bf16),
            jax.ShapeDtypeStruct((weight.shape[1], features), bf16),
            jax.ShapeDtypeStruct((narrow, *own.shape), bf16),
        ),
        scratch_shapes=[
            dma((lines, CHUNKS, 2)), dma((lines, CHUNKS)), dma((lines, CHUNKS)), dma((lines, CHUNKS)),
            *Gather.scratch(wide, narrow, own.shape[3:]),
        ],
        compiler_params=pltpu.CompilerParams(
            vmem_limit_bytes=58 << 20, collective_id=1, has_side_effects=True
        ),
        name="start",
    )(tokens, gain, bias, weight, own)


def body(
    tokens, cotangent, item_lengths, attn_gain, attn_bias, qkv_weight, proj_weight,
    mlp_gain, mlp_bias, up_weight, down_weight,
):
    items = item_lengths.shape[1]
    heads = qkv_weight.shape[1] // (3 * HEAD_DIM)
    wide, narrow = lax.axis_size("wide"), lax.axis_size("narrow")
    side = math.isqrt(wide)
    rows = narrow * tokens.shape[0]

    def cut(shard):
        return shard.reshape(side, side, 2, shard.shape[0] // (2 * wide), shard.shape[1])

    def split_parts(total):
        return total.reshape(narrow, side, side, 2, -1, total.shape[1])

    first = down_weight.shape[0] // (2 * wide)
    extras = mask_rows(item_lengths, rows)
    normed_all, packed, qkv_turned, up_all = start(
        wide, narrow, tokens, attn_gain, attn_bias, qkv_weight, cut(up_weight)
    )
    normed_all = normed_all.reshape(rows, -1)
    packed = packed.reshape(heads, 3, HEAD_DIM, rows)
    attended, log_total, attended_rows, rest_all = attend_forward(
        wide, narrow, packed, extras, cut(down_weight), cut(proj_weight)
    )
    attended_rows = attended_rows.reshape(-1, tokens.shape[0])
    proj_all = rest_all[:, :, :, :, first:].reshape(-1, tokens.shape[1])
    output, grad_middle, grad_attended, grad_proj, grad_parts, norm_parts = mlp(
        attended_rows, proj_all, tokens, cotangent, mlp_gain, mlp_bias, up_all, rest_all, first
    )
    grad_attended = grad_attended.reshape(narrow, heads, HEAD_DIM, -1)
    grad_proj_parts = split_parts(grad_proj)
    grad_tokens, grad_qkv, grad_shard, shares, _ = backward(
        wide, narrow, extras, packed, attended, log_total, grad_attended, grad_parts,
        grad_proj_parts, qkv_turned, normed_all, tokens, grad_middle, attn_gain, norm_parts, items,
    )
    grad_qkv, grad_proj, grad_up, grad_down = unpack(
        grad_shard, grad_qkv, proj_weight.shape, up_weight.shape, down_weight.shape
    )
    return (
        output, grad_tokens, shares[0], shares[1], grad_qkv, grad_proj,
        shares[2], shares[3], grad_up, grad_down,
    )


def solution(mesh):
    by_rows = P(("wide", "narrow"), None)
    return jax.shard_map(
        body,
        mesh=mesh,
        in_specs=(
            by_rows, by_rows, P("wide", None), P(), P(), P(None, "narrow"), P("narrow", None),
            P(), P(), P(None, "narrow"), P("narrow", None),
        ),
        out_specs=(
            by_rows, by_rows, P("narrow"), P("narrow"), P(None, "narrow"), P("narrow", None),
            P("narrow"), P("narrow"), P(None, "narrow"), P("narrow", None),
        ),
        check_vma=False,
    )
```

```python
import functools
import math

import jax
import jax.numpy as jnp
from jax import lax
from jax.experimental import pallas as pl
from jax.experimental.pallas import tpu as pltpu
from jax.sharding import PartitionSpec as P

HEAD_DIM = 64
EXTRA = 16
CHUNKS = 2
REDUCE_START, REDUCE_STEP, REDUCE_FIRST, REDUCE_SECOND, SPREAD_AT = 2, 11, 8, 12, 8
EARLY_RELAY = 17
EXCLUDED = -1e30
bf16 = jnp.bfloat16
f32 = jnp.float32
MESH = pl.DeviceIdType.MESH
epsilon = 1e-05


def mask_rows(length_ref, extras):
    items = length_ref.shape[1]
    rows = extras.shape[2]
    position = lax.broadcasted_iota(jnp.int32, (EXTRA, rows), 1)
    extra = lax.broadcasted_iota(jnp.int32, (EXTRA, rows), 0)
    segment, end = jnp.zeros((EXTRA, rows), jnp.int32), 0
    for i in range(items):
        end = end + length_ref[0, i]
        segment = segment + jnp.where(position >= end, 1, 0)
    own = jnp.where(segment == extra, 1.0, 0.0)
    mask = jnp.where(extra <= items, 1.0, 0.0)
    ones = jnp.where(extra <= items + 3, 1.0, 0.0) * (1.0 - mask)
    extras[0] = (own * mask).astype(bf16)
    extras[1] = ((1.0 - own) * mask * EXCLUDED + ones).astype(bf16)


def forward_kernel(
    wide, narrow, qx_ref, kx_ref, q_ref, k_ref, v_ref, own_ref, more_ref, o_ref, log_ref, rows_ref, gathered,
    keys, ready, copied, sent, got, *gather_refs,
):
    gather = Gather(wide, narrow, [own_ref, more_ref], gathered, *gather_refs)
    w, n, lines = gather.w, gather.n, gather.lines
    head, step = pl.program_id(0), pl.program_id(1)
    moment = head * narrow + step
    width = q_ref.shape[-1] // narrow
    last = heads_of(ready, narrow) * narrow - 1

    moves = []
    for d in range(1, lines):
        moves += [
            (3.0 * d, functools.partial(gather.sides, d, gather.one)),
            (3.0 * d + 2.1, functools.partial(gather.sides, d, gather.two)),
            (3.0 * d + 5.2, functools.partial(gather.sides, d, gather.three)),
        ]
    moves.append((900.0, gather.finish))
    moves.sort(key=lambda move: move[0])

    def perform(lower, upper):
        for time, move in moves:
            if lower <= time < upper:
                move()

    @pl.when(moment == 0)
    def _():
        greet_all(wide, narrow, w, n)

    @pl.when(step == 0)
    def _():
        keys[...] = jnp.concatenate([k_ref[0], kx_ref[...]], axis=0).T

    @pl.when(moment == 0)
    def _():
        greeted(wide, narrow)
        gather.begin()

    for tick in range(last + 1):

        @pl.when(moment == tick)
        def _():
            perform(tick, tick + 1)

    owner = lax.rem(n + 1 + step, narrow)
    columns = pl.ds(pl.multiple_of(owner * width, width), width)
    query = jnp.concatenate(
        [q_ref[0, :, columns], qx_ref[:, columns]], axis=0
    )
    scores = jnp.dot(keys[...], query, preferred_element_type=f32)
    maximum = jnp.max(scores, axis=0, keepdims=True)
    raised = jnp.exp(scores - maximum)
    total = jnp.sum(raised, axis=0, keepdims=True)
    gathered_values = jnp.dot(v_ref[0], raised.astype(bf16), preferred_element_type=f32)
    result = (gathered_values / total).astype(bf16)
    o_ref[0, :, columns] = result
    log_ref[0, :, columns] = maximum + jnp.log(total)
    ready[moment] = result

    def deliver(k, owner, h):
        return remote(ready.at[k], rows_ref.at[n, h], sent.at[k], got.at[n, h], w, owner)

    def deliver_here(k, h):
        return pltpu.make_async_copy(ready.at[k], rows_ref.at[n, h], copied.at[h])

    @pl.when(step < narrow - 1)
    def _():
        deliver(moment, owner, head).start()

    @pl.when(step == narrow - 1)
    def _():
        deliver_here(moment, head).start()

    @pl.when(moment == last)
    def _():
        perform(last + 1, 1000)
        for h in range((last + 1) // narrow):
            deliver_here(h * narrow + narrow - 1, h).wait()
            for t in range(narrow - 1):
                deliver(h * narrow + t, lax.rem(n + 1 + t, narrow), h).wait_send()
                source = lax.rem(n + narrow - 1 - t, narrow)
                arrived(rows_ref.at[source, h], got.at[source, h])


def heads_of(ready, narrow):
    return ready.shape[0] // narrow


def attend_forward(wide, narrow, packed, extras, own, more):
    heads, _, _, rows = packed.shape
    width = rows // narrow
    gathered = (narrow, *own.shape[:3], own.shape[3] + more.shape[3], own.shape[4])
    dma = pltpu.SemaphoreType.DMA

    def whole(j):
        return pl.BlockSpec((1, None, HEAD_DIM, rows), lambda h, i: (h, j, 0, 0))

    def extra(j):
        return pl.BlockSpec((None, EXTRA, rows), lambda h, i: (j, 0, 0))

    anywhere = pl.BlockSpec(memory_space=pl.ANY)
    return pl.pallas_call(
        functools.partial(forward_kernel, wide, narrow),
        grid=(heads, narrow),
        in_specs=[extra(0), extra(1), whole(0), whole(1), whole(2), anywhere, anywhere],
        out_specs=(
            pl.BlockSpec((1, HEAD_DIM, rows), lambda h, i: (h, 0, 0)),
            pl.BlockSpec((1, 1, rows), lambda h, i: (h, 0, 0)),
            anywhere,
            anywhere,
        ),
        out_shape=(
            jax.ShapeDtypeStruct((heads, HEAD_DIM, rows), bf16),
            jax.ShapeDtypeStruct((heads, 1, rows), f32),
            jax.ShapeDtypeStruct((narrow, heads, HEAD_DIM, width), bf16),
            jax.ShapeDtypeStruct(gathered, bf16),
        ),
        scratch_shapes=[
            pltpu.VMEM((rows, HEAD_DIM + EXTRA), bf16),
            pltpu.VMEM((heads * narrow, HEAD_DIM, width), bf16),
            dma((heads,)),
            dma((heads * narrow,)),
            dma((narrow, heads)),
            *Gather.scratch(wide, narrow, gathered[4:]),
        ],
        compiler_params=pltpu.CompilerParams(
            vmem_limit_bytes=58 << 20, collective_id=4, has_side_effects=True
        ),
        name="attend_forward",
    )(extras, extras, packed, packed, packed, own, more)


def remote(src, dst, sent, received, wide_to, narrow_to):
    return pltpu.make_async_remote_copy(
        src_ref=src,
        dst_ref=dst,
        send_sem=sent,
        recv_sem=received,
        device_id=(wide_to, narrow_to),
        device_id_type=MESH,
    )


def arrived(ref, semaphore):
    pltpu.make_async_copy(ref, ref, semaphore).wait()


def greet_all(wide, narrow, w, n):
    barrier = pltpu.get_barrier_semaphore()

    def column(t, carry):
        pl.semaphore_signal(
            barrier, inc=1, device_id=(w, lax.rem(n + t, narrow)), device_id_type=MESH
        )
        return carry

    def plane(t, carry):
        pl.semaphore_signal(
            barrier, inc=1, device_id=(lax.rem(w + t, wide), n), device_id_type=MESH
        )
        return carry

    lax.fori_loop(1, narrow, column, 0)
    lax.fori_loop(1, wide, plane, 0)


def greeted(wide, narrow):
    pl.semaphore_wait(pltpu.get_barrier_semaphore(), narrow + wide - 2)


def accumulate(into, *others):
    rows = into.shape[0]
    few = max([d for d in (16, 32, 48, 64) if rows % d == 0], default=rows)

    def piece(j, carry):
        part = pl.ds(j * few if rows == few else pl.multiple_of(j * few, few), few)
        total = into[part, :].astype(f32)
        for other in others:
            total = total + other[part, :].astype(f32)
        into[part, :] = total.astype(bf16)
        return carry

    if rows == few:
        piece(0, 0)
    else:
        lax.fori_loop(0, rows // few, piece, 0)


def reduce_steps(
    wide, narrow, parts, proj_parts, landed, final, held, staged, from_first, from_second, from_line,
    mine, loaded, sib_sent, sib_got, first_sent, first_got, second_sent, second_got, line_sent, line_got,
):
    w, n = lax.axis_index("wide"), lax.axis_index("narrow")
    side, lines = math.isqrt(wide), narrow // 2
    a, b, z, core = w // side, lax.rem(w, side), n // 2, lax.rem(n, 2)
    sibling = n + 1 - 2 * core
    slots = held.shape[0]
    most, least = parts.shape[4], proj_parts.shape[4]
    sources = [(parts, pl.ds(0, most)), (proj_parts, pl.ds(most, least))]
    order = [lax.rem(z + 1 + j, lines) for j in range(lines)]
    halves = [(h, i) for i in range(1, side) for h in (0, 1)]

    def other_a(i):
        return lax.rem(a + i, side)

    def other_b(i):
        return lax.rem(b + i, side)

    def to_sibling(j):
        shard = 2 * order[j] + 1 - core
        return [
            remote(
                src.at[shard], landed.at[j, :, :, :, rows],
                sib_sent.at[k, j], sib_got.at[k, j], w, sibling,
            )
            for k, (src, rows) in enumerate(sources)
        ]

    def load(j):
        shard, slot = 2 * order[j] + core, j % slots
        return [
            pltpu.make_async_copy(src.at[shard], held.at[slot, :, :, :, rows], loaded.at[k])
            for k, (src, rows) in enumerate(sources)
        ]

    def stage(j):
        return pltpu.make_async_copy(landed.at[j], staged, loaded.at[2])

    def first(j, h, i):
        slot, k = j % slots, i - 1
        if h == 0:
            src, to = held.at[slot, other_a(i), :, 0], other_a(i) * side + b
        else:
            src, to = held.at[slot, :, other_b(i), 1], a * side + other_b(i)
        return remote(
            src, from_first.at[j, h, k], first_sent.at[j, h, k], first_got.at[j, h, k], to, n
        )

    def second(j, h, i):
        slot, k = j % slots, i - 1
        if h == 0:
            src, to = held.at[slot, a, other_b(i), 0], a * side + other_b(i)
        else:
            src, to = held.at[slot, other_a(i), b, 1], other_a(i) * side + b
        return remote(
            src, from_second.at[j, h, k], second_sent.at[j, h, k], second_got.at[j, h, k], to, n
        )

    def along(j):
        zs = order[j]
        place = jnp.where(z < zs, z, z - 1)
        return remote(
            held.at[j % slots, a, b], from_line.at[place], line_sent.at[j], line_got.at[place],
            w, 2 * zs + core,
        )

    def begin():
        for j in range(lines):
            for copy in to_sibling(j):
                copy.start()

    def sent(j):
        for h, i in halves:
            first(j, h, i).wait_send()
            second(j, h, i).wait_send()

        if j < lines - 1:
            along(j).wait_send()

    def combine(j):
        slot = j % slots
        if j >= slots:
            sent(j - slots)
        for copy in load(j):
            copy.start()
        for k, (_, rows) in enumerate(sources):
            arrived(landed.at[j, :, :, :, rows], sib_got.at[k, j])
        stage(j).start()
        for copy in load(j):
            copy.wait()
        stage(j).wait()

        def piece(t, carry):
            p, q = t // side, lax.rem(t, side)
            for h in (0, 1):
                accumulate(held.at[slot, p, q, h], staged.at[p, q, h])
            return carry

        lax.fori_loop(0, wide, piece, 0)
        for h, i in halves:
            first(j, h, i).start()

    def narrow_down(j):
        slot = j % slots
        for h in (0, 1):
            for i in range(1, side):
                arrived(from_first.at[j, h, i - 1], first_got.at[j, h, i - 1])

            def piece(t, carry, h=h):
                into = held.at[slot, a, t, 0] if h == 0 else held.at[slot, t, b, 1]
                accumulate(into, *[from_first.at[j, h, i, t] for i in range(side - 1)])
                return carry

            lax.fori_loop(0, side, piece, 0)
        for h, i in halves:
            second(j, h, i).start()

    def send_home(j):
        slot = j % slots
        for h, i in halves:
            arrived(from_second.at[j, h, i - 1], second_got.at[j, h, i - 1])
        for h in (0, 1):
            accumulate(
                held.at[slot, a, b, h], *[from_second.at[j, h, i] for i in range(side - 1)]
            )

        if j < lines - 1:
            along(j).start()
        else:
            mine[...] = held[slot, a, b]

    def finish():
        for place in range(lines - 1):
            arrived(from_line.at[place], line_got.at[place])
        for h in (0, 1):
            total = mine[h].astype(f32)
            for place in range(lines - 1):
                total = total + from_line[place, h].astype(f32)
            final[h] = total.astype(bf16)

    def close():
        for j in range(lines):
            for copy in to_sibling(j):
                copy.wait_send()
        for j in range(max(0, lines - slots), lines):
            sent(j)

    steps = [(0.0, begin)]
    for j in range(lines):
        at = REDUCE_START + REDUCE_STEP * j
        steps += [
            (at, functools.partial(combine, j)),
            (at + REDUCE_FIRST, functools.partial(narrow_down, j)),
            (at + REDUCE_SECOND, functools.partial(send_home, j)),
        ]
    return sorted(steps, key=lambda step: step[0]), finish, close


def reduce_scratch(wide, narrow, rows, features, slots=3):
    side, lines = math.isqrt(wide), narrow // 2
    dma = pltpu.SemaphoreType.DMA
    plane = (lines, 2, side - 1)
    return [
        pltpu.VMEM((slots, side, side, 2, rows, features), bf16),
        pltpu.VMEM((side, side, 2, rows, features), bf16),
        pltpu.VMEM((lines, 2, side - 1, side, rows, features), bf16),
        pltpu.VMEM((lines, 2, side - 1, rows, features), bf16),
        pltpu.VMEM((lines - 1, 2, rows, features), bf16),
        pltpu.VMEM((2, rows, features), bf16),
        *[dma(shape) for shape in [(3,), (2, lines), (2, lines), plane, plane, plane, plane]],
        dma((lines,)),
        dma((lines - 1,)),
    ]


def as_row(ref):
    return ref[...].astype(f32).reshape(1, -1)


def contract(left, right, left_axis, right_axis):
    return lax.dot_general(
        left, right, (((left_axis,), (right_axis,)), ((), ())), preferred_element_type=f32
    )


def gelu_pair(values):
    half = 0.5 + 0.5 * lax.erf(values * 0.7071067811865476)
    slope = half + values * (jnp.exp(values * values * -0.5) * 0.3989422804014327)
    return values * half, slope


def mlp_kernel(
    att_ref, rest_ref, token_ref, cot_ref, gain_ref, bias_ref, up_ref, down_ref,
    out_ref, middle_out, att_out, proj_out, parts_ref, norm_ref,
    middle, expand, out_total, expand_total, proj_ref, proj_got,
):
    step = pl.program_id(0)
    rows, features = token_ref.shape
    few = 64

    def by_rows(change):
        def body(j, carry):
            return change(pl.ds(pl.multiple_of(j * few, few), few), carry)

        return body

    if rest_ref.ndim == 2:
        fetch = pltpu.make_async_copy(rest_ref, proj_ref, proj_got)
    else:
        few_rows = rest_ref.shape[4] - down_ref.shape[4]
        fetch = pltpu.make_async_copy(
            rest_ref.at[:, :, :, :, pl.ds(down_ref.shape[4], few_rows)],
            proj_ref.reshape(*rest_ref.shape[:4], few_rows, features),
            proj_got,
        )

    @pl.when(step == 0)
    def _():
        fetch.start()
        fetch.wait()
        middle[...] = token_ref[...].astype(f32) + contract(att_ref[...], proj_ref[...], 0, 0)
        out_total[...] = jnp.zeros_like(out_total)
        expand_total[...] = jnp.zeros_like(expand_total)

        def norm(part, carry):
            values = middle[part, :]
            centred = values - jnp.mean(values, axis=-1, keepdims=True)
            variance = jnp.mean(centred * centred, axis=-1, keepdims=True)
            expand[part, :] = (
                centred * lax.rsqrt(variance + epsilon) * as_row(gain_ref) + as_row(bias_ref)
            ).astype(bf16)
            return carry

        lax.fori_loop(0, rows // few, by_rows(norm), 0)

    def flat(ref):
        if ref.shape[4] % 16:
            return ref[0].astype(f32).reshape(-1, ref.shape[5]).astype(bf16)
        return ref[0].reshape(-1, ref.shape[5])

    up, down = flat(up_ref), flat(down_ref)
    units = down_ref.shape[4]
    pieces = up_ref.shape[1:4]
    columns = up_ref.shape[5]
    hidden_parts, grad_parts = [], []
    for part in (pl.ds(0, rows // 2), pl.ds(rows // 2, rows // 2)):
        hidden, slope = gelu_pair(
            jnp.dot(expand[part, :], up, preferred_element_type=f32)
        )
        grad_pre = (contract(cot_ref[part, :], down, 1, 1) * slope).astype(bf16)
        hidden = hidden.astype(bf16)
        out_total[part, :] += jnp.dot(hidden, down, preferred_element_type=f32)
        expand_total[part, :] += contract(grad_pre, up, 1, 1)
        hidden_parts.append(hidden)
        grad_parts.append(grad_pre)
    grad_up = contract(expand[...], jnp.concatenate(grad_parts, axis=0), 0, 0)
    grad_down = contract(jnp.concatenate(hidden_parts, axis=0), cot_ref[...], 0, 0)
    groups = features // columns
    grad_up = grad_up.reshape(*pieces, groups, units, columns)
    for g in range(groups):
        parts_ref[0, :, :, :, 0:units, g * columns : (g + 1) * columns] = grad_up[
            :, :, :, g
        ].astype(bf16)
    parts_ref[0, :, :, :, units : 2 * units, :] = grad_down.reshape(
        *pieces, units, features
    ).astype(bf16)

    @pl.when(step == pl.num_programs(0) - 1)
    def _():
        def finish_rows(part, carry):
            gain_sum, bias_sum = carry
            values = middle[part, :]
            out_ref[part, :] = (values + out_total[part, :]).astype(bf16)
            centred = values - jnp.mean(values, axis=-1, keepdims=True)
            inverse = lax.rsqrt(jnp.mean(centred * centred, axis=-1, keepdims=True) + epsilon)
            scaled = centred * inverse
            grad = expand_total[part, :]
            term = grad * as_row(gain_ref)
            back = inverse * (
                term
                - jnp.mean(term, axis=-1, keepdims=True)
                - scaled * jnp.mean(term * scaled, axis=-1, keepdims=True)
            )
            total = cot_ref[part, :].astype(f32) + back
            middle_out[part, :] = total
            expand[part, :] = total.astype(bf16)
            gain_sum = gain_sum + jnp.sum(grad * scaled, axis=0, keepdims=True)
            bias_sum = bias_sum + jnp.sum(grad, axis=0, keepdims=True)
            return gain_sum, bias_sum

        start = (jnp.zeros((1, features), f32), jnp.zeros((1, features), f32))
        gain_sum, bias_sum = lax.fori_loop(0, rows // few, by_rows(finish_rows), start)
        row = lax.broadcasted_iota(jnp.int32, (8, features), 0)
        norm_ref[...] = jnp.where(row == 2, gain_sum, jnp.where(row == 3, bias_sum, 0.0))
        branch = expand[...]
        att_out[...] = contract(proj_ref[...], branch, 1, 1).astype(bf16)
        proj_out[...] = jnp.dot(att_ref[...], branch, preferred_element_type=f32).astype(bf16)


def mlp(attended, rest, tokens, cotangent, gain, bias, up_all, down_all, units):
    rows, features = tokens.shape
    narrow, side = up_all.shape[:2]
    proj_shape = (attended.shape[0], features)

    def whole(*shape):
        return pl.BlockSpec(shape, lambda i: (0,) * len(shape))

    def weights(*piece):
        return pl.BlockSpec((1, side, side, 2, *piece), lambda i: (i, 0, 0, 0, 0, 0))

    return pl.pallas_call(
        mlp_kernel,
        grid=(narrow,),
        in_specs=[
            whole(*attended.shape),
            pl.BlockSpec(memory_space=pl.ANY),
            whole(rows, features),
            whole(rows, features),
            whole(*gain.shape),
            whole(*bias.shape),
            weights(*up_all.shape[4:]),
            weights(units, features),
        ],
        out_specs=(
            whole(rows, features),
            whole(rows, features),
            whole(*attended.shape),
            whole(*proj_shape),
            pl.BlockSpec(
                (1, side, side, 2, 2 * units, features), lambda i: (i, 0, 0, 0, 0, 0)
            ),
            whole(8, features),
        ),
        out_shape=(
            jax.ShapeDtypeStruct((rows, features), bf16),
            jax.ShapeDtypeStruct((rows, features), f32),
            jax.ShapeDtypeStruct(attended.shape, bf16),
            jax.ShapeDtypeStruct(proj_shape, bf16),
            jax.ShapeDtypeStruct((narrow, side, side, 2, 2 * units, features), bf16),
            jax.ShapeDtypeStruct((8, features), f32),
        ),
        scratch_shapes=[
            pltpu.VMEM((rows, features), f32),
            pltpu.VMEM((rows, features), bf16),
            pltpu.VMEM((rows, features), f32),
            pltpu.VMEM((rows, features), f32),
            pltpu.VMEM(proj_shape, bf16),
            pltpu.SemaphoreType.DMA(()),
        ],
        compiler_params=pltpu.CompilerParams(vmem_limit_bytes=58 << 20),
        name="mlp",
    )(attended, rest, tokens, cotangent, gain, bias, up_all, down_all)


def backward_kernel(
    wide, narrow, items, chunks,
    extra_ref, packed_ref, att_ref, log_ref, own_ref, parts_ref, proj_parts_ref, weight_ref,
    normed_ref, token_ref, middle_ref, gain_ref, norm_ref,
    tokens_out, qkv_out, shard_out, norms_out, landed,
    keys, values, queries, grads, grad_q, grad_k, grad_v, block_grad,
    normed, total_qkv, for_sibling, from_sibling, held, from_line,
    first_qkv, second_qkv, norms, norm_column, norm_half, norm_plane, piece,
    middle,
    packed_got, own_got, do_sent, do_got, normed_got, middle_got, copied, sib_sent, sib_got,
    line_sent, line_got, piece_sent, piece_got, first_sent, first_got, second_sent, second_got,
    column_sent, column_got, plane_sent, plane_got, *reduce_refs,
):
    w, n = lax.axis_index("wide"), lax.axis_index("narrow")
    side, lines = math.isqrt(wide), narrow // 2
    a, b, z, core = w // side, lax.rem(w, side), n // 2, lax.rem(n, 2)
    sibling = n + 1 - 2 * core
    heads = keys.shape[0]
    rows, features = token_ref.shape
    step = rows // chunks
    lower = z < lines // 2
    moves, reduce_finish, reduce_close = reduce_steps(
        wide, narrow, parts_ref, proj_parts_ref, landed, piece, *reduce_refs
    )

    def line_at(k):
        climbing = jnp.where(
            k < lines - 1 - z, lines - 1 - k, jnp.where(k < lines - 1, k - (lines - 1 - z), z)
        )
        falling = jnp.where(k < z, k, jnp.where(k < lines - 1, lines - 1 - (k - z), z))
        return jnp.where(lower, climbing, falling)

    def block_at(j):
        odd = lax.rem(j, 2)
        return 2 * line_at(j // 2) + jnp.where(odd == 1, core, 1 - core)

    def columns(owner):
        return pl.ds(pl.multiple_of(owner * rows, rows), rows)

    def packed_copy(h, j):
        into = (queries, keys, values)[j]
        return pltpu.make_async_copy(
            packed_ref.at[h, j], into.at[h, pl.ds(0, HEAD_DIM)], packed_got.at[h, j]
        )

    def keep(h):
        return pltpu.make_async_copy(
            own_ref.at[n, h], grads.at[h, pl.ds(0, HEAD_DIM), columns(n)], own_got.at[h]
        )

    def deliver(t, h):
        to = lax.rem(n + t, narrow)
        return remote(
            own_ref.at[to, h], grads.at[h, pl.ds(0, HEAD_DIM), columns(n)],
            do_sent.at[t, h], do_got.at[n, h], w, to,
        )

    def fetch(j):
        owner = block_at(j)
        return pltpu.make_async_copy(
            normed_ref.at[pl.ds(pl.multiple_of(owner * rows, rows), rows)],
            normed.at[lax.rem(j, 2)], normed_got.at[lax.rem(j, 2)],
        )

    for h in range(heads):
        for j in range(3):
            packed_copy(h, j).start()
        keep(h).start()
    fetch(0).start()
    greet_all(wide, narrow, w, n)
    grad_q[...] = jnp.zeros_like(grad_q)
    grad_k[...] = jnp.zeros_like(grad_k)
    grad_v[...] = jnp.zeros_like(grad_v)
    total_qkv[...] = jnp.zeros_like(total_qkv)
    greeted(wide, narrow)
    for t in range(1, narrow):
        for h in range(heads):
            deliver(t, h).start()
    for h in range(heads):
        keys[h, HEAD_DIM:, :] = extra_ref[1]
        values[h, HEAD_DIM:, :] = extra_ref[1]
    for h in range(heads):
        for j in range(3):
            packed_copy(h, j).wait()
        keep(h).wait()

    row = lax.broadcasted_iota(jnp.int32, (EXTRA, rows), 0) - items

    def pieces(term, base):
        high = term.astype(bf16).astype(f32)
        mid = (term - high).astype(bf16).astype(f32)
        small = term - high - mid
        return jnp.where(
            row == 1, high, jnp.where(row == 2, mid, jnp.where(row == 3, small, base))
        ).astype(bf16)

    def prepare(j):
        owner = block_at(j)
        where = columns(owner)

        @pl.when(owner != n)
        def _():
            for h in range(heads):
                arrived(grads.at[h, pl.ds(0, HEAD_DIM), where], do_got.at[owner, h])

        for h in range(heads):
            grad = grads[h, 0:HEAD_DIM, where].astype(f32)
            inner = jnp.sum(grad * att_ref[h, :, where].astype(f32), axis=0, keepdims=True)
            grads[h, HEAD_DIM:, where] = pieces(-inner, jnp.zeros((EXTRA, rows), f32))
            queries[h, HEAD_DIM:, where] = pieces(
                -log_ref[h, :, where], extra_ref[0, :, where].astype(f32)
            )

    def to_sibling(zs, slot):
        return remote(
            for_sibling.at[slot], from_sibling.at[zs], sib_sent.at[slot], sib_got.at[zs], w, sibling
        )

    def pass_on(zs, c, up):
        part = pl.ds(c * step, step)
        place = zs if up else jnp.where(z - 1 == zs, lines, zs)
        return remote(
            held.at[zs, part], from_line.at[place, part], line_sent.at[zs, c],
            line_got.at[place, c], w, n + 2 if up else n - 2,
        )

    def relay(zs, c, up):
        part = pl.ds(c * step, step)
        arrived(from_line.at[zs, part], line_got.at[zs, c])
        accumulate(held.at[zs, part], from_line.at[zs, part])
        pass_on(zs, c, up).start()

    def early_relay():
        @pl.when(jnp.logical_and(lower, z >= 1))
        def _():
            for c in range(chunks):
                relay(lines - 1, c, True)

        @pl.when(jnp.logical_and(z >= lines // 2, z <= lines - 2))
        def _():
            for c in range(chunks):
                relay(0, c, False)

    def emit(j):
        j = jnp.asarray(j, jnp.int32)
        owner = block_at(j)
        where = columns(owner)
        for h in range(heads):
            for k, total in enumerate((grad_q, grad_k, grad_v)):
                at = (h * 3 + k) * HEAD_DIM
                value = total[h, :, where]
                block_grad[at : at + HEAD_DIM, :] = (
                    value * HEAD_DIM**-0.5 if k == 0 else value
                ).astype(bf16)
        zs, slot = line_at(j // 2), lax.rem(j // 2, 2)
        product = contract(block_grad[...], weight_ref[...], 0, 0).astype(bf16)

        @pl.when(lax.rem(j, 2) == 0)
        def _():
            @pl.when(j >= 4)
            def _():
                to_sibling(zs, slot).wait_send()

            for_sibling[slot] = product
            to_sibling(zs, slot).start()

        @pl.when(lax.rem(j, 2) == 1)
        def _():
            held[zs] = product

        fetch(j).wait()

        @pl.when(j < narrow - 1)
        def _():
            fetch(j + 1).start()

        total_qkv[...] += jnp.dot(
            block_grad[...], normed[lax.rem(j, 2)], preferred_element_type=f32
        )

        @pl.when(lax.rem(j, 2) == 1)
        def _():
            arrived(from_sibling.at[zs], sib_got.at[zs])
            accumulate(held.at[zs], from_sibling.at[zs])

            @pl.when(jnp.logical_and(z == 0, zs != z))
            def _():
                for c in range(chunks):
                    pass_on(zs, c, True).start()

            @pl.when(jnp.logical_and(z == lines - 1, zs != z))
            def _():
                for c in range(chunks):
                    pass_on(zs, c, False).start()

    def spread(t):
        return remote(
            piece, shard_out.at[w], piece_sent.at[t], piece_got.at[t], lax.rem(w + t, wide), n
        )

    stay = pltpu.make_async_copy(piece, shard_out.at[w], copied)

    def spread_all():
        reduce_finish()
        stay.start()
        for t in range(1, wide):
            spread(t).start()

    prepare(narrow - 1)
    pairs = narrow * narrow
    moves = moves + [(6 * narrow - 8 + EARLY_RELAY, early_relay), (pairs - SPREAD_AT, spread_all)]
    moves.sort(key=lambda move: move[0])
    ticks = {}
    for time, move in moves:
        ticks.setdefault(min(int(time), pairs - 1), []).append(move)

    def pair(p, carry):
        for tick, group in ticks.items():

            @pl.when(p == tick)
            def _():
                for move in group:
                    move()

        late = p - 2 * narrow
        stage = sum(
            (late >= j * (2 * narrow - 2 - j)).astype(jnp.int32) for j in range(1, narrow - 2)
        )
        r = late - stage * (2 * narrow - 2 - stage)
        across = r < narrow - stage
        near = late < 0
        qi = jnp.where(
            near,
            jnp.where(p < narrow, narrow - 1, narrow - 2),
            jnp.where(across, stage, 2 * stage + 1 + r - narrow),
        )
        ki = jnp.where(near, lax.rem(p, narrow), jnp.where(across, stage + r, stage))

        @pl.when((p == narrow) | (late == 0) | ((stage == 0) & (r >= narrow)))
        def _():
            prepare(qi)

        at_q, at_k = columns(block_at(qi)), columns(block_at(ki))
        for h in range(heads):
            probs = jnp.exp(contract(queries[h, :, at_q], keys[h, :, at_k], 0, 0))
            scores = (probs * contract(grads[h, :, at_q], values[h, :, at_k], 0, 0)).astype(bf16)
            grad_v[h, :, at_k] += jnp.dot(
                grads[h, 0:HEAD_DIM, at_q], probs.astype(bf16), preferred_element_type=f32
            )
            grad_k[h, :, at_k] += jnp.dot(
                queries[h, 0:HEAD_DIM, at_q], scores, preferred_element_type=f32
            )
            grad_q[h, :, at_q] += contract(keys[h, 0:HEAD_DIM, at_k], scores, 1, 1)

        @pl.when(r == 2 * (narrow - stage) - 4)
        def _():
            emit(stage)

        return carry

    lax.fori_loop(0, pairs, pair, 0)
    emit(narrow - 2)
    emit(narrow - 1)

    half = total_qkv.shape[0] // 2
    own_qkv, half_qkv = for_sibling.at[:, 0:half], normed.at[:, 0:half]
    for slot in range(min(2, lines)):
        to_sibling(0, slot).wait_send()
    for h in (0, 1):
        own_qkv[h] = total_qkv[h * half : (h + 1) * half].astype(bf16)
    halves = [(h, i) for i in range(1, side) for h in (0, 1)]

    def plane_at(h, i):
        if h == 0:
            return lax.rem(a + i, side) * side + b
        return a * side + lax.rem(b + i, side)

    def first(h, i):
        return remote(
            own_qkv.at[h], first_qkv.at[h, i - 1], first_sent.at[h, i - 1], first_got.at[h, i - 1],
            plane_at(h, i), n,
        )

    def second(h, i):
        return remote(
            half_qkv.at[h], second_qkv.at[h, i - 1], second_sent.at[h, i - 1],
            second_got.at[h, i - 1], plane_at(1 - h, i), n,
        )

    def qkv_second():
        for h, i in halves:
            arrived(first_qkv.at[h, i - 1], first_got.at[h, i - 1])
        for h in (0, 1):
            total = own_qkv[h].astype(f32)
            for i in range(1, side):
                total = total + first_qkv[h, i - 1].astype(f32)
            half_qkv[h] = total.astype(bf16)
        for h, i in halves:
            second(h, i).start()

    def qkv_last():
        for h, i in halves:
            arrived(second_qkv.at[h, i - 1], second_got.at[h, i - 1])
        for h in (0, 1):
            total = half_qkv[h].astype(f32)
            for i in range(1, side):
                total = total + second_qkv[h, i - 1].astype(f32)
            qkv_out[h * half : (h + 1) * half] = total.astype(bf16)

    for h, i in halves:
        first(h, i).start()

    def fetch_middle(c):
        return pltpu.make_async_copy(middle_ref.at[pl.ds(c * step, step)], middle, middle_got)

    fetch_middle(0).start()
    for t in range(1, lines):
        below, above = lines - 1 - (t - z), t - (lines - 1 - z)
        for c in range(chunks):
            if t < lines - 1:

                @pl.when((z >= 1) & (t >= z) & ~(lower & (t == z)))
                def _():
                    relay(below, c, True)

                @pl.when((z <= lines - 2) & (above >= 0) & ~((z >= lines // 2) & (above == 0)))
                def _():
                    relay(above, c, False)

    qkv_second()

    def zero_edges(at_edge, place):
        @pl.when(at_edge)
        def _():
            from_line[place] = jnp.zeros((rows, features), bf16)

    zero_edges(z == 0, z)
    zero_edges(z == lines - 1, lines)
    gain_sum = bias_sum = jnp.zeros((1, features), f32)
    for c in range(chunks):
        part = pl.ds(c * step, step)

        @pl.when(z >= 1)
        def _():
            arrived(from_line.at[z, part], line_got.at[z, c])

        @pl.when(z <= lines - 2)
        def _():
            arrived(from_line.at[lines, part], line_got.at[lines, c])

        fetch_middle(c).wait()

        def norm_rows(j, carry):
            gain_sum, bias_sum = carry
            few = pl.ds(pl.multiple_of(c * step + j * 32, 32), 32)
            near = pl.ds(pl.multiple_of(j * 32, 32), 32)
            grad = (
                held[z, few].astype(f32)
                + from_line[z, few].astype(f32)
                + from_line[lines, few].astype(f32)
            )
            values = token_ref[few, :].astype(f32)
            centred = values - jnp.mean(values, axis=-1, keepdims=True)
            inverse = lax.rsqrt(jnp.mean(centred * centred, axis=-1, keepdims=True) + epsilon)
            scaled = centred * inverse
            term = grad * as_row(gain_ref)
            back = inverse * (
                term
                - jnp.mean(term, axis=-1, keepdims=True)
                - scaled * jnp.mean(term * scaled, axis=-1, keepdims=True)
            )
            tokens_out[few, :] = (middle[near, :] + back).astype(bf16)
            gain_sum = gain_sum + jnp.sum(grad * scaled, axis=0, keepdims=True)
            bias_sum = bias_sum + jnp.sum(grad, axis=0, keepdims=True)
            return gain_sum, bias_sum

        gain_sum, bias_sum = lax.fori_loop(0, step // 32, norm_rows, (gain_sum, bias_sum))
        if c + 1 < chunks:
            fetch_middle(c + 1).start()

    row = lax.broadcasted_iota(jnp.int32, (8, features), 0)
    parts = jnp.where(row == 0, gain_sum, jnp.where(row == 1, bias_sum, norm_ref[...]))
    share = features // narrow
    for owner in range(narrow):
        norms[owner] = parts[:, owner * share : (owner + 1) * share]

    def down_column(t):
        to = lax.rem(n + t, narrow)
        return remote(
            norms.at[to], norm_column.at[t - 1], column_sent.at[t - 1], column_got.at[t - 1], w, to
        )

    def over_plane(t):
        return remote(
            norm_half, norm_plane.at[t - 1], plane_sent.at[t - 1], plane_got.at[t - 1],
            lax.rem(w + t, wide), n,
        )

    for t in range(1, narrow):
        down_column(t).start()
    total = norms[n]
    for t in range(1, narrow):
        arrived(norm_column.at[t - 1], column_got.at[t - 1])
        total = total + norm_column[t - 1]
    norm_half[...] = total
    for t in range(1, wide):
        over_plane(t).start()
    for t in range(1, wide):
        arrived(norm_plane.at[t - 1], plane_got.at[t - 1])
        total = total + norm_plane[t - 1]
    norms_out[...] = total

    qkv_last()
    stay.wait()
    reduce_close()
    for t in range(1, wide):
        spread(t).wait_send()
        arrived(shard_out.at[lax.rem(w + wide - t, wide)], piece_got.at[t])
        over_plane(t).wait_send()
    for t in range(1, narrow):
        down_column(t).wait_send()
        for h in range(heads):
            deliver(t, h).wait_send()
    for h, i in halves:
        first(h, i).wait_send()
        second(h, i).wait_send()
    for zs in range(lines):
        for c in range(chunks):

            @pl.when(zs > z)
            def _():
                pass_on(zs, c, True).wait_send()

            @pl.when(zs < z)
            def _():
                pass_on(zs, c, False).wait_send()


def backward(
    wide, narrow, extras, packed, attended, log_total, grad, parts, proj_parts, weight, normed,
    tokens, middle, gain, norm_parts, items, chunks=4,
):
    side, lines = math.isqrt(wide), narrow // 2
    heads, _, _, total_rows = packed.shape
    rows, features = tokens.shape
    held_columns = weight.shape[0]
    piece = (parts.shape[4] + proj_parts.shape[4], features)
    depth = HEAD_DIM + EXTRA
    dma = pltpu.SemaphoreType.DMA
    vmem = pl.BlockSpec(memory_space=pltpu.VMEM)
    anywhere = pl.BlockSpec(memory_space=pl.ANY)
    plane = (2, side - 1)
    return pl.pallas_call(
        functools.partial(backward_kernel, wide, narrow, items, chunks),
        in_specs=[
            vmem, anywhere, vmem, vmem, anywhere, anywhere, anywhere, vmem,
            anywhere, vmem, anywhere, vmem, vmem,
        ],
        out_specs=(vmem, vmem, anywhere, vmem, anywhere),
        out_shape=(
            jax.ShapeDtypeStruct((rows, features), bf16),
            jax.ShapeDtypeStruct((held_columns, features), bf16),
            jax.ShapeDtypeStruct((wide, 2, *piece), bf16),
            jax.ShapeDtypeStruct((8, features // narrow), f32),
            jax.ShapeDtypeStruct((lines, side, side, 2, *piece), bf16),
        ),
        scratch_shapes=[
            *[pltpu.VMEM((heads, depth, total_rows), bf16)] * 4,
            *[pltpu.VMEM((heads, HEAD_DIM, total_rows), f32)] * 3,
            pltpu.VMEM((held_columns, rows), bf16),
            pltpu.VMEM((2, rows, features), bf16),
            pltpu.VMEM((held_columns, features), f32),
            pltpu.VMEM((2, rows, features), bf16),
            pltpu.VMEM((lines, rows, features), bf16),
            pltpu.VMEM((lines, rows, features), bf16),
            pltpu.VMEM((lines + 1, rows, features), bf16),
            pltpu.VMEM((2, side - 1, held_columns // 2, features), bf16),
            pltpu.VMEM((2, side - 1, held_columns // 2, features), bf16),
            pltpu.VMEM((narrow, 8, features // narrow), f32),
            pltpu.VMEM((narrow - 1, 8, features // narrow), f32),
            pltpu.VMEM((8, features // narrow), f32),
            pltpu.VMEM((wide - 1, 8, features // narrow), f32),
            pltpu.VMEM((2, *piece), bf16),
            pltpu.VMEM((rows // chunks, features), f32),
            dma((heads, 3)),
            dma((heads,)),
            dma((narrow, heads)),
            dma((narrow, heads)),
            dma((2,)),
            dma(()),
            dma(()),
            dma((2,)),
            dma((lines,)),
            dma((lines, chunks)),
            dma((lines + 1, chunks)),
            dma((wide,)),
            dma((wide,)),
            dma(plane),
            dma(plane),
            dma(plane),
            dma(plane),
            dma((narrow - 1,)),
            dma((narrow - 1,)),
            dma((wide - 1,)),
            dma((wide - 1,)),
            *reduce_scratch(wide, narrow, *piece),
        ],
        compiler_params=pltpu.CompilerParams(
            vmem_limit_bytes=61 << 20, collective_id=2, has_side_effects=True
        ),
        name="backward",
    )(
        extras, packed, attended, log_total, grad, parts, proj_parts, weight, normed,
        tokens, middle, gain, norm_parts,
    )


def unpack_kernel(shard_ref, qkv_ref, qkv_out, proj_out, up_out, down_out):
    wide = shard_ref.shape[0]
    features = shard_ref.shape[3]
    columns = up_out.shape[1]
    groups = features // columns
    units, few = down_out.shape[0] // (2 * wide), proj_out.shape[0] // (2 * wide)
    for j in range(2 * wide):
        w, h = divmod(j, 2)
        for g in range(groups):
            up_out[(j * groups + g) * units : (j * groups + g + 1) * units, :] = shard_ref[
                w, h, 0:units, g * columns : (g + 1) * columns
            ].astype(f32)
        down_out[j * units : (j + 1) * units, :] = shard_ref[w, h, units : 2 * units, :].astype(f32)
        proj_out[j * few : (j + 1) * few, :] = shard_ref[w, h, 2 * units :, :].astype(f32)
    qkv_out[...] = qkv_ref[...].astype(f32).T


def unpack(shard, qkv, proj_shape, up_shape, down_shape):
    return pl.pallas_call(
        unpack_kernel,
        out_shape=tuple(
            jax.ShapeDtypeStruct(shape, f32)
            for shape in (qkv.shape[::-1], proj_shape, up_shape, down_shape)
        ),
        compiler_params=pltpu.CompilerParams(vmem_limit_bytes=48 << 20),
        name="unpack",
    )(shard, qkv)


class Gather:
    def __init__(self, wide, narrow, owns, out, mine, *semaphores):
        self.owns, self.out, self.mine = owns, out, mine
        self.w, self.n = lax.axis_index("wide"), lax.axis_index("narrow")
        self.side, self.lines = math.isqrt(wide), narrow // 2
        self.a, self.b = self.w // self.side, lax.rem(self.w, self.side)
        self.z, self.core = self.n // 2, lax.rem(self.n, 2)
        self.sibling = self.n + 1 - 2 * self.core
        (
            self.loaded, self.copied, self.own_sent, self.passed, self.line_got, self.first_sent, self.first_got,
            self.second_sent, self.second_got, self.f0_sent, self.f0_got, self.f1_sent, self.f1_got,
            self.f2_sent, self.f2_got, self.f3_sent, self.f3_got,
        ) = semaphores
        self.pairs = [(h, i) for i in range(1, self.side) for h in (0, 1)]

    @staticmethod
    def scratch(wide, narrow, piece):
        side, lines = math.isqrt(wide), narrow // 2
        dma = pltpu.SemaphoreType.DMA
        line, plane = (lines,), (lines, 2, side)
        shapes = [(2,), (), line, line, line, plane, plane, plane, plane, (), (), line, line]
        mine = pltpu.VMEM((side, side, 2, *piece), bf16)
        return [mine, *[dma(shape) for shape in shapes + [plane] * 4]]

    def other_a(self, i):
        return lax.rem(self.a + i, self.side)

    def other_b(self, i):
        return lax.rem(self.b + i, self.side)

    def own_on(self, way):
        return remote(
            self.mine.at[self.a, self.b], self.out.at[self.n, self.a, self.b],
            self.own_sent.at[self.z + way], self.line_got.at[self.z], self.w, self.n + 2 * way,
        )

    def pass_on(self, zs, way):
        piece = self.out.at[2 * zs + self.core, self.a, self.b]
        return remote(
            piece, piece, self.passed.at[zs], self.line_got.at[zs], self.w, self.n + 2 * way
        )

    def first(self, zs, h, i):
        shard = 2 * zs + self.core
        piece = self.out.at[shard, self.a, self.b, h]
        if h == 0:
            to, mine = self.a * self.side + self.other_b(i), self.b
        else:
            to, mine = self.other_a(i) * self.side + self.b, self.a
        return remote(
            piece, piece, self.first_sent.at[zs, h, i], self.first_got.at[zs, h, mine], to, self.n
        )

    def second(self, zs, h, i):
        shard = 2 * zs + self.core
        if h == 0:
            piece = self.out.at[shard, self.a, :, 0]
            to, mine = self.other_a(i) * self.side + self.b, self.a
        else:
            piece = self.out.at[shard, :, self.b, 1]
            to, mine = self.a * self.side + self.other_b(i), self.b
        return remote(
            piece, piece, self.second_sent.at[zs, h, i], self.second_got.at[zs, h, mine], to, self.n
        )

    def first_from(self, shard, h, i):
        if h == 0:
            return self.out.at[shard, self.a, self.other_b(i), 0], self.other_b(i)
        return self.out.at[shard, self.other_a(i), self.b, 1], self.other_a(i)

    def second_from(self, shard, h, i):
        if h == 0:
            return self.out.at[shard, self.other_a(i), :, 0], self.other_a(i)
        return self.out.at[shard, :, self.other_b(i), 1], self.other_b(i)

    def hand0(self):
        return remote(
            self.mine, self.out.at[self.n], self.f0_sent, self.f0_got, self.w, self.sibling
        )

    def hand1(self, zs):
        piece = self.out.at[2 * zs + self.core, self.a, self.b]
        return remote(piece, piece, self.f1_sent.at[zs], self.f1_got.at[zs], self.w, self.sibling)

    def hand2(self, zs, h, i):
        piece, k = self.first_from(2 * zs + self.core, h, i)
        return remote(
            piece, piece, self.f2_sent.at[zs, h, k], self.f2_got.at[zs, h, k], self.w, self.sibling
        )

    def hand3(self, zs, h, i):
        piece, k = self.second_from(2 * zs + self.core, h, i)
        return remote(
            piece, piece, self.f3_sent.at[zs, h, k], self.f3_got.at[zs, h, k], self.w, self.sibling
        )

    def load(self):
        copies, row = [], 0
        for k, own in enumerate(self.owns):
            part = self.mine.at[:, :, :, pl.ds(row, own.shape[3])]
            copies.append(pltpu.make_async_copy(own, part, self.loaded.at[k]))
            row += own.shape[3]
        return copies

    def keep(self):
        return pltpu.make_async_copy(self.mine, self.out.at[self.n], self.copied)

    def sides(self, d, act):
        if not 1 <= d <= self.lines - 1:
            return
        z, last = self.z, self.lines - 1

        @pl.when(z >= d)
        def _():
            act(z - d, 1, z < last)

        @pl.when(z + d <= last)
        def _():
            act(z + d, -1, z > 0)

    def begin(self):
        for copy in self.load():
            copy.start()
        for copy in self.load():
            copy.wait()

        @pl.when(self.z < self.lines - 1)
        def _():
            self.own_on(1).start()

        @pl.when(self.z > 0)
        def _():
            self.own_on(-1).start()

        self.keep().start()
        self.hand0().start()

    def one(self, zs, way, more):
        arrived(self.out.at[2 * zs + self.core, self.a, self.b], self.line_got.at[zs])

        @pl.when(more)
        def _():
            self.pass_on(zs, way).start()

        for h, i in self.pairs:
            self.first(zs, h, i).start()
        self.hand1(zs).start()

    def two(self, zs, way, more):
        for h in (0, 1):
            for i in range(1, self.side):
                piece, k = self.first_from(2 * zs + self.core, h, i)
                arrived(piece, self.first_got.at[zs, h, k])
            for i in range(1, self.side):
                self.second(zs, h, i).start()
        for h, i in self.pairs:
            self.hand2(zs, h, i).start()

    def three(self, zs, way, more):
        for h, i in self.pairs:
            piece, k = self.second_from(2 * zs + self.core, h, i)
            arrived(piece, self.second_got.at[zs, h, k])
            self.hand3(zs, h, i).start()

    def round(self, d):
        self.sides(d, self.one)
        self.sides(d - 1, self.two)
        self.sides(d - 2, self.three)

    def finish_side(self, zs, way, more):
        theirs = 2 * zs + 1 - self.core

        @pl.when(more)
        def _():
            self.pass_on(zs, way).wait_send()

        self.hand1(zs).wait_send()
        arrived(self.out.at[theirs, self.a, self.b], self.f1_got.at[zs])
        for h, i in self.pairs:
            self.first(zs, h, i).wait_send()
            self.second(zs, h, i).wait_send()
            self.hand2(zs, h, i).wait_send()
            self.hand3(zs, h, i).wait_send()
            piece, k = self.first_from(theirs, h, i)
            arrived(piece, self.f2_got.at[zs, h, k])
            piece, k = self.second_from(theirs, h, i)
            arrived(piece, self.f3_got.at[zs, h, k])

    def finish(self):
        @pl.when(self.z < self.lines - 1)
        def _():
            self.own_on(1).wait_send()

        @pl.when(self.z > 0)
        def _():
            self.own_on(-1).wait_send()

        self.keep().wait()
        self.hand0().wait_send()
        arrived(self.out.at[self.sibling], self.f0_got)
        for d in range(1, self.lines):
            self.sides(d, self.finish_side)


def start_kernel(
    wide, narrow, length_ref, token_ref, gain_ref, bias_ref, weight_ref, own_ref,
    normed, packed, turned, extras, gathered, line_sent, line_got, sib_sent, sib_got, *gather_refs,
):
    gather = Gather(wide, narrow, [own_ref], gathered, *gather_refs)
    w, n, z, core = gather.w, gather.n, gather.z, gather.core
    lines, sibling = gather.lines, gather.sibling
    rows = token_ref.shape[0]

    greet_all(wide, narrow, w, n)

    def norm_rows(j, carry):
        part = pl.ds(pl.multiple_of(j * 64, 64), 64)
        values = token_ref[part, :].astype(f32)
        centred = values - jnp.mean(values, axis=-1, keepdims=True)
        variance = jnp.mean(centred * centred, axis=-1, keepdims=True)
        normed[n, part, :] = (
            centred * lax.rsqrt(variance + epsilon) * as_row(gain_ref) + as_row(bias_ref)
        ).astype(bf16)
        return carry

    step = rows // CHUNKS

    def part_of(shard, c):
        return normed.at[shard, pl.ds(c * step, step)]

    def pass_on(zs, c, way):
        block = part_of(2 * zs + core, c)
        k = (1 - way) // 2
        return remote(block, block, line_sent.at[zs, c, k], line_got.at[zs, c], w, n + 2 * way)

    def hand(zs, c):
        block = part_of(2 * zs + core, c)
        return remote(block, block, sib_sent.at[zs, c], sib_got.at[zs, c], w, sibling)

    def project(owner, c):
        columns = pl.ds(pl.multiple_of(owner * rows + c * step, step), step)
        product = contract(turned[...], normed[owner, pl.ds(c * step, step)], 1, 1).astype(bf16)
        for j in range(product.shape[0] // HEAD_DIM):
            part = product[j * HEAD_DIM : (j + 1) * HEAD_DIM]
            if j % 3 == 0:
                part = part * jnp.asarray(HEAD_DIM**-0.5, bf16)
            packed[j * HEAD_DIM : (j + 1) * HEAD_DIM, columns] = part

    norm_blocks = rows // 64 // CHUNKS
    for c in range(CHUNKS):
        lax.fori_loop(c * norm_blocks, (c + 1) * norm_blocks, norm_rows, 0)
        if c == 0:
            greeted(wide, narrow)
            gather.begin()

        @pl.when(z < lines - 1)
        def _():
            pass_on(z, c, 1).start()

        @pl.when(z > 0)
        def _():
            pass_on(z, c, -1).start()

        hand(z, c).start()
    turned[...] = weight_ref[...].T
    mask_rows(length_ref, extras)
    for c in range(CHUNKS):
        project(n, c)

    def receive(c, zs, way, more):
        arrived(part_of(2 * zs + core, c), line_got.at[zs, c])

        @pl.when(more)
        def _():
            pass_on(zs, c, way).start()

        hand(zs, c).start()

    def project_side(zs, way, more):
        for c in range(CHUNKS):
            project(2 * zs + core, c)

    def project_sibling(zs, way, more):
        for c in range(CHUNKS):
            arrived(part_of(2 * zs + 1 - core, c), sib_got.at[zs, c])
            project(2 * zs + 1 - core, c)

    project_sibling(z, 0, None)
    for d in range(1, lines):
        gather.round(d)
        if d == lines - 1:
            gather.round(lines)
            gather.round(lines + 1)
        for c in range(CHUNKS):
            gather.sides(d, functools.partial(receive, c))
        if d > 1:
            gather.sides(d - 1, project_sibling)
        gather.sides(d, project_side)
    gather.sides(lines - 1, project_sibling)
    gather.finish()

    def sent_side(zs, way, more):
        for c in range(CHUNKS):
            hand(zs, c).wait_send()

            @pl.when(more)
            def _():
                pass_on(zs, c, way).wait_send()

    for c in range(CHUNKS):

        @pl.when(z < lines - 1)
        def _():
            pass_on(z, c, 1).wait_send()

        @pl.when(z > 0)
        def _():
            pass_on(z, c, -1).wait_send()

        hand(z, c).wait_send()
    for d in range(1, lines):
        gather.sides(d, sent_side)


def start(wide, narrow, lengths, tokens, gain, bias, weight, own):
    rows, features = tokens.shape
    lines = narrow // 2
    dma = pltpu.SemaphoreType.DMA
    vmem = pl.BlockSpec(memory_space=pltpu.VMEM)
    anywhere = pl.BlockSpec(memory_space=pl.ANY)
    return pl.pallas_call(
        functools.partial(start_kernel, wide, narrow),
        in_specs=[pl.BlockSpec(memory_space=pltpu.SMEM), vmem, vmem, vmem, vmem, anywhere],
        out_specs=(vmem, vmem, vmem, vmem, anywhere),
        out_shape=(
            jax.ShapeDtypeStruct((narrow, rows, features), bf16),
            jax.ShapeDtypeStruct((weight.shape[1], narrow * rows), bf16),
            jax.ShapeDtypeStruct((weight.shape[1], features), bf16),
            jax.ShapeDtypeStruct((2, EXTRA, narrow * rows), bf16),
            jax.ShapeDtypeStruct((narrow, *own.shape), bf16),
        ),
        scratch_shapes=[
            dma((lines, CHUNKS, 2)), dma((lines, CHUNKS)), dma((lines, CHUNKS)), dma((lines, CHUNKS)),
            *Gather.scratch(wide, narrow, own.shape[3:]),
        ],
        compiler_params=pltpu.CompilerParams(
            vmem_limit_bytes=58 << 20, collective_id=1, has_side_effects=True
        ),
        name="start",
    )(lengths, tokens, gain, bias, weight, own)


def body(
    tokens, cotangent, item_lengths, attn_gain, attn_bias, qkv_weight, proj_weight,
    mlp_gain, mlp_bias, up_weight, down_weight,
):
    items = item_lengths.shape[1]
    heads = qkv_weight.shape[1] // (3 * HEAD_DIM)
    wide, narrow = lax.axis_size("wide"), lax.axis_size("narrow")
    side = math.isqrt(wide)
    rows = narrow * tokens.shape[0]

    def cut(shard):
        return shard.reshape(side, side, 2, shard.shape[0] // (2 * wide), shard.shape[1])

    def split_parts(total):
        return total.reshape(narrow, side, side, 2, -1, total.shape[1])

    first = down_weight.shape[0] // (2 * wide)
    normed_all, packed, qkv_turned, extras, up_all = start(
        wide, narrow, item_lengths, tokens, attn_gain, attn_bias, qkv_weight, cut(up_weight)
    )
    normed_all = normed_all.reshape(rows, -1)
    packed = packed.reshape(heads, 3, HEAD_DIM, rows)
    attended, log_total, attended_rows, rest_all = attend_forward(
        wide, narrow, packed, extras, cut(down_weight), cut(proj_weight)
    )
    attended_rows = attended_rows.reshape(-1, tokens.shape[0])
    proj_all = rest_all
    if (rest_all.shape[4] - first) % 16:
        proj_all = rest_all[:, :, :, :, first:].reshape(-1, tokens.shape[1])
    output, grad_middle, grad_attended, grad_proj, grad_parts, norm_parts = mlp(
        attended_rows, proj_all, tokens, cotangent, mlp_gain, mlp_bias, up_all, rest_all, first
    )
    grad_attended = grad_attended.reshape(narrow, heads, HEAD_DIM, -1)
    grad_proj_parts = split_parts(grad_proj)
    grad_tokens, grad_qkv, grad_shard, shares, _ = backward(
        wide, narrow, extras, packed, attended, log_total, grad_attended, grad_parts,
        grad_proj_parts, qkv_turned, normed_all, tokens, grad_middle, attn_gain, norm_parts, items,
    )
    grad_qkv, grad_proj, grad_up, grad_down = unpack(
        grad_shard, grad_qkv, proj_weight.shape, up_weight.shape, down_weight.shape
    )
    return (
        output, grad_tokens, shares[0], shares[1], grad_qkv, grad_proj,
        shares[2], shares[3], grad_up, grad_down,
    )


def solution(mesh):
    by_rows = P(("wide", "narrow"), None)
    return jax.shard_map(
        body,
        mesh=mesh,
        in_specs=(
            by_rows, by_rows, P("wide", None), P(), P(), P(None, "narrow"), P("narrow", None),
            P(), P(), P(None, "narrow"), P("narrow", None),
        ),
        out_specs=(
            by_rows, by_rows, P("narrow"), P("narrow"), P(None, "narrow"), P("narrow", None),
            P("narrow"), P("narrow"), P(None, "narrow"), P("narrow", None),
        ),
        check_vma=False,
    )
```

```python
import functools
import math

import jax
import jax.numpy as jnp
from jax import lax
from jax.experimental import pallas as pl
from jax.experimental.pallas import tpu as pltpu
from jax.sharding import PartitionSpec as P

HEAD_DIM = 64
EXTRA = 16
CHUNKS = 2
REDUCE_START, REDUCE_STEP, REDUCE_FIRST, REDUCE_SECOND, SPREAD_AT = 3, 11, 8, 12, 8
EARLY_RELAY = 17
EXCLUDED = -1e30
bf16 = jnp.bfloat16
f32 = jnp.float32
MESH = pl.DeviceIdType.MESH
epsilon = 1e-05


def mask_rows(length_ref, extras):
    items = length_ref.shape[1]
    rows = extras.shape[2]
    position = lax.broadcasted_iota(jnp.int32, (EXTRA, rows), 1)
    extra = lax.broadcasted_iota(jnp.int32, (EXTRA, rows), 0)
    segment, end = jnp.zeros((EXTRA, rows), jnp.int32), 0
    for i in range(items):
        end = end + length_ref[0, i]
        segment = segment + jnp.where(position >= end, 1, 0)
    own = jnp.where(segment == extra, 1.0, 0.0)
    mask = jnp.where(extra <= items, 1.0, 0.0)
    ones = jnp.where(extra <= items + 3, 1.0, 0.0) * (1.0 - mask)
    extras[0] = (own * mask).astype(bf16)
    extras[1] = ((1.0 - own) * mask * EXCLUDED + ones).astype(bf16)


def forward_kernel(
    wide, narrow, qx_ref, kx_ref, q_ref, k_ref, v_ref, own_ref, more_ref, o_ref, log_ref, rows_ref, gathered,
    keys, ready, copied, sent, got, *gather_refs,
):
    gather = Gather(wide, narrow, [own_ref, more_ref], gathered, *gather_refs)
    w, n, lines = gather.w, gather.n, gather.lines
    head, step = pl.program_id(0), pl.program_id(1)
    moment = head * narrow + step
    width = q_ref.shape[-1] // narrow
    last = heads_of(ready, narrow) * narrow - 1

    moves = []
    for d in range(1, lines):
        moves += [
            (3.5 * d, functools.partial(gather.sides, d, gather.one)),
            (3.5 * d + 2.5, functools.partial(gather.sides, d, gather.two)),
            (3.5 * d + 5.5, functools.partial(gather.sides, d, gather.three)),
        ]
    moves.append((900.0, gather.finish))
    moves.sort(key=lambda move: move[0])

    def perform(lower, upper):
        for time, move in moves:
            if lower <= time < upper:
                move()

    @pl.when(moment == 0)
    def _():
        greet_all(wide, narrow, w, n)

    @pl.when(step == 0)
    def _():
        keys[...] = jnp.concatenate([k_ref[0], kx_ref[...]], axis=0).T

    @pl.when(moment == 0)
    def _():
        greeted(wide, narrow)
        gather.begin()

    for tick in range(last + 1):

        @pl.when(moment == tick)
        def _():
            perform(tick, tick + 1)

    owner = lax.rem(n + 1 + step, narrow)
    columns = pl.ds(pl.multiple_of(owner * width, width), width)
    query = jnp.concatenate(
        [q_ref[0, :, columns], qx_ref[:, columns]], axis=0
    )
    maximum = jnp.full((1, width), -3e38, f32)
    total, gathered_values = 0.0, 0.0
    half = keys.shape[0] // 2
    for part in (pl.ds(0, half), pl.ds(half, half)):
        scores = jnp.dot(keys[part, :], query, preferred_element_type=f32)
        larger = jnp.maximum(maximum, jnp.max(scores, axis=0, keepdims=True))
        shrink = jnp.exp(maximum - larger)
        raised = jnp.exp(scores - larger)
        total = shrink * total + jnp.sum(raised, axis=0, keepdims=True)
        gathered_values = shrink * gathered_values + jnp.dot(
            v_ref[0, :, part], raised.astype(bf16), preferred_element_type=f32
        )
        maximum = larger
    result = (gathered_values / total).astype(bf16)
    o_ref[0, :, columns] = result
    log_ref[0, :, columns] = maximum + jnp.log(total)
    ready[moment] = result

    def deliver(k, owner, h):
        return remote(ready.at[k], rows_ref.at[n, h], sent.at[k], got.at[n, h], w, owner)

    def deliver_here(k, h):
        return pltpu.make_async_copy(ready.at[k], rows_ref.at[n, h], copied.at[h])

    @pl.when(step < narrow - 1)
    def _():
        deliver(moment, owner, head).start()

    @pl.when(step == narrow - 1)
    def _():
        deliver_here(moment, head).start()

    @pl.when(moment == last)
    def _():
        perform(last + 1, 1000)
        for h in range((last + 1) // narrow):
            deliver_here(h * narrow + narrow - 1, h).wait()
            for t in range(narrow - 1):
                deliver(h * narrow + t, lax.rem(n + 1 + t, narrow), h).wait_send()
                source = lax.rem(n + narrow - 1 - t, narrow)
                arrived(rows_ref.at[source, h], got.at[source, h])


def heads_of(ready, narrow):
    return ready.shape[0] // narrow


def attend_forward(wide, narrow, packed, extras, own, more):
    heads, _, _, rows = packed.shape
    width = rows // narrow
    gathered = (narrow, *own.shape[:3], own.shape[3] + more.shape[3], own.shape[4])
    dma = pltpu.SemaphoreType.DMA

    def whole(j):
        return pl.BlockSpec((1, None, HEAD_DIM, rows), lambda h, i: (h, j, 0, 0))

    def extra(j):
        return pl.BlockSpec((None, EXTRA, rows), lambda h, i: (j, 0, 0))

    anywhere = pl.BlockSpec(memory_space=pl.ANY)
    return pl.pallas_call(
        functools.partial(forward_kernel, wide, narrow),
        grid=(heads, narrow),
        in_specs=[extra(0), extra(1), whole(0), whole(1), whole(2), anywhere, anywhere],
        out_specs=(
            pl.BlockSpec((1, HEAD_DIM, rows), lambda h, i: (h, 0, 0)),
            pl.BlockSpec((1, 1, rows), lambda h, i: (h, 0, 0)),
            anywhere,
            anywhere,
        ),
        out_shape=(
            jax.ShapeDtypeStruct((heads, HEAD_DIM, rows), bf16),
            jax.ShapeDtypeStruct((heads, 1, rows), f32),
            jax.ShapeDtypeStruct((narrow, heads, HEAD_DIM, width), bf16),
            jax.ShapeDtypeStruct(gathered, bf16),
        ),
        scratch_shapes=[
            pltpu.VMEM((rows, HEAD_DIM + EXTRA), bf16),
            pltpu.VMEM((heads * narrow, HEAD_DIM, width), bf16),
            dma((heads,)),
            dma((heads * narrow,)),
            dma((narrow, heads)),
            *Gather.scratch(wide, narrow, gathered[4:]),
        ],
        compiler_params=pltpu.CompilerParams(
            vmem_limit_bytes=58 << 20, collective_id=4, has_side_effects=True
        ),
        name="attend_forward",
    )(extras, extras, packed, packed, packed, own, more)


def remote(src, dst, sent, received, wide_to, narrow_to):
    return pltpu.make_async_remote_copy(
        src_ref=src,
        dst_ref=dst,
        send_sem=sent,
        recv_sem=received,
        device_id=(wide_to, narrow_to),
        device_id_type=MESH,
    )


def arrived(ref, semaphore):
    pltpu.make_async_copy(ref, ref, semaphore).wait()


def greet_all(wide, narrow, w, n):
    barrier = pltpu.get_barrier_semaphore()

    def column(t, carry):
        pl.semaphore_signal(
            barrier, inc=1, device_id=(w, lax.rem(n + t, narrow)), device_id_type=MESH
        )
        return carry

    def plane(t, carry):
        pl.semaphore_signal(
            barrier, inc=1, device_id=(lax.rem(w + t, wide), n), device_id_type=MESH
        )
        return carry

    lax.fori_loop(1, narrow, column, 0)
    lax.fori_loop(1, wide, plane, 0)


def greeted(wide, narrow):
    pl.semaphore_wait(pltpu.get_barrier_semaphore(), narrow + wide - 2)


def accumulate(into, *others):
    rows = into.shape[0]
    few = max([d for d in (16, 32, 48, 64) if rows % d == 0], default=rows)

    def piece(j, carry):
        part = pl.ds(j * few if rows == few else pl.multiple_of(j * few, few), few)
        total = into[part, :].astype(f32)
        for other in others:
            total = total + other[part, :].astype(f32)
        into[part, :] = total.astype(bf16)
        return carry

    if rows == few:
        piece(0, 0)
    else:
        lax.fori_loop(0, rows // few, piece, 0)


def reduce_steps(
    wide, narrow, parts, proj_parts, landed, final, held, staged, from_first, from_second, from_line,
    mine, loaded, sib_sent, sib_got, first_sent, first_got, second_sent, second_got, line_sent, line_got,
):
    w, n = lax.axis_index("wide"), lax.axis_index("narrow")
    side, lines = math.isqrt(wide), narrow // 2
    a, b, z, core = w // side, lax.rem(w, side), n // 2, lax.rem(n, 2)
    sibling = n + 1 - 2 * core
    slots = held.shape[0]
    most, least = parts.shape[4], proj_parts.shape[4]
    sources = [(parts, pl.ds(0, most)), (proj_parts, pl.ds(most, least))]
    order = [lax.rem(z + 1 + j, lines) for j in range(lines)]
    halves = [(h, i) for i in range(1, side) for h in (0, 1)]

    def other_a(i):
        return lax.rem(a + i, side)

    def other_b(i):
        return lax.rem(b + i, side)

    def to_sibling(j):
        shard = 2 * order[j] + 1 - core
        return [
            remote(
                src.at[shard], landed.at[j, :, :, :, rows],
                sib_sent.at[k, j], sib_got.at[k, j], w, sibling,
            )
            for k, (src, rows) in enumerate(sources)
        ]

    def load(j):
        shard, slot = 2 * order[j] + core, j % slots
        return [
            pltpu.make_async_copy(src.at[shard], held.at[slot, :, :, :, rows], loaded.at[k])
            for k, (src, rows) in enumerate(sources)
        ]

    def stage(j):
        return pltpu.make_async_copy(landed.at[j], staged, loaded.at[2])

    def first(j, h, i):
        slot, k = j % slots, i - 1
        if h == 0:
            src, to = held.at[slot, other_a(i), :, 0], other_a(i) * side + b
        else:
            src, to = held.at[slot, :, other_b(i), 1], a * side + other_b(i)
        return remote(
            src, from_first.at[j, h, k], first_sent.at[j, h, k], first_got.at[j, h, k], to, n
        )

    def second(j, h, i):
        slot, k = j % slots, i - 1
        if h == 0:
            src, to = held.at[slot, a, other_b(i), 0], a * side + other_b(i)
        else:
            src, to = held.at[slot, other_a(i), b, 1], other_a(i) * side + b
        return remote(
            src, from_second.at[j, h, k], second_sent.at[j, h, k], second_got.at[j, h, k], to, n
        )

    def along(j):
        zs = order[j]
        place = jnp.where(z < zs, z, z - 1)
        return remote(
            held.at[j % slots, a, b], from_line.at[place], line_sent.at[j], line_got.at[place],
            w, 2 * zs + core,
        )

    def begin():
        for j in range(lines):
            for copy in to_sibling(j):
                copy.start()

    def sent(j):
        for h, i in halves:
            first(j, h, i).wait_send()
            second(j, h, i).wait_send()

        if j < lines - 1:
            along(j).wait_send()

    def combine(j):
        slot = j % slots
        if j >= slots:
            sent(j - slots)
        for copy in load(j):
            copy.start()
        for k, (_, rows) in enumerate(sources):
            arrived(landed.at[j, :, :, :, rows], sib_got.at[k, j])
        stage(j).start()
        for copy in load(j):
            copy.wait()
        stage(j).wait()

        def piece(t, carry):
            p, q = t // side, lax.rem(t, side)
            for h in (0, 1):
                accumulate(held.at[slot, p, q, h], staged.at[p, q, h])
            return carry

        lax.fori_loop(0, wide, piece, 0)
        for h, i in halves:
            first(j, h, i).start()

    def narrow_down(j):
        slot = j % slots
        for h in (0, 1):
            for i in range(1, side):
                arrived(from_first.at[j, h, i - 1], first_got.at[j, h, i - 1])

            def piece(t, carry, h=h):
                into = held.at[slot, a, t, 0] if h == 0 else held.at[slot, t, b, 1]
                accumulate(into, *[from_first.at[j, h, i, t] for i in range(side - 1)])
                return carry

            lax.fori_loop(0, side, piece, 0)
        for h, i in halves:
            second(j, h, i).start()

    def send_home(j):
        slot = j % slots
        for h, i in halves:
            arrived(from_second.at[j, h, i - 1], second_got.at[j, h, i - 1])
        for h in (0, 1):
            accumulate(
                held.at[slot, a, b, h], *[from_second.at[j, h, i] for i in range(side - 1)]
            )

        if j < lines - 1:
            along(j).start()
        else:
            mine[...] = held[slot, a, b]

    def finish():
        for place in range(lines - 1):
            arrived(from_line.at[place], line_got.at[place])
        for h in (0, 1):
            total = mine[h].astype(f32)
            for place in range(lines - 1):
                total = total + from_line[place, h].astype(f32)
            final[h] = total.astype(bf16)

    def close():
        for j in range(lines):
            for copy in to_sibling(j):
                copy.wait_send()
        for j in range(max(0, lines - slots), lines):
            sent(j)

    steps = [(0.0, begin)]
    for j in range(lines):
        at = REDUCE_START + REDUCE_STEP * j
        steps += [
            (at, functools.partial(combine, j)),
            (at + REDUCE_FIRST, functools.partial(narrow_down, j)),
            (at + REDUCE_SECOND, functools.partial(send_home, j)),
        ]
    return sorted(steps, key=lambda step: step[0]), finish, close


def reduce_scratch(wide, narrow, rows, features, slots=3):
    side, lines = math.isqrt(wide), narrow // 2
    dma = pltpu.SemaphoreType.DMA
    plane = (lines, 2, side - 1)
    return [
        pltpu.VMEM((slots, side, side, 2, rows, features), bf16),
        pltpu.VMEM((side, side, 2, rows, features), bf16),
        pltpu.VMEM((lines, 2, side - 1, side, rows, features), bf16),
        pltpu.VMEM((lines, 2, side - 1, rows, features), bf16),
        pltpu.VMEM((lines - 1, 2, rows, features), bf16),
        pltpu.VMEM((2, rows, features), bf16),
        *[dma(shape) for shape in [(3,), (2, lines), (2, lines), plane, plane, plane, plane]],
        dma((lines,)),
        dma((lines - 1,)),
    ]


def as_row(ref):
    return ref[...].astype(f32).reshape(1, -1)


def contract(left, right, left_axis, right_axis):
    return lax.dot_general(
        left, right, (((left_axis,), (right_axis,)), ((), ())), preferred_element_type=f32
    )


def gelu_pair(values):
    half = 0.5 + 0.5 * lax.erf(values * 0.7071067811865476)
    slope = half + values * (jnp.exp(values * values * -0.5) * 0.3989422804014327)
    return values * half, slope


def mlp_kernel(
    att_ref, rest_ref, token_ref, cot_ref, gain_ref, bias_ref, up_ref, down_ref,
    out_ref, middle_out, att_out, proj_out, parts_ref, norm_ref,
    middle, expand, out_total, expand_total, proj_ref, proj_got,
):
    step = pl.program_id(0)
    rows, features = token_ref.shape
    few = 64

    def by_rows(change):
        def body(j, carry):
            return change(pl.ds(pl.multiple_of(j * few, few), few), carry)

        return body

    if rest_ref.ndim == 2:
        fetch = pltpu.make_async_copy(rest_ref, proj_ref, proj_got)
    else:
        few_rows = rest_ref.shape[4] - down_ref.shape[4]
        fetch = pltpu.make_async_copy(
            rest_ref.at[:, :, :, :, pl.ds(down_ref.shape[4], few_rows)],
            proj_ref.reshape(*rest_ref.shape[:4], few_rows, features),
            proj_got,
        )

    @pl.when(step == 0)
    def _():
        fetch.start()
        fetch.wait()
        middle[...] = token_ref[...].astype(f32) + contract(att_ref[...], proj_ref[...], 0, 0)
        out_total[...] = jnp.zeros_like(out_total)
        expand_total[...] = jnp.zeros_like(expand_total)

        def norm(part, carry):
            values = middle[part, :]
            centred = values - jnp.mean(values, axis=-1, keepdims=True)
            variance = jnp.mean(centred * centred, axis=-1, keepdims=True)
            expand[part, :] = (
                centred * lax.rsqrt(variance + epsilon) * as_row(gain_ref) + as_row(bias_ref)
            ).astype(bf16)
            return carry

        lax.fori_loop(0, rows // few, by_rows(norm), 0)

    def flat(ref):
        if ref.shape[4] % 16:
            return ref[0].astype(f32).reshape(-1, ref.shape[5]).astype(bf16)
        return ref[0].reshape(-1, ref.shape[5])

    up, down = flat(up_ref), flat(down_ref)
    units = down_ref.shape[4]
    pieces = up_ref.shape[1:4]
    columns = up_ref.shape[5]
    hidden_parts, grad_parts = [], []
    for part in (pl.ds(0, rows // 2), pl.ds(rows // 2, rows // 2)):
        hidden, slope = gelu_pair(
            jnp.dot(expand[part, :], up, preferred_element_type=f32)
        )
        grad_pre = (contract(cot_ref[part, :], down, 1, 1) * slope).astype(bf16)
        hidden = hidden.astype(bf16)
        out_total[part, :] += jnp.dot(hidden, down, preferred_element_type=f32)
        expand_total[part, :] += contract(grad_pre, up, 1, 1)
        hidden_parts.append(hidden)
        grad_parts.append(grad_pre)
    grad_up = contract(expand[...], jnp.concatenate(grad_parts, axis=0), 0, 0)
    grad_down = contract(jnp.concatenate(hidden_parts, axis=0), cot_ref[...], 0, 0)
    groups = features // columns
    grad_up = grad_up.reshape(*pieces, groups, units, columns)
    for g in range(groups):
        parts_ref[0, :, :, :, 0:units, g * columns : (g + 1) * columns] = grad_up[
            :, :, :, g
        ].astype(bf16)
    parts_ref[0, :, :, :, units : 2 * units, :] = grad_down.reshape(
        *pieces, units, features
    ).astype(bf16)

    @pl.when(step == pl.num_programs(0) - 1)
    def _():
        def finish_rows(part, carry):
            gain_sum, bias_sum = carry
            values = middle[part, :]
            out_ref[part, :] = (values + out_total[part, :]).astype(bf16)
            centred = values - jnp.mean(values, axis=-1, keepdims=True)
            inverse = lax.rsqrt(jnp.mean(centred * centred, axis=-1, keepdims=True) + epsilon)
            scaled = centred * inverse
            grad = expand_total[part, :]
            term = grad * as_row(gain_ref)
            back = inverse * (
                term
                - jnp.mean(term, axis=-1, keepdims=True)
                - scaled * jnp.mean(term * scaled, axis=-1, keepdims=True)
            )
            total = cot_ref[part, :].astype(f32) + back
            middle_out[part, :] = total
            expand[part, :] = total.astype(bf16)
            gain_sum = gain_sum + jnp.sum(grad * scaled, axis=0, keepdims=True)
            bias_sum = bias_sum + jnp.sum(grad, axis=0, keepdims=True)
            return gain_sum, bias_sum

        start = (jnp.zeros((1, features), f32), jnp.zeros((1, features), f32))
        gain_sum, bias_sum = lax.fori_loop(0, rows // few, by_rows(finish_rows), start)
        row = lax.broadcasted_iota(jnp.int32, (8, features), 0)
        norm_ref[...] = jnp.where(row == 2, gain_sum, jnp.where(row == 3, bias_sum, 0.0))
        branch = expand[...]
        att_out[...] = contract(proj_ref[...], branch, 1, 1).astype(bf16)
        proj_out[...] = jnp.dot(att_ref[...], branch, preferred_element_type=f32).astype(bf16)


def mlp(attended, rest, tokens, cotangent, gain, bias, up_all, down_all, units):
    rows, features = tokens.shape
    narrow, side = up_all.shape[:2]
    proj_shape = (attended.shape[0], features)

    def whole(*shape):
        return pl.BlockSpec(shape, lambda i: (0,) * len(shape))

    def weights(*piece):
        return pl.BlockSpec((1, side, side, 2, *piece), lambda i: (i, 0, 0, 0, 0, 0))

    return pl.pallas_call(
        mlp_kernel,
        grid=(narrow,),
        in_specs=[
            whole(*attended.shape),
            pl.BlockSpec(memory_space=pl.ANY),
            whole(rows, features),
            whole(rows, features),
            whole(*gain.shape),
            whole(*bias.shape),
            weights(*up_all.shape[4:]),
            weights(units, features),
        ],
        out_specs=(
            whole(rows, features),
            whole(rows, features),
            whole(*attended.shape),
            whole(*proj_shape),
            pl.BlockSpec(
                (1, side, side, 2, 2 * units, features), lambda i: (i, 0, 0, 0, 0, 0)
            ),
            whole(8, features),
        ),
        out_shape=(
            jax.ShapeDtypeStruct((rows, features), bf16),
            jax.ShapeDtypeStruct((rows, features), f32),
            jax.ShapeDtypeStruct(attended.shape, bf16),
            jax.ShapeDtypeStruct(proj_shape, bf16),
            jax.ShapeDtypeStruct((narrow, side, side, 2, 2 * units, features), bf16),
            jax.ShapeDtypeStruct((8, features), f32),
        ),
        scratch_shapes=[
            pltpu.VMEM((rows, features), f32),
            pltpu.VMEM((rows, features), bf16),
            pltpu.VMEM((rows, features), f32),
            pltpu.VMEM((rows, features), f32),
            pltpu.VMEM(proj_shape, bf16),
            pltpu.SemaphoreType.DMA(()),
        ],
        compiler_params=pltpu.CompilerParams(vmem_limit_bytes=58 << 20),
        name="mlp",
    )(attended, rest, tokens, cotangent, gain, bias, up_all, down_all)


def backward_kernel(
    wide, narrow, items, chunks,
    extra_ref, packed_ref, att_ref, log_ref, own_ref, parts_ref, proj_parts_ref, weight_ref,
    normed_ref, token_ref, middle_ref, gain_ref, norm_ref,
    tokens_out, qkv_out, shard_out, norms_out, landed,
    keys, values, queries, grads, grad_q, grad_k, grad_v, block_grad,
    normed, total_qkv, for_sibling, from_sibling, held, from_line,
    first_qkv, second_qkv, norms, norm_column, norm_half, norm_plane, piece,
    middle,
    packed_got, own_got, do_sent, do_got, normed_got, middle_got, copied, sib_sent, sib_got,
    line_sent, line_got, piece_sent, piece_got, first_sent, first_got, second_sent, second_got,
    column_sent, column_got, plane_sent, plane_got, *reduce_refs,
):
    w, n = lax.axis_index("wide"), lax.axis_index("narrow")
    side, lines = math.isqrt(wide), narrow // 2
    a, b, z, core = w // side, lax.rem(w, side), n // 2, lax.rem(n, 2)
    sibling = n + 1 - 2 * core
    heads = keys.shape[0]
    rows, features = token_ref.shape
    step = rows // chunks
    lower = z < lines // 2
    moves, reduce_finish, reduce_close = reduce_steps(
        wide, narrow, parts_ref, proj_parts_ref, landed, piece, *reduce_refs
    )

    def line_at(k):
        climbing = jnp.where(
            k < lines - 1 - z, lines - 1 - k, jnp.where(k < lines - 1, k - (lines - 1 - z), z)
        )
        falling = jnp.where(k < z, k, jnp.where(k < lines - 1, lines - 1 - (k - z), z))
        return jnp.where(lower, climbing, falling)

    def block_at(j):
        odd = lax.rem(j, 2)
        return 2 * line_at(j // 2) + jnp.where(odd == 1, core, 1 - core)

    def columns(owner):
        return pl.ds(pl.multiple_of(owner * rows, rows), rows)

    def packed_copy(h, j):
        into = (queries, keys, values)[j]
        return pltpu.make_async_copy(
            packed_ref.at[h, j], into.at[h, pl.ds(0, HEAD_DIM)], packed_got.at[h, j]
        )

    def keep(h):
        return pltpu.make_async_copy(
            own_ref.at[n, h], grads.at[h, pl.ds(0, HEAD_DIM), columns(n)], own_got.at[h]
        )

    def deliver(t, h):
        to = lax.rem(n + t, narrow)
        return remote(
            own_ref.at[to, h], grads.at[h, pl.ds(0, HEAD_DIM), columns(n)],
            do_sent.at[t, h], do_got.at[n, h], w, to,
        )

    def fetch(j):
        owner = block_at(j)
        return pltpu.make_async_copy(
            normed_ref.at[pl.ds(pl.multiple_of(owner * rows, rows), rows)],
            normed.at[lax.rem(j, 2)], normed_got.at[lax.rem(j, 2)],
        )

    for h in range(heads):
        for j in range(3):
            packed_copy(h, j).start()
        keep(h).start()
    fetch(0).start()
    greet_all(wide, narrow, w, n)
    grad_q[...] = jnp.zeros_like(grad_q)
    grad_k[...] = jnp.zeros_like(grad_k)
    grad_v[...] = jnp.zeros_like(grad_v)
    total_qkv[...] = jnp.zeros_like(total_qkv)
    greeted(wide, narrow)
    for t in range(1, narrow):
        for h in range(heads):
            deliver(t, h).start()
    for h in range(heads):
        keys[h, HEAD_DIM:, :] = extra_ref[1]
        values[h, HEAD_DIM:, :] = extra_ref[1]
    for h in range(heads):
        for j in range(3):
            packed_copy(h, j).wait()
        keep(h).wait()

    row = lax.broadcasted_iota(jnp.int32, (EXTRA, rows), 0) - items

    def pieces(term, base):
        high = term.astype(bf16).astype(f32)
        mid = (term - high).astype(bf16).astype(f32)
        small = term - high - mid
        return jnp.where(
            row == 1, high, jnp.where(row == 2, mid, jnp.where(row == 3, small, base))
        ).astype(bf16)

    def prepare(j):
        owner = block_at(j)
        where = columns(owner)

        @pl.when(owner != n)
        def _():
            for h in range(heads):
                arrived(grads.at[h, pl.ds(0, HEAD_DIM), where], do_got.at[owner, h])

        for h in range(heads):
            grad = grads[h, 0:HEAD_DIM, where].astype(f32)
            inner = jnp.sum(grad * att_ref[h, :, where].astype(f32), axis=0, keepdims=True)
            grads[h, HEAD_DIM:, where] = pieces(-inner, jnp.zeros((EXTRA, rows), f32))
            queries[h, HEAD_DIM:, where] = pieces(
                -log_ref[h, :, where], extra_ref[0, :, where].astype(f32)
            )

    def to_sibling(zs, slot):
        return remote(
            for_sibling.at[slot], from_sibling.at[zs], sib_sent.at[slot], sib_got.at[zs], w, sibling
        )

    def pass_on(zs, c, up):
        part = pl.ds(c * step, step)
        place = zs if up else jnp.where(z - 1 == zs, lines, zs)
        return remote(
            held.at[zs, part], from_line.at[place, part], line_sent.at[zs, c],
            line_got.at[place, c], w, n + 2 if up else n - 2,
        )

    def relay(zs, c, up):
        part = pl.ds(c * step, step)
        arrived(from_line.at[zs, part], line_got.at[zs, c])
        accumulate(held.at[zs, part], from_line.at[zs, part])
        pass_on(zs, c, up).start()

    def early_relay():
        @pl.when(jnp.logical_and(lower, z >= 1))
        def _():
            for c in range(chunks):
                relay(lines - 1, c, True)

        @pl.when(jnp.logical_and(z >= lines // 2, z <= lines - 2))
        def _():
            for c in range(chunks):
                relay(0, c, False)

    def emit(j):
        j = jnp.asarray(j, jnp.int32)
        owner = block_at(j)
        where = columns(owner)
        for h in range(heads):
            for k, total in enumerate((grad_q, grad_k, grad_v)):
                at = (h * 3 + k) * HEAD_DIM
                value = total[h, :, where]
                block_grad[at : at + HEAD_DIM, :] = (
                    value * HEAD_DIM**-0.5 if k == 0 else value
                ).astype(bf16)
        zs, slot = line_at(j // 2), lax.rem(j // 2, 2)
        product = contract(block_grad[...], weight_ref[...], 0, 0).astype(bf16)

        @pl.when(lax.rem(j, 2) == 0)
        def _():
            @pl.when(j >= 4)
            def _():
                to_sibling(zs, slot).wait_send()

            for_sibling[slot] = product
            to_sibling(zs, slot).start()

        @pl.when(lax.rem(j, 2) == 1)
        def _():
            held[zs] = product

        fetch(j).wait()

        @pl.when(j < narrow - 1)
        def _():
            fetch(j + 1).start()

        total_qkv[...] += jnp.dot(
            block_grad[...], normed[lax.rem(j, 2)], preferred_element_type=f32
        )

        @pl.when(lax.rem(j, 2) == 1)
        def _():
            arrived(from_sibling.at[zs], sib_got.at[zs])
            accumulate(held.at[zs], from_sibling.at[zs])

            @pl.when(jnp.logical_and(z == 0, zs != z))
            def _():
                for c in range(chunks):
                    pass_on(zs, c, True).start()

            @pl.when(jnp.logical_and(z == lines - 1, zs != z))
            def _():
                for c in range(chunks):
                    pass_on(zs, c, False).start()

    def spread(t):
        return remote(
            piece, shard_out.at[w], piece_sent.at[t], piece_got.at[t], lax.rem(w + t, wide), n
        )

    stay = pltpu.make_async_copy(piece, shard_out.at[w], copied)

    def spread_all():
        reduce_finish()
        stay.start()
        for t in range(1, wide):
            spread(t).start()

    prepare(narrow - 1)
    pairs = narrow * narrow
    moves = moves + [(6 * narrow - 8 + EARLY_RELAY, early_relay), (pairs - SPREAD_AT, spread_all)]
    moves.sort(key=lambda move: move[0])
    ticks = {}
    for time, move in moves:
        ticks.setdefault(min(int(time), pairs - 1), []).append(move)

    def pair(p, carry):
        for tick, group in ticks.items():

            @pl.when(p == tick)
            def _():
                for move in group:
                    move()

        late = p - 2 * narrow
        stage = sum(
            (late >= j * (2 * narrow - 2 - j)).astype(jnp.int32) for j in range(1, narrow - 2)
        )
        r = late - stage * (2 * narrow - 2 - stage)
        across = r < narrow - stage
        near = late < 0
        qi = jnp.where(
            near,
            jnp.where(p < narrow, narrow - 1, narrow - 2),
            jnp.where(across, stage, 2 * stage + 1 + r - narrow),
        )
        ki = jnp.where(near, lax.rem(p, narrow), jnp.where(across, stage + r, stage))

        @pl.when((p == narrow) | (late == 0) | ((stage == 0) & (r >= narrow)))
        def _():
            prepare(qi)

        at_q, at_k = columns(block_at(qi)), columns(block_at(ki))
        for h in range(heads):
            probs = jnp.exp(contract(queries[h, :, at_q], keys[h, :, at_k], 0, 0))
            scores = (probs * contract(grads[h, :, at_q], values[h, :, at_k], 0, 0)).astype(bf16)
            grad_v[h, :, at_k] += jnp.dot(
                grads[h, 0:HEAD_DIM, at_q], probs.astype(bf16), preferred_element_type=f32
            )
            grad_k[h, :, at_k] += jnp.dot(
                queries[h, 0:HEAD_DIM, at_q], scores, preferred_element_type=f32
            )
            grad_q[h, :, at_q] += contract(keys[h, 0:HEAD_DIM, at_k], scores, 1, 1)

        @pl.when(r == 2 * (narrow - stage) - 4)
        def _():
            emit(stage)

        return carry

    lax.fori_loop(0, pairs, pair, 0)
    emit(narrow - 2)
    emit(narrow - 1)

    half = total_qkv.shape[0] // 2
    own_qkv, half_qkv = for_sibling.at[:, 0:half], normed.at[:, 0:half]
    for slot in range(min(2, lines)):
        to_sibling(0, slot).wait_send()
    for h in (0, 1):
        own_qkv[h] = total_qkv[h * half : (h + 1) * half].astype(bf16)
    halves = [(h, i) for i in range(1, side) for h in (0, 1)]

    def plane_at(h, i):
        if h == 0:
            return lax.rem(a + i, side) * side + b
        return a * side + lax.rem(b + i, side)

    def first(h, i):
        return remote(
            own_qkv.at[h], first_qkv.at[h, i - 1], first_sent.at[h, i - 1], first_got.at[h, i - 1],
            plane_at(h, i), n,
        )

    def second(h, i):
        return remote(
            half_qkv.at[h], second_qkv.at[h, i - 1], second_sent.at[h, i - 1],
            second_got.at[h, i - 1], plane_at(1 - h, i), n,
        )

    def qkv_second():
        for h, i in halves:
            arrived(first_qkv.at[h, i - 1], first_got.at[h, i - 1])
        for h in (0, 1):
            total = own_qkv[h].astype(f32)
            for i in range(1, side):
                total = total + first_qkv[h, i - 1].astype(f32)
            half_qkv[h] = total.astype(bf16)
        for h, i in halves:
            second(h, i).start()

    def qkv_last():
        for h, i in halves:
            arrived(second_qkv.at[h, i - 1], second_got.at[h, i - 1])
        for h in (0, 1):
            total = half_qkv[h].astype(f32)
            for i in range(1, side):
                total = total + second_qkv[h, i - 1].astype(f32)
            qkv_out[h * half : (h + 1) * half] = total.astype(bf16)

    for h, i in halves:
        first(h, i).start()

    def fetch_middle(c):
        return pltpu.make_async_copy(middle_ref.at[pl.ds(c * step, step)], middle, middle_got)

    fetch_middle(0).start()
    for t in range(1, lines):
        below, above = lines - 1 - (t - z), t - (lines - 1 - z)
        for c in range(chunks):
            if t < lines - 1:

                @pl.when((z >= 1) & (t >= z) & ~(lower & (t == z)))
                def _():
                    relay(below, c, True)

                @pl.when((z <= lines - 2) & (above >= 0) & ~((z >= lines // 2) & (above == 0)))
                def _():
                    relay(above, c, False)

    qkv_second()

    def zero_edges(at_edge, place):
        @pl.when(at_edge)
        def _():
            from_line[place] = jnp.zeros((rows, features), bf16)

    zero_edges(z == 0, z)
    zero_edges(z == lines - 1, lines)
    gain_sum = bias_sum = jnp.zeros((1, features), f32)
    for c in range(chunks):
        part = pl.ds(c * step, step)

        @pl.when(z >= 1)
        def _():
            arrived(from_line.at[z, part], line_got.at[z, c])

        @pl.when(z <= lines - 2)
        def _():
            arrived(from_line.at[lines, part], line_got.at[lines, c])

        fetch_middle(c).wait()

        def norm_rows(j, carry):
            gain_sum, bias_sum = carry
            few = pl.ds(pl.multiple_of(c * step + j * 32, 32), 32)
            near = pl.ds(pl.multiple_of(j * 32, 32), 32)
            grad = (
                held[z, few].astype(f32)
                + from_line[z, few].astype(f32)
                + from_line[lines, few].astype(f32)
            )
            values = token_ref[few, :].astype(f32)
            centred = values - jnp.mean(values, axis=-1, keepdims=True)
            inverse = lax.rsqrt(jnp.mean(centred * centred, axis=-1, keepdims=True) + epsilon)
            scaled = centred * inverse
            term = grad * as_row(gain_ref)
            back = inverse * (
                term
                - jnp.mean(term, axis=-1, keepdims=True)
                - scaled * jnp.mean(term * scaled, axis=-1, keepdims=True)
            )
            tokens_out[few, :] = (middle[near, :] + back).astype(bf16)
            gain_sum = gain_sum + jnp.sum(grad * scaled, axis=0, keepdims=True)
            bias_sum = bias_sum + jnp.sum(grad, axis=0, keepdims=True)
            return gain_sum, bias_sum

        gain_sum, bias_sum = lax.fori_loop(0, step // 32, norm_rows, (gain_sum, bias_sum))
        if c + 1 < chunks:
            fetch_middle(c + 1).start()

    row = lax.broadcasted_iota(jnp.int32, (8, features), 0)
    parts = jnp.where(row == 0, gain_sum, jnp.where(row == 1, bias_sum, norm_ref[...]))
    share = features // narrow
    for owner in range(narrow):
        norms[owner] = parts[:, owner * share : (owner + 1) * share]

    def down_column(t):
        to = lax.rem(n + t, narrow)
        return remote(
            norms.at[to], norm_column.at[t - 1], column_sent.at[t - 1], column_got.at[t - 1], w, to
        )

    def over_plane(t):
        return remote(
            norm_half, norm_plane.at[t - 1], plane_sent.at[t - 1], plane_got.at[t - 1],
            lax.rem(w + t, wide), n,
        )

    for t in range(1, narrow):
        down_column(t).start()
    total = norms[n]
    for t in range(1, narrow):
        arrived(norm_column.at[t - 1], column_got.at[t - 1])
        total = total + norm_column[t - 1]
    norm_half[...] = total
    for t in range(1, wide):
        over_plane(t).start()
    for t in range(1, wide):
        arrived(norm_plane.at[t - 1], plane_got.at[t - 1])
        total = total + norm_plane[t - 1]
    norms_out[...] = total

    qkv_last()
    stay.wait()
    reduce_close()
    for t in range(1, wide):
        spread(t).wait_send()
        arrived(shard_out.at[lax.rem(w + wide - t, wide)], piece_got.at[t])
        over_plane(t).wait_send()
    for t in range(1, narrow):
        down_column(t).wait_send()
        for h in range(heads):
            deliver(t, h).wait_send()
    for h, i in halves:
        first(h, i).wait_send()
        second(h, i).wait_send()
    for zs in range(lines):
        for c in range(chunks):

            @pl.when(zs > z)
            def _():
                pass_on(zs, c, True).wait_send()

            @pl.when(zs < z)
            def _():
                pass_on(zs, c, False).wait_send()


def backward(
    wide, narrow, extras, packed, attended, log_total, grad, parts, proj_parts, weight, normed,
    tokens, middle, gain, norm_parts, items, chunks=4,
):
    side, lines = math.isqrt(wide), narrow // 2
    heads, _, _, total_rows = packed.shape
    rows, features = tokens.shape
    held_columns = weight.shape[0]
    piece = (parts.shape[4] + proj_parts.shape[4], features)
    depth = HEAD_DIM + EXTRA
    dma = pltpu.SemaphoreType.DMA
    vmem = pl.BlockSpec(memory_space=pltpu.VMEM)
    anywhere = pl.BlockSpec(memory_space=pl.ANY)
    plane = (2, side - 1)
    return pl.pallas_call(
        functools.partial(backward_kernel, wide, narrow, items, chunks),
        in_specs=[
            vmem, anywhere, vmem, vmem, anywhere, anywhere, anywhere, vmem,
            anywhere, vmem, anywhere, vmem, vmem,
        ],
        out_specs=(vmem, vmem, anywhere, vmem, anywhere),
        out_shape=(
            jax.ShapeDtypeStruct((rows, features), bf16),
            jax.ShapeDtypeStruct((held_columns, features), bf16),
            jax.ShapeDtypeStruct((wide, 2, *piece), bf16),
            jax.ShapeDtypeStruct((8, features // narrow), f32),
            jax.ShapeDtypeStruct((lines, side, side, 2, *piece), bf16),
        ),
        scratch_shapes=[
            *[pltpu.VMEM((heads, depth, total_rows), bf16)] * 4,
            *[pltpu.VMEM((heads, HEAD_DIM, total_rows), f32)] * 3,
            pltpu.VMEM((held_columns, rows), bf16),
            pltpu.VMEM((2, rows, features), bf16),
            pltpu.VMEM((held_columns, features), f32),
            pltpu.VMEM((2, rows, features), bf16),
            pltpu.VMEM((lines, rows, features), bf16),
            pltpu.VMEM((lines, rows, features), bf16),
            pltpu.VMEM((lines + 1, rows, features), bf16),
            pltpu.VMEM((2, side - 1, held_columns // 2, features), bf16),
            pltpu.VMEM((2, side - 1, held_columns // 2, features), bf16),
            pltpu.VMEM((narrow, 8, features // narrow), f32),
            pltpu.VMEM((narrow - 1, 8, features // narrow), f32),
            pltpu.VMEM((8, features // narrow), f32),
            pltpu.VMEM((wide - 1, 8, features // narrow), f32),
            pltpu.VMEM((2, *piece), bf16),
            pltpu.VMEM((rows // chunks, features), f32),
            dma((heads, 3)),
            dma((heads,)),
            dma((narrow, heads)),
            dma((narrow, heads)),
            dma((2,)),
            dma(()),
            dma(()),
            dma((2,)),
            dma((lines,)),
            dma((lines, chunks)),
            dma((lines + 1, chunks)),
            dma((wide,)),
            dma((wide,)),
            dma(plane),
            dma(plane),
            dma(plane),
            dma(plane),
            dma((narrow - 1,)),
            dma((narrow - 1,)),
            dma((wide - 1,)),
            dma((wide - 1,)),
            *reduce_scratch(wide, narrow, *piece),
        ],
        compiler_params=pltpu.CompilerParams(
            vmem_limit_bytes=61 << 20, collective_id=2, has_side_effects=True
        ),
        name="backward",
    )(
        extras, packed, attended, log_total, grad, parts, proj_parts, weight, normed,
        tokens, middle, gain, norm_parts,
    )


def unpack_kernel(shard_ref, qkv_ref, qkv_out, proj_out, up_out, down_out):
    wide = shard_ref.shape[0]
    features = shard_ref.shape[3]
    columns = up_out.shape[1]
    groups = features // columns
    units, few = down_out.shape[0] // (2 * wide), proj_out.shape[0] // (2 * wide)
    for j in range(2 * wide):
        w, h = divmod(j, 2)
        for g in range(groups):
            up_out[(j * groups + g) * units : (j * groups + g + 1) * units, :] = shard_ref[
                w, h, 0:units, g * columns : (g + 1) * columns
            ].astype(f32)
        down_out[j * units : (j + 1) * units, :] = shard_ref[w, h, units : 2 * units, :].astype(f32)
        proj_out[j * few : (j + 1) * few, :] = shard_ref[w, h, 2 * units :, :].astype(f32)
    qkv_out[...] = qkv_ref[...].astype(f32).T


def unpack(shard, qkv, proj_shape, up_shape, down_shape):
    return pl.pallas_call(
        unpack_kernel,
        out_shape=tuple(
            jax.ShapeDtypeStruct(shape, f32)
            for shape in (qkv.shape[::-1], proj_shape, up_shape, down_shape)
        ),
        compiler_params=pltpu.CompilerParams(vmem_limit_bytes=48 << 20),
        name="unpack",
    )(shard, qkv)


class Gather:
    def __init__(self, wide, narrow, owns, out, mine, *semaphores):
        self.owns, self.out, self.mine = owns, out, mine
        self.w, self.n = lax.axis_index("wide"), lax.axis_index("narrow")
        self.side, self.lines = math.isqrt(wide), narrow // 2
        self.a, self.b = self.w // self.side, lax.rem(self.w, self.side)
        self.z, self.core = self.n // 2, lax.rem(self.n, 2)
        self.sibling = self.n + 1 - 2 * self.core
        (
            self.loaded, self.copied, self.own_sent, self.passed, self.line_got, self.first_sent, self.first_got,
            self.second_sent, self.second_got, self.f0_sent, self.f0_got, self.f1_sent, self.f1_got,
            self.f2_sent, self.f2_got, self.f3_sent, self.f3_got,
        ) = semaphores
        self.pairs = [(h, i) for i in range(1, self.side) for h in (0, 1)]

    @staticmethod
    def scratch(wide, narrow, piece):
        side, lines = math.isqrt(wide), narrow // 2
        dma = pltpu.SemaphoreType.DMA
        line, plane = (lines,), (lines, 2, side)
        shapes = [(2,), (), line, line, line, plane, plane, plane, plane, (), (), line, line]
        mine = pltpu.VMEM((side, side, 2, *piece), bf16)
        return [mine, *[dma(shape) for shape in shapes + [plane] * 4]]

    def other_a(self, i):
        return lax.rem(self.a + i, self.side)

    def other_b(self, i):
        return lax.rem(self.b + i, self.side)

    def own_on(self, way):
        return remote(
            self.mine.at[self.a, self.b], self.out.at[self.n, self.a, self.b],
            self.own_sent.at[self.z + way], self.line_got.at[self.z], self.w, self.n + 2 * way,
        )

    def pass_on(self, zs, way):
        piece = self.out.at[2 * zs + self.core, self.a, self.b]
        return remote(
            piece, piece, self.passed.at[zs], self.line_got.at[zs], self.w, self.n + 2 * way
        )

    def first(self, zs, h, i):
        shard = 2 * zs + self.core
        piece = self.out.at[shard, self.a, self.b, h]
        if h == 0:
            to, mine = self.a * self.side + self.other_b(i), self.b
        else:
            to, mine = self.other_a(i) * self.side + self.b, self.a
        return remote(
            piece, piece, self.first_sent.at[zs, h, i], self.first_got.at[zs, h, mine], to, self.n
        )

    def second(self, zs, h, i):
        shard = 2 * zs + self.core
        if h == 0:
            piece = self.out.at[shard, self.a, :, 0]
            to, mine = self.other_a(i) * self.side + self.b, self.a
        else:
            piece = self.out.at[shard, :, self.b, 1]
            to, mine = self.a * self.side + self.other_b(i), self.b
        return remote(
            piece, piece, self.second_sent.at[zs, h, i], self.second_got.at[zs, h, mine], to, self.n
        )

    def first_from(self, shard, h, i):
        if h == 0:
            return self.out.at[shard, self.a, self.other_b(i), 0], self.other_b(i)
        return self.out.at[shard, self.other_a(i), self.b, 1], self.other_a(i)

    def second_from(self, shard, h, i):
        if h == 0:
            return self.out.at[shard, self.other_a(i), :, 0], self.other_a(i)
        return self.out.at[shard, :, self.other_b(i), 1], self.other_b(i)

    def hand0(self):
        return remote(
            self.mine, self.out.at[self.n], self.f0_sent, self.f0_got, self.w, self.sibling
        )

    def hand1(self, zs):
        piece = self.out.at[2 * zs + self.core, self.a, self.b]
        return remote(piece, piece, self.f1_sent.at[zs], self.f1_got.at[zs], self.w, self.sibling)

    def hand2(self, zs, h, i):
        piece, k = self.first_from(2 * zs + self.core, h, i)
        return remote(
            piece, piece, self.f2_sent.at[zs, h, k], self.f2_got.at[zs, h, k], self.w, self.sibling
        )

    def hand3(self, zs, h, i):
        piece, k = self.second_from(2 * zs + self.core, h, i)
        return remote(
            piece, piece, self.f3_sent.at[zs, h, k], self.f3_got.at[zs, h, k], self.w, self.sibling
        )

    def load(self):
        copies, row = [], 0
        for k, own in enumerate(self.owns):
            part = self.mine.at[:, :, :, pl.ds(row, own.shape[3])]
            copies.append(pltpu.make_async_copy(own, part, self.loaded.at[k]))
            row += own.shape[3]
        return copies

    def keep(self):
        return pltpu.make_async_copy(self.mine, self.out.at[self.n], self.copied)

    def sides(self, d, act):
        if not 1 <= d <= self.lines - 1:
            return
        z, last = self.z, self.lines - 1

        @pl.when(z >= d)
        def _():
            act(z - d, 1, z < last)

        @pl.when(z + d <= last)
        def _():
            act(z + d, -1, z > 0)

    def begin(self):
        for copy in self.load():
            copy.start()
        for copy in self.load():
            copy.wait()

        @pl.when(self.z < self.lines - 1)
        def _():
            self.own_on(1).start()

        @pl.when(self.z > 0)
        def _():
            self.own_on(-1).start()

        self.keep().start()
        self.hand0().start()

    def one(self, zs, way, more):
        arrived(self.out.at[2 * zs + self.core, self.a, self.b], self.line_got.at[zs])

        @pl.when(more)
        def _():
            self.pass_on(zs, way).start()

        for h, i in self.pairs:
            self.first(zs, h, i).start()
        self.hand1(zs).start()

    def two(self, zs, way, more):
        for h in (0, 1):
            for i in range(1, self.side):
                piece, k = self.first_from(2 * zs + self.core, h, i)
                arrived(piece, self.first_got.at[zs, h, k])
            for i in range(1, self.side):
                self.second(zs, h, i).start()
        for h, i in self.pairs:
            self.hand2(zs, h, i).start()

    def three(self, zs, way, more):
        for h, i in self.pairs:
            piece, k = self.second_from(2 * zs + self.core, h, i)
            arrived(piece, self.second_got.at[zs, h, k])
            self.hand3(zs, h, i).start()

    def round(self, d):
        self.sides(d, self.one)
        self.sides(d - 1, self.two)
        self.sides(d - 2, self.three)

    def finish_side(self, zs, way, more):
        theirs = 2 * zs + 1 - self.core

        @pl.when(more)
        def _():
            self.pass_on(zs, way).wait_send()

        self.hand1(zs).wait_send()
        arrived(self.out.at[theirs, self.a, self.b], self.f1_got.at[zs])
        for h, i in self.pairs:
            self.first(zs, h, i).wait_send()
            self.second(zs, h, i).wait_send()
            self.hand2(zs, h, i).wait_send()
            self.hand3(zs, h, i).wait_send()
            piece, k = self.first_from(theirs, h, i)
            arrived(piece, self.f2_got.at[zs, h, k])
            piece, k = self.second_from(theirs, h, i)
            arrived(piece, self.f3_got.at[zs, h, k])

    def finish(self):
        @pl.when(self.z < self.lines - 1)
        def _():
            self.own_on(1).wait_send()

        @pl.when(self.z > 0)
        def _():
            self.own_on(-1).wait_send()

        self.keep().wait()
        self.hand0().wait_send()
        arrived(self.out.at[self.sibling], self.f0_got)
        for d in range(1, self.lines):
            self.sides(d, self.finish_side)


def start_kernel(
    wide, narrow, length_ref, token_ref, gain_ref, bias_ref, weight_ref, own_ref,
    normed, packed, turned, extras, gathered, line_sent, line_got, sib_sent, sib_got, *gather_refs,
):
    gather = Gather(wide, narrow, [own_ref], gathered, *gather_refs)
    w, n, z, core = gather.w, gather.n, gather.z, gather.core
    lines, sibling = gather.lines, gather.sibling
    rows = token_ref.shape[0]

    greet_all(wide, narrow, w, n)

    def norm_rows(j, carry):
        part = pl.ds(pl.multiple_of(j * 64, 64), 64)
        values = token_ref[part, :].astype(f32)
        centred = values - jnp.mean(values, axis=-1, keepdims=True)
        variance = jnp.mean(centred * centred, axis=-1, keepdims=True)
        normed[n, part, :] = (
            centred * lax.rsqrt(variance + epsilon) * as_row(gain_ref) + as_row(bias_ref)
        ).astype(bf16)
        return carry

    step = rows // CHUNKS

    def part_of(shard, c):
        return normed.at[shard, pl.ds(c * step, step)]

    def pass_on(zs, c, way):
        block = part_of(2 * zs + core, c)
        k = (1 - way) // 2
        return remote(block, block, line_sent.at[zs, c, k], line_got.at[zs, c], w, n + 2 * way)

    def hand(zs, c):
        block = part_of(2 * zs + core, c)
        return remote(block, block, sib_sent.at[zs, c], sib_got.at[zs, c], w, sibling)

    def project(owner, c):
        columns = pl.ds(pl.multiple_of(owner * rows + c * step, step), step)
        product = contract(turned[...], normed[owner, pl.ds(c * step, step)], 1, 1).astype(bf16)
        for j in range(product.shape[0] // HEAD_DIM):
            part = product[j * HEAD_DIM : (j + 1) * HEAD_DIM]
            if j % 3 == 0:
                part = part * jnp.asarray(HEAD_DIM**-0.5, bf16)
            packed[j * HEAD_DIM : (j + 1) * HEAD_DIM, columns] = part

    norm_blocks = rows // 64 // CHUNKS
    for c in range(CHUNKS):
        lax.fori_loop(c * norm_blocks, (c + 1) * norm_blocks, norm_rows, 0)
        if c == 0:
            greeted(wide, narrow)
            gather.begin()

        @pl.when(z < lines - 1)
        def _():
            pass_on(z, c, 1).start()

        @pl.when(z > 0)
        def _():
            pass_on(z, c, -1).start()

        hand(z, c).start()
    turned[...] = weight_ref[...].T
    mask_rows(length_ref, extras)
    for c in range(CHUNKS):
        project(n, c)

    def receive(c, zs, way, more):
        arrived(part_of(2 * zs + core, c), line_got.at[zs, c])

        @pl.when(more)
        def _():
            pass_on(zs, c, way).start()

        hand(zs, c).start()

    def project_side(zs, way, more):
        for c in range(CHUNKS):
            project(2 * zs + core, c)

    def project_sibling(zs, way, more):
        for c in range(CHUNKS):
            arrived(part_of(2 * zs + 1 - core, c), sib_got.at[zs, c])
            project(2 * zs + 1 - core, c)

    project_sibling(z, 0, None)
    for d in range(1, lines):
        gather.round(d)
        if d == lines - 1:
            gather.round(lines)
            gather.round(lines + 1)
        for c in range(CHUNKS):
            gather.sides(d, functools.partial(receive, c))
        if d > 1:
            gather.sides(d - 1, project_sibling)
        gather.sides(d, project_side)
    gather.sides(lines - 1, project_sibling)
    gather.finish()

    def sent_side(zs, way, more):
        for c in range(CHUNKS):
            hand(zs, c).wait_send()

            @pl.when(more)
            def _():
                pass_on(zs, c, way).wait_send()

    for c in range(CHUNKS):

        @pl.when(z < lines - 1)
        def _():
            pass_on(z, c, 1).wait_send()

        @pl.when(z > 0)
        def _():
            pass_on(z, c, -1).wait_send()

        hand(z, c).wait_send()
    for d in range(1, lines):
        gather.sides(d, sent_side)


def start(wide, narrow, lengths, tokens, gain, bias, weight, own):
    rows, features = tokens.shape
    lines = narrow // 2
    dma = pltpu.SemaphoreType.DMA
    vmem = pl.BlockSpec(memory_space=pltpu.VMEM)
    anywhere = pl.BlockSpec(memory_space=pl.ANY)
    return pl.pallas_call(
        functools.partial(start_kernel, wide, narrow),
        in_specs=[pl.BlockSpec(memory_space=pltpu.SMEM), vmem, vmem, vmem, vmem, anywhere],
        out_specs=(vmem, vmem, vmem, vmem, anywhere),
        out_shape=(
            jax.ShapeDtypeStruct((narrow, rows, features), bf16),
            jax.ShapeDtypeStruct((weight.shape[1], narrow * rows), bf16),
            jax.ShapeDtypeStruct((weight.shape[1], features), bf16),
            jax.ShapeDtypeStruct((2, EXTRA, narrow * rows), bf16),
            jax.ShapeDtypeStruct((narrow, *own.shape), bf16),
        ),
        scratch_shapes=[
            dma((lines, CHUNKS, 2)), dma((lines, CHUNKS)), dma((lines, CHUNKS)), dma((lines, CHUNKS)),
            *Gather.scratch(wide, narrow, own.shape[3:]),
        ],
        compiler_params=pltpu.CompilerParams(
            vmem_limit_bytes=58 << 20, collective_id=1, has_side_effects=True
        ),
        name="start",
    )(lengths, tokens, gain, bias, weight, own)


def body(
    tokens, cotangent, item_lengths, attn_gain, attn_bias, qkv_weight, proj_weight,
    mlp_gain, mlp_bias, up_weight, down_weight,
):
    items = item_lengths.shape[1]
    heads = qkv_weight.shape[1] // (3 * HEAD_DIM)
    wide, narrow = lax.axis_size("wide"), lax.axis_size("narrow")
    side = math.isqrt(wide)
    rows = narrow * tokens.shape[0]

    def cut(shard):
        return shard.reshape(side, side, 2, shard.shape[0] // (2 * wide), shard.shape[1])

    def split_parts(total):
        return total.reshape(narrow, side, side, 2, -1, total.shape[1])

    first = down_weight.shape[0] // (2 * wide)
    normed_all, packed, qkv_turned, extras, up_all = start(
        wide, narrow, item_lengths, tokens, attn_gain, attn_bias, qkv_weight, cut(up_weight)
    )
    normed_all = normed_all.reshape(rows, -1)
    packed = packed.reshape(heads, 3, HEAD_DIM, rows)
    attended, log_total, attended_rows, rest_all = attend_forward(
        wide, narrow, packed, extras, cut(down_weight), cut(proj_weight)
    )
    attended_rows = attended_rows.reshape(-1, tokens.shape[0])
    proj_all = rest_all
    if (rest_all.shape[4] - first) % 16:
        proj_all = rest_all[:, :, :, :, first:].reshape(-1, tokens.shape[1])
    output, grad_middle, grad_attended, grad_proj, grad_parts, norm_parts = mlp(
        attended_rows, proj_all, tokens, cotangent, mlp_gain, mlp_bias, up_all, rest_all, first
    )
    grad_attended = grad_attended.reshape(narrow, heads, HEAD_DIM, -1)
    grad_proj_parts = split_parts(grad_proj)
    grad_tokens, grad_qkv, grad_shard, shares, _ = backward(
        wide, narrow, extras, packed, attended, log_total, grad_attended, grad_parts,
        grad_proj_parts, qkv_turned, normed_all, tokens, grad_middle, attn_gain, norm_parts, items,
    )
    grad_qkv, grad_proj, grad_up, grad_down = unpack(
        grad_shard, grad_qkv, proj_weight.shape, up_weight.shape, down_weight.shape
    )
    return (
        output, grad_tokens, shares[0], shares[1], grad_qkv, grad_proj,
        shares[2], shares[3], grad_up, grad_down,
    )


def solution(mesh):
    by_rows = P(("wide", "narrow"), None)
    return jax.shard_map(
        body,
        mesh=mesh,
        in_specs=(
            by_rows, by_rows, P("wide", None), P(), P(), P(None, "narrow"), P("narrow", None),
            P(), P(), P(None, "narrow"), P("narrow", None),
        ),
        out_specs=(
            by_rows, by_rows, P("narrow"), P("narrow"), P(None, "narrow"), P("narrow", None),
            P("narrow"), P("narrow"), P(None, "narrow"), P("narrow", None),
        ),
        check_vma=False,
    )
```

```python
import functools
import math

import jax
import jax.numpy as jnp
from jax import lax
from jax.experimental import pallas as pl
from jax.experimental.pallas import tpu as pltpu
from jax.sharding import PartitionSpec as P

HEAD_DIM = 64
EXTRA = 16
CHUNKS = 2
REDUCE_START, REDUCE_STEP, REDUCE_FIRST, REDUCE_SECOND, SPREAD_AT = 3, 11, 9, 13, 8
EARLY_RELAY = 17
EXCLUDED = -1e30
bf16 = jnp.bfloat16
f32 = jnp.float32
MESH = pl.DeviceIdType.MESH
epsilon = 1e-05


def mask_rows(length_ref, extras):
    items = length_ref.shape[1]
    rows = extras.shape[2]
    position = lax.broadcasted_iota(jnp.int32, (EXTRA, rows), 1)
    extra = lax.broadcasted_iota(jnp.int32, (EXTRA, rows), 0)
    segment, end = jnp.zeros((EXTRA, rows), jnp.int32), 0
    for i in range(items):
        end = end + length_ref[0, i]
        segment = segment + jnp.where(position >= end, 1, 0)
    own = jnp.where(segment == extra, 1.0, 0.0)
    mask = jnp.where(extra <= items, 1.0, 0.0)
    ones = jnp.where(extra <= items + 3, 1.0, 0.0) * (1.0 - mask)
    extras[0] = (own * mask).astype(bf16)
    extras[1] = ((1.0 - own) * mask * EXCLUDED + ones).astype(bf16)


def forward_kernel(
    wide, narrow, qx_ref, kx_ref, q_ref, k_ref, v_ref, own_ref, more_ref, o_ref, log_ref, rows_ref, gathered,
    keys, ready, copied, sent, got, *gather_refs,
):
    gather = Gather(wide, narrow, [own_ref, more_ref], gathered, *gather_refs)
    w, n, lines = gather.w, gather.n, gather.lines
    head, step = pl.program_id(0), pl.program_id(1)
    moment = head * narrow + step
    width = q_ref.shape[-1] // narrow
    last = heads_of(ready, narrow) * narrow - 1

    moves = []
    for d in range(1, lines):
        moves += [
            (3.5 * d, functools.partial(gather.sides, d, gather.one)),
            (3.5 * d + 2.5, functools.partial(gather.sides, d, gather.two)),
            (3.5 * d + 5.5, functools.partial(gather.sides, d, gather.three)),
        ]
    moves.append((900.0, gather.finish))
    moves.sort(key=lambda move: move[0])

    def perform(lower, upper):
        for time, move in moves:
            if lower <= time < upper:
                move()

    @pl.when(moment == 0)
    def _():
        greet_all(wide, narrow, w, n)

    @pl.when(step == 0)
    def _():
        keys[...] = jnp.concatenate([k_ref[0], kx_ref[...]], axis=0).T

    @pl.when(moment == 0)
    def _():
        greeted(wide, narrow)
        gather.begin()

    for tick in range(last + 1):

        @pl.when(moment == tick)
        def _():
            perform(tick, tick + 1)

    owner = lax.rem(n + 1 + step, narrow)
    columns = pl.ds(pl.multiple_of(owner * width, width), width)
    query = jnp.concatenate(
        [q_ref[0, :, columns], qx_ref[:, columns]], axis=0
    )
    maximum = jnp.full((1, width), -3e38, f32)
    total, gathered_values = 0.0, 0.0
    half = keys.shape[0] // 2
    for part in (pl.ds(0, half), pl.ds(half, half)):
        scores = jnp.dot(keys[part, :], query, preferred_element_type=f32)
        larger = jnp.maximum(maximum, jnp.max(scores, axis=0, keepdims=True))
        shrink = jnp.exp(maximum - larger)
        raised = jnp.exp(scores - larger)
        total = shrink * total + jnp.sum(raised, axis=0, keepdims=True)
        gathered_values = shrink * gathered_values + jnp.dot(
            v_ref[0, :, part], raised.astype(bf16), preferred_element_type=f32
        )
        maximum = larger
    result = (gathered_values / total).astype(bf16)
    o_ref[0, :, columns] = result
    log_ref[0, :, columns] = maximum + jnp.log(total)
    ready[moment] = result

    def deliver(k, owner, h):
        return remote(ready.at[k], rows_ref.at[n, h], sent.at[k], got.at[n, h], w, owner)

    def deliver_here(k, h):
        return pltpu.make_async_copy(ready.at[k], rows_ref.at[n, h], copied.at[h])

    @pl.when(step < narrow - 1)
    def _():
        deliver(moment, owner, head).start()

    @pl.when(step == narrow - 1)
    def _():
        deliver_here(moment, head).start()

    @pl.when(moment == last)
    def _():
        perform(last + 1, 1000)
        for h in range((last + 1) // narrow):
            deliver_here(h * narrow + narrow - 1, h).wait()
            for t in range(narrow - 1):
                deliver(h * narrow + t, lax.rem(n + 1 + t, narrow), h).wait_send()
                source = lax.rem(n + narrow - 1 - t, narrow)
                arrived(rows_ref.at[source, h], got.at[source, h])


def heads_of(ready, narrow):
    return ready.shape[0] // narrow


def attend_forward(wide, narrow, packed, extras, own, more):
    heads, _, _, rows = packed.shape
    width = rows // narrow
    gathered = (narrow, *own.shape[:3], own.shape[3] + more.shape[3], own.shape[4])
    dma = pltpu.SemaphoreType.DMA

    def whole(j):
        return pl.BlockSpec((1, None, HEAD_DIM, rows), lambda h, i: (h, j, 0, 0))

    def extra(j):
        return pl.BlockSpec((None, EXTRA, rows), lambda h, i: (j, 0, 0))

    anywhere = pl.BlockSpec(memory_space=pl.ANY)
    return pl.pallas_call(
        functools.partial(forward_kernel, wide, narrow),
        grid=(heads, narrow),
        in_specs=[extra(0), extra(1), whole(0), whole(1), whole(2), anywhere, anywhere],
        out_specs=(
            pl.BlockSpec((1, HEAD_DIM, rows), lambda h, i: (h, 0, 0)),
            pl.BlockSpec((1, 1, rows), lambda h, i: (h, 0, 0)),
            anywhere,
            anywhere,
        ),
        out_shape=(
            jax.ShapeDtypeStruct((heads, HEAD_DIM, rows), bf16),
            jax.ShapeDtypeStruct((heads, 1, rows), f32),
            jax.ShapeDtypeStruct((narrow, heads, HEAD_DIM, width), bf16),
            jax.ShapeDtypeStruct(gathered, bf16),
        ),
        scratch_shapes=[
            pltpu.VMEM((rows, HEAD_DIM + EXTRA), bf16),
            pltpu.VMEM((heads * narrow, HEAD_DIM, width), bf16),
            dma((heads,)),
            dma((heads * narrow,)),
            dma((narrow, heads)),
            *Gather.scratch(wide, narrow, gathered[4:]),
        ],
        compiler_params=pltpu.CompilerParams(
            vmem_limit_bytes=58 << 20, collective_id=4, has_side_effects=True
        ),
        name="attend_forward",
    )(extras, extras, packed, packed, packed, own, more)


def remote(src, dst, sent, received, wide_to, narrow_to):
    return pltpu.make_async_remote_copy(
        src_ref=src,
        dst_ref=dst,
        send_sem=sent,
        recv_sem=received,
        device_id=(wide_to, narrow_to),
        device_id_type=MESH,
    )


def arrived(ref, semaphore):
    pltpu.make_async_copy(ref, ref, semaphore).wait()


def greet_all(wide, narrow, w, n):
    barrier = pltpu.get_barrier_semaphore()

    def column(t, carry):
        pl.semaphore_signal(
            barrier, inc=1, device_id=(w, lax.rem(n + t, narrow)), device_id_type=MESH
        )
        return carry

    def plane(t, carry):
        pl.semaphore_signal(
            barrier, inc=1, device_id=(lax.rem(w + t, wide), n), device_id_type=MESH
        )
        return carry

    lax.fori_loop(1, narrow, column, 0)
    lax.fori_loop(1, wide, plane, 0)


def greeted(wide, narrow):
    pl.semaphore_wait(pltpu.get_barrier_semaphore(), narrow + wide - 2)


def accumulate(into, *others):
    rows = into.shape[0]
    few = max([d for d in (16, 32, 48, 64) if rows % d == 0], default=rows)

    def piece(j, carry):
        part = pl.ds(j * few if rows == few else pl.multiple_of(j * few, few), few)
        total = into[part, :].astype(f32)
        for other in others:
            total = total + other[part, :].astype(f32)
        into[part, :] = total.astype(bf16)
        return carry

    if rows == few:
        piece(0, 0)
    else:
        lax.fori_loop(0, rows // few, piece, 0)


def reduce_steps(
    wide, narrow, parts, proj_parts, landed, final, held, staged, from_first, from_second, from_line,
    mine, loaded, sib_sent, sib_got, first_sent, first_got, second_sent, second_got, line_sent, line_got,
):
    w, n = lax.axis_index("wide"), lax.axis_index("narrow")
    side, lines = math.isqrt(wide), narrow // 2
    a, b, z, core = w // side, lax.rem(w, side), n // 2, lax.rem(n, 2)
    sibling = n + 1 - 2 * core
    slots = held.shape[0]
    most, least = parts.shape[4], proj_parts.shape[4]
    sources = [(parts, pl.ds(0, most)), (proj_parts, pl.ds(most, least))]
    order = [lax.rem(z + 1 + j, lines) for j in range(lines)]
    halves = [(h, i) for i in range(1, side) for h in (0, 1)]

    def other_a(i):
        return lax.rem(a + i, side)

    def other_b(i):
        return lax.rem(b + i, side)

    def to_sibling(j):
        shard = 2 * order[j] + 1 - core
        return [
            remote(
                src.at[shard], landed.at[j, :, :, :, rows],
                sib_sent.at[k, j], sib_got.at[k, j], w, sibling,
            )
            for k, (src, rows) in enumerate(sources)
        ]

    def load(j):
        shard, slot = 2 * order[j] + core, j % slots
        return [
            pltpu.make_async_copy(src.at[shard], held.at[slot, :, :, :, rows], loaded.at[k])
            for k, (src, rows) in enumerate(sources)
        ]

    def stage(j):
        return pltpu.make_async_copy(landed.at[j], staged, loaded.at[2])

    def first(j, h, i):
        slot, k = j % slots, i - 1
        if h == 0:
            src, to = held.at[slot, other_a(i), :, 0], other_a(i) * side + b
        else:
            src, to = held.at[slot, :, other_b(i), 1], a * side + other_b(i)
        return remote(
            src, from_first.at[j, h, k], first_sent.at[j, h, k], first_got.at[j, h, k], to, n
        )

    def second(j, h, i):
        slot, k = j % slots, i - 1
        if h == 0:
            src, to = held.at[slot, a, other_b(i), 0], a * side + other_b(i)
        else:
            src, to = held.at[slot, other_a(i), b, 1], other_a(i) * side + b
        return remote(
            src, from_second.at[j, h, k], second_sent.at[j, h, k], second_got.at[j, h, k], to, n
        )

    def along(j):
        zs = order[j]
        place = jnp.where(z < zs, z, z - 1)
        return remote(
            held.at[j % slots, a, b], from_line.at[place], line_sent.at[j], line_got.at[place],
            w, 2 * zs + core,
        )

    def begin():
        for j in range(lines):
            for copy in to_sibling(j):
                copy.start()

    def sent(j):
        for h, i in halves:
            first(j, h, i).wait_send()
            second(j, h, i).wait_send()

        if j < lines - 1:
            along(j).wait_send()

    def combine(j):
        slot = j % slots
        if j >= slots:
            sent(j - slots)
        for copy in load(j):
            copy.start()
        for k, (_, rows) in enumerate(sources):
            arrived(landed.at[j, :, :, :, rows], sib_got.at[k, j])
        stage(j).start()
        for copy in load(j):
            copy.wait()
        stage(j).wait()

        def piece(t, carry):
            p, q = t // side, lax.rem(t, side)
            for h in (0, 1):
                accumulate(held.at[slot, p, q, h], staged.at[p, q, h])
            return carry

        lax.fori_loop(0, wide, piece, 0)
        for h, i in halves:
            first(j, h, i).start()

    def narrow_down(j):
        slot = j % slots
        for h in (0, 1):
            for i in range(1, side):
                arrived(from_first.at[j, h, i - 1], first_got.at[j, h, i - 1])

            def piece(t, carry, h=h):
                into = held.at[slot, a, t, 0] if h == 0 else held.at[slot, t, b, 1]
                accumulate(into, *[from_first.at[j, h, i, t] for i in range(side - 1)])
                return carry

            lax.fori_loop(0, side, piece, 0)
        for h, i in halves:
            second(j, h, i).start()

    def send_home(j):
        slot = j % slots
        for h, i in halves:
            arrived(from_second.at[j, h, i - 1], second_got.at[j, h, i - 1])
        for h in (0, 1):
            accumulate(
                held.at[slot, a, b, h], *[from_second.at[j, h, i] for i in range(side - 1)]
            )

        if j < lines - 1:
            along(j).start()
        else:
            mine[...] = held[slot, a, b]

    def finish():
        for place in range(lines - 1):
            arrived(from_line.at[place], line_got.at[place])
        for h in (0, 1):
            total = mine[h].astype(f32)
            for place in range(lines - 1):
                total = total + from_line[place, h].astype(f32)
            final[h] = total.astype(bf16)

    def close():
        for j in range(lines):
            for copy in to_sibling(j):
                copy.wait_send()
        for j in range(max(0, lines - slots), lines):
            sent(j)

    steps = [(0.0, begin)]
    for j in range(lines):
        at = REDUCE_START + REDUCE_STEP * j
        steps += [
            (at, functools.partial(combine, j)),
            (at + REDUCE_FIRST, functools.partial(narrow_down, j)),
            (at + REDUCE_SECOND, functools.partial(send_home, j)),
        ]
    return sorted(steps, key=lambda step: step[0]), finish, close


def reduce_scratch(wide, narrow, rows, features, slots=3):
    side, lines = math.isqrt(wide), narrow // 2
    dma = pltpu.SemaphoreType.DMA
    plane = (lines, 2, side - 1)
    return [
        pltpu.VMEM((slots, side, side, 2, rows, features), bf16),
        pltpu.VMEM((side, side, 2, rows, features), bf16),
        pltpu.VMEM((lines, 2, side - 1, side, rows, features), bf16),
        pltpu.VMEM((lines, 2, side - 1, rows, features), bf16),
        pltpu.VMEM((lines - 1, 2, rows, features), bf16),
        pltpu.VMEM((2, rows, features), bf16),
        *[dma(shape) for shape in [(3,), (2, lines), (2, lines), plane, plane, plane, plane]],
        dma((lines,)),
        dma((lines - 1,)),
    ]


def as_row(ref):
    return ref[...].astype(f32).reshape(1, -1)


def contract(left, right, left_axis, right_axis):
    return lax.dot_general(
        left, right, (((left_axis,), (right_axis,)), ((), ())), preferred_element_type=f32
    )


def gelu_pair(values):
    half = 0.5 + 0.5 * lax.erf(values * 0.7071067811865476)
    slope = half + values * (jnp.exp(values * values * -0.5) * 0.3989422804014327)
    return values * half, slope


def mlp_kernel(
    att_ref, rest_ref, token_ref, cot_ref, gain_ref, bias_ref, up_ref, down_ref,
    out_ref, middle_out, att_out, proj_out, parts_ref, norm_ref,
    middle, expand, out_total, expand_total, proj_ref, proj_got,
):
    step = pl.program_id(0)
    rows, features = token_ref.shape
    few = 64

    def by_rows(change):
        def body(j, carry):
            return change(pl.ds(pl.multiple_of(j * few, few), few), carry)

        return body

    if rest_ref.ndim == 2:
        fetch = pltpu.make_async_copy(rest_ref, proj_ref, proj_got)
    else:
        few_rows = rest_ref.shape[4] - down_ref.shape[4]
        fetch = pltpu.make_async_copy(
            rest_ref.at[:, :, :, :, pl.ds(down_ref.shape[4], few_rows)],
            proj_ref.reshape(*rest_ref.shape[:4], few_rows, features),
            proj_got,
        )

    @pl.when(step == 0)
    def _():
        fetch.start()
        fetch.wait()
        middle[...] = token_ref[...].astype(f32) + contract(att_ref[...], proj_ref[...], 0, 0)
        out_total[...] = jnp.zeros_like(out_total)
        expand_total[...] = jnp.zeros_like(expand_total)

        def norm(part, carry):
            values = middle[part, :]
            centred = values - jnp.mean(values, axis=-1, keepdims=True)
            variance = jnp.mean(centred * centred, axis=-1, keepdims=True)
            expand[part, :] = (
                centred * lax.rsqrt(variance + epsilon) * as_row(gain_ref) + as_row(bias_ref)
            ).astype(bf16)
            return carry

        lax.fori_loop(0, rows // few, by_rows(norm), 0)

    def flat(ref):
        if ref.shape[4] % 16:
            return ref[0].astype(f32).reshape(-1, ref.shape[5]).astype(bf16)
        return ref[0].reshape(-1, ref.shape[5])

    up, down = flat(up_ref), flat(down_ref)
    units = down_ref.shape[4]
    pieces = up_ref.shape[1:4]
    columns = up_ref.shape[5]
    hidden_parts, grad_parts = [], []
    for part in (pl.ds(0, rows // 2), pl.ds(rows // 2, rows // 2)):
        hidden, slope = gelu_pair(
            jnp.dot(expand[part, :], up, preferred_element_type=f32)
        )
        grad_pre = (contract(cot_ref[part, :], down, 1, 1) * slope).astype(bf16)
        hidden = hidden.astype(bf16)
        out_total[part, :] += jnp.dot(hidden, down, preferred_element_type=f32)
        expand_total[part, :] += contract(grad_pre, up, 1, 1)
        hidden_parts.append(hidden)
        grad_parts.append(grad_pre)
    grad_up = contract(expand[...], jnp.concatenate(grad_parts, axis=0), 0, 0)
    grad_down = contract(jnp.concatenate(hidden_parts, axis=0), cot_ref[...], 0, 0)
    groups = features // columns
    grad_up = grad_up.reshape(*pieces, groups, units, columns)
    for g in range(groups):
        parts_ref[0, :, :, :, 0:units, g * columns : (g + 1) * columns] = grad_up[
            :, :, :, g
        ].astype(bf16)
    parts_ref[0, :, :, :, units : 2 * units, :] = grad_down.reshape(
        *pieces, units, features
    ).astype(bf16)

    @pl.when(step == pl.num_programs(0) - 1)
    def _():
        def finish_rows(part, carry):
            gain_sum, bias_sum = carry
            values = middle[part, :]
            out_ref[part, :] = (values + out_total[part, :]).astype(bf16)
            centred = values - jnp.mean(values, axis=-1, keepdims=True)
            inverse = lax.rsqrt(jnp.mean(centred * centred, axis=-1, keepdims=True) + epsilon)
            scaled = centred * inverse
            grad = expand_total[part, :]
            term = grad * as_row(gain_ref)
            back = inverse * (
                term
                - jnp.mean(term, axis=-1, keepdims=True)
                - scaled * jnp.mean(term * scaled, axis=-1, keepdims=True)
            )
            total = cot_ref[part, :].astype(f32) + back
            middle_out[part, :] = total
            expand[part, :] = total.astype(bf16)
            gain_sum = gain_sum + jnp.sum(grad * scaled, axis=0, keepdims=True)
            bias_sum = bias_sum + jnp.sum(grad, axis=0, keepdims=True)
            return gain_sum, bias_sum

        start = (jnp.zeros((1, features), f32), jnp.zeros((1, features), f32))
        gain_sum, bias_sum = lax.fori_loop(0, rows // few, by_rows(finish_rows), start)
        row = lax.broadcasted_iota(jnp.int32, (8, features), 0)
        norm_ref[...] = jnp.where(row == 2, gain_sum, jnp.where(row == 3, bias_sum, 0.0))
        branch = expand[...]
        att_out[...] = contract(proj_ref[...], branch, 1, 1).astype(bf16)
        proj_out[...] = jnp.dot(att_ref[...], branch, preferred_element_type=f32).astype(bf16)


def mlp(attended, rest, tokens, cotangent, gain, bias, up_all, down_all, units):
    rows, features = tokens.shape
    narrow, side = up_all.shape[:2]
    proj_shape = (attended.shape[0], features)

    def whole(*shape):
        return pl.BlockSpec(shape, lambda i: (0,) * len(shape))

    def weights(*piece):
        return pl.BlockSpec((1, side, side, 2, *piece), lambda i: (i, 0, 0, 0, 0, 0))

    return pl.pallas_call(
        mlp_kernel,
        grid=(narrow,),
        in_specs=[
            whole(*attended.shape),
            pl.BlockSpec(memory_space=pl.ANY),
            whole(rows, features),
            whole(rows, features),
            whole(*gain.shape),
            whole(*bias.shape),
            weights(*up_all.shape[4:]),
            weights(units, features),
        ],
        out_specs=(
            whole(rows, features),
            whole(rows, features),
            whole(*attended.shape),
            whole(*proj_shape),
            pl.BlockSpec(
                (1, side, side, 2, 2 * units, features), lambda i: (i, 0, 0, 0, 0, 0)
            ),
            whole(8, features),
        ),
        out_shape=(
            jax.ShapeDtypeStruct((rows, features), bf16),
            jax.ShapeDtypeStruct((rows, features), f32),
            jax.ShapeDtypeStruct(attended.shape, bf16),
            jax.ShapeDtypeStruct(proj_shape, bf16),
            jax.ShapeDtypeStruct((narrow, side, side, 2, 2 * units, features), bf16),
            jax.ShapeDtypeStruct((8, features), f32),
        ),
        scratch_shapes=[
            pltpu.VMEM((rows, features), f32),
            pltpu.VMEM((rows, features), bf16),
            pltpu.VMEM((rows, features), f32),
            pltpu.VMEM((rows, features), f32),
            pltpu.VMEM(proj_shape, bf16),
            pltpu.SemaphoreType.DMA(()),
        ],
        compiler_params=pltpu.CompilerParams(vmem_limit_bytes=58 << 20),
        name="mlp",
    )(attended, rest, tokens, cotangent, gain, bias, up_all, down_all)


def backward_kernel(
    wide, narrow, items, chunks,
    extra_ref, packed_ref, att_ref, log_ref, own_ref, parts_ref, proj_parts_ref, weight_ref,
    normed_ref, token_ref, middle_ref, gain_ref, norm_ref,
    tokens_out, qkv_out, shard_out, norms_out, landed,
    keys, values, queries, grads, grad_q, grad_k, grad_v, block_grad,
    normed, total_qkv, for_sibling, from_sibling, held, from_line,
    first_qkv, second_qkv, norms, norm_column, norm_half, norm_plane, piece,
    middle,
    packed_got, own_got, do_sent, do_got, normed_got, middle_got, copied, sib_sent, sib_got,
    line_sent, line_got, piece_sent, piece_got, first_sent, first_got, second_sent, second_got,
    column_sent, column_got, plane_sent, plane_got, *reduce_refs,
):
    w, n = lax.axis_index("wide"), lax.axis_index("narrow")
    side, lines = math.isqrt(wide), narrow // 2
    a, b, z, core = w // side, lax.rem(w, side), n // 2, lax.rem(n, 2)
    sibling = n + 1 - 2 * core
    heads = keys.shape[0]
    rows, features = token_ref.shape
    step = rows // chunks
    lower = z < lines // 2
    moves, reduce_finish, reduce_close = reduce_steps(
        wide, narrow, parts_ref, proj_parts_ref, landed, piece, *reduce_refs
    )

    def line_at(k):
        climbing = jnp.where(
            k < lines - 1 - z, lines - 1 - k, jnp.where(k < lines - 1, k - (lines - 1 - z), z)
        )
        falling = jnp.where(k < z, k, jnp.where(k < lines - 1, lines - 1 - (k - z), z))
        return jnp.where(lower, climbing, falling)

    def block_at(j):
        odd = lax.rem(j, 2)
        return 2 * line_at(j // 2) + jnp.where(odd == 1, core, 1 - core)

    def columns(owner):
        return pl.ds(pl.multiple_of(owner * rows, rows), rows)

    def packed_copy(h, j):
        into = (queries, keys, values)[j]
        return pltpu.make_async_copy(
            packed_ref.at[h, j], into.at[h, pl.ds(0, HEAD_DIM)], packed_got.at[h, j]
        )

    def keep(h):
        return pltpu.make_async_copy(
            own_ref.at[n, h], grads.at[h, pl.ds(0, HEAD_DIM), columns(n)], own_got.at[h]
        )

    def deliver(t, h):
        to = lax.rem(n + t, narrow)
        return remote(
            own_ref.at[to, h], grads.at[h, pl.ds(0, HEAD_DIM), columns(n)],
            do_sent.at[t, h], do_got.at[n, h], w, to,
        )

    def fetch(j):
        owner = block_at(j)
        return pltpu.make_async_copy(
            normed_ref.at[pl.ds(pl.multiple_of(owner * rows, rows), rows)],
            normed.at[lax.rem(j, 2)], normed_got.at[lax.rem(j, 2)],
        )

    for h in range(heads):
        for j in range(3):
            packed_copy(h, j).start()
        keep(h).start()
    fetch(0).start()
    greet_all(wide, narrow, w, n)
    grad_q[...] = jnp.zeros_like(grad_q)
    grad_k[...] = jnp.zeros_like(grad_k)
    grad_v[...] = jnp.zeros_like(grad_v)
    total_qkv[...] = jnp.zeros_like(total_qkv)
    greeted(wide, narrow)
    for t in range(1, narrow):
        for h in range(heads):
            deliver(t, h).start()
    for h in range(heads):
        keys[h, HEAD_DIM:, :] = extra_ref[1]
        values[h, HEAD_DIM:, :] = extra_ref[1]
    for h in range(heads):
        for j in range(3):
            packed_copy(h, j).wait()
        keep(h).wait()

    row = lax.broadcasted_iota(jnp.int32, (EXTRA, rows), 0) - items

    def pieces(term, base):
        high = term.astype(bf16).astype(f32)
        mid = (term - high).astype(bf16).astype(f32)
        small = term - high - mid
        return jnp.where(
            row == 1, high, jnp.where(row == 2, mid, jnp.where(row == 3, small, base))
        ).astype(bf16)

    def prepare(j):
        owner = block_at(j)
        where = columns(owner)

        @pl.when(owner != n)
        def _():
            for h in range(heads):
                arrived(grads.at[h, pl.ds(0, HEAD_DIM), where], do_got.at[owner, h])

        for h in range(heads):
            grad = grads[h, 0:HEAD_DIM, where].astype(f32)
            inner = jnp.sum(grad * att_ref[h, :, where].astype(f32), axis=0, keepdims=True)
            grads[h, HEAD_DIM:, where] = pieces(-inner, jnp.zeros((EXTRA, rows), f32))
            queries[h, HEAD_DIM:, where] = pieces(
                -log_ref[h, :, where], extra_ref[0, :, where].astype(f32)
            )

    def to_sibling(zs, slot):
        return remote(
            for_sibling.at[slot], from_sibling.at[zs], sib_sent.at[slot], sib_got.at[zs], w, sibling
        )

    def pass_on(zs, c, up):
        part = pl.ds(c * step, step)
        place = zs if up else jnp.where(z - 1 == zs, lines, zs)
        return remote(
            held.at[zs, part], from_line.at[place, part], line_sent.at[zs, c],
            line_got.at[place, c], w, n + 2 if up else n - 2,
        )

    def relay(zs, c, up):
        part = pl.ds(c * step, step)
        arrived(from_line.at[zs, part], line_got.at[zs, c])
        accumulate(held.at[zs, part], from_line.at[zs, part])
        pass_on(zs, c, up).start()

    def early_relay():
        @pl.when(jnp.logical_and(lower, z >= 1))
        def _():
            for c in range(chunks):
                relay(lines - 1, c, True)

        @pl.when(jnp.logical_and(z >= lines // 2, z <= lines - 2))
        def _():
            for c in range(chunks):
                relay(0, c, False)

    def emit(j):
        j = jnp.asarray(j, jnp.int32)
        owner = block_at(j)
        where = columns(owner)
        for h in range(heads):
            for k, total in enumerate((grad_q, grad_k, grad_v)):
                at = (h * 3 + k) * HEAD_DIM
                value = total[h, :, where]
                block_grad[at : at + HEAD_DIM, :] = (
                    value * HEAD_DIM**-0.5 if k == 0 else value
                ).astype(bf16)
        zs, slot = line_at(j // 2), lax.rem(j // 2, 2)
        product = contract(block_grad[...], weight_ref[...], 0, 0).astype(bf16)

        @pl.when(lax.rem(j, 2) == 0)
        def _():
            @pl.when(j >= 4)
            def _():
                to_sibling(zs, slot).wait_send()

            for_sibling[slot] = product
            to_sibling(zs, slot).start()

        @pl.when(lax.rem(j, 2) == 1)
        def _():
            held[zs] = product

        fetch(j).wait()

        @pl.when(j < narrow - 1)
        def _():
            fetch(j + 1).start()

        total_qkv[...] += jnp.dot(
            block_grad[...], normed[lax.rem(j, 2)], preferred_element_type=f32
        )

        @pl.when(lax.rem(j, 2) == 1)
        def _():
            arrived(from_sibling.at[zs], sib_got.at[zs])
            accumulate(held.at[zs], from_sibling.at[zs])

            @pl.when(jnp.logical_and(z == 0, zs != z))
            def _():
                for c in range(chunks):
                    pass_on(zs, c, True).start()

            @pl.when(jnp.logical_and(z == lines - 1, zs != z))
            def _():
                for c in range(chunks):
                    pass_on(zs, c, False).start()

    def spread(t):
        return remote(
            piece, shard_out.at[w], piece_sent.at[t], piece_got.at[t], lax.rem(w + t, wide), n
        )

    stay = pltpu.make_async_copy(piece, shard_out.at[w], copied)

    def spread_all():
        reduce_finish()
        stay.start()
        for t in range(1, wide):
            spread(t).start()

    prepare(narrow - 1)
    pairs = narrow * narrow
    moves = moves + [(6 * narrow - 8 + EARLY_RELAY, early_relay), (pairs - SPREAD_AT, spread_all)]
    moves.sort(key=lambda move: move[0])
    ticks = {}
    for time, move in moves:
        ticks.setdefault(min(int(time), pairs - 1), []).append(move)

    def pair(p, carry):
        for tick, group in ticks.items():

            @pl.when(p == tick)
            def _():
                for move in group:
                    move()

        late = p - 2 * narrow
        stage = sum(
            (late >= j * (2 * narrow - 2 - j)).astype(jnp.int32) for j in range(1, narrow - 2)
        )
        r = late - stage * (2 * narrow - 2 - stage)
        across = r < narrow - stage
        near = late < 0
        qi = jnp.where(
            near,
            jnp.where(p < narrow, narrow - 1, narrow - 2),
            jnp.where(across, stage, 2 * stage + 1 + r - narrow),
        )
        ki = jnp.where(near, lax.rem(p, narrow), jnp.where(across, stage + r, stage))

        @pl.when((p == narrow) | (late == 0) | ((stage == 0) & (r >= narrow)))
        def _():
            prepare(qi)

        at_q, at_k = columns(block_at(qi)), columns(block_at(ki))
        for h in range(heads):
            probs = jnp.exp(contract(queries[h, :, at_q], keys[h, :, at_k], 0, 0))
            scores = (probs * contract(grads[h, :, at_q], values[h, :, at_k], 0, 0)).astype(bf16)
            grad_v[h, :, at_k] += jnp.dot(
                grads[h, 0:HEAD_DIM, at_q], probs.astype(bf16), preferred_element_type=f32
            )
            grad_k[h, :, at_k] += jnp.dot(
                queries[h, 0:HEAD_DIM, at_q], scores, preferred_element_type=f32
            )
            grad_q[h, :, at_q] += contract(keys[h, 0:HEAD_DIM, at_k], scores, 1, 1)

        @pl.when(r == 2 * (narrow - stage) - 4)
        def _():
            emit(stage)

        return carry

    lax.fori_loop(0, pairs, pair, 0)
    emit(narrow - 2)
    emit(narrow - 1)

    half = total_qkv.shape[0] // 2
    own_qkv, half_qkv = for_sibling.at[:, 0:half], normed.at[:, 0:half]
    for slot in range(min(2, lines)):
        to_sibling(0, slot).wait_send()
    for h in (0, 1):
        own_qkv[h] = total_qkv[h * half : (h + 1) * half].astype(bf16)
    halves = [(h, i) for i in range(1, side) for h in (0, 1)]

    def plane_at(h, i):
        if h == 0:
            return lax.rem(a + i, side) * side + b
        return a * side + lax.rem(b + i, side)

    def first(h, i):
        return remote(
            own_qkv.at[h], first_qkv.at[h, i - 1], first_sent.at[h, i - 1], first_got.at[h, i - 1],
            plane_at(h, i), n,
        )

    def second(h, i):
        return remote(
            half_qkv.at[h], second_qkv.at[h, i - 1], second_sent.at[h, i - 1],
            second_got.at[h, i - 1], plane_at(1 - h, i), n,
        )

    def qkv_second():
        for h, i in halves:
            arrived(first_qkv.at[h, i - 1], first_got.at[h, i - 1])
        for h in (0, 1):
            total = own_qkv[h].astype(f32)
            for i in range(1, side):
                total = total + first_qkv[h, i - 1].astype(f32)
            half_qkv[h] = total.astype(bf16)
        for h, i in halves:
            second(h, i).start()

    def qkv_last():
        for h, i in halves:
            arrived(second_qkv.at[h, i - 1], second_got.at[h, i - 1])
        for h in (0, 1):
            total = half_qkv[h].astype(f32)
            for i in range(1, side):
                total = total + second_qkv[h, i - 1].astype(f32)
            qkv_out[h * half : (h + 1) * half] = total.astype(bf16)

    for h, i in halves:
        first(h, i).start()

    def fetch_middle(c):
        return pltpu.make_async_copy(middle_ref.at[pl.ds(c * step, step)], middle, middle_got)

    fetch_middle(0).start()
    for t in range(1, lines):
        below, above = lines - 1 - (t - z), t - (lines - 1 - z)
        for c in range(chunks):
            if t < lines - 1:

                @pl.when((z >= 1) & (t >= z) & ~(lower & (t == z)))
                def _():
                    relay(below, c, True)

                @pl.when((z <= lines - 2) & (above >= 0) & ~((z >= lines // 2) & (above == 0)))
                def _():
                    relay(above, c, False)

    qkv_second()

    def zero_edges(at_edge, place):
        @pl.when(at_edge)
        def _():
            from_line[place] = jnp.zeros((rows, features), bf16)

    zero_edges(z == 0, z)
    zero_edges(z == lines - 1, lines)
    gain_sum = bias_sum = jnp.zeros((1, features), f32)
    for c in range(chunks):
        part = pl.ds(c * step, step)

        @pl.when(z >= 1)
        def _():
            arrived(from_line.at[z, part], line_got.at[z, c])

        @pl.when(z <= lines - 2)
        def _():
            arrived(from_line.at[lines, part], line_got.at[lines, c])

        fetch_middle(c).wait()

        def norm_rows(j, carry):
            gain_sum, bias_sum = carry
            few = pl.ds(pl.multiple_of(c * step + j * 32, 32), 32)
            near = pl.ds(pl.multiple_of(j * 32, 32), 32)
            grad = (
                held[z, few].astype(f32)
                + from_line[z, few].astype(f32)
                + from_line[lines, few].astype(f32)
            )
            values = token_ref[few, :].astype(f32)
            centred = values - jnp.mean(values, axis=-1, keepdims=True)
            inverse = lax.rsqrt(jnp.mean(centred * centred, axis=-1, keepdims=True) + epsilon)
            scaled = centred * inverse
            term = grad * as_row(gain_ref)
            back = inverse * (
                term
                - jnp.mean(term, axis=-1, keepdims=True)
                - scaled * jnp.mean(term * scaled, axis=-1, keepdims=True)
            )
            tokens_out[few, :] = (middle[near, :] + back).astype(bf16)
            gain_sum = gain_sum + jnp.sum(grad * scaled, axis=0, keepdims=True)
            bias_sum = bias_sum + jnp.sum(grad, axis=0, keepdims=True)
            return gain_sum, bias_sum

        gain_sum, bias_sum = lax.fori_loop(0, step // 32, norm_rows, (gain_sum, bias_sum))
        if c + 1 < chunks:
            fetch_middle(c + 1).start()

    row = lax.broadcasted_iota(jnp.int32, (8, features), 0)
    parts = jnp.where(row == 0, gain_sum, jnp.where(row == 1, bias_sum, norm_ref[...]))
    share = features // narrow
    for owner in range(narrow):
        norms[owner] = parts[:, owner * share : (owner + 1) * share]

    def down_column(t):
        to = lax.rem(n + t, narrow)
        return remote(
            norms.at[to], norm_column.at[t - 1], column_sent.at[t - 1], column_got.at[t - 1], w, to
        )

    def over_plane(t):
        return remote(
            norm_half, norm_plane.at[t - 1], plane_sent.at[t - 1], plane_got.at[t - 1],
            lax.rem(w + t, wide), n,
        )

    for t in range(1, narrow):
        down_column(t).start()
    total = norms[n]
    for t in range(1, narrow):
        arrived(norm_column.at[t - 1], column_got.at[t - 1])
        total = total + norm_column[t - 1]
    norm_half[...] = total
    for t in range(1, wide):
        over_plane(t).start()
    for t in range(1, wide):
        arrived(norm_plane.at[t - 1], plane_got.at[t - 1])
        total = total + norm_plane[t - 1]
    norms_out[...] = total

    qkv_last()
    stay.wait()
    reduce_close()
    for t in range(1, wide):
        spread(t).wait_send()
        arrived(shard_out.at[lax.rem(w + wide - t, wide)], piece_got.at[t])
        over_plane(t).wait_send()
    for t in range(1, narrow):
        down_column(t).wait_send()
        for h in range(heads):
            deliver(t, h).wait_send()
    for h, i in halves:
        first(h, i).wait_send()
        second(h, i).wait_send()
    for zs in range(lines):
        for c in range(chunks):

            @pl.when(zs > z)
            def _():
                pass_on(zs, c, True).wait_send()

            @pl.when(zs < z)
            def _():
                pass_on(zs, c, False).wait_send()


def backward(
    wide, narrow, extras, packed, attended, log_total, grad, parts, proj_parts, weight, normed,
    tokens, middle, gain, norm_parts, items, chunks=4,
):
    side, lines = math.isqrt(wide), narrow // 2
    heads, _, _, total_rows = packed.shape
    rows, features = tokens.shape
    held_columns = weight.shape[0]
    piece = (parts.shape[4] + proj_parts.shape[4], features)
    depth = HEAD_DIM + EXTRA
    dma = pltpu.SemaphoreType.DMA
    vmem = pl.BlockSpec(memory_space=pltpu.VMEM)
    anywhere = pl.BlockSpec(memory_space=pl.ANY)
    plane = (2, side - 1)
    return pl.pallas_call(
        functools.partial(backward_kernel, wide, narrow, items, chunks),
        in_specs=[
            vmem, anywhere, vmem, vmem, anywhere, anywhere, anywhere, vmem,
            anywhere, vmem, anywhere, vmem, vmem,
        ],
        out_specs=(vmem, vmem, anywhere, vmem, anywhere),
        out_shape=(
            jax.ShapeDtypeStruct((rows, features), bf16),
            jax.ShapeDtypeStruct((held_columns, features), bf16),
            jax.ShapeDtypeStruct((wide, 2, *piece), bf16),
            jax.ShapeDtypeStruct((8, features // narrow), f32),
            jax.ShapeDtypeStruct((lines, side, side, 2, *piece), bf16),
        ),
        scratch_shapes=[
            *[pltpu.VMEM((heads, depth, total_rows), bf16)] * 4,
            *[pltpu.VMEM((heads, HEAD_DIM, total_rows), f32)] * 3,
            pltpu.VMEM((held_columns, rows), bf16),
            pltpu.VMEM((2, rows, features), bf16),
            pltpu.VMEM((held_columns, features), f32),
            pltpu.VMEM((2, rows, features), bf16),
            pltpu.VMEM((lines, rows, features), bf16),
            pltpu.VMEM((lines, rows, features), bf16),
            pltpu.VMEM((lines + 1, rows, features), bf16),
            pltpu.VMEM((2, side - 1, held_columns // 2, features), bf16),
            pltpu.VMEM((2, side - 1, held_columns // 2, features), bf16),
            pltpu.VMEM((narrow, 8, features // narrow), f32),
            pltpu.VMEM((narrow - 1, 8, features // narrow), f32),
            pltpu.VMEM((8, features // narrow), f32),
            pltpu.VMEM((wide - 1, 8, features // narrow), f32),
            pltpu.VMEM((2, *piece), bf16),
            pltpu.VMEM((rows // chunks, features), f32),
            dma((heads, 3)),
            dma((heads,)),
            dma((narrow, heads)),
            dma((narrow, heads)),
            dma((2,)),
            dma(()),
            dma(()),
            dma((2,)),
            dma((lines,)),
            dma((lines, chunks)),
            dma((lines + 1, chunks)),
            dma((wide,)),
            dma((wide,)),
            dma(plane),
            dma(plane),
            dma(plane),
            dma(plane),
            dma((narrow - 1,)),
            dma((narrow - 1,)),
            dma((wide - 1,)),
            dma((wide - 1,)),
            *reduce_scratch(wide, narrow, *piece),
        ],
        compiler_params=pltpu.CompilerParams(
            vmem_limit_bytes=61 << 20, collective_id=2, has_side_effects=True
        ),
        name="backward",
    )(
        extras, packed, attended, log_total, grad, parts, proj_parts, weight, normed,
        tokens, middle, gain, norm_parts,
    )


def unpack_kernel(shard_ref, qkv_ref, qkv_out, proj_out, up_out, down_out):
    wide = shard_ref.shape[0]
    features = shard_ref.shape[3]
    columns = up_out.shape[1]
    groups = features // columns
    units, few = down_out.shape[0] // (2 * wide), proj_out.shape[0] // (2 * wide)
    for j in range(2 * wide):
        w, h = divmod(j, 2)
        for g in range(groups):
            up_out[(j * groups + g) * units : (j * groups + g + 1) * units, :] = shard_ref[
                w, h, 0:units, g * columns : (g + 1) * columns
            ].astype(f32)
        down_out[j * units : (j + 1) * units, :] = shard_ref[w, h, units : 2 * units, :].astype(f32)
        proj_out[j * few : (j + 1) * few, :] = shard_ref[w, h, 2 * units :, :].astype(f32)
    qkv_out[...] = qkv_ref[...].astype(f32).T


def unpack(shard, qkv, proj_shape, up_shape, down_shape):
    return pl.pallas_call(
        unpack_kernel,
        out_shape=tuple(
            jax.ShapeDtypeStruct(shape, f32)
            for shape in (qkv.shape[::-1], proj_shape, up_shape, down_shape)
        ),
        compiler_params=pltpu.CompilerParams(vmem_limit_bytes=48 << 20),
        name="unpack",
    )(shard, qkv)


class Gather:
    def __init__(self, wide, narrow, owns, out, mine, *semaphores):
        self.owns, self.out, self.mine = owns, out, mine
        self.w, self.n = lax.axis_index("wide"), lax.axis_index("narrow")
        self.side, self.lines = math.isqrt(wide), narrow // 2
        self.a, self.b = self.w // self.side, lax.rem(self.w, self.side)
        self.z, self.core = self.n // 2, lax.rem(self.n, 2)
        self.sibling = self.n + 1 - 2 * self.core
        (
            self.loaded, self.copied, self.own_sent, self.passed, self.line_got, self.first_sent, self.first_got,
            self.second_sent, self.second_got, self.f0_sent, self.f0_got, self.f1_sent, self.f1_got,
            self.f2_sent, self.f2_got, self.f3_sent, self.f3_got,
        ) = semaphores
        self.pairs = [(h, i) for i in range(1, self.side) for h in (0, 1)]

    @staticmethod
    def scratch(wide, narrow, piece):
        side, lines = math.isqrt(wide), narrow // 2
        dma = pltpu.SemaphoreType.DMA
        line, plane = (lines,), (lines, 2, side)
        shapes = [(2,), (), line, line, line, plane, plane, plane, plane, (), (), line, line]
        mine = pltpu.VMEM((side, side, 2, *piece), bf16)
        return [mine, *[dma(shape) for shape in shapes + [plane] * 4]]

    def other_a(self, i):
        return lax.rem(self.a + i, self.side)

    def other_b(self, i):
        return lax.rem(self.b + i, self.side)

    def own_on(self, way):
        return remote(
            self.mine.at[self.a, self.b], self.out.at[self.n, self.a, self.b],
            self.own_sent.at[self.z + way], self.line_got.at[self.z], self.w, self.n + 2 * way,
        )

    def pass_on(self, zs, way):
        piece = self.out.at[2 * zs + self.core, self.a, self.b]
        return remote(
            piece, piece, self.passed.at[zs], self.line_got.at[zs], self.w, self.n + 2 * way
        )

    def first(self, zs, h, i):
        shard = 2 * zs + self.core
        piece = self.out.at[shard, self.a, self.b, h]
        if h == 0:
            to, mine = self.a * self.side + self.other_b(i), self.b
        else:
            to, mine = self.other_a(i) * self.side + self.b, self.a
        return remote(
            piece, piece, self.first_sent.at[zs, h, i], self.first_got.at[zs, h, mine], to, self.n
        )

    def second(self, zs, h, i):
        shard = 2 * zs + self.core
        if h == 0:
            piece = self.out.at[shard, self.a, :, 0]
            to, mine = self.other_a(i) * self.side + self.b, self.a
        else:
            piece = self.out.at[shard, :, self.b, 1]
            to, mine = self.a * self.side + self.other_b(i), self.b
        return remote(
            piece, piece, self.second_sent.at[zs, h, i], self.second_got.at[zs, h, mine], to, self.n
        )

    def first_from(self, shard, h, i):
        if h == 0:
            return self.out.at[shard, self.a, self.other_b(i), 0], self.other_b(i)
        return self.out.at[shard, self.other_a(i), self.b, 1], self.other_a(i)

    def second_from(self, shard, h, i):
        if h == 0:
            return self.out.at[shard, self.other_a(i), :, 0], self.other_a(i)
        return self.out.at[shard, :, self.other_b(i), 1], self.other_b(i)

    def hand0(self):
        return remote(
            self.mine, self.out.at[self.n], self.f0_sent, self.f0_got, self.w, self.sibling
        )

    def hand1(self, zs):
        piece = self.out.at[2 * zs + self.core, self.a, self.b]
        return remote(piece, piece, self.f1_sent.at[zs], self.f1_got.at[zs], self.w, self.sibling)

    def hand2(self, zs, h, i):
        piece, k = self.first_from(2 * zs + self.core, h, i)
        return remote(
            piece, piece, self.f2_sent.at[zs, h, k], self.f2_got.at[zs, h, k], self.w, self.sibling
        )

    def hand3(self, zs, h, i):
        piece, k = self.second_from(2 * zs + self.core, h, i)
        return remote(
            piece, piece, self.f3_sent.at[zs, h, k], self.f3_got.at[zs, h, k], self.w, self.sibling
        )

    def load(self):
        copies, row = [], 0
        for k, own in enumerate(self.owns):
            part = self.mine.at[:, :, :, pl.ds(row, own.shape[3])]
            copies.append(pltpu.make_async_copy(own, part, self.loaded.at[k]))
            row += own.shape[3]
        return copies

    def keep(self):
        return pltpu.make_async_copy(self.mine, self.out.at[self.n], self.copied)

    def sides(self, d, act):
        if not 1 <= d <= self.lines - 1:
            return
        z, last = self.z, self.lines - 1

        @pl.when(z >= d)
        def _():
            act(z - d, 1, z < last)

        @pl.when(z + d <= last)
        def _():
            act(z + d, -1, z > 0)

    def begin(self):
        for copy in self.load():
            copy.start()
        for copy in self.load():
            copy.wait()

        @pl.when(self.z < self.lines - 1)
        def _():
            self.own_on(1).start()

        @pl.when(self.z > 0)
        def _():
            self.own_on(-1).start()

        self.keep().start()
        self.hand0().start()

    def one(self, zs, way, more):
        arrived(self.out.at[2 * zs + self.core, self.a, self.b], self.line_got.at[zs])

        @pl.when(more)
        def _():
            self.pass_on(zs, way).start()

        for h, i in self.pairs:
            self.first(zs, h, i).start()
        self.hand1(zs).start()

    def two(self, zs, way, more):
        for h in (0, 1):
            for i in range(1, self.side):
                piece, k = self.first_from(2 * zs + self.core, h, i)
                arrived(piece, self.first_got.at[zs, h, k])
            for i in range(1, self.side):
                self.second(zs, h, i).start()
        for h, i in self.pairs:
            self.hand2(zs, h, i).start()

    def three(self, zs, way, more):
        for h, i in self.pairs:
            piece, k = self.second_from(2 * zs + self.core, h, i)
            arrived(piece, self.second_got.at[zs, h, k])
            self.hand3(zs, h, i).start()

    def round(self, d):
        self.sides(d, self.one)
        self.sides(d - 1, self.two)
        self.sides(d - 2, self.three)

    def finish_side(self, zs, way, more):
        theirs = 2 * zs + 1 - self.core

        @pl.when(more)
        def _():
            self.pass_on(zs, way).wait_send()

        self.hand1(zs).wait_send()
        arrived(self.out.at[theirs, self.a, self.b], self.f1_got.at[zs])
        for h, i in self.pairs:
            self.first(zs, h, i).wait_send()
            self.second(zs, h, i).wait_send()
            self.hand2(zs, h, i).wait_send()
            self.hand3(zs, h, i).wait_send()
            piece, k = self.first_from(theirs, h, i)
            arrived(piece, self.f2_got.at[zs, h, k])
            piece, k = self.second_from(theirs, h, i)
            arrived(piece, self.f3_got.at[zs, h, k])

    def finish(self):
        @pl.when(self.z < self.lines - 1)
        def _():
            self.own_on(1).wait_send()

        @pl.when(self.z > 0)
        def _():
            self.own_on(-1).wait_send()

        self.keep().wait()
        self.hand0().wait_send()
        arrived(self.out.at[self.sibling], self.f0_got)
        for d in range(1, self.lines):
            self.sides(d, self.finish_side)


def start_kernel(
    wide, narrow, length_ref, token_ref, gain_ref, bias_ref, weight_ref, own_ref,
    normed, packed, turned, extras, gathered, line_sent, line_got, sib_sent, sib_got, *gather_refs,
):
    gather = Gather(wide, narrow, [own_ref], gathered, *gather_refs)
    w, n, z, core = gather.w, gather.n, gather.z, gather.core
    lines, sibling = gather.lines, gather.sibling
    rows = token_ref.shape[0]

    greet_all(wide, narrow, w, n)

    def norm_rows(j, carry):
        part = pl.ds(pl.multiple_of(j * 64, 64), 64)
        values = token_ref[part, :].astype(f32)
        centred = values - jnp.mean(values, axis=-1, keepdims=True)
        variance = jnp.mean(centred * centred, axis=-1, keepdims=True)
        normed[n, part, :] = (
            centred * lax.rsqrt(variance + epsilon) * as_row(gain_ref) + as_row(bias_ref)
        ).astype(bf16)
        return carry

    step = rows // CHUNKS

    def part_of(shard, c):
        return normed.at[shard, pl.ds(c * step, step)]

    def pass_on(zs, c, way):
        block = part_of(2 * zs + core, c)
        k = (1 - way) // 2
        return remote(block, block, line_sent.at[zs, c, k], line_got.at[zs, c], w, n + 2 * way)

    def hand(zs, c):
        block = part_of(2 * zs + core, c)
        return remote(block, block, sib_sent.at[zs, c], sib_got.at[zs, c], w, sibling)

    def project(owner, c):
        columns = pl.ds(pl.multiple_of(owner * rows + c * step, step), step)
        product = contract(turned[...], normed[owner, pl.ds(c * step, step)], 1, 1).astype(bf16)
        for j in range(product.shape[0] // HEAD_DIM):
            part = product[j * HEAD_DIM : (j + 1) * HEAD_DIM]
            if j % 3 == 0:
                part = part * jnp.asarray(HEAD_DIM**-0.5, bf16)
            packed[j * HEAD_DIM : (j + 1) * HEAD_DIM, columns] = part

    norm_blocks = rows // 64 // CHUNKS
    for c in range(CHUNKS):
        lax.fori_loop(c * norm_blocks, (c + 1) * norm_blocks, norm_rows, 0)
        if c == 0:
            greeted(wide, narrow)
            gather.begin()

        @pl.when(z < lines - 1)
        def _():
            pass_on(z, c, 1).start()

        @pl.when(z > 0)
        def _():
            pass_on(z, c, -1).start()

        hand(z, c).start()
    turned[...] = weight_ref[...].T
    mask_rows(length_ref, extras)
    for c in range(CHUNKS):
        project(n, c)

    def receive(c, zs, way, more):
        arrived(part_of(2 * zs + core, c), line_got.at[zs, c])

        @pl.when(more)
        def _():
            pass_on(zs, c, way).start()

        hand(zs, c).start()

    def project_side(zs, way, more):
        for c in range(CHUNKS):
            project(2 * zs + core, c)

    def project_sibling(zs, way, more):
        for c in range(CHUNKS):
            arrived(part_of(2 * zs + 1 - core, c), sib_got.at[zs, c])
            project(2 * zs + 1 - core, c)

    project_sibling(z, 0, None)
    for d in range(1, lines):
        gather.round(d)
        if d == lines - 1:
            gather.round(lines)
            gather.round(lines + 1)
        for c in range(CHUNKS):
            gather.sides(d, functools.partial(receive, c))
        if d > 1:
            gather.sides(d - 1, project_sibling)
        gather.sides(d, project_side)
    gather.sides(lines - 1, project_sibling)
    gather.finish()

    def sent_side(zs, way, more):
        for c in range(CHUNKS):
            hand(zs, c).wait_send()

            @pl.when(more)
            def _():
                pass_on(zs, c, way).wait_send()

    for c in range(CHUNKS):

        @pl.when(z < lines - 1)
        def _():
            pass_on(z, c, 1).wait_send()

        @pl.when(z > 0)
        def _():
            pass_on(z, c, -1).wait_send()

        hand(z, c).wait_send()
    for d in range(1, lines):
        gather.sides(d, sent_side)


def start(wide, narrow, lengths, tokens, gain, bias, weight, own):
    rows, features = tokens.shape
    lines = narrow // 2
    dma = pltpu.SemaphoreType.DMA
    vmem = pl.BlockSpec(memory_space=pltpu.VMEM)
    anywhere = pl.BlockSpec(memory_space=pl.ANY)
    return pl.pallas_call(
        functools.partial(start_kernel, wide, narrow),
        in_specs=[pl.BlockSpec(memory_space=pltpu.SMEM), vmem, vmem, vmem, vmem, anywhere],
        out_specs=(vmem, vmem, vmem, vmem, anywhere),
        out_shape=(
            jax.ShapeDtypeStruct((narrow, rows, features), bf16),
            jax.ShapeDtypeStruct((weight.shape[1], narrow * rows), bf16),
            jax.ShapeDtypeStruct((weight.shape[1], features), bf16),
            jax.ShapeDtypeStruct((2, EXTRA, narrow * rows), bf16),
            jax.ShapeDtypeStruct((narrow, *own.shape), bf16),
        ),
        scratch_shapes=[
            dma((lines, CHUNKS, 2)), dma((lines, CHUNKS)), dma((lines, CHUNKS)), dma((lines, CHUNKS)),
            *Gather.scratch(wide, narrow, own.shape[3:]),
        ],
        compiler_params=pltpu.CompilerParams(
            vmem_limit_bytes=58 << 20, collective_id=1, has_side_effects=True
        ),
        name="start",
    )(lengths, tokens, gain, bias, weight, own)


def body(
    tokens, cotangent, item_lengths, attn_gain, attn_bias, qkv_weight, proj_weight,
    mlp_gain, mlp_bias, up_weight, down_weight,
):
    items = item_lengths.shape[1]
    heads = qkv_weight.shape[1] // (3 * HEAD_DIM)
    wide, narrow = lax.axis_size("wide"), lax.axis_size("narrow")
    side = math.isqrt(wide)
    rows = narrow * tokens.shape[0]

    def cut(shard):
        return shard.reshape(side, side, 2, shard.shape[0] // (2 * wide), shard.shape[1])

    def split_parts(total):
        return total.reshape(narrow, side, side, 2, -1, total.shape[1])

    first = down_weight.shape[0] // (2 * wide)
    normed_all, packed, qkv_turned, extras, up_all = start(
        wide, narrow, item_lengths, tokens, attn_gain, attn_bias, qkv_weight, cut(up_weight)
    )
    normed_all = normed_all.reshape(rows, -1)
    packed = packed.reshape(heads, 3, HEAD_DIM, rows)
    attended, log_total, attended_rows, rest_all = attend_forward(
        wide, narrow, packed, extras, cut(down_weight), cut(proj_weight)
    )
    attended_rows = attended_rows.reshape(-1, tokens.shape[0])
    proj_all = rest_all
    if (rest_all.shape[4] - first) % 16:
        proj_all = rest_all[:, :, :, :, first:].reshape(-1, tokens.shape[1])
    output, grad_middle, grad_attended, grad_proj, grad_parts, norm_parts = mlp(
        attended_rows, proj_all, tokens, cotangent, mlp_gain, mlp_bias, up_all, rest_all, first
    )
    grad_attended = grad_attended.reshape(narrow, heads, HEAD_DIM, -1)
    grad_proj_parts = split_parts(grad_proj)
    grad_tokens, grad_qkv, grad_shard, shares, _ = backward(
        wide, narrow, extras, packed, attended, log_total, grad_attended, grad_parts,
        grad_proj_parts, qkv_turned, normed_all, tokens, grad_middle, attn_gain, norm_parts, items,
    )
    grad_qkv, grad_proj, grad_up, grad_down = unpack(
        grad_shard, grad_qkv, proj_weight.shape, up_weight.shape, down_weight.shape
    )
    return (
        output, grad_tokens, shares[0], shares[1], grad_qkv, grad_proj,
        shares[2], shares[3], grad_up, grad_down,
    )


def solution(mesh):
    by_rows = P(("wide", "narrow"), None)
    return jax.shard_map(
        body,
        mesh=mesh,
        in_specs=(
            by_rows, by_rows, P("wide", None), P(), P(), P(None, "narrow"), P("narrow", None),
            P(), P(), P(None, "narrow"), P("narrow", None),
        ),
        out_specs=(
            by_rows, by_rows, P("narrow"), P("narrow"), P(None, "narrow"), P("narrow", None),
            P("narrow"), P("narrow"), P(None, "narrow"), P("narrow", None),
        ),
        check_vma=False,
    )
```

```python
import functools
import math

import jax
import jax.numpy as jnp
from jax import lax
from jax.experimental import pallas as pl
from jax.experimental.pallas import tpu as pltpu
from jax.sharding import PartitionSpec as P

HEAD_DIM = 64
EXTRA = 16
CHUNKS = 2
REDUCE_START, REDUCE_STEP, REDUCE_FIRST, REDUCE_SECOND, SPREAD_AT = 3, 11, 9, 13, 8
EARLY_RELAY = 17
EXCLUDED = -1e30
bf16 = jnp.bfloat16
f32 = jnp.float32
MESH = pl.DeviceIdType.MESH
epsilon = 1e-05


def mask_rows(length_ref, extras):
    items = length_ref.shape[1]
    rows = extras.shape[2]
    position = lax.broadcasted_iota(jnp.int32, (EXTRA, rows), 1)
    extra = lax.broadcasted_iota(jnp.int32, (EXTRA, rows), 0)
    segment, end = jnp.zeros((EXTRA, rows), jnp.int32), 0
    for i in range(items):
        end = end + length_ref[0, i]
        segment = segment + jnp.where(position >= end, 1, 0)
    own = jnp.where(segment == extra, 1.0, 0.0)
    mask = jnp.where(extra <= items, 1.0, 0.0)
    ones = jnp.where(extra <= items + 3, 1.0, 0.0) * (1.0 - mask)
    extras[0] = (own * mask).astype(bf16)
    extras[1] = ((1.0 - own) * mask * EXCLUDED + ones).astype(bf16)


def forward_kernel(
    wide, narrow, qx_ref, kx_ref, q_ref, k_ref, v_ref, own_ref, more_ref, o_ref, log_ref, rows_ref, gathered,
    keys, ready, copied, sent, got, *gather_refs,
):
    gather = Gather(wide, narrow, [own_ref, more_ref], gathered, *gather_refs)
    w, n, lines = gather.w, gather.n, gather.lines
    head, step = pl.program_id(0), pl.program_id(1)
    moment = head * narrow + step
    width = q_ref.shape[-1] // narrow
    last = heads_of(ready, narrow) * narrow - 1

    moves = []
    for d in range(1, lines):
        moves += [
            (3.5 * d, functools.partial(gather.sides, d, gather.one)),
            (3.5 * d + 2.5, functools.partial(gather.sides, d, gather.two)),
            (3.5 * d + 5.5, functools.partial(gather.sides, d, gather.three)),
        ]
    moves.append((900.0, gather.finish))
    moves.sort(key=lambda move: move[0])

    def perform(lower, upper):
        for time, move in moves:
            if lower <= time < upper:
                move()

    @pl.when(moment == 0)
    def _():
        greet_all(wide, narrow, w, n)

    @pl.when(step == 0)
    def _():
        keys[...] = jnp.concatenate([k_ref[0], kx_ref[...]], axis=0).T

    @pl.when(moment == 0)
    def _():
        greeted(wide, narrow)
        gather.begin()

    for tick in range(last + 1):

        @pl.when(moment == tick)
        def _():
            perform(tick, tick + 1)

    owner = lax.rem(n + 1 + step, narrow)
    columns = pl.ds(pl.multiple_of(owner * width, width), width)
    query = jnp.concatenate(
        [q_ref[0, :, columns], qx_ref[:, columns]], axis=0
    )
    maximum = jnp.full((1, width), -3e38, f32)
    total, gathered_values = 0.0, 0.0
    half = keys.shape[0] // 2
    for part in (pl.ds(0, half), pl.ds(half, half)):
        scores = jnp.dot(keys[part, :], query, preferred_element_type=f32)
        larger = jnp.maximum(maximum, jnp.max(scores, axis=0, keepdims=True))
        shrink = jnp.exp(maximum - larger)
        raised = jnp.exp(scores - larger)
        total = shrink * total + jnp.sum(raised, axis=0, keepdims=True)
        gathered_values = shrink * gathered_values + jnp.dot(
            v_ref[0, :, part], raised.astype(bf16), preferred_element_type=f32
        )
        maximum = larger
    result = (gathered_values / total).astype(bf16)
    o_ref[0, :, columns] = result
    log_ref[0, :, columns] = maximum + jnp.log(total)
    ready[moment] = result

    def deliver(k, owner, h):
        return remote(ready.at[k], rows_ref.at[n, h], sent.at[k], got.at[n, h], w, owner)

    def deliver_here(k, h):
        return pltpu.make_async_copy(ready.at[k], rows_ref.at[n, h], copied.at[h])

    @pl.when(step < narrow - 1)
    def _():
        deliver(moment, owner, head).start()

    @pl.when(step == narrow - 1)
    def _():
        deliver_here(moment, head).start()

    @pl.when(moment == last)
    def _():
        perform(last + 1, 1000)
        for h in range((last + 1) // narrow):
            deliver_here(h * narrow + narrow - 1, h).wait()
            for t in range(narrow - 1):
                deliver(h * narrow + t, lax.rem(n + 1 + t, narrow), h).wait_send()
                source = lax.rem(n + narrow - 1 - t, narrow)
                arrived(rows_ref.at[source, h], got.at[source, h])


def heads_of(ready, narrow):
    return ready.shape[0] // narrow


def attend_forward(wide, narrow, packed, extras, own, more):
    heads, _, _, rows = packed.shape
    width = rows // narrow
    gathered = (narrow, *own.shape[:3], own.shape[3] + more.shape[3], own.shape[4])
    dma = pltpu.SemaphoreType.DMA

    def whole(j):
        return pl.BlockSpec((1, None, HEAD_DIM, rows), lambda h, i: (h, j, 0, 0))

    def extra(j):
        return pl.BlockSpec((None, EXTRA, rows), lambda h, i: (j, 0, 0))

    anywhere = pl.BlockSpec(memory_space=pl.ANY)
    return pl.pallas_call(
        functools.partial(forward_kernel, wide, narrow),
        grid=(heads, narrow),
        in_specs=[extra(0), extra(1), whole(0), whole(1), whole(2), anywhere, anywhere],
        out_specs=(
            pl.BlockSpec((1, HEAD_DIM, rows), lambda h, i: (h, 0, 0)),
            pl.BlockSpec((1, 1, rows), lambda h, i: (h, 0, 0)),
            anywhere,
            anywhere,
        ),
        out_shape=(
            jax.ShapeDtypeStruct((heads, HEAD_DIM, rows), bf16),
            jax.ShapeDtypeStruct((heads, 1, rows), f32),
            jax.ShapeDtypeStruct((narrow, heads, HEAD_DIM, width), bf16),
            jax.ShapeDtypeStruct(gathered, bf16),
        ),
        scratch_shapes=[
            pltpu.VMEM((rows, HEAD_DIM + EXTRA), bf16),
            pltpu.VMEM((heads * narrow, HEAD_DIM, width), bf16),
            dma((heads,)),
            dma((heads * narrow,)),
            dma((narrow, heads)),
            *Gather.scratch(wide, narrow, gathered[4:]),
        ],
        compiler_params=pltpu.CompilerParams(
            vmem_limit_bytes=58 << 20, collective_id=4, has_side_effects=True
        ),
        name="attend_forward",
    )(extras, extras, packed, packed, packed, own, more)


def remote(src, dst, sent, received, wide_to, narrow_to):
    return pltpu.make_async_remote_copy(
        src_ref=src,
        dst_ref=dst,
        send_sem=sent,
        recv_sem=received,
        device_id=(wide_to, narrow_to),
        device_id_type=MESH,
    )


def arrived(ref, semaphore):
    pltpu.make_async_copy(ref, ref, semaphore).wait()


def greet_all(wide, narrow, w, n):
    barrier = pltpu.get_barrier_semaphore()

    def column(t, carry):
        pl.semaphore_signal(
            barrier, inc=1, device_id=(w, lax.rem(n + t, narrow)), device_id_type=MESH
        )
        return carry

    def plane(t, carry):
        pl.semaphore_signal(
            barrier, inc=1, device_id=(lax.rem(w + t, wide), n), device_id_type=MESH
        )
        return carry

    lax.fori_loop(1, narrow, column, 0)
    lax.fori_loop(1, wide, plane, 0)


def greeted(wide, narrow):
    pl.semaphore_wait(pltpu.get_barrier_semaphore(), narrow + wide - 2)


def accumulate(into, *others):
    rows = into.shape[0]
    few = max([d for d in (16, 32, 48, 64) if rows % d == 0], default=rows)

    def piece(j, carry):
        part = pl.ds(j * few if rows == few else pl.multiple_of(j * few, few), few)
        total = into[part, :].astype(f32)
        for other in others:
            total = total + other[part, :].astype(f32)
        into[part, :] = total.astype(bf16)
        return carry

    if rows == few:
        piece(0, 0)
    else:
        lax.fori_loop(0, rows // few, piece, 0)


def reduce_steps(
    wide, narrow, parts, proj_parts, landed, final, held, staged, from_first, from_second, from_line,
    mine, loaded, sib_sent, sib_got, first_sent, first_got, second_sent, second_got, line_sent, line_got,
):
    w, n = lax.axis_index("wide"), lax.axis_index("narrow")
    side, lines = math.isqrt(wide), narrow // 2
    a, b, z, core = w // side, lax.rem(w, side), n // 2, lax.rem(n, 2)
    sibling = n + 1 - 2 * core
    slots = held.shape[0]
    most, least = parts.shape[4], proj_parts.shape[4]
    sources = [(parts, pl.ds(0, most)), (proj_parts, pl.ds(most, least))]
    order = [lax.rem(z + 1 + j, lines) for j in range(lines)]
    halves = [(h, i) for i in range(1, side) for h in (0, 1)]

    def other_a(i):
        return lax.rem(a + i, side)

    def other_b(i):
        return lax.rem(b + i, side)

    def to_sibling(j):
        shard = 2 * order[j] + 1 - core
        return [
            remote(
                src.at[shard], landed.at[j, :, :, :, rows],
                sib_sent.at[k, j], sib_got.at[k, j], w, sibling,
            )
            for k, (src, rows) in enumerate(sources)
        ]

    def load(j):
        shard, slot = 2 * order[j] + core, j % slots
        return [
            pltpu.make_async_copy(src.at[shard], held.at[slot, :, :, :, rows], loaded.at[k])
            for k, (src, rows) in enumerate(sources)
        ]

    def stage(j):
        return pltpu.make_async_copy(landed.at[j], staged, loaded.at[2])

    def first(j, h, i):
        slot, k = j % slots, i - 1
        if h == 0:
            src, to = held.at[slot, other_a(i), :, 0], other_a(i) * side + b
        else:
            src, to = held.at[slot, :, other_b(i), 1], a * side + other_b(i)
        return remote(
            src, from_first.at[j, h, k], first_sent.at[j, h, k], first_got.at[j, h, k], to, n
        )

    def second(j, h, i):
        slot, k = j % slots, i - 1
        if h == 0:
            src, to = held.at[slot, a, other_b(i), 0], a * side + other_b(i)
        else:
            src, to = held.at[slot, other_a(i), b, 1], other_a(i) * side + b
        return remote(
            src, from_second.at[j, h, k], second_sent.at[j, h, k], second_got.at[j, h, k], to, n
        )

    def along(j):
        zs = order[j]
        place = jnp.where(z < zs, z, z - 1)
        return remote(
            held.at[j % slots, a, b], from_line.at[place], line_sent.at[j], line_got.at[place],
            w, 2 * zs + core,
        )

    def begin():
        for copy in to_sibling(0):
            copy.start()

    def sent(j):
        for h, i in halves:
            first(j, h, i).wait_send()
            second(j, h, i).wait_send()

        if j < lines - 1:
            along(j).wait_send()

    def combine(j):
        slot = j % slots
        if j + 1 < lines:
            for copy in to_sibling(j + 1):
                copy.start()
        if j >= slots:
            sent(j - slots)
        for copy in load(j):
            copy.start()
        for k, (_, rows) in enumerate(sources):
            arrived(landed.at[j, :, :, :, rows], sib_got.at[k, j])
        stage(j).start()
        for copy in load(j):
            copy.wait()
        stage(j).wait()

        def piece(t, carry):
            p, q = t // side, lax.rem(t, side)
            for h in (0, 1):
                accumulate(held.at[slot, p, q, h], staged.at[p, q, h])
            return carry

        lax.fori_loop(0, wide, piece, 0)
        for h, i in halves:
            first(j, h, i).start()

    def narrow_down(j):
        slot = j % slots
        for h in (0, 1):
            for i in range(1, side):
                arrived(from_first.at[j, h, i - 1], first_got.at[j, h, i - 1])

            def piece(t, carry, h=h):
                into = held.at[slot, a, t, 0] if h == 0 else held.at[slot, t, b, 1]
                accumulate(into, *[from_first.at[j, h, i, t] for i in range(side - 1)])
                return carry

            lax.fori_loop(0, side, piece, 0)
        for h, i in halves:
            second(j, h, i).start()

    def send_home(j):
        slot = j % slots
        for h, i in halves:
            arrived(from_second.at[j, h, i - 1], second_got.at[j, h, i - 1])
        for h in (0, 1):
            accumulate(
                held.at[slot, a, b, h], *[from_second.at[j, h, i] for i in range(side - 1)]
            )

        if j < lines - 1:
            along(j).start()
        else:
            mine[...] = held[slot, a, b]

    def finish():
        for place in range(lines - 1):
            arrived(from_line.at[place], line_got.at[place])
        for h in (0, 1):
            total = mine[h].astype(f32)
            for place in range(lines - 1):
                total = total + from_line[place, h].astype(f32)
            final[h] = total.astype(bf16)

    def close():
        for j in range(lines):
            for copy in to_sibling(j):
                copy.wait_send()
        for j in range(max(0, lines - slots), lines):
            sent(j)

    steps = [(0.0, begin)]
    for j in range(lines):
        at = REDUCE_START + REDUCE_STEP * j
        steps += [
            (at, functools.partial(combine, j)),
            (at + REDUCE_FIRST, functools.partial(narrow_down, j)),
            (at + REDUCE_SECOND, functools.partial(send_home, j)),
        ]
    return sorted(steps, key=lambda step: step[0]), finish, close


def reduce_scratch(wide, narrow, rows, features, slots=3):
    side, lines = math.isqrt(wide), narrow // 2
    dma = pltpu.SemaphoreType.DMA
    plane = (lines, 2, side - 1)
    return [
        pltpu.VMEM((slots, side, side, 2, rows, features), bf16),
        pltpu.VMEM((side, side, 2, rows, features), bf16),
        pltpu.VMEM((lines, 2, side - 1, side, rows, features), bf16),
        pltpu.VMEM((lines, 2, side - 1, rows, features), bf16),
        pltpu.VMEM((lines - 1, 2, rows, features), bf16),
        pltpu.VMEM((2, rows, features), bf16),
        *[dma(shape) for shape in [(3,), (2, lines), (2, lines), plane, plane, plane, plane]],
        dma((lines,)),
        dma((lines - 1,)),
    ]


def as_row(ref):
    return ref[...].astype(f32).reshape(1, -1)


def contract(left, right, left_axis, right_axis):
    return lax.dot_general(
        left, right, (((left_axis,), (right_axis,)), ((), ())), preferred_element_type=f32
    )


def gelu_pair(values):
    half = 0.5 + 0.5 * lax.erf(values * 0.7071067811865476)
    slope = half + values * (jnp.exp(values * values * -0.5) * 0.3989422804014327)
    return values * half, slope


def mlp_kernel(
    att_ref, rest_ref, token_ref, cot_ref, gain_ref, bias_ref, up_ref, down_ref,
    out_ref, middle_out, att_out, proj_out, parts_ref, norm_ref,
    middle, expand, out_total, expand_total, proj_ref, proj_got,
):
    step = pl.program_id(0)
    rows, features = token_ref.shape
    few = 64

    def by_rows(change):
        def body(j, carry):
            return change(pl.ds(pl.multiple_of(j * few, few), few), carry)

        return body

    if rest_ref.ndim == 2:
        fetch = pltpu.make_async_copy(rest_ref, proj_ref, proj_got)
    else:
        few_rows = rest_ref.shape[4] - down_ref.shape[4]
        fetch = pltpu.make_async_copy(
            rest_ref.at[:, :, :, :, pl.ds(down_ref.shape[4], few_rows)],
            proj_ref.reshape(*rest_ref.shape[:4], few_rows, features),
            proj_got,
        )

    @pl.when(step == 0)
    def _():
        fetch.start()
        fetch.wait()
        middle[...] = token_ref[...].astype(f32) + contract(att_ref[...], proj_ref[...], 0, 0)
        out_total[...] = jnp.zeros_like(out_total)
        expand_total[...] = jnp.zeros_like(expand_total)

        def norm(part, carry):
            values = middle[part, :]
            centred = values - jnp.mean(values, axis=-1, keepdims=True)
            variance = jnp.mean(centred * centred, axis=-1, keepdims=True)
            expand[part, :] = (
                centred * lax.rsqrt(variance + epsilon) * as_row(gain_ref) + as_row(bias_ref)
            ).astype(bf16)
            return carry

        lax.fori_loop(0, rows // few, by_rows(norm), 0)

    def flat(ref):
        if ref.shape[4] % 16:
            return ref[0].astype(f32).reshape(-1, ref.shape[5]).astype(bf16)
        return ref[0].reshape(-1, ref.shape[5])

    up, down = flat(up_ref), flat(down_ref)
    units = down_ref.shape[4]
    pieces = up_ref.shape[1:4]
    columns = up_ref.shape[5]
    hidden_parts, grad_parts = [], []
    for part in (pl.ds(0, rows // 2), pl.ds(rows // 2, rows // 2)):
        hidden, slope = gelu_pair(
            jnp.dot(expand[part, :], up, preferred_element_type=f32)
        )
        grad_pre = (contract(cot_ref[part, :], down, 1, 1) * slope).astype(bf16)
        hidden = hidden.astype(bf16)
        out_total[part, :] += jnp.dot(hidden, down, preferred_element_type=f32)
        expand_total[part, :] += contract(grad_pre, up, 1, 1)
        hidden_parts.append(hidden)
        grad_parts.append(grad_pre)
    grad_up = contract(expand[...], jnp.concatenate(grad_parts, axis=0), 0, 0)
    grad_down = contract(jnp.concatenate(hidden_parts, axis=0), cot_ref[...], 0, 0)
    groups = features // columns
    grad_up = grad_up.reshape(*pieces, groups, units, columns)
    for g in range(groups):
        parts_ref[0, :, :, :, 0:units, g * columns : (g + 1) * columns] = grad_up[
            :, :, :, g
        ].astype(bf16)
    parts_ref[0, :, :, :, units : 2 * units, :] = grad_down.reshape(
        *pieces, units, features
    ).astype(bf16)

    @pl.when(step == pl.num_programs(0) - 1)
    def _():
        def finish_rows(part, carry):
            gain_sum, bias_sum = carry
            values = middle[part, :]
            out_ref[part, :] = (values + out_total[part, :]).astype(bf16)
            centred = values - jnp.mean(values, axis=-1, keepdims=True)
            inverse = lax.rsqrt(jnp.mean(centred * centred, axis=-1, keepdims=True) + epsilon)
            scaled = centred * inverse
            grad = expand_total[part, :]
            term = grad * as_row(gain_ref)
            back = inverse * (
                term
                - jnp.mean(term, axis=-1, keepdims=True)
                - scaled * jnp.mean(term * scaled, axis=-1, keepdims=True)
            )
            total = cot_ref[part, :].astype(f32) + back
            middle_out[part, :] = total
            expand[part, :] = total.astype(bf16)
            gain_sum = gain_sum + jnp.sum(grad * scaled, axis=0, keepdims=True)
            bias_sum = bias_sum + jnp.sum(grad, axis=0, keepdims=True)
            return gain_sum, bias_sum

        start = (jnp.zeros((1, features), f32), jnp.zeros((1, features), f32))
        gain_sum, bias_sum = lax.fori_loop(0, rows // few, by_rows(finish_rows), start)
        row = lax.broadcasted_iota(jnp.int32, (8, features), 0)
        norm_ref[...] = jnp.where(row == 2, gain_sum, jnp.where(row == 3, bias_sum, 0.0))
        branch = expand[...]
        att_out[...] = contract(proj_ref[...], branch, 1, 1).astype(bf16)
        proj_out[...] = jnp.dot(att_ref[...], branch, preferred_element_type=f32).astype(bf16)


def mlp(attended, rest, tokens, cotangent, gain, bias, up_all, down_all, units):
    rows, features = tokens.shape
    narrow, side = up_all.shape[:2]
    proj_shape = (attended.shape[0], features)

    def whole(*shape):
        return pl.BlockSpec(shape, lambda i: (0,) * len(shape))

    def weights(*piece):
        return pl.BlockSpec((1, side, side, 2, *piece), lambda i: (i, 0, 0, 0, 0, 0))

    return pl.pallas_call(
        mlp_kernel,
        grid=(narrow,),
        in_specs=[
            whole(*attended.shape),
            pl.BlockSpec(memory_space=pl.ANY),
            whole(rows, features),
            whole(rows, features),
            whole(*gain.shape),
            whole(*bias.shape),
            weights(*up_all.shape[4:]),
            weights(units, features),
        ],
        out_specs=(
            whole(rows, features),
            whole(rows, features),
            whole(*attended.shape),
            whole(*proj_shape),
            pl.BlockSpec(
                (1, side, side, 2, 2 * units, features), lambda i: (i, 0, 0, 0, 0, 0)
            ),
            whole(8, features),
        ),
        out_shape=(
            jax.ShapeDtypeStruct((rows, features), bf16),
            jax.ShapeDtypeStruct((rows, features), f32),
            jax.ShapeDtypeStruct(attended.shape, bf16),
            jax.ShapeDtypeStruct(proj_shape, bf16),
            jax.ShapeDtypeStruct((narrow, side, side, 2, 2 * units, features), bf16),
            jax.ShapeDtypeStruct((8, features), f32),
        ),
        scratch_shapes=[
            pltpu.VMEM((rows, features), f32),
            pltpu.VMEM((rows, features), bf16),
            pltpu.VMEM((rows, features), f32),
            pltpu.VMEM((rows, features), f32),
            pltpu.VMEM(proj_shape, bf16),
            pltpu.SemaphoreType.DMA(()),
        ],
        compiler_params=pltpu.CompilerParams(vmem_limit_bytes=58 << 20),
        name="mlp",
    )(attended, rest, tokens, cotangent, gain, bias, up_all, down_all)


def backward_kernel(
    wide, narrow, items, chunks,
    extra_ref, packed_ref, att_ref, log_ref, own_ref, parts_ref, proj_parts_ref, weight_ref,
    normed_ref, token_ref, middle_ref, gain_ref, norm_ref,
    tokens_out, qkv_out, shard_out, norms_out, landed,
    keys, values, queries, grads, grad_q, grad_k, grad_v, block_grad,
    normed, total_qkv, for_sibling, from_sibling, held, from_line,
    first_qkv, second_qkv, norms, norm_column, norm_half, norm_plane, piece,
    middle,
    packed_got, own_got, do_sent, do_got, normed_got, middle_got, copied, sib_sent, sib_got,
    line_sent, line_got, piece_sent, piece_got, first_sent, first_got, second_sent, second_got,
    column_sent, column_got, plane_sent, plane_got, *reduce_refs,
):
    w, n = lax.axis_index("wide"), lax.axis_index("narrow")
    side, lines = math.isqrt(wide), narrow // 2
    a, b, z, core = w // side, lax.rem(w, side), n // 2, lax.rem(n, 2)
    sibling = n + 1 - 2 * core
    heads = keys.shape[0]
    rows, features = token_ref.shape
    step = rows // chunks
    lower = z < lines // 2
    moves, reduce_finish, reduce_close = reduce_steps(
        wide, narrow, parts_ref, proj_parts_ref, landed, piece, *reduce_refs
    )

    def line_at(k):
        climbing = jnp.where(
            k < lines - 1 - z, lines - 1 - k, jnp.where(k < lines - 1, k - (lines - 1 - z), z)
        )
        falling = jnp.where(k < z, k, jnp.where(k < lines - 1, lines - 1 - (k - z), z))
        return jnp.where(lower, climbing, falling)

    def block_at(j):
        odd = lax.rem(j, 2)
        return 2 * line_at(j // 2) + jnp.where(odd == 1, core, 1 - core)

    def columns(owner):
        return pl.ds(pl.multiple_of(owner * rows, rows), rows)

    def packed_copy(h, j):
        into = (queries, keys, values)[j]
        return pltpu.make_async_copy(
            packed_ref.at[h, j], into.at[h, pl.ds(0, HEAD_DIM)], packed_got.at[h, j]
        )

    def keep(h):
        return pltpu.make_async_copy(
            own_ref.at[n, h], grads.at[h, pl.ds(0, HEAD_DIM), columns(n)], own_got.at[h]
        )

    def deliver(t, h):
        to = lax.rem(n + t, narrow)
        return remote(
            own_ref.at[to, h], grads.at[h, pl.ds(0, HEAD_DIM), columns(n)],
            do_sent.at[t, h], do_got.at[n, h], w, to,
        )

    def fetch(j):
        owner = block_at(j)
        return pltpu.make_async_copy(
            normed_ref.at[pl.ds(pl.multiple_of(owner * rows, rows), rows)],
            normed.at[lax.rem(j, 2)], normed_got.at[lax.rem(j, 2)],
        )

    for h in range(heads):
        for j in range(3):
            packed_copy(h, j).start()
        keep(h).start()
    fetch(0).start()
    greet_all(wide, narrow, w, n)
    grad_q[...] = jnp.zeros_like(grad_q)
    grad_k[...] = jnp.zeros_like(grad_k)
    grad_v[...] = jnp.zeros_like(grad_v)
    total_qkv[...] = jnp.zeros_like(total_qkv)
    greeted(wide, narrow)
    for t in range(1, narrow):
        for h in range(heads):
            deliver(t, h).start()
    for h in range(heads):
        keys[h, HEAD_DIM:, :] = extra_ref[1]
        values[h, HEAD_DIM:, :] = extra_ref[1]
    for h in range(heads):
        for j in range(3):
            packed_copy(h, j).wait()
        keep(h).wait()

    row = lax.broadcasted_iota(jnp.int32, (EXTRA, rows), 0) - items

    def pieces(term, base):
        high = term.astype(bf16).astype(f32)
        mid = (term - high).astype(bf16).astype(f32)
        small = term - high - mid
        return jnp.where(
            row == 1, high, jnp.where(row == 2, mid, jnp.where(row == 3, small, base))
        ).astype(bf16)

    def prepare(j):
        owner = block_at(j)
        where = columns(owner)

        @pl.when(owner != n)
        def _():
            for h in range(heads):
                arrived(grads.at[h, pl.ds(0, HEAD_DIM), where], do_got.at[owner, h])

        for h in range(heads):
            grad = grads[h, 0:HEAD_DIM, where].astype(f32)
            inner = jnp.sum(grad * att_ref[h, :, where].astype(f32), axis=0, keepdims=True)
            grads[h, HEAD_DIM:, where] = pieces(-inner, jnp.zeros((EXTRA, rows), f32))
            queries[h, HEAD_DIM:, where] = pieces(
                -log_ref[h, :, where], extra_ref[0, :, where].astype(f32)
            )

    def to_sibling(zs, slot):
        return remote(
            for_sibling.at[slot], from_sibling.at[zs], sib_sent.at[slot], sib_got.at[zs], w, sibling
        )

    def pass_on(zs, c, up):
        part = pl.ds(c * step, step)
        place = zs if up else jnp.where(z - 1 == zs, lines, zs)
        return remote(
            held.at[zs, part], from_line.at[place, part], line_sent.at[zs, c],
            line_got.at[place, c], w, n + 2 if up else n - 2,
        )

    def relay(zs, c, up):
        part = pl.ds(c * step, step)
        arrived(from_line.at[zs, part], line_got.at[zs, c])
        accumulate(held.at[zs, part], from_line.at[zs, part])
        pass_on(zs, c, up).start()

    def early_relay():
        @pl.when(jnp.logical_and(lower, z >= 1))
        def _():
            for c in range(chunks):
                relay(lines - 1, c, True)

        @pl.when(jnp.logical_and(z >= lines // 2, z <= lines - 2))
        def _():
            for c in range(chunks):
                relay(0, c, False)

    def emit(j):
        j = jnp.asarray(j, jnp.int32)
        owner = block_at(j)
        where = columns(owner)
        for h in range(heads):
            for k, total in enumerate((grad_q, grad_k, grad_v)):
                at = (h * 3 + k) * HEAD_DIM
                value = total[h, :, where]
                block_grad[at : at + HEAD_DIM, :] = (
                    value * HEAD_DIM**-0.5 if k == 0 else value
                ).astype(bf16)
        zs, slot = line_at(j // 2), lax.rem(j // 2, 2)
        product = contract(block_grad[...], weight_ref[...], 0, 0).astype(bf16)

        @pl.when(lax.rem(j, 2) == 0)
        def _():
            @pl.when(j >= 4)
            def _():
                to_sibling(zs, slot).wait_send()

            for_sibling[slot] = product
            to_sibling(zs, slot).start()

        @pl.when(lax.rem(j, 2) == 1)
        def _():
            held[zs] = product

        fetch(j).wait()

        @pl.when(j < narrow - 1)
        def _():
            fetch(j + 1).start()

        total_qkv[...] += jnp.dot(
            block_grad[...], normed[lax.rem(j, 2)], preferred_element_type=f32
        )

        @pl.when(lax.rem(j, 2) == 1)
        def _():
            arrived(from_sibling.at[zs], sib_got.at[zs])
            accumulate(held.at[zs], from_sibling.at[zs])

            @pl.when(jnp.logical_and(z == 0, zs != z))
            def _():
                for c in range(chunks):
                    pass_on(zs, c, True).start()

            @pl.when(jnp.logical_and(z == lines - 1, zs != z))
            def _():
                for c in range(chunks):
                    pass_on(zs, c, False).start()

    def spread(t):
        return remote(
            piece, shard_out.at[w], piece_sent.at[t], piece_got.at[t], lax.rem(w + t, wide), n
        )

    stay = pltpu.make_async_copy(piece, shard_out.at[w], copied)

    def spread_all():
        reduce_finish()
        stay.start()
        for t in range(1, wide):
            spread(t).start()

    prepare(narrow - 1)
    pairs = narrow * narrow
    moves = moves + [(6 * narrow - 8 + EARLY_RELAY, early_relay), (pairs - SPREAD_AT, spread_all)]
    moves.sort(key=lambda move: move[0])
    ticks = {}
    for time, move in moves:
        ticks.setdefault(min(int(time), pairs - 1), []).append(move)

    def pair(p, carry):
        for tick, group in ticks.items():

            @pl.when(p == tick)
            def _():
                for move in group:
                    move()

        late = p - 2 * narrow
        stage = sum(
            (late >= j * (2 * narrow - 2 - j)).astype(jnp.int32) for j in range(1, narrow - 2)
        )
        r = late - stage * (2 * narrow - 2 - stage)
        across = r < narrow - stage
        near = late < 0
        qi = jnp.where(
            near,
            jnp.where(p < narrow, narrow - 1, narrow - 2),
            jnp.where(across, stage, 2 * stage + 1 + r - narrow),
        )
        ki = jnp.where(near, lax.rem(p, narrow), jnp.where(across, stage + r, stage))

        @pl.when((p == narrow) | (late == 0) | ((stage == 0) & (r >= narrow)))
        def _():
            prepare(qi)

        at_q, at_k = columns(block_at(qi)), columns(block_at(ki))
        for h in range(heads):
            probs = jnp.exp(contract(queries[h, :, at_q], keys[h, :, at_k], 0, 0))
            scores = (probs * contract(grads[h, :, at_q], values[h, :, at_k], 0, 0)).astype(bf16)
            grad_v[h, :, at_k] += jnp.dot(
                grads[h, 0:HEAD_DIM, at_q], probs.astype(bf16), preferred_element_type=f32
            )
            grad_k[h, :, at_k] += jnp.dot(
                queries[h, 0:HEAD_DIM, at_q], scores, preferred_element_type=f32
            )
            grad_q[h, :, at_q] += contract(keys[h, 0:HEAD_DIM, at_k], scores, 1, 1)

        @pl.when(r == 2 * (narrow - stage) - 4)
        def _():
            emit(stage)

        return carry

    lax.fori_loop(0, pairs, pair, 0)
    emit(narrow - 2)
    emit(narrow - 1)

    half = total_qkv.shape[0] // 2
    own_qkv, half_qkv = for_sibling.at[:, 0:half], normed.at[:, 0:half]
    for slot in range(min(2, lines)):
        to_sibling(0, slot).wait_send()
    for h in (0, 1):
        own_qkv[h] = total_qkv[h * half : (h + 1) * half].astype(bf16)
    halves = [(h, i) for i in range(1, side) for h in (0, 1)]

    def plane_at(h, i):
        if h == 0:
            return lax.rem(a + i, side) * side + b
        return a * side + lax.rem(b + i, side)

    def first(h, i):
        return remote(
            own_qkv.at[h], first_qkv.at[h, i - 1], first_sent.at[h, i - 1], first_got.at[h, i - 1],
            plane_at(h, i), n,
        )

    def second(h, i):
        return remote(
            half_qkv.at[h], second_qkv.at[h, i - 1], second_sent.at[h, i - 1],
            second_got.at[h, i - 1], plane_at(1 - h, i), n,
        )

    def qkv_second():
        for h, i in halves:
            arrived(first_qkv.at[h, i - 1], first_got.at[h, i - 1])
        for h in (0, 1):
            total = own_qkv[h].astype(f32)
            for i in range(1, side):
                total = total + first_qkv[h, i - 1].astype(f32)
            half_qkv[h] = total.astype(bf16)
        for h, i in halves:
            second(h, i).start()

    def qkv_last():
        for h, i in halves:
            arrived(second_qkv.at[h, i - 1], second_got.at[h, i - 1])
        for h in (0, 1):
            total = half_qkv[h].astype(f32)
            for i in range(1, side):
                total = total + second_qkv[h, i - 1].astype(f32)
            qkv_out[h * half : (h + 1) * half] = total.astype(bf16)

    for h, i in halves:
        first(h, i).start()

    def fetch_middle(c):
        return pltpu.make_async_copy(middle_ref.at[pl.ds(c * step, step)], middle, middle_got)

    fetch_middle(0).start()
    for t in range(1, lines):
        below, above = lines - 1 - (t - z), t - (lines - 1 - z)
        for c in range(chunks):
            if t < lines - 1:

                @pl.when((z >= 1) & (t >= z) & ~(lower & (t == z)))
                def _():
                    relay(below, c, True)

                @pl.when((z <= lines - 2) & (above >= 0) & ~((z >= lines // 2) & (above == 0)))
                def _():
                    relay(above, c, False)

    qkv_second()

    def zero_edges(at_edge, place):
        @pl.when(at_edge)
        def _():
            from_line[place] = jnp.zeros((rows, features), bf16)

    zero_edges(z == 0, z)
    zero_edges(z == lines - 1, lines)
    gain_sum = bias_sum = jnp.zeros((1, features), f32)
    for c in range(chunks):
        part = pl.ds(c * step, step)

        @pl.when(z >= 1)
        def _():
            arrived(from_line.at[z, part], line_got.at[z, c])

        @pl.when(z <= lines - 2)
        def _():
            arrived(from_line.at[lines, part], line_got.at[lines, c])

        fetch_middle(c).wait()

        def norm_rows(j, carry):
            gain_sum, bias_sum = carry
            few = pl.ds(pl.multiple_of(c * step + j * 32, 32), 32)
            near = pl.ds(pl.multiple_of(j * 32, 32), 32)
            grad = (
                held[z, few].astype(f32)
                + from_line[z, few].astype(f32)
                + from_line[lines, few].astype(f32)
            )
            values = token_ref[few, :].astype(f32)
            centred = values - jnp.mean(values, axis=-1, keepdims=True)
            inverse = lax.rsqrt(jnp.mean(centred * centred, axis=-1, keepdims=True) + epsilon)
            scaled = centred * inverse
            term = grad * as_row(gain_ref)
            back = inverse * (
                term
                - jnp.mean(term, axis=-1, keepdims=True)
                - scaled * jnp.mean(term * scaled, axis=-1, keepdims=True)
            )
            tokens_out[few, :] = (middle[near, :] + back).astype(bf16)
            gain_sum = gain_sum + jnp.sum(grad * scaled, axis=0, keepdims=True)
            bias_sum = bias_sum + jnp.sum(grad, axis=0, keepdims=True)
            return gain_sum, bias_sum

        gain_sum, bias_sum = lax.fori_loop(0, step // 32, norm_rows, (gain_sum, bias_sum))
        if c + 1 < chunks:
            fetch_middle(c + 1).start()

    row = lax.broadcasted_iota(jnp.int32, (8, features), 0)
    parts = jnp.where(row == 0, gain_sum, jnp.where(row == 1, bias_sum, norm_ref[...]))
    share = features // narrow
    for owner in range(narrow):
        norms[owner] = parts[:, owner * share : (owner + 1) * share]

    def down_column(t):
        to = lax.rem(n + t, narrow)
        return remote(
            norms.at[to], norm_column.at[t - 1], column_sent.at[t - 1], column_got.at[t - 1], w, to
        )

    def over_plane(t):
        return remote(
            norm_half, norm_plane.at[t - 1], plane_sent.at[t - 1], plane_got.at[t - 1],
            lax.rem(w + t, wide), n,
        )

    for t in range(1, narrow):
        down_column(t).start()
    total = norms[n]
    for t in range(1, narrow):
        arrived(norm_column.at[t - 1], column_got.at[t - 1])
        total = total + norm_column[t - 1]
    norm_half[...] = total
    for t in range(1, wide):
        over_plane(t).start()
    for t in range(1, wide):
        arrived(norm_plane.at[t - 1], plane_got.at[t - 1])
        total = total + norm_plane[t - 1]
    norms_out[...] = total

    qkv_last()
    stay.wait()
    reduce_close()
    for t in range(1, wide):
        spread(t).wait_send()
        arrived(shard_out.at[lax.rem(w + wide - t, wide)], piece_got.at[t])
        over_plane(t).wait_send()
    for t in range(1, narrow):
        down_column(t).wait_send()
        for h in range(heads):
            deliver(t, h).wait_send()
    for h, i in halves:
        first(h, i).wait_send()
        second(h, i).wait_send()
    for zs in range(lines):
        for c in range(chunks):

            @pl.when(zs > z)
            def _():
                pass_on(zs, c, True).wait_send()

            @pl.when(zs < z)
            def _():
                pass_on(zs, c, False).wait_send()


def backward(
    wide, narrow, extras, packed, attended, log_total, grad, parts, proj_parts, weight, normed,
    tokens, middle, gain, norm_parts, items, chunks=4,
):
    side, lines = math.isqrt(wide), narrow // 2
    heads, _, _, total_rows = packed.shape
    rows, features = tokens.shape
    held_columns = weight.shape[0]
    piece = (parts.shape[4] + proj_parts.shape[4], features)
    depth = HEAD_DIM + EXTRA
    dma = pltpu.SemaphoreType.DMA
    vmem = pl.BlockSpec(memory_space=pltpu.VMEM)
    anywhere = pl.BlockSpec(memory_space=pl.ANY)
    plane = (2, side - 1)
    return pl.pallas_call(
        functools.partial(backward_kernel, wide, narrow, items, chunks),
        in_specs=[
            vmem, anywhere, vmem, vmem, anywhere, anywhere, anywhere, vmem,
            anywhere, vmem, anywhere, vmem, vmem,
        ],
        out_specs=(vmem, vmem, anywhere, vmem, anywhere),
        out_shape=(
            jax.ShapeDtypeStruct((rows, features), bf16),
            jax.ShapeDtypeStruct((held_columns, features), bf16),
            jax.ShapeDtypeStruct((wide, 2, *piece), bf16),
            jax.ShapeDtypeStruct((8, features // narrow), f32),
            jax.ShapeDtypeStruct((lines, side, side, 2, *piece), bf16),
        ),
        scratch_shapes=[
            *[pltpu.VMEM((heads, depth, total_rows), bf16)] * 4,
            *[pltpu.VMEM((heads, HEAD_DIM, total_rows), f32)] * 3,
            pltpu.VMEM((held_columns, rows), bf16),
            pltpu.VMEM((2, rows, features), bf16),
            pltpu.VMEM((held_columns, features), f32),
            pltpu.VMEM((2, rows, features), bf16),
            pltpu.VMEM((lines, rows, features), bf16),
            pltpu.VMEM((lines, rows, features), bf16),
            pltpu.VMEM((lines + 1, rows, features), bf16),
            pltpu.VMEM((2, side - 1, held_columns // 2, features), bf16),
            pltpu.VMEM((2, side - 1, held_columns // 2, features), bf16),
            pltpu.VMEM((narrow, 8, features // narrow), f32),
            pltpu.VMEM((narrow - 1, 8, features // narrow), f32),
            pltpu.VMEM((8, features // narrow), f32),
            pltpu.VMEM((wide - 1, 8, features // narrow), f32),
            pltpu.VMEM((2, *piece), bf16),
            pltpu.VMEM((rows // chunks, features), f32),
            dma((heads, 3)),
            dma((heads,)),
            dma((narrow, heads)),
            dma((narrow, heads)),
            dma((2,)),
            dma(()),
            dma(()),
            dma((2,)),
            dma((lines,)),
            dma((lines, chunks)),
            dma((lines + 1, chunks)),
            dma((wide,)),
            dma((wide,)),
            dma(plane),
            dma(plane),
            dma(plane),
            dma(plane),
            dma((narrow - 1,)),
            dma((narrow - 1,)),
            dma((wide - 1,)),
            dma((wide - 1,)),
            *reduce_scratch(wide, narrow, *piece),
        ],
        compiler_params=pltpu.CompilerParams(
            vmem_limit_bytes=61 << 20, collective_id=2, has_side_effects=True
        ),
        name="backward",
    )(
        extras, packed, attended, log_total, grad, parts, proj_parts, weight, normed,
        tokens, middle, gain, norm_parts,
    )


def unpack_kernel(shard_ref, qkv_ref, qkv_out, proj_out, up_out, down_out):
    wide = shard_ref.shape[0]
    features = shard_ref.shape[3]
    columns = up_out.shape[1]
    groups = features // columns
    units, few = down_out.shape[0] // (2 * wide), proj_out.shape[0] // (2 * wide)
    for j in range(2 * wide):
        w, h = divmod(j, 2)
        for g in range(groups):
            up_out[(j * groups + g) * units : (j * groups + g + 1) * units, :] = shard_ref[
                w, h, 0:units, g * columns : (g + 1) * columns
            ].astype(f32)
        down_out[j * units : (j + 1) * units, :] = shard_ref[w, h, units : 2 * units, :].astype(f32)
        proj_out[j * few : (j + 1) * few, :] = shard_ref[w, h, 2 * units :, :].astype(f32)
    qkv_out[...] = qkv_ref[...].astype(f32).T


def unpack(shard, qkv, proj_shape, up_shape, down_shape):
    return pl.pallas_call(
        unpack_kernel,
        out_shape=tuple(
            jax.ShapeDtypeStruct(shape, f32)
            for shape in (qkv.shape[::-1], proj_shape, up_shape, down_shape)
        ),
        compiler_params=pltpu.CompilerParams(vmem_limit_bytes=48 << 20),
        name="unpack",
    )(shard, qkv)


class Gather:
    def __init__(self, wide, narrow, owns, out, mine, *semaphores):
        self.owns, self.out, self.mine = owns, out, mine
        self.w, self.n = lax.axis_index("wide"), lax.axis_index("narrow")
        self.side, self.lines = math.isqrt(wide), narrow // 2
        self.a, self.b = self.w // self.side, lax.rem(self.w, self.side)
        self.z, self.core = self.n // 2, lax.rem(self.n, 2)
        self.sibling = self.n + 1 - 2 * self.core
        (
            self.loaded, self.copied, self.own_sent, self.passed, self.line_got, self.first_sent, self.first_got,
            self.second_sent, self.second_got, self.f0_sent, self.f0_got, self.f1_sent, self.f1_got,
            self.f2_sent, self.f2_got, self.f3_sent, self.f3_got,
        ) = semaphores
        self.pairs = [(h, i) for i in range(1, self.side) for h in (0, 1)]

    @staticmethod
    def scratch(wide, narrow, piece):
        side, lines = math.isqrt(wide), narrow // 2
        dma = pltpu.SemaphoreType.DMA
        line, plane = (lines,), (lines, 2, side)
        shapes = [(2,), (), line, line, line, plane, plane, plane, plane, (), (), line, line]
        mine = pltpu.VMEM((side, side, 2, *piece), bf16)
        return [mine, *[dma(shape) for shape in shapes + [plane] * 4]]

    def other_a(self, i):
        return lax.rem(self.a + i, self.side)

    def other_b(self, i):
        return lax.rem(self.b + i, self.side)

    def own_on(self, way):
        return remote(
            self.mine.at[self.a, self.b], self.out.at[self.n, self.a, self.b],
            self.own_sent.at[self.z + way], self.line_got.at[self.z], self.w, self.n + 2 * way,
        )

    def pass_on(self, zs, way):
        piece = self.out.at[2 * zs + self.core, self.a, self.b]
        return remote(
            piece, piece, self.passed.at[zs], self.line_got.at[zs], self.w, self.n + 2 * way
        )

    def first(self, zs, h, i):
        shard = 2 * zs + self.core
        piece = self.out.at[shard, self.a, self.b, h]
        if h == 0:
            to, mine = self.a * self.side + self.other_b(i), self.b
        else:
            to, mine = self.other_a(i) * self.side + self.b, self.a
        return remote(
            piece, piece, self.first_sent.at[zs, h, i], self.first_got.at[zs, h, mine], to, self.n
        )

    def second(self, zs, h, i):
        shard = 2 * zs + self.core
        if h == 0:
            piece = self.out.at[shard, self.a, :, 0]
            to, mine = self.other_a(i) * self.side + self.b, self.a
        else:
            piece = self.out.at[shard, :, self.b, 1]
            to, mine = self.a * self.side + self.other_b(i), self.b
        return remote(
            piece, piece, self.second_sent.at[zs, h, i], self.second_got.at[zs, h, mine], to, self.n
        )

    def first_from(self, shard, h, i):
        if h == 0:
            return self.out.at[shard, self.a, self.other_b(i), 0], self.other_b(i)
        return self.out.at[shard, self.other_a(i), self.b, 1], self.other_a(i)

    def second_from(self, shard, h, i):
        if h == 0:
            return self.out.at[shard, self.other_a(i), :, 0], self.other_a(i)
        return self.out.at[shard, :, self.other_b(i), 1], self.other_b(i)

    def hand0(self):
        return remote(
            self.mine, self.out.at[self.n], self.f0_sent, self.f0_got, self.w, self.sibling
        )

    def hand1(self, zs):
        piece = self.out.at[2 * zs + self.core, self.a, self.b]
        return remote(piece, piece, self.f1_sent.at[zs], self.f1_got.at[zs], self.w, self.sibling)

    def hand2(self, zs, h, i):
        piece, k = self.first_from(2 * zs + self.core, h, i)
        return remote(
            piece, piece, self.f2_sent.at[zs, h, k], self.f2_got.at[zs, h, k], self.w, self.sibling
        )

    def hand3(self, zs, h, i):
        piece, k = self.second_from(2 * zs + self.core, h, i)
        return remote(
            piece, piece, self.f3_sent.at[zs, h, k], self.f3_got.at[zs, h, k], self.w, self.sibling
        )

    def load(self):
        copies, row = [], 0
        for k, own in enumerate(self.owns):
            part = self.mine.at[:, :, :, pl.ds(row, own.shape[3])]
            copies.append(pltpu.make_async_copy(own, part, self.loaded.at[k]))
            row += own.shape[3]
        return copies

    def keep(self):
        return pltpu.make_async_copy(self.mine, self.out.at[self.n], self.copied)

    def sides(self, d, act):
        if not 1 <= d <= self.lines - 1:
            return
        z, last = self.z, self.lines - 1

        @pl.when(z >= d)
        def _():
            act(z - d, 1, z < last)

        @pl.when(z + d <= last)
        def _():
            act(z + d, -1, z > 0)

    def begin(self):
        for copy in self.load():
            copy.start()
        for copy in self.load():
            copy.wait()

        @pl.when(self.z < self.lines - 1)
        def _():
            self.own_on(1).start()

        @pl.when(self.z > 0)
        def _():
            self.own_on(-1).start()

        self.keep().start()
        self.hand0().start()

    def one(self, zs, way, more):
        arrived(self.out.at[2 * zs + self.core, self.a, self.b], self.line_got.at[zs])

        @pl.when(more)
        def _():
            self.pass_on(zs, way).start()

        for h, i in self.pairs:
            self.first(zs, h, i).start()
        self.hand1(zs).start()

    def two(self, zs, way, more):
        for h in (0, 1):
            for i in range(1, self.side):
                piece, k = self.first_from(2 * zs + self.core, h, i)
                arrived(piece, self.first_got.at[zs, h, k])
            for i in range(1, self.side):
                self.second(zs, h, i).start()
        for h, i in self.pairs:
            self.hand2(zs, h, i).start()

    def three(self, zs, way, more):
        for h, i in self.pairs:
            piece, k = self.second_from(2 * zs + self.core, h, i)
            arrived(piece, self.second_got.at[zs, h, k])
            self.hand3(zs, h, i).start()

    def round(self, d):
        self.sides(d, self.one)
        self.sides(d - 1, self.two)
        self.sides(d - 2, self.three)

    def finish_side(self, zs, way, more):
        theirs = 2 * zs + 1 - self.core

        @pl.when(more)
        def _():
            self.pass_on(zs, way).wait_send()

        self.hand1(zs).wait_send()
        arrived(self.out.at[theirs, self.a, self.b], self.f1_got.at[zs])
        for h, i in self.pairs:
            self.first(zs, h, i).wait_send()
            self.second(zs, h, i).wait_send()
            self.hand2(zs, h, i).wait_send()
            self.hand3(zs, h, i).wait_send()
            piece, k = self.first_from(theirs, h, i)
            arrived(piece, self.f2_got.at[zs, h, k])
            piece, k = self.second_from(theirs, h, i)
            arrived(piece, self.f3_got.at[zs, h, k])

    def finish(self):
        @pl.when(self.z < self.lines - 1)
        def _():
            self.own_on(1).wait_send()

        @pl.when(self.z > 0)
        def _():
            self.own_on(-1).wait_send()

        self.keep().wait()
        self.hand0().wait_send()
        arrived(self.out.at[self.sibling], self.f0_got)
        for d in range(1, self.lines):
            self.sides(d, self.finish_side)


def start_kernel(
    wide, narrow, length_ref, token_ref, gain_ref, bias_ref, weight_ref, own_ref,
    normed, packed, turned, extras, gathered, line_sent, line_got, sib_sent, sib_got, *gather_refs,
):
    gather = Gather(wide, narrow, [own_ref], gathered, *gather_refs)
    w, n, z, core = gather.w, gather.n, gather.z, gather.core
    lines, sibling = gather.lines, gather.sibling
    rows = token_ref.shape[0]

    greet_all(wide, narrow, w, n)

    def norm_rows(j, carry):
        part = pl.ds(pl.multiple_of(j * 64, 64), 64)
        values = token_ref[part, :].astype(f32)
        centred = values - jnp.mean(values, axis=-1, keepdims=True)
        variance = jnp.mean(centred * centred, axis=-1, keepdims=True)
        normed[n, part, :] = (
            centred * lax.rsqrt(variance + epsilon) * as_row(gain_ref) + as_row(bias_ref)
        ).astype(bf16)
        return carry

    step = rows // CHUNKS

    def part_of(shard, c):
        return normed.at[shard, pl.ds(c * step, step)]

    def pass_on(zs, c, way):
        block = part_of(2 * zs + core, c)
        k = (1 - way) // 2
        return remote(block, block, line_sent.at[zs, c, k], line_got.at[zs, c], w, n + 2 * way)

    def hand(zs, c):
        block = part_of(2 * zs + core, c)
        return remote(block, block, sib_sent.at[zs, c], sib_got.at[zs, c], w, sibling)

    def project(owner, c):
        columns = pl.ds(pl.multiple_of(owner * rows + c * step, step), step)
        product = contract(turned[...], normed[owner, pl.ds(c * step, step)], 1, 1).astype(bf16)
        for j in range(product.shape[0] // HEAD_DIM):
            part = product[j * HEAD_DIM : (j + 1) * HEAD_DIM]
            if j % 3 == 0:
                part = part * jnp.asarray(HEAD_DIM**-0.5, bf16)
            packed[j * HEAD_DIM : (j + 1) * HEAD_DIM, columns] = part

    norm_blocks = rows // 64 // CHUNKS
    for c in range(CHUNKS):
        lax.fori_loop(c * norm_blocks, (c + 1) * norm_blocks, norm_rows, 0)
        if c == 0:
            greeted(wide, narrow)
            gather.begin()

        @pl.when(z < lines - 1)
        def _():
            pass_on(z, c, 1).start()

        @pl.when(z > 0)
        def _():
            pass_on(z, c, -1).start()

        hand(z, c).start()
    turned[...] = weight_ref[...].T
    mask_rows(length_ref, extras)
    for c in range(CHUNKS):
        project(n, c)

    def receive(c, zs, way, more):
        arrived(part_of(2 * zs + core, c), line_got.at[zs, c])

        @pl.when(more)
        def _():
            pass_on(zs, c, way).start()

        hand(zs, c).start()

    def project_side(zs, way, more):
        for c in range(CHUNKS):
            project(2 * zs + core, c)

    def project_sibling(zs, way, more):
        for c in range(CHUNKS):
            arrived(part_of(2 * zs + 1 - core, c), sib_got.at[zs, c])
            project(2 * zs + 1 - core, c)

    project_sibling(z, 0, None)
    for d in range(1, lines):
        gather.round(d)
        if d == lines - 1:
            gather.round(lines)
            gather.round(lines + 1)
        for c in range(CHUNKS):
            gather.sides(d, functools.partial(receive, c))
        if d > 1:
            gather.sides(d - 1, project_sibling)
        gather.sides(d, project_side)
    gather.sides(lines - 1, project_sibling)
    gather.finish()

    def sent_side(zs, way, more):
        for c in range(CHUNKS):
            hand(zs, c).wait_send()

            @pl.when(more)
            def _():
                pass_on(zs, c, way).wait_send()

    for c in range(CHUNKS):

        @pl.when(z < lines - 1)
        def _():
            pass_on(z, c, 1).wait_send()

        @pl.when(z > 0)
        def _():
            pass_on(z, c, -1).wait_send()

        hand(z, c).wait_send()
    for d in range(1, lines):
        gather.sides(d, sent_side)


def start(wide, narrow, lengths, tokens, gain, bias, weight, own):
    rows, features = tokens.shape
    lines = narrow // 2
    dma = pltpu.SemaphoreType.DMA
    vmem = pl.BlockSpec(memory_space=pltpu.VMEM)
    anywhere = pl.BlockSpec(memory_space=pl.ANY)
    return pl.pallas_call(
        functools.partial(start_kernel, wide, narrow),
        in_specs=[pl.BlockSpec(memory_space=pltpu.SMEM), vmem, vmem, vmem, vmem, anywhere],
        out_specs=(vmem, vmem, vmem, vmem, anywhere),
        out_shape=(
            jax.ShapeDtypeStruct((narrow, rows, features), bf16),
            jax.ShapeDtypeStruct((weight.shape[1], narrow * rows), bf16),
            jax.ShapeDtypeStruct((weight.shape[1], features), bf16),
            jax.ShapeDtypeStruct((2, EXTRA, narrow * rows), bf16),
            jax.ShapeDtypeStruct((narrow, *own.shape), bf16),
        ),
        scratch_shapes=[
            dma((lines, CHUNKS, 2)), dma((lines, CHUNKS)), dma((lines, CHUNKS)), dma((lines, CHUNKS)),
            *Gather.scratch(wide, narrow, own.shape[3:]),
        ],
        compiler_params=pltpu.CompilerParams(
            vmem_limit_bytes=58 << 20, collective_id=1, has_side_effects=True
        ),
        name="start",
    )(lengths, tokens, gain, bias, weight, own)


def body(
    tokens, cotangent, item_lengths, attn_gain, attn_bias, qkv_weight, proj_weight,
    mlp_gain, mlp_bias, up_weight, down_weight,
):
    items = item_lengths.shape[1]
    heads = qkv_weight.shape[1] // (3 * HEAD_DIM)
    wide, narrow = lax.axis_size("wide"), lax.axis_size("narrow")
    side = math.isqrt(wide)
    rows = narrow * tokens.shape[0]

    def cut(shard):
        return shard.reshape(side, side, 2, shard.shape[0] // (2 * wide), shard.shape[1])

    def split_parts(total):
        return total.reshape(narrow, side, side, 2, -1, total.shape[1])

    first = down_weight.shape[0] // (2 * wide)
    normed_all, packed, qkv_turned, extras, up_all = start(
        wide, narrow, item_lengths, tokens, attn_gain, attn_bias, qkv_weight, cut(up_weight)
    )
    normed_all = normed_all.reshape(rows, -1)
    packed = packed.reshape(heads, 3, HEAD_DIM, rows)
    attended, log_total, attended_rows, rest_all = attend_forward(
        wide, narrow, packed, extras, cut(down_weight), cut(proj_weight)
    )
    attended_rows = attended_rows.reshape(-1, tokens.shape[0])
    proj_all = rest_all
    if (rest_all.shape[4] - first) % 16:
        proj_all = rest_all[:, :, :, :, first:].reshape(-1, tokens.shape[1])
    output, grad_middle, grad_attended, grad_proj, grad_parts, norm_parts = mlp(
        attended_rows, proj_all, tokens, cotangent, mlp_gain, mlp_bias, up_all, rest_all, first
    )
    grad_attended = grad_attended.reshape(narrow, heads, HEAD_DIM, -1)
    grad_proj_parts = split_parts(grad_proj)
    grad_tokens, grad_qkv, grad_shard, shares, _ = backward(
        wide, narrow, extras, packed, attended, log_total, grad_attended, grad_parts,
        grad_proj_parts, qkv_turned, normed_all, tokens, grad_middle, attn_gain, norm_parts, items,
    )
    grad_qkv, grad_proj, grad_up, grad_down = unpack(
        grad_shard, grad_qkv, proj_weight.shape, up_weight.shape, down_weight.shape
    )
    return (
        output, grad_tokens, shares[0], shares[1], grad_qkv, grad_proj,
        shares[2], shares[3], grad_up, grad_down,
    )


def solution(mesh):
    by_rows = P(("wide", "narrow"), None)
    return jax.shard_map(
        body,
        mesh=mesh,
        in_specs=(
            by_rows, by_rows, P("wide", None), P(), P(), P(None, "narrow"), P("narrow", None),
            P(), P(), P(None, "narrow"), P("narrow", None),
        ),
        out_specs=(
            by_rows, by_rows, P("narrow"), P("narrow"), P(None, "narrow"), P("narrow", None),
            P("narrow"), P("narrow"), P(None, "narrow"), P("narrow", None),
        ),
        check_vma=False,
    )
```
